128 devices in a mesh: seq: 32 (over x, y, core), tp: 4 (over z).
Axes of the slice: x: 4, y: 4, z: 4, core: 2. Of those that a mesh axis runs over, the one named last changes fastest.
Arguments:
- token_ids: int32 [64, 4], replicated, may hold values from 0 to 51199
- embedding: bfloat16 [51200, 2048], P(('seq', 'tp')), may hold values from -8 to 8
- group_of: int32 [64], replicated, may hold values from 0 to 7, as said below
- prefix_len: int32 [8], replicated, may hold values from 1 to 2048, as said below
- tail_len: int32 [64], replicated, may hold values from 1 to 512, as said below
- block_map: int32 [512, 2], P('seq'), may hold values from -1 to 71, as said below
- k_cache: bfloat16 [2, 65536, 2048], P(None, 'seq', 'tp'), may hold values from -100 to 100
- v_cache: bfloat16 [2, 65536, 2048], P(None, 'seq', 'tp'), may hold values from -12 to 12
- ln_gain: float32 [2, 2048], replicated, may hold values from 0.25 to 1.75
- ln_bias: float32 [2, 2048], replicated, may hold values from -1.5 to 1.5
- w_qkv: bfloat16 [2, 2048, 3, 2048], P(None, 'seq', None, 'tp'), may hold values from -0.125 to 0.125
- w_fc1: bfloat16 [2, 2048, 8192], P(None, 'seq', 'tp'), may hold values from -0.125 to 0.125
- b_fc1: float32 [2, 8192], P(None, 'tp'), may hold values from -2.5 to 2.5
- w_out: bfloat16 [2, 2048, 2048], P(None, ('tp', 'seq')), may hold values from -0.125 to 0.125
- w_fc2: bfloat16 [2, 8192, 2048], P(None, ('tp', 'seq')), may hold values from -0.0625 to 0.0625
Outputs:
- hidden_out: float32 [64, 4, 2048], replicated
The draws below stay inside these ranges and needn't reach their ends.
Inputs may be any that keep to these rules, and one draw needn't show every extreme that they name: `group_of`: every group holds exactly 8 requests. `prefix_len`: some group's prompt is 2048 long. `tail_len`: some request's tail is 512 long. `block_map`: row b gives the segment held by cache block b (slots b * 128 to b * 128 + 127): g for group g's prompt, 8 + r for request r's tail, -1 for none; and its rank within the segment. A segment of length L holds ranks 0 to ceil(L / 128) - 1, each in exactly one block; a block with segment -1 has rank 0.
All inputs are finite; a program needn't handle non-finite values.
Results may differ from the reference program's by a relative error of at most 0.04.
The reference program's roundings to bfloat16 on the way count: a program that leaves them out, or rounds other values in their place, can miss the bound.
Values may be sent and summed in bfloat16 or wider, within the bound.
A program may use at most 192 MiB of HBM per device.

```python
import math
import jax
import jax.numpy as jnp
import numpy as np
from jax import lax

D = 2048
HEADS = 32
HEAD_DIM = 64
FF = 8192
ROT = 32
VOCAB = 51200
LAYERS = 2
NEW = 4
RPG = 8
BLOCK = 128
REQS = 64
GROUPS = 8
SLOTS = 65536
NBLK = 512
PREFIX_MAX = 2048
TAIL_MAX = 512


def layout_helper(key):
    key_prompt = jax.random.fold_in(key, 101)
    key_prompt_top = jax.random.fold_in(key, 102)
    key_tail = jax.random.fold_in(key, 103)
    key_tail_top = jax.random.fold_in(key, 104)
    key_order = jax.random.fold_in(key, 105)
    prompt_lengths = jax.random.randint(key_prompt, (GROUPS,), 1, PREFIX_MAX + 1).astype(jnp.int32)
    prompt_lengths = prompt_lengths.at[jax.random.randint(key_prompt_top, (), 0, GROUPS)].set(PREFIX_MAX)
    tail_lengths = jax.random.randint(key_tail, (REQS,), 1, TAIL_MAX + 1).astype(jnp.int32)
    tail_lengths = tail_lengths.at[jax.random.randint(key_tail_top, (), 0, REQS)].set(TAIL_MAX)
    lengths = jnp.concatenate([prompt_lengths, tail_lengths])
    block_counts = (lengths + BLOCK - 1) // BLOCK
    segment_count = GROUPS + REQS
    order = jax.random.permutation(key_order, segment_count).astype(jnp.int32)
    sizes_sorted = block_counts[order]
    ends = jnp.cumsum(sizes_sorted).astype(jnp.int32)
    starts = ends - sizes_sorted
    block_ids = jnp.arange(NBLK, dtype=jnp.int32)
    where_in = jnp.searchsorted(ends, block_ids, side='right').astype(jnp.int32)
    used = where_in < segment_count
    clipped = jnp.minimum(where_in, segment_count - 1)
    segment = jnp.where(used, order[clipped], -1)
    rank = jnp.where(used, block_ids - starts[clipped], 0)
    return (prompt_lengths, tail_lengths, jnp.stack([segment, rank], axis=1).astype(jnp.int32))


def draw_prefix_len(key, part):
    return layout_helper(key)[0]


def draw_tail_len(key, part):
    return layout_helper(key)[1]


def draw_block_map(key, part):
    return layout_helper(key)[2]


def draw_group_of(key, part):
    order = jax.random.permutation(jax.random.fold_in(key, 201), REQS).astype(jnp.int32)
    return (order // RPG).astype(jnp.int32)


def draw_embedding(key, part):
    column = jnp.arange(D, dtype=jnp.float32) / D
    base = jnp.clip(jax.random.normal(key, (VOCAB, D), jnp.float32), -4.0, 4.0)
    spread = 0.6 * jnp.exp(column * jnp.log(3.0))
    return (base * spread[None, :]).astype(jnp.bfloat16)


def draw_k_cache(key, part):
    base = jnp.clip(jax.random.normal(key, (LAYERS, SLOTS, D), jnp.float32), -5.0, 5.0)
    return base.astype(jnp.bfloat16)


def set_ends(values, stream_key, least, high):
    shape = values.shape
    spot = [jax.random.randint(jax.random.fold_in(stream_key, axis), (), 0, shape[axis]) for axis in range(len(shape))]
    values = values.at[tuple(spot)].set(least)
    longest = shape.index(max(shape))
    spot[longest] = (spot[longest] + 1) % shape[longest]
    return values.at[tuple(spot)].set(high)


def levels(key, shape, split, smallest, high):
    def one(position, shards_of):
        steps = jax.random.uniform(jax.random.fold_in(jax.random.fold_in(key, 6), position), (shards_of,), jnp.float32, smallest / len(split), high / len(split))
        return jnp.repeat(jnp.exp(steps), shape[position] // shards_of).reshape((-1,) + (1,) * (len(shape) - position - 1))

    level = one(*split[0])
    for cut in split[1:]:
        level = level * one(*cut)
    return level


def rank_table(count, skew):
    weights = [(1 << 20) // math.isqrt(grade ** skew) + 1 for grade in range(1, count + 1)]
    deviation = 1 + sum(weights) // (1 << 30)
    return np.cumsum(np.array([max(1, weight // deviation) for weight in weights]))


def ranked_ids(stream_key, extent, amount, lean):
    grid = rank_table(amount, lean)
    ticket = jax.random.randint(jax.random.fold_in(stream_key, 1), extent, 0, int(grid[amount - 1]))
    standing = jnp.searchsorted(jnp.asarray(grid, jnp.int32), ticket, side="right")
    return jax.random.permutation(jax.random.fold_in(stream_key, 2), amount)[standing].astype(jnp.int32)


def scatter_about(rng, shape, width, reach, split=(), held_as=jnp.bfloat16):
    loudness = levels(rng, shape, split, -0.22, 0.18) if split else 1.0
    drawn = jax.random.normal(rng, shape, jnp.float32) * width * loudness
    return jnp.minimum(jnp.maximum(drawn, -reach), reach).astype(held_as)


def setup_inputs(seed: int = 0) -> dict:
    keys = jax.random.split(jax.random.key(seed), 16)
    return {
        "token_ids": set_ends(ranked_ids(keys[0], (REQS, NEW), VOCAB, 2), jax.random.fold_in(keys[0], 3), 0, VOCAB - 1).astype(jnp.int32),
        "embedding": draw_embedding(jax.random.fold_in(keys[15], 71), 0),
        "group_of": draw_group_of(jax.random.fold_in(keys[15], 71), 0),
        "prefix_len": draw_prefix_len(jax.random.fold_in(keys[15], 71), 0),
        "tail_len": draw_tail_len(jax.random.fold_in(keys[15], 71), 0),
        "block_map": draw_block_map(jax.random.fold_in(keys[15], 71), 0),
        "k_cache": draw_k_cache(jax.random.fold_in(keys[15], 71), 0),
        "v_cache": scatter_about(keys[7], (LAYERS, SLOTS, D), 2.0, 12.0, ((1, 32), (2, 4))),
        "ln_gain": jnp.clip(1.0 + 0.15 * jax.random.normal(keys[8], (LAYERS, D), jnp.float32), 0.25, 1.75),
        "ln_bias": scatter_about(keys[9], (LAYERS, D), 0.3, 1.5, (), jnp.float32),
        "w_qkv": scatter_about(keys[10], (LAYERS, D, 3, D), D ** -0.5, 0.125, ((1, 32), (3, 4))),
        "w_fc1": scatter_about(keys[11], (LAYERS, D, FF), D ** -0.5, 0.125, ((1, 32), (2, 4))),
        "b_fc1": scatter_about(keys[12], (LAYERS, FF), 0.5, 2.5, ((1, 4),), jnp.float32),
        "w_out": scatter_about(keys[13], (LAYERS, D, D), D ** -0.5, 0.125, ((1, 128),)),
        "w_fc2": scatter_about(keys[14], (LAYERS, FF, D), FF ** -0.5, 0.0625, ((1, 128),)),
    }


def layer_norm(values, gain_row, bias_row):
    average = lax.optimization_barrier(jnp.mean(values, axis=-1, keepdims=True))
    centred = values - average
    variance = lax.optimization_barrier(jnp.mean(centred * centred, axis=-1, keepdims=True))
    return centred * lax.rsqrt(variance + 1e-05) * gain_row + bias_row

def rotary(values, positions):
    half_width = ROT // 2
    frequency = jnp.exp(jnp.arange(half_width, dtype=jnp.float32) * (-2.0 * math.log(10000.0) / ROT))
    angles = positions.astype(jnp.float32)[:, None] * frequency[None, :]
    cosine = jnp.cos(angles)[:, None, :]
    sine_part = jnp.sin(angles)[:, None, :]
    low_half = values[..., :half_width]
    high_half = values[..., half_width:ROT]
    return jnp.concatenate([low_half * cosine - high_half * sine_part, high_half * cosine + low_half * sine_part, values[..., ROT:]], axis=-1)

def rounded_weights(weights):
    return lax.optimization_barrier(weights.astype(jnp.bfloat16)).astype(jnp.float32)

def reference(token_ids, embedding, group_of, prefix_len, tail_len, block_map, k_cache, v_cache, ln_gain, ln_bias, w_qkv, w_fc1, b_fc1, w_out, w_fc2):
    groups = prefix_len.shape[0]
    requests = group_of.shape[0]
    new_tokens = token_ids.shape[1]
    very_negative = -1e+30
    score_scale = 1.0 / math.sqrt(HEAD_DIM)
    prompt_blocks = PREFIX_MAX // BLOCK
    tail_blocks = TAIL_MAX // BLOCK
    widest = max(prompt_blocks, tail_blocks)
    seg_blk = block_map[:, 0]
    rank_blk = block_map[:, 1]
    target = jnp.where(seg_blk >= 0, seg_blk, groups + requests).astype(jnp.int32)
    table = jnp.zeros((groups + requests, widest), jnp.int32).at[target, rank_blk].set(jnp.arange(NBLK, dtype=jnp.int32), mode='drop')
    members = jnp.argsort(group_of, stable=True).astype(jnp.int32).reshape(groups, RPG)
    prompt_valid = jnp.arange(prompt_blocks * BLOCK, dtype=jnp.int32)[None, :] < prefix_len[:, None]
    tail_valid = jnp.arange(tail_blocks * BLOCK, dtype=jnp.int32)[None, :] < tail_len[:, None]
    states = embedding[token_ids].astype(jnp.float32)
    shared_len = prefix_len[group_of]

    def attend(layer_index, queries, keys_new, values_new, token_step):
        key_blocks = k_cache[layer_index].reshape(NBLK, BLOCK, HEADS, HEAD_DIM)
        value_blocks = v_cache[layer_index].reshape(NBLK, BLOCK, HEADS, HEAD_DIM)
        visible = jnp.arange(new_tokens, dtype=jnp.int32) <= token_step

        def one_group(group_index):
            member_ids = members[group_index]
            prompt_ids = table[group_index, :prompt_blocks]
            tail_ids = table[groups + member_ids, :tail_blocks]
            keys_p = key_blocks[prompt_ids].reshape(-1, HEADS, HEAD_DIM).astype(jnp.float32)
            vals_p = value_blocks[prompt_ids].reshape(-1, HEADS, HEAD_DIM).astype(jnp.float32)
            keys_t = key_blocks[tail_ids].reshape(RPG, -1, HEADS, HEAD_DIM).astype(jnp.float32)
            vals_t = value_blocks[tail_ids].reshape(RPG, -1, HEADS, HEAD_DIM).astype(jnp.float32)
            keys_n = keys_new[member_ids].astype(jnp.float32)
            vals_n = values_new[member_ids].astype(jnp.float32)
            query_rows = queries[member_ids].astype(jnp.float32)
            valid_p = prompt_valid[group_index][None, None, :]
            valid_t = tail_valid[member_ids][:, None, :]
            valid_n = visible[None, None, :]
            score_p = jnp.einsum('rhd,shd->rhs', query_rows, keys_p) * score_scale
            score_t = jnp.einsum('rhd,rshd->rhs', query_rows, keys_t) * score_scale
            score_n = jnp.einsum('rhd,rjhd->rhj', query_rows, keys_n) * score_scale
            top_p = lax.optimization_barrier(jnp.max(jnp.where(valid_p, score_p, very_negative), axis=2))
            top_t = lax.optimization_barrier(jnp.max(jnp.where(valid_t, score_t, very_negative), axis=2))
            top_n = lax.optimization_barrier(jnp.max(jnp.where(valid_n, score_n, very_negative), axis=2))
            top_value = jnp.maximum(jnp.maximum(top_p, top_t), top_n)[..., None]
            weight_p = jnp.where(valid_p, jnp.exp(score_p - top_value), 0.0)
            weight_t = jnp.where(valid_t, jnp.exp(score_t - top_value), 0.0)
            weight_n = jnp.where(valid_n, jnp.exp(score_n - top_value), 0.0)
            denom = lax.optimization_barrier(jnp.sum(weight_p, axis=2)) + lax.optimization_barrier(jnp.sum(weight_t, axis=2)) + lax.optimization_barrier(jnp.sum(weight_n, axis=2))
            summed = jnp.einsum('rhs,shd->rhd', rounded_weights(weight_p), vals_p)
            summed = summed + jnp.einsum('rhs,rshd->rhd', rounded_weights(weight_t), vals_t)
            summed = summed + jnp.einsum('rhj,rjhd->rhd', rounded_weights(weight_n), vals_n)
            return summed / denom[..., None]
        outputs = lax.map(one_group, jnp.arange(groups, dtype=jnp.int32))
        gathered = jnp.zeros((requests, HEADS, HEAD_DIM), jnp.float32).at[members.reshape(-1)].set(outputs.reshape(requests, HEADS, HEAD_DIM))
        return gathered.astype(jnp.bfloat16).reshape(requests, D)
    new_keys = [jnp.zeros((requests, new_tokens, HEADS, HEAD_DIM), jnp.bfloat16) for layer_index in range(LAYERS)]
    new_values = [jnp.zeros((requests, new_tokens, HEADS, HEAD_DIM), jnp.bfloat16) for layer_index in range(LAYERS)]
    results = []
    for token_step in range(new_tokens):
        hidden_state = states[:, token_step]
        positions = shared_len + tail_len + token_step
        for layer_index in range(LAYERS):
            normed = layer_norm(hidden_state, ln_gain[layer_index], ln_bias[layer_index]).astype(jnp.bfloat16)
            joined = jnp.dot(normed, w_qkv[layer_index].reshape(D, 3 * D), preferred_element_type=jnp.float32)
            joined = joined.reshape(requests, 3, HEADS, HEAD_DIM)
            queries = rotary(joined[:, 0], positions).astype(jnp.bfloat16)
            key_rows = rotary(joined[:, 1], positions).astype(jnp.bfloat16)
            value_rows = joined[:, 2].astype(jnp.bfloat16)
            new_keys[layer_index] = new_keys[layer_index].at[:, token_step].set(key_rows)
            new_values[layer_index] = new_values[layer_index].at[:, token_step].set(value_rows)
            attended = attend(layer_index, queries, new_keys[layer_index], new_values[layer_index], token_step)
            pre_act = jnp.dot(normed, w_fc1[layer_index], preferred_element_type=jnp.float32) + b_fc1[layer_index]
            activated = jax.nn.gelu(pre_act, approximate=True).astype(jnp.bfloat16)
            update = jnp.dot(attended, w_out[layer_index], preferred_element_type=jnp.float32)
            update = update + jnp.dot(activated, w_fc2[layer_index], preferred_element_type=jnp.float32)
            hidden_state = hidden_state + update
        results.append(hidden_state)
    return jnp.stack(results, axis=1)
```

```python
import functools
import math

import jax
import jax.numpy as jnp
from jax import lax
from jax.experimental import pallas as pl
from jax.experimental.pallas import tpu as pltpu
from jax.sharding import PartitionSpec as P

HEADS = 32
HEAD_DIM = 64
ROT = 32
LAYERS = 2
BLOCK = 128
SPAN = 512
MESH_IDS = pl.DeviceIdType.MESH

very_negative = -1e30


def layer_norm(values, gain_row, bias_row):
    average = jnp.mean(values, axis=-1, keepdims=True)
    centred = values - average
    variance = jnp.mean(centred * centred, axis=-1, keepdims=True)
    return centred * lax.rsqrt(variance + 1e-05) * gain_row + bias_row


def rotary(values, positions):
    half_width = ROT // 2
    frequency = jnp.exp(
        jnp.arange(half_width, dtype=jnp.float32) * (-2.0 * math.log(10000.0) / ROT)
    )
    angles = positions.astype(jnp.float32)[:, None] * frequency[None, :]
    cosine = jnp.cos(angles)[:, None, :]
    sine_part = jnp.sin(angles)[:, None, :]
    low_half = values[..., :half_width]
    high_half = values[..., half_width:ROT]
    return jnp.concatenate(
        [
            low_half * cosine - high_half * sine_part,
            high_half * cosine + low_half * sine_part,
            values[..., ROT:],
        ],
        axis=-1,
    )


def _group_ids(whole, tp_count):
    seq_index = lax.axis_index("seq")
    tp_index = lax.axis_index("tp")
    if whole:
        me = seq_index * tp_count + tp_index

        def peer(j):
            return (j // tp_count, j % tp_count)

    else:
        me = seq_index

        def peer(j):
            return (j, tp_index)

    return me, peer


def _rcopy(src, dst, send_sem, recv_sem, device):
    return pltpu.make_async_remote_copy(
        src_ref=src,
        dst_ref=dst,
        send_sem=send_sem,
        recv_sem=recv_sem,
        device_id=device,
        device_id_type=MESH_IDS,
    )


def _allreduce_kernel(n, whole, tp_count, x_ref, o_ref, rs_buf, ag_buf, s1, r1, s2, r2):
    me, peer = _group_ids(whole, tp_count)

    def start_scatter(i, carry):
        j = lax.rem(me + i, n)
        _rcopy(x_ref.at[j], rs_buf.at[me], s1.at[j], r1.at[me], peer(j)).start()
        return carry

    lax.fori_loop(1, n, start_scatter, 0)

    def gather_sum(i, acc):
        j = lax.rem(me + i, n)
        _rcopy(x_ref.at[j], rs_buf.at[j], s1.at[j], r1.at[j], peer(j)).wait_recv()
        return acc + rs_buf[j].astype(jnp.float32)

    total = lax.fori_loop(1, n, gather_sum, x_ref[me].astype(jnp.float32))
    ag_buf[me] = total.astype(ag_buf.dtype)

    def start_gather(i, carry):
        j = lax.rem(me + i, n)
        _rcopy(ag_buf.at[me], ag_buf.at[me], s2.at[j], r2.at[me], peer(j)).start()
        return carry

    lax.fori_loop(1, n, start_gather, 0)

    def finish(i, carry):
        j = lax.rem(me + i, n)
        _rcopy(ag_buf.at[j], ag_buf.at[j], s2.at[j], r2.at[j], peer(j)).wait_recv()
        _rcopy(x_ref.at[j], rs_buf.at[me], s1.at[j], r1.at[me], peer(j)).wait_send()
        _rcopy(ag_buf.at[me], ag_buf.at[me], s2.at[j], r2.at[me], peer(j)).wait_send()
        return carry

    lax.fori_loop(1, n, finish, 0)
    o_ref[...] = ag_buf[...]


def allreduce(x, whole, tp_count):
    n = x.shape[0]
    return pl.pallas_call(
        functools.partial(_allreduce_kernel, n, whole, tp_count),
        out_shape=jax.ShapeDtypeStruct(x.shape, x.dtype),
        in_specs=[pl.BlockSpec(memory_space=pltpu.VMEM)],
        out_specs=pl.BlockSpec(memory_space=pltpu.VMEM),
        scratch_shapes=[
            pltpu.VMEM(x.shape, x.dtype),
            pltpu.VMEM(x.shape, x.dtype),
            pltpu.SemaphoreType.DMA((n,)),
            pltpu.SemaphoreType.DMA((n,)),
            pltpu.SemaphoreType.DMA((n,)),
            pltpu.SemaphoreType.DMA((n,)),
        ],
        compiler_params=pltpu.CompilerParams(has_side_effects=True),
    )(x)


def _all_to_all_kernel(n, whole, tp_count, x_ref, o_ref, buf, s1, r1):
    me, peer = _group_ids(whole, tp_count)

    def start(i, carry):
        j = lax.rem(me + i, n)
        _rcopy(x_ref.at[j], buf.at[me], s1.at[j], r1.at[me], peer(j)).start()
        return carry

    lax.fori_loop(1, n, start, 0)

    def finish(i, carry):
        j = lax.rem(me + i, n)
        _rcopy(x_ref.at[j], buf.at[j], s1.at[j], r1.at[j], peer(j)).wait_recv()
        _rcopy(x_ref.at[j], buf.at[me], s1.at[j], r1.at[me], peer(j)).wait_send()
        return carry

    lax.fori_loop(1, n, finish, 0)
    buf[me] = x_ref[me]
    o_ref[...] = buf[...]


def all_to_all(x, whole, tp_count):
    n = x.shape[0]
    return pl.pallas_call(
        functools.partial(_all_to_all_kernel, n, whole, tp_count),
        out_shape=jax.ShapeDtypeStruct(x.shape, x.dtype),
        in_specs=[pl.BlockSpec(memory_space=pltpu.VMEM)],
        out_specs=pl.BlockSpec(memory_space=pltpu.VMEM),
        scratch_shapes=[
            pltpu.VMEM(x.shape, x.dtype),
            pltpu.SemaphoreType.DMA((n,)),
            pltpu.SemaphoreType.DMA((n,)),
        ],
        compiler_params=pltpu.CompilerParams(has_side_effects=True),
    )(x)


def per_device(
    token_ids,
    embedding,
    group_of,
    prefix_len,
    tail_len,
    block_map,
    k_cache,
    v_cache,
    ln_gain,
    ln_bias,
    w_qkv,
    w_fc1,
    b_fc1,
    w_out,
    w_fc2,
):
    tp_count = lax.axis_size("tp")
    seq_count = lax.axis_size("seq")
    all_count = tp_count * seq_count
    seq_index = lax.axis_index("seq")
    tp_index = lax.axis_index("tp")
    requests = token_ids.shape[0]
    new_tokens = token_ids.shape[1]
    rows = requests * new_tokens
    groups = prefix_len.shape[0]
    heads_local = HEADS // tp_count
    width = embedding.shape[1]
    score_scale = 1.0 / math.sqrt(HEAD_DIM)

    vocab_rows = embedding.shape[0]
    first_row = (seq_index * tp_count + tp_index) * vocab_rows
    local_ids = token_ids.reshape(-1) - first_row
    inside = (local_ids >= 0) & (local_ids < vocab_rows)
    picked = jnp.take(embedding, jnp.clip(local_ids, 0, vocab_rows - 1), axis=0)
    picked = jnp.where(inside[:, None], picked, jnp.zeros_like(picked))
    start_states = allreduce(picked.reshape(all_count, -1, 128), True, tp_count)
    hidden_state = start_states.reshape(rows, width).astype(jnp.float32)

    group_hit = group_of[:, None] == jnp.arange(groups, dtype=jnp.int32)[None, :]
    shared_len = jnp.sum(jnp.where(group_hit, prefix_len[None, :], 0), axis=1)
    base_positions = shared_len + tail_len
    positions = (base_positions[:, None] + jnp.arange(new_tokens, dtype=jnp.int32)[None, :]).reshape(-1)
    seg_len = jnp.concatenate([prefix_len, tail_len])
    seg_count = seg_len.shape[0]
    blocks_local = block_map.shape[0]
    seg_blk = block_map[:, 0]
    rank_blk = block_map[:, 1]
    seg_hit = seg_blk[:, None] == jnp.arange(seg_count, dtype=jnp.int32)[None, :]
    len_blk = jnp.sum(jnp.where(seg_hit, seg_len[None, :], 0), axis=1)
    slot_positions = rank_blk[:, None] * BLOCK + jnp.arange(BLOCK, dtype=jnp.int32)[None, :]
    live_slot = ((seg_blk[:, None] >= 0) & (slot_positions < len_blk[:, None])).reshape(-1)
    seg_slot = jnp.broadcast_to(seg_blk[:, None], (blocks_local, BLOCK)).reshape(-1)
    own_tail = seg_slot[None, :] == (groups + jnp.arange(requests, dtype=jnp.int32))[:, None]
    own_prompt = seg_slot[None, :] == group_of[:, None]
    allowed = (own_tail | own_prompt) & live_slot[None, :]
    allowed = jnp.repeat(allowed, new_tokens, axis=0)
    step_count = allowed.shape[1] // SPAN
    allowed_steps = allowed.reshape(rows, step_count, SPAN).transpose(1, 0, 2)

    rows_local = w_qkv.shape[1]
    unit_count = w_fc2.shape[1]
    sub_width = w_out.shape[1]
    pieces = HEAD_DIM // sub_width
    my_head = seq_index // pieces
    my_piece = seq_index % pieces
    proj_width = 3 * heads_local * HEAD_DIM
    causal = (
        jnp.arange(new_tokens, dtype=jnp.int32)[None, :]
        <= jnp.arange(new_tokens, dtype=jnp.int32)[:, None]
    )
    for layer_index in range(LAYERS):
        normed = layer_norm(hidden_state, ln_gain[layer_index], ln_bias[layer_index]).astype(
            jnp.bfloat16
        )
        my_rows = lax.dynamic_slice_in_dim(normed, seq_index * rows_local, rows_local, 1)
        part_proj = jnp.dot(
            my_rows,
            w_qkv[layer_index].reshape(rows_local, -1),
            preferred_element_type=jnp.float32,
        )
        part_fc1 = jnp.dot(my_rows, w_fc1[layer_index], preferred_element_type=jnp.float32)
        joined = jnp.concatenate([part_proj, part_fc1], axis=1)
        joined = allreduce(joined.reshape(seq_count, rows // seq_count, -1), False, tp_count)
        joined = joined.reshape(rows, -1)
        attention_proj = joined[:, :proj_width]
        fc1_all = joined[:, proj_width:]
        pre_act = lax.dynamic_slice_in_dim(fc1_all, seq_index * unit_count, unit_count, 1)
        pre_act = (
            pre_act
            + lax.dynamic_slice_in_dim(b_fc1[layer_index], seq_index * unit_count, unit_count, 0)[
                None, :
            ]
        )
        activated = jax.nn.gelu(pre_act, approximate=True).astype(jnp.bfloat16)
        attention_proj = attention_proj.reshape(rows, 3, heads_local, HEAD_DIM)
        queries = rotary(attention_proj[:, 0], positions).astype(jnp.bfloat16)
        key_rows = rotary(attention_proj[:, 1], positions).astype(jnp.bfloat16)
        value_rows = attention_proj[:, 2].astype(jnp.bfloat16)
        key_steps = k_cache[layer_index].reshape(step_count, SPAN, heads_local, HEAD_DIM)
        value_steps = v_cache[layer_index].reshape(step_count, SPAN, heads_local, HEAD_DIM)

        def cache_step(carry, inputs):
            run_max, run_sum, run_out = carry
            key_block, value_block, allow_block = inputs
            scores = (
                jnp.einsum("rhd,shd->hrs", queries, key_block, preferred_element_type=jnp.float32)
                * score_scale
            )
            scores = jnp.where(allow_block[None], scores, very_negative)
            next_max = jnp.maximum(run_max, jnp.max(scores, axis=2))
            weights = jnp.where(allow_block[None], jnp.exp(scores - next_max[..., None]), 0.0)
            shrink = jnp.exp(run_max - next_max)
            next_sum = run_sum * shrink + jnp.sum(weights, axis=2)
            next_out = run_out * shrink[..., None] + jnp.einsum(
                "hrs,shd->hrd",
                weights.astype(jnp.bfloat16),
                value_block,
                preferred_element_type=jnp.float32,
            )
            return ((next_max, next_sum, next_out), None)

        start_carry = (
            jnp.full((heads_local, rows), very_negative, jnp.float32),
            jnp.zeros((heads_local, rows), jnp.float32),
            jnp.zeros((heads_local, rows, HEAD_DIM), jnp.float32),
        )
        (part_max, part_sum, part_out), unused = lax.scan(
            cache_step, start_carry, (key_steps, value_steps, allowed_steps)
        )
        out_pieces = (
            part_out.reshape(heads_local, rows, pieces, sub_width)
            .transpose(0, 2, 3, 1)
            .reshape(heads_local * pieces, sub_width, rows)
        )
        max_rows = jnp.repeat(part_max, pieces, axis=0)[:, None, :]
        sum_rows = jnp.repeat(part_sum, pieces, axis=0)[:, None, :]
        pad_rows = jnp.zeros((heads_local * pieces, 6, rows), jnp.float32)
        message = jnp.concatenate([out_pieces, max_rows, sum_rows, pad_rows], axis=1)
        received = all_to_all(message, False, tp_count)
        got_out = received[:, :sub_width, :]
        got_max = received[:, sub_width, :]
        got_sum = received[:, sub_width + 1, :]

        q4 = queries.reshape(requests, new_tokens, heads_local, HEAD_DIM)
        k4 = key_rows.reshape(requests, new_tokens, heads_local, HEAD_DIM)
        v4 = value_rows.reshape(requests, new_tokens, heads_local, HEAD_DIM)
        q_h = lax.dynamic_index_in_dim(q4, my_head, 2, keepdims=False)
        k_h = lax.dynamic_index_in_dim(k4, my_head, 2, keepdims=False)
        v_h = lax.dynamic_index_in_dim(v4, my_head, 2, keepdims=False)
        v_h = lax.dynamic_slice_in_dim(v_h, my_piece * sub_width, sub_width, 2)
        fresh_scores = (
            jnp.einsum("rtd,rud->rtu", q_h, k_h, preferred_element_type=jnp.float32) * score_scale
        )
        fresh_scores = jnp.where(causal[None], fresh_scores, very_negative)
        fresh_max = jnp.max(fresh_scores, axis=2)
        fresh_weights = jnp.where(causal[None], jnp.exp(fresh_scores - fresh_max[..., None]), 0.0)
        fresh_sum = jnp.sum(fresh_weights, axis=2)
        fresh_out = jnp.einsum(
            "rtu,rud->rtd",
            fresh_weights.astype(jnp.bfloat16),
            v_h,
            preferred_element_type=jnp.float32,
        )
        fresh_max = fresh_max.reshape(rows)
        fresh_sum = fresh_sum.reshape(rows)
        fresh_out = fresh_out.reshape(rows, sub_width)

        top = jnp.maximum(jnp.max(got_max, axis=0), fresh_max)
        scale_cache = jnp.exp(got_max - top[None, :])
        scale_fresh = jnp.exp(fresh_max - top)
        denom = jnp.sum(got_sum * scale_cache, axis=0) + fresh_sum * scale_fresh
        numer = jnp.sum(got_out * scale_cache[:, None, :], axis=0).T + fresh_out * scale_fresh[:, None]
        my_cols = (numer / denom[:, None]).astype(jnp.bfloat16)

        update = jnp.dot(my_cols, w_out[layer_index], preferred_element_type=jnp.float32)
        update = update + jnp.dot(activated, w_fc2[layer_index], preferred_element_type=jnp.float32)
        update = allreduce(update.reshape(all_count, -1, 128), True, tp_count)
        hidden_state = hidden_state + update.reshape(rows, width)
    return hidden_state.reshape(requests, new_tokens, width)


def solution(mesh):
    in_specs = (
        P(),
        P(("seq", "tp"), None),
        P(),
        P(),
        P(),
        P("seq", None),
        P(None, "seq", "tp"),
        P(None, "seq", "tp"),
        P(),
        P(),
        P(None, "seq", None, "tp"),
        P(None, "seq", "tp"),
        P(None, "tp"),
        P(None, ("tp", "seq"), None),
        P(None, ("tp", "seq"), None),
    )
    out_specs = P()
    return jax.shard_map(
        per_device, mesh=mesh, in_specs=in_specs, out_specs=out_specs, check_vma=False
    )
```

```python
import functools
import math

import jax
import jax.numpy as jnp
from jax import lax
from jax.experimental import pallas as pl
from jax.experimental.pallas import tpu as pltpu
from jax.sharding import PartitionSpec as P

HEADS = 32
HEAD_DIM = 64
ROT = 32
LAYERS = 2
BLOCK = 128
SPAN = 512
MESH_IDS = pl.DeviceIdType.MESH

very_negative = -1e30


def layer_norm(values, gain_row, bias_row):
    average = jnp.mean(values, axis=-1, keepdims=True)
    centred = values - average
    variance = jnp.mean(centred * centred, axis=-1, keepdims=True)
    return centred * lax.rsqrt(variance + 1e-05) * gain_row + bias_row


def rotary(values, positions):
    half_width = ROT // 2
    frequency = jnp.exp(
        jnp.arange(half_width, dtype=jnp.float32) * (-2.0 * math.log(10000.0) / ROT)
    )
    angles = positions.astype(jnp.float32)[:, None] * frequency[None, :]
    cosine = jnp.cos(angles)[:, None, :]
    sine_part = jnp.sin(angles)[:, None, :]
    low_half = values[..., :half_width]
    high_half = values[..., half_width:ROT]
    return jnp.concatenate(
        [
            low_half * cosine - high_half * sine_part,
            high_half * cosine + low_half * sine_part,
            values[..., ROT:],
        ],
        axis=-1,
    )


def _group_ids(whole, tp_count):
    seq_index = lax.axis_index("seq")
    tp_index = lax.axis_index("tp")
    if whole:
        me = seq_index * tp_count + tp_index

        def peer(j):
            return (j // tp_count, j % tp_count)

    else:
        me = seq_index

        def peer(j):
            return (j, tp_index)

    return me, peer


def _rcopy(src, dst, send_sem, recv_sem, device):
    return pltpu.make_async_remote_copy(
        src_ref=src,
        dst_ref=dst,
        send_sem=send_sem,
        recv_sem=recv_sem,
        device_id=device,
        device_id_type=MESH_IDS,
    )


def _allreduce_kernel(n, whole, tp_count, x_ref, o_ref, rs_buf, ag_buf, s1, r1, s2, r2):
    me, peer = _group_ids(whole, tp_count)

    def start_scatter(i, carry):
        j = lax.rem(me + i, n)
        _rcopy(x_ref.at[j], rs_buf.at[me], s1.at[j], r1.at[me], peer(j)).start()
        return carry

    lax.fori_loop(1, n, start_scatter, 0)

    def gather_sum(i, acc):
        j = lax.rem(me + i, n)
        _rcopy(x_ref.at[j], rs_buf.at[j], s1.at[j], r1.at[j], peer(j)).wait_recv()
        return acc + rs_buf[j].astype(jnp.float32)

    total = lax.fori_loop(1, n, gather_sum, x_ref[me].astype(jnp.float32))
    ag_buf[me] = total.astype(ag_buf.dtype)

    def start_gather(i, carry):
        j = lax.rem(me + i, n)
        _rcopy(ag_buf.at[me], ag_buf.at[me], s2.at[j], r2.at[me], peer(j)).start()
        return carry

    lax.fori_loop(1, n, start_gather, 0)

    def finish(i, carry):
        j = lax.rem(me + i, n)
        _rcopy(ag_buf.at[j], ag_buf.at[j], s2.at[j], r2.at[j], peer(j)).wait_recv()
        _rcopy(x_ref.at[j], rs_buf.at[me], s1.at[j], r1.at[me], peer(j)).wait_send()
        _rcopy(ag_buf.at[me], ag_buf.at[me], s2.at[j], r2.at[me], peer(j)).wait_send()
        return carry

    lax.fori_loop(1, n, finish, 0)
    o_ref[...] = ag_buf[...]


def allreduce(x, whole, tp_count):
    n = x.shape[0]
    return pl.pallas_call(
        functools.partial(_allreduce_kernel, n, whole, tp_count),
        out_shape=jax.ShapeDtypeStruct(x.shape, x.dtype),
        in_specs=[pl.BlockSpec(memory_space=pltpu.VMEM)],
        out_specs=pl.BlockSpec(memory_space=pltpu.VMEM),
        scratch_shapes=[
            pltpu.VMEM(x.shape, x.dtype),
            pltpu.VMEM(x.shape, x.dtype),
            pltpu.SemaphoreType.DMA((n,)),
            pltpu.SemaphoreType.DMA((n,)),
            pltpu.SemaphoreType.DMA((n,)),
            pltpu.SemaphoreType.DMA((n,)),
        ],
        compiler_params=pltpu.CompilerParams(has_side_effects=True),
    )(x)


def _all_to_all_kernel(n, whole, tp_count, x_ref, o_ref, buf, s1, r1):
    me, peer = _group_ids(whole, tp_count)

    def start(i, carry):
        j = lax.rem(me + i, n)
        _rcopy(x_ref.at[j], buf.at[me], s1.at[j], r1.at[me], peer(j)).start()
        return carry

    lax.fori_loop(1, n, start, 0)

    def finish(i, carry):
        j = lax.rem(me + i, n)
        _rcopy(x_ref.at[j], buf.at[j], s1.at[j], r1.at[j], peer(j)).wait_recv()
        _rcopy(x_ref.at[j], buf.at[me], s1.at[j], r1.at[me], peer(j)).wait_send()
        return carry

    lax.fori_loop(1, n, finish, 0)
    buf[me] = x_ref[me]
    o_ref[...] = buf[...]


def all_to_all(x, whole, tp_count):
    n = x.shape[0]
    return pl.pallas_call(
        functools.partial(_all_to_all_kernel, n, whole, tp_count),
        out_shape=jax.ShapeDtypeStruct(x.shape, x.dtype),
        in_specs=[pl.BlockSpec(memory_space=pltpu.VMEM)],
        out_specs=pl.BlockSpec(memory_space=pltpu.VMEM),
        scratch_shapes=[
            pltpu.VMEM(x.shape, x.dtype),
            pltpu.SemaphoreType.DMA((n,)),
            pltpu.SemaphoreType.DMA((n,)),
        ],
        compiler_params=pltpu.CompilerParams(has_side_effects=True),
    )(x)


def per_device(
    token_ids,
    embedding,
    group_of,
    prefix_len,
    tail_len,
    block_map,
    k_cache,
    v_cache,
    ln_gain,
    ln_bias,
    w_qkv,
    w_fc1,
    b_fc1,
    w_out,
    w_fc2,
):
    tp_count = lax.axis_size("tp")
    seq_count = lax.axis_size("seq")
    all_count = tp_count * seq_count
    seq_index = lax.axis_index("seq")
    tp_index = lax.axis_index("tp")
    requests = token_ids.shape[0]
    new_tokens = token_ids.shape[1]
    rows = requests * new_tokens
    groups = prefix_len.shape[0]
    heads_local = HEADS // tp_count
    width = embedding.shape[1]
    score_scale = 1.0 / math.sqrt(HEAD_DIM)

    vocab_rows = embedding.shape[0]
    first_row = (seq_index * tp_count + tp_index) * vocab_rows
    local_ids = token_ids.reshape(-1) - first_row
    inside = (local_ids >= 0) & (local_ids < vocab_rows)
    picked = jnp.take(embedding, jnp.clip(local_ids, 0, vocab_rows - 1), axis=0)
    picked = jnp.where(inside[:, None], picked, jnp.zeros_like(picked))
    start_states = allreduce(picked.reshape(all_count, -1, 128), True, tp_count)
    hidden_state = start_states.reshape(rows, width).astype(jnp.float32)

    group_hit = group_of[:, None] == jnp.arange(groups, dtype=jnp.int32)[None, :]
    shared_len = jnp.sum(jnp.where(group_hit, prefix_len[None, :], 0), axis=1)
    base_positions = shared_len + tail_len
    positions = (base_positions[:, None] + jnp.arange(new_tokens, dtype=jnp.int32)[None, :]).reshape(-1)
    seg_len = jnp.concatenate([prefix_len, tail_len])
    seg_count = seg_len.shape[0]
    blocks_local = block_map.shape[0]
    seg_blk = block_map[:, 0]
    rank_blk = block_map[:, 1]
    seg_hit = seg_blk[:, None] == jnp.arange(seg_count, dtype=jnp.int32)[None, :]
    len_blk = jnp.sum(jnp.where(seg_hit, seg_len[None, :], 0), axis=1)
    slot_positions = rank_blk[:, None] * BLOCK + jnp.arange(BLOCK, dtype=jnp.int32)[None, :]
    live_slot = ((seg_blk[:, None] >= 0) & (slot_positions < len_blk[:, None])).reshape(-1)
    seg_slot = jnp.broadcast_to(seg_blk[:, None], (blocks_local, BLOCK)).reshape(-1)
    own_tail = seg_slot[None, :] == (groups + jnp.arange(requests, dtype=jnp.int32))[:, None]
    own_prompt = seg_slot[None, :] == group_of[:, None]
    allowed = (own_tail | own_prompt) & live_slot[None, :]
    allowed = jnp.repeat(allowed, new_tokens, axis=0)
    step_count = allowed.shape[1] // SPAN
    allowed_steps = allowed.reshape(rows, step_count, SPAN).transpose(1, 0, 2)

    rows_local = w_qkv.shape[1]
    unit_count = w_fc2.shape[1]
    sub_width = w_out.shape[1]
    pieces = HEAD_DIM // sub_width
    my_head = seq_index // pieces
    my_piece = seq_index % pieces
    causal = (
        jnp.arange(new_tokens, dtype=jnp.int32)[None, :]
        <= jnp.arange(new_tokens, dtype=jnp.int32)[:, None]
    )

    head_of = jnp.arange(seq_count, dtype=jnp.int32) // pieces
    qkv_heads = w_qkv.reshape(LAYERS, rows_local, 3, heads_local, HEAD_DIM)
    qkv_part = jnp.take(qkv_heads, head_of, axis=3)
    qkv_part = qkv_part.transpose(3, 0, 1, 2, 4).reshape(seq_count, LAYERS, rows_local, 3 * HEAD_DIM)
    fc1_part = w_fc1.reshape(LAYERS, rows_local, seq_count, unit_count).transpose(2, 0, 1, 3)
    message = jnp.concatenate([qkv_part, fc1_part], axis=-1)
    cols_mine = message.shape[-1]
    got_w = all_to_all(message.reshape(seq_count, LAYERS * rows_local, cols_mine), False, tp_count)
    w_mine = (
        got_w.reshape(seq_count, LAYERS, rows_local, cols_mine)
        .transpose(1, 0, 2, 3)
        .reshape(LAYERS, seq_count * rows_local, cols_mine)
    )
    for layer_index in range(LAYERS):
        normed = layer_norm(hidden_state, ln_gain[layer_index], ln_bias[layer_index]).astype(
            jnp.bfloat16
        )
        local = jnp.dot(normed, w_mine[layer_index], preferred_element_type=jnp.float32)
        q_h = rotary(local[:, None, 0:HEAD_DIM], positions)[:, 0].astype(jnp.bfloat16)
        k_h = rotary(local[:, None, HEAD_DIM : 2 * HEAD_DIM], positions)[:, 0].astype(jnp.bfloat16)
        v_h = local[:, 2 * HEAD_DIM : 3 * HEAD_DIM].astype(jnp.bfloat16)
        pre_act = local[:, 3 * HEAD_DIM :]
        pre_act = (
            pre_act
            + lax.dynamic_slice_in_dim(b_fc1[layer_index], seq_index * unit_count, unit_count, 0)[
                None, :
            ]
        )
        activated = jax.nn.gelu(pre_act, approximate=True).astype(jnp.bfloat16)
        q_piece = lax.dynamic_slice_in_dim(q_h, my_piece * sub_width, sub_width, 1).T
        q_all = all_to_all(jnp.broadcast_to(q_piece[None], (seq_count,) + q_piece.shape), False, tp_count)
        queries = (
            q_all.reshape(heads_local, pieces, sub_width, rows)
            .transpose(3, 0, 1, 2)
            .reshape(rows, heads_local, HEAD_DIM)
        )
        key_steps = k_cache[layer_index].reshape(step_count, SPAN, heads_local, HEAD_DIM)
        value_steps = v_cache[layer_index].reshape(step_count, SPAN, heads_local, HEAD_DIM)

        def cache_step(carry, inputs):
            run_max, run_sum, run_out = carry
            key_block, value_block, allow_block = inputs
            scores = (
                jnp.einsum("rhd,shd->hrs", queries, key_block, preferred_element_type=jnp.float32)
                * score_scale
            )
            scores = jnp.where(allow_block[None], scores, very_negative)
            next_max = jnp.maximum(run_max, jnp.max(scores, axis=2))
            weights = jnp.where(allow_block[None], jnp.exp(scores - next_max[..., None]), 0.0)
            shrink = jnp.exp(run_max - next_max)
            next_sum = run_sum * shrink + jnp.sum(weights, axis=2)
            next_out = run_out * shrink[..., None] + jnp.einsum(
                "hrs,shd->hrd",
                weights.astype(jnp.bfloat16),
                value_block,
                preferred_element_type=jnp.float32,
            )
            return ((next_max, next_sum, next_out), None)

        start_carry = (
            jnp.full((heads_local, rows), very_negative, jnp.float32),
            jnp.zeros((heads_local, rows), jnp.float32),
            jnp.zeros((heads_local, rows, HEAD_DIM), jnp.float32),
        )
        (part_max, part_sum, part_out), unused = lax.scan(
            cache_step, start_carry, (key_steps, value_steps, allowed_steps)
        )
        out_pieces = (
            part_out.reshape(heads_local, rows, pieces, sub_width)
            .transpose(0, 2, 3, 1)
            .reshape(heads_local * pieces, sub_width, rows)
        )
        max_rows = jnp.repeat(part_max, pieces, axis=0)[:, None, :]
        sum_rows = jnp.repeat(part_sum, pieces, axis=0)[:, None, :]
        pad_rows = jnp.zeros((heads_local * pieces, 6, rows), jnp.float32)
        message = jnp.concatenate([out_pieces, max_rows, sum_rows, pad_rows], axis=1)
        received = all_to_all(message, False, tp_count)
        got_out = received[:, :sub_width, :]
        got_max = received[:, sub_width, :]
        got_sum = received[:, sub_width + 1, :]

        q_h = q_h.reshape(requests, new_tokens, HEAD_DIM)
        k_h = k_h.reshape(requests, new_tokens, HEAD_DIM)
        v_h = lax.dynamic_slice_in_dim(v_h, my_piece * sub_width, sub_width, 1)
        v_h = v_h.reshape(requests, new_tokens, sub_width)
        fresh_scores = (
            jnp.einsum("rtd,rud->rtu", q_h, k_h, preferred_element_type=jnp.float32) * score_scale
        )
        fresh_scores = jnp.where(causal[None], fresh_scores, very_negative)
        fresh_max = jnp.max(fresh_scores, axis=2)
        fresh_weights = jnp.where(causal[None], jnp.exp(fresh_scores - fresh_max[..., None]), 0.0)
        fresh_sum = jnp.sum(fresh_weights, axis=2)
        fresh_out = jnp.einsum(
            "rtu,rud->rtd",
            fresh_weights.astype(jnp.bfloat16),
            v_h,
            preferred_element_type=jnp.float32,
        )
        fresh_max = fresh_max.reshape(rows)
        fresh_sum = fresh_sum.reshape(rows)
        fresh_out = fresh_out.reshape(rows, sub_width)

        top = jnp.maximum(jnp.max(got_max, axis=0), fresh_max)
        scale_cache = jnp.exp(got_max - top[None, :])
        scale_fresh = jnp.exp(fresh_max - top)
        denom = jnp.sum(got_sum * scale_cache, axis=0) + fresh_sum * scale_fresh
        numer = jnp.sum(got_out * scale_cache[:, None, :], axis=0).T + fresh_out * scale_fresh[:, None]
        my_cols = (numer / denom[:, None]).astype(jnp.bfloat16)

        update = jnp.dot(my_cols, w_out[layer_index], preferred_element_type=jnp.float32)
        update = update + jnp.dot(activated, w_fc2[layer_index], preferred_element_type=jnp.float32)
        update = allreduce(update.reshape(all_count, -1, 128), True, tp_count)
        hidden_state = hidden_state + update.reshape(rows, width)
    return hidden_state.reshape(requests, new_tokens, width)


def solution(mesh):
    in_specs = (
        P(),
        P(("seq", "tp"), None),
        P(),
        P(),
        P(),
        P("seq", None),
        P(None, "seq", "tp"),
        P(None, "seq", "tp"),
        P(),
        P(),
        P(None, "seq", None, "tp"),
        P(None, "seq", "tp"),
        P(None, "tp"),
        P(None, ("tp", "seq"), None),
        P(None, ("tp", "seq"), None),
    )
    out_specs = P()
    return jax.shard_map(
        per_device, mesh=mesh, in_specs=in_specs, out_specs=out_specs, check_vma=False
    )
```

```python
import functools
import math

import jax
import jax.numpy as jnp
from jax import lax
from jax.experimental import pallas as pl
from jax.experimental.pallas import tpu as pltpu
from jax.sharding import PartitionSpec as P

HEADS = 32
HEAD_DIM = 64
ROT = 32
LAYERS = 2
BLOCK = 128
SPAN = 512
MESH_IDS = pl.DeviceIdType.MESH

very_negative = -1e30


def layer_norm(values, gain_row, bias_row):
    average = jnp.mean(values, axis=-1, keepdims=True)
    centred = values - average
    variance = jnp.mean(centred * centred, axis=-1, keepdims=True)
    return centred * lax.rsqrt(variance + 1e-05) * gain_row + bias_row


def rotary(values, positions):
    half_width = ROT // 2
    frequency = jnp.exp(
        jnp.arange(half_width, dtype=jnp.float32) * (-2.0 * math.log(10000.0) / ROT)
    )
    angles = positions.astype(jnp.float32)[:, None] * frequency[None, :]
    cosine = jnp.cos(angles)[:, None, :]
    sine_part = jnp.sin(angles)[:, None, :]
    low_half = values[..., :half_width]
    high_half = values[..., half_width:ROT]
    return jnp.concatenate(
        [
            low_half * cosine - high_half * sine_part,
            high_half * cosine + low_half * sine_part,
            values[..., ROT:],
        ],
        axis=-1,
    )


def _group_ids(whole, tp_count):
    seq_index = lax.axis_index("seq")
    tp_index = lax.axis_index("tp")
    if whole:
        me = seq_index * tp_count + tp_index

        def peer(j):
            return (j // tp_count, j % tp_count)

    else:
        me = seq_index

        def peer(j):
            return (j, tp_index)

    return me, peer


def _rcopy(src, dst, send_sem, recv_sem, device):
    return pltpu.make_async_remote_copy(
        src_ref=src,
        dst_ref=dst,
        send_sem=send_sem,
        recv_sem=recv_sem,
        device_id=device,
        device_id_type=MESH_IDS,
    )


def _allreduce_kernel(n, whole, tp_count, x_ref, o_ref, rs_buf, ag_buf, s1, r1, s2, r2):
    me, peer = _group_ids(whole, tp_count)

    def start_scatter(i, carry):
        j = lax.rem(me + i, n)
        _rcopy(x_ref.at[j], rs_buf.at[me], s1.at[j], r1.at[me], peer(j)).start()
        return carry

    lax.fori_loop(1, n, start_scatter, 0)

    def gather_sum(i, acc):
        j = lax.rem(me + i, n)
        _rcopy(x_ref.at[j], rs_buf.at[j], s1.at[j], r1.at[j], peer(j)).wait_recv()
        return acc + rs_buf[j].astype(jnp.float32)

    total = lax.fori_loop(1, n, gather_sum, x_ref[me].astype(jnp.float32))
    ag_buf[me] = total.astype(ag_buf.dtype)

    def start_gather(i, carry):
        j = lax.rem(me + i, n)
        _rcopy(ag_buf.at[me], ag_buf.at[me], s2.at[j], r2.at[me], peer(j)).start()
        return carry

    lax.fori_loop(1, n, start_gather, 0)

    def finish(i, carry):
        j = lax.rem(me + i, n)
        _rcopy(ag_buf.at[j], ag_buf.at[j], s2.at[j], r2.at[j], peer(j)).wait_recv()
        _rcopy(x_ref.at[j], rs_buf.at[me], s1.at[j], r1.at[me], peer(j)).wait_send()
        _rcopy(ag_buf.at[me], ag_buf.at[me], s2.at[j], r2.at[me], peer(j)).wait_send()
        return carry

    lax.fori_loop(1, n, finish, 0)
    o_ref[...] = ag_buf[...]


def allreduce(x, whole, tp_count):
    n = x.shape[0]
    return pl.pallas_call(
        functools.partial(_allreduce_kernel, n, whole, tp_count),
        out_shape=jax.ShapeDtypeStruct(x.shape, x.dtype),
        in_specs=[pl.BlockSpec(memory_space=pltpu.VMEM)],
        out_specs=pl.BlockSpec(memory_space=pltpu.VMEM),
        scratch_shapes=[
            pltpu.VMEM(x.shape, x.dtype),
            pltpu.VMEM(x.shape, x.dtype),
            pltpu.SemaphoreType.DMA((n,)),
            pltpu.SemaphoreType.DMA((n,)),
            pltpu.SemaphoreType.DMA((n,)),
            pltpu.SemaphoreType.DMA((n,)),
        ],
        compiler_params=pltpu.CompilerParams(has_side_effects=True),
    )(x)


def _all_to_all_kernel(n, whole, tp_count, x_ref, o_ref, buf, s1, r1):
    me, peer = _group_ids(whole, tp_count)

    def start(i, carry):
        j = lax.rem(me + i, n)
        _rcopy(x_ref.at[j], buf.at[me], s1.at[j], r1.at[me], peer(j)).start()
        return carry

    lax.fori_loop(1, n, start, 0)

    def finish(i, carry):
        j = lax.rem(me + i, n)
        _rcopy(x_ref.at[j], buf.at[j], s1.at[j], r1.at[j], peer(j)).wait_recv()
        _rcopy(x_ref.at[j], buf.at[me], s1.at[j], r1.at[me], peer(j)).wait_send()
        return carry

    lax.fori_loop(1, n, finish, 0)
    buf[me] = x_ref[me]
    o_ref[...] = buf[...]


def all_to_all(x, whole, tp_count):
    n = x.shape[0]
    return pl.pallas_call(
        functools.partial(_all_to_all_kernel, n, whole, tp_count),
        out_shape=jax.ShapeDtypeStruct(x.shape, x.dtype),
        in_specs=[pl.BlockSpec(memory_space=pltpu.VMEM)],
        out_specs=pl.BlockSpec(memory_space=pltpu.VMEM),
        scratch_shapes=[
            pltpu.VMEM(x.shape, x.dtype),
            pltpu.SemaphoreType.DMA((n,)),
            pltpu.SemaphoreType.DMA((n,)),
        ],
        compiler_params=pltpu.CompilerParams(has_side_effects=True),
    )(x)


def per_device(
    token_ids,
    embedding,
    group_of,
    prefix_len,
    tail_len,
    block_map,
    k_cache,
    v_cache,
    ln_gain,
    ln_bias,
    w_qkv,
    w_fc1,
    b_fc1,
    w_out,
    w_fc2,
):
    tp_count = lax.axis_size("tp")
    seq_count = lax.axis_size("seq")
    all_count = tp_count * seq_count
    seq_index = lax.axis_index("seq")
    tp_index = lax.axis_index("tp")
    requests = token_ids.shape[0]
    new_tokens = token_ids.shape[1]
    rows = requests * new_tokens
    groups = prefix_len.shape[0]
    heads_local = HEADS // tp_count
    width = embedding.shape[1]
    score_scale = 1.0 / math.sqrt(HEAD_DIM)

    vocab_rows = embedding.shape[0]
    first_row = (seq_index * tp_count + tp_index) * vocab_rows
    local_ids = token_ids.reshape(-1) - first_row
    inside = (local_ids >= 0) & (local_ids < vocab_rows)
    picked = jnp.take(embedding, jnp.clip(local_ids, 0, vocab_rows - 1), axis=0)
    picked = jnp.where(inside[:, None], picked, jnp.zeros_like(picked))
    start_states = allreduce(picked.reshape(all_count, -1, 128), True, tp_count)
    hidden_state = start_states.reshape(rows, width).astype(jnp.float32)

    group_hit = group_of[:, None] == jnp.arange(groups, dtype=jnp.int32)[None, :]
    shared_len = jnp.sum(jnp.where(group_hit, prefix_len[None, :], 0), axis=1)
    base_positions = shared_len + tail_len
    positions = (base_positions[:, None] + jnp.arange(new_tokens, dtype=jnp.int32)[None, :]).reshape(-1)
    seg_len = jnp.concatenate([prefix_len, tail_len])
    seg_count = seg_len.shape[0]
    blocks_local = block_map.shape[0]
    seg_blk = block_map[:, 0]
    rank_blk = block_map[:, 1]
    seg_hit = seg_blk[:, None] == jnp.arange(seg_count, dtype=jnp.int32)[None, :]
    len_blk = jnp.sum(jnp.where(seg_hit, seg_len[None, :], 0), axis=1)
    slot_positions = rank_blk[:, None] * BLOCK + jnp.arange(BLOCK, dtype=jnp.int32)[None, :]
    live_slot = ((seg_blk[:, None] >= 0) & (slot_positions < len_blk[:, None])).reshape(-1)
    seg_slot = jnp.broadcast_to(seg_blk[:, None], (blocks_local, BLOCK)).reshape(-1)
    own_tail = seg_slot[None, :] == (groups + jnp.arange(requests, dtype=jnp.int32))[:, None]
    own_prompt = seg_slot[None, :] == group_of[:, None]
    allowed = (own_tail | own_prompt) & live_slot[None, :]
    allowed = jnp.repeat(allowed, new_tokens, axis=0)

    rows_local = w_qkv.shape[1]
    unit_count = w_fc2.shape[1]
    sub_width = w_out.shape[1]
    pieces = HEAD_DIM // sub_width
    my_head = seq_index // pieces
    my_piece = seq_index % pieces
    causal = (
        jnp.arange(new_tokens, dtype=jnp.int32)[None, :]
        <= jnp.arange(new_tokens, dtype=jnp.int32)[:, None]
    )

    head_of = jnp.arange(seq_count, dtype=jnp.int32) // pieces
    qkv_heads = w_qkv.reshape(LAYERS, rows_local, 3, heads_local, HEAD_DIM)
    qkv_part = jnp.take(qkv_heads, head_of, axis=3)
    qkv_part = qkv_part.transpose(3, 0, 1, 2, 4).reshape(seq_count, LAYERS, rows_local, 3 * HEAD_DIM)
    fc1_part = w_fc1.reshape(LAYERS, rows_local, seq_count, unit_count).transpose(2, 0, 1, 3)
    message = jnp.concatenate([qkv_part, fc1_part], axis=-1)
    cols_mine = message.shape[-1]
    got_w = all_to_all(message.reshape(seq_count, LAYERS * rows_local, cols_mine), False, tp_count)
    w_mine = (
        got_w.reshape(seq_count, LAYERS, rows_local, cols_mine)
        .transpose(1, 0, 2, 3)
        .reshape(LAYERS, seq_count * rows_local, cols_mine)
    )
    for layer_index in range(LAYERS):
        normed = layer_norm(hidden_state, ln_gain[layer_index], ln_bias[layer_index]).astype(
            jnp.bfloat16
        )
        local = jnp.dot(normed, w_mine[layer_index], preferred_element_type=jnp.float32)
        q_h = rotary(local[:, None, 0:HEAD_DIM], positions)[:, 0].astype(jnp.bfloat16)
        k_h = rotary(local[:, None, HEAD_DIM : 2 * HEAD_DIM], positions)[:, 0].astype(jnp.bfloat16)
        v_h = local[:, 2 * HEAD_DIM : 3 * HEAD_DIM].astype(jnp.bfloat16)
        pre_act = local[:, 3 * HEAD_DIM :]
        pre_act = (
            pre_act
            + lax.dynamic_slice_in_dim(b_fc1[layer_index], seq_index * unit_count, unit_count, 0)[
                None, :
            ]
        )
        activated = jax.nn.gelu(pre_act, approximate=True).astype(jnp.bfloat16)
        q_piece = lax.dynamic_slice_in_dim(q_h, my_piece * sub_width, sub_width, 1).T
        q_all = all_to_all(jnp.broadcast_to(q_piece[None], (seq_count,) + q_piece.shape), False, tp_count)
        queries = (
            q_all.reshape(heads_local, pieces, sub_width, rows)
            .transpose(3, 0, 1, 2)
            .reshape(rows, heads_local, HEAD_DIM)
        )
        head_cols = (
            jnp.arange(heads_local * HEAD_DIM, dtype=jnp.int32)[None, :] // HEAD_DIM
            == jnp.arange(heads_local, dtype=jnp.int32)[:, None]
        )
        q_block = jnp.where(
            head_cols[:, None, :], queries.reshape(rows, heads_local * HEAD_DIM)[None], 0
        ).astype(jnp.bfloat16)
        scores = (
            jnp.einsum(
                "hrc,sc->hrs", q_block, k_cache[layer_index], preferred_element_type=jnp.float32
            )
            * score_scale
        )
        scores = jnp.where(allowed[None], scores, very_negative)
        part_max = jnp.max(scores, axis=2)
        weights = jnp.where(allowed[None], jnp.exp(scores - part_max[..., None]), 0.0)
        part_sum = jnp.sum(weights, axis=2)
        out_all = jnp.einsum(
            "hrs,sc->hrc",
            weights.astype(jnp.bfloat16),
            v_cache[layer_index],
            preferred_element_type=jnp.float32,
        ).reshape(heads_local, rows, heads_local, HEAD_DIM)
        part_out = jnp.sum(
            jnp.where(
                (
                    jnp.arange(heads_local, dtype=jnp.int32)[:, None]
                    == jnp.arange(heads_local, dtype=jnp.int32)[None, :]
                )[:, None, :, None],
                out_all,
                0.0,
            ),
            axis=2,
        )
        out_pieces = (
            part_out.reshape(heads_local, rows, pieces, sub_width)
            .transpose(0, 2, 3, 1)
            .reshape(heads_local * pieces, sub_width, rows)
        )
        max_rows = jnp.repeat(part_max, pieces, axis=0)[:, None, :]
        sum_rows = jnp.repeat(part_sum, pieces, axis=0)[:, None, :]
        pad_rows = jnp.zeros((heads_local * pieces, 6, rows), jnp.float32)
        message = jnp.concatenate([out_pieces, max_rows, sum_rows, pad_rows], axis=1)
        received = all_to_all(message, False, tp_count)
        got_out = received[:, :sub_width, :]
        got_max = received[:, sub_width, :]
        got_sum = received[:, sub_width + 1, :]

        q_h = q_h.reshape(requests, new_tokens, HEAD_DIM)
        k_h = k_h.reshape(requests, new_tokens, HEAD_DIM)
        v_h = lax.dynamic_slice_in_dim(v_h, my_piece * sub_width, sub_width, 1)
        v_h = v_h.reshape(requests, new_tokens, sub_width)
        fresh_scores = (
            jnp.einsum("rtd,rud->rtu", q_h, k_h, preferred_element_type=jnp.float32) * score_scale
        )
        fresh_scores = jnp.where(causal[None], fresh_scores, very_negative)
        fresh_max = jnp.max(fresh_scores, axis=2)
        fresh_weights = jnp.where(causal[None], jnp.exp(fresh_scores - fresh_max[..., None]), 0.0)
        fresh_sum = jnp.sum(fresh_weights, axis=2)
        fresh_out = jnp.einsum(
            "rtu,rud->rtd",
            fresh_weights.astype(jnp.bfloat16),
            v_h,
            preferred_element_type=jnp.float32,
        )
        fresh_max = fresh_max.reshape(rows)
        fresh_sum = fresh_sum.reshape(rows)
        fresh_out = fresh_out.reshape(rows, sub_width)

        top = jnp.maximum(jnp.max(got_max, axis=0), fresh_max)
        scale_cache = jnp.exp(got_max - top[None, :])
        scale_fresh = jnp.exp(fresh_max - top)
        denom = jnp.sum(got_sum * scale_cache, axis=0) + fresh_sum * scale_fresh
        numer = jnp.sum(got_out * scale_cache[:, None, :], axis=0).T + fresh_out * scale_fresh[:, None]
        my_cols = (numer / denom[:, None]).astype(jnp.bfloat16)

        update = jnp.dot(my_cols, w_out[layer_index], preferred_element_type=jnp.float32)
        update = update + jnp.dot(activated, w_fc2[layer_index], preferred_element_type=jnp.float32)
        update = allreduce(update.reshape(all_count, -1, 128), True, tp_count)
        hidden_state = hidden_state + update.reshape(rows, width)
    return hidden_state.reshape(requests, new_tokens, width)


def solution(mesh):
    in_specs = (
        P(),
        P(("seq", "tp"), None),
        P(),
        P(),
        P(),
        P("seq", None),
        P(None, "seq", "tp"),
        P(None, "seq", "tp"),
        P(),
        P(),
        P(None, "seq", None, "tp"),
        P(None, "seq", "tp"),
        P(None, "tp"),
        P(None, ("tp", "seq"), None),
        P(None, ("tp", "seq"), None),
    )
    out_specs = P()
    return jax.shard_map(
        per_device, mesh=mesh, in_specs=in_specs, out_specs=out_specs, check_vma=False
    )
```

```python
import functools
import math

import jax
import jax.numpy as jnp
from jax import lax
from jax.experimental import pallas as pl
from jax.experimental.pallas import tpu as pltpu
from jax.sharding import PartitionSpec as P

HEADS = 32
HEAD_DIM = 64
ROT = 32
LAYERS = 2
BLOCK = 128
SPAN = 512
MESH_IDS = pl.DeviceIdType.MESH

very_negative = -1e30


def layer_norm(values, gain_row, bias_row):
    average = jnp.mean(values, axis=-1, keepdims=True)
    centred = values - average
    variance = jnp.mean(centred * centred, axis=-1, keepdims=True)
    return centred * lax.rsqrt(variance + 1e-05) * gain_row + bias_row


def rotary(values, positions):
    half_width = ROT // 2
    frequency = jnp.exp(
        jnp.arange(half_width, dtype=jnp.float32) * (-2.0 * math.log(10000.0) / ROT)
    )
    angles = positions.astype(jnp.float32)[:, None] * frequency[None, :]
    cosine = jnp.cos(angles)[:, None, :]
    sine_part = jnp.sin(angles)[:, None, :]
    low_half = values[..., :half_width]
    high_half = values[..., half_width:ROT]
    return jnp.concatenate(
        [
            low_half * cosine - high_half * sine_part,
            high_half * cosine + low_half * sine_part,
            values[..., ROT:],
        ],
        axis=-1,
    )


def _group_ids(whole, tp_count):
    seq_index = lax.axis_index("seq")
    tp_index = lax.axis_index("tp")
    if whole:
        me = seq_index * tp_count + tp_index

        def peer(j):
            return (j // tp_count, j % tp_count)

    else:
        me = seq_index

        def peer(j):
            return (j, tp_index)

    return me, peer


_KERNEL_IDS = {}


def _kernel_id(key):
    if key not in _KERNEL_IDS:
        _KERNEL_IDS[key] = len(_KERNEL_IDS)
    return _KERNEL_IDS[key]


def _enter(n, me, peer):
    barrier = pltpu.get_barrier_semaphore()

    def greet(i, carry):
        j = lax.rem(me + i, n)
        pl.semaphore_signal(barrier, 1, device_id=peer(j), device_id_type=MESH_IDS)
        return carry

    lax.fori_loop(1, n, greet, 0)
    pl.semaphore_wait(barrier, n - 1)


def _rcopy(src, dst, send_sem, recv_sem, device):
    return pltpu.make_async_remote_copy(
        src_ref=src,
        dst_ref=dst,
        send_sem=send_sem,
        recv_sem=recv_sem,
        device_id=device,
        device_id_type=MESH_IDS,
    )


def _allreduce_kernel(n, whole, tp_count, x_ref, o_ref, rs_buf, ag_buf, s1, r1, s2, r2):
    me, peer = _group_ids(whole, tp_count)
    _enter(n, me, peer)

    def start_scatter(i, carry):
        j = lax.rem(me + i, n)
        _rcopy(x_ref.at[j], rs_buf.at[me], s1.at[j], r1.at[me], peer(j)).start()
        return carry

    lax.fori_loop(1, n, start_scatter, 0)

    def gather_sum(i, acc):
        j = lax.rem(me + i, n)
        _rcopy(x_ref.at[j], rs_buf.at[j], s1.at[j], r1.at[j], peer(j)).wait_recv()
        return acc + rs_buf[j].astype(jnp.float32)

    total = lax.fori_loop(1, n, gather_sum, x_ref[me].astype(jnp.float32))
    ag_buf[me] = total.astype(ag_buf.dtype)

    def start_gather(i, carry):
        j = lax.rem(me + i, n)
        _rcopy(ag_buf.at[me], ag_buf.at[me], s2.at[j], r2.at[me], peer(j)).start()
        return carry

    lax.fori_loop(1, n, start_gather, 0)

    def finish(i, carry):
        j = lax.rem(me + i, n)
        _rcopy(ag_buf.at[j], ag_buf.at[j], s2.at[j], r2.at[j], peer(j)).wait_recv()
        _rcopy(x_ref.at[j], rs_buf.at[me], s1.at[j], r1.at[me], peer(j)).wait_send()
        _rcopy(ag_buf.at[me], ag_buf.at[me], s2.at[j], r2.at[me], peer(j)).wait_send()
        return carry

    lax.fori_loop(1, n, finish, 0)
    o_ref[...] = ag_buf[...]


def allreduce(x, whole, tp_count):
    n = x.shape[0]
    return pl.pallas_call(
        functools.partial(_allreduce_kernel, n, whole, tp_count),
        out_shape=jax.ShapeDtypeStruct(x.shape, x.dtype),
        in_specs=[pl.BlockSpec(memory_space=pltpu.VMEM)],
        out_specs=pl.BlockSpec(memory_space=pltpu.VMEM),
        scratch_shapes=[
            pltpu.VMEM(x.shape, x.dtype),
            pltpu.VMEM(x.shape, x.dtype),
            pltpu.SemaphoreType.DMA((n,)),
            pltpu.SemaphoreType.DMA((n,)),
            pltpu.SemaphoreType.DMA((n,)),
            pltpu.SemaphoreType.DMA((n,)),
        ],
        compiler_params=pltpu.CompilerParams(
            has_side_effects=True,
            collective_id=_kernel_id(("allreduce", whole, x.shape, str(x.dtype))),
        ),
    )(x)


def _all_to_all_kernel(n, whole, tp_count, x_ref, o_ref, buf, s1, r1):
    me, peer = _group_ids(whole, tp_count)
    _enter(n, me, peer)

    def start(i, carry):
        j = lax.rem(me + i, n)
        _rcopy(x_ref.at[j], buf.at[me], s1.at[j], r1.at[me], peer(j)).start()
        return carry

    lax.fori_loop(1, n, start, 0)

    def finish(i, carry):
        j = lax.rem(me + i, n)
        _rcopy(x_ref.at[j], buf.at[j], s1.at[j], r1.at[j], peer(j)).wait_recv()
        _rcopy(x_ref.at[j], buf.at[me], s1.at[j], r1.at[me], peer(j)).wait_send()
        return carry

    lax.fori_loop(1, n, finish, 0)
    buf[me] = x_ref[me]
    o_ref[...] = buf[...]


def all_to_all(x, whole, tp_count):
    n = x.shape[0]
    return pl.pallas_call(
        functools.partial(_all_to_all_kernel, n, whole, tp_count),
        out_shape=jax.ShapeDtypeStruct(x.shape, x.dtype),
        in_specs=[pl.BlockSpec(memory_space=pltpu.VMEM)],
        out_specs=pl.BlockSpec(memory_space=pltpu.VMEM),
        scratch_shapes=[
            pltpu.VMEM(x.shape, x.dtype),
            pltpu.SemaphoreType.DMA((n,)),
            pltpu.SemaphoreType.DMA((n,)),
        ],
        compiler_params=pltpu.CompilerParams(
            has_side_effects=True,
            collective_id=_kernel_id(("all_to_all", whole, x.shape, str(x.dtype))),
        ),
    )(x)


def per_device(
    token_ids,
    embedding,
    group_of,
    prefix_len,
    tail_len,
    block_map,
    k_cache,
    v_cache,
    ln_gain,
    ln_bias,
    w_qkv,
    w_fc1,
    b_fc1,
    w_out,
    w_fc2,
):
    tp_count = lax.axis_size("tp")
    seq_count = lax.axis_size("seq")
    all_count = tp_count * seq_count
    seq_index = lax.axis_index("seq")
    tp_index = lax.axis_index("tp")
    requests = token_ids.shape[0]
    new_tokens = token_ids.shape[1]
    rows = requests * new_tokens
    groups = prefix_len.shape[0]
    heads_local = HEADS // tp_count
    width = embedding.shape[1]
    score_scale = 1.0 / math.sqrt(HEAD_DIM)

    vocab_rows = embedding.shape[0]
    first_row = (seq_index * tp_count + tp_index) * vocab_rows
    local_ids = token_ids.reshape(-1) - first_row
    inside = (local_ids >= 0) & (local_ids < vocab_rows)
    picked = jnp.take(embedding, jnp.clip(local_ids, 0, vocab_rows - 1), axis=0)
    picked = jnp.where(inside[:, None], picked, jnp.zeros_like(picked))
    start_states = allreduce(picked.reshape(all_count, -1, 128), True, tp_count)
    hidden_state = start_states.reshape(rows, width).astype(jnp.float32)

    group_hit = group_of[:, None] == jnp.arange(groups, dtype=jnp.int32)[None, :]
    shared_len = jnp.sum(jnp.where(group_hit, prefix_len[None, :], 0), axis=1)
    base_positions = shared_len + tail_len
    positions = (base_positions[:, None] + jnp.arange(new_tokens, dtype=jnp.int32)[None, :]).reshape(-1)
    seg_len = jnp.concatenate([prefix_len, tail_len])
    seg_count = seg_len.shape[0]
    blocks_local = block_map.shape[0]
    seg_blk = block_map[:, 0]
    rank_blk = block_map[:, 1]
    seg_hit = seg_blk[:, None] == jnp.arange(seg_count, dtype=jnp.int32)[None, :]
    len_blk = jnp.sum(jnp.where(seg_hit, seg_len[None, :], 0), axis=1)
    slot_positions = rank_blk[:, None] * BLOCK + jnp.arange(BLOCK, dtype=jnp.int32)[None, :]
    live_slot = ((seg_blk[:, None] >= 0) & (slot_positions < len_blk[:, None])).reshape(-1)
    seg_slot = jnp.broadcast_to(seg_blk[:, None], (blocks_local, BLOCK)).reshape(-1)
    own_tail = seg_slot[None, :] == (groups + jnp.arange(requests, dtype=jnp.int32))[:, None]
    own_prompt = seg_slot[None, :] == group_of[:, None]
    allowed = (own_tail | own_prompt) & live_slot[None, :]
    allowed = jnp.repeat(allowed, new_tokens, axis=0)

    rows_local = w_qkv.shape[1]
    unit_count = w_fc2.shape[1]
    sub_width = w_out.shape[1]
    pieces = HEAD_DIM // sub_width
    my_head = seq_index // pieces
    my_piece = seq_index % pieces
    causal = (
        jnp.arange(new_tokens, dtype=jnp.int32)[None, :]
        <= jnp.arange(new_tokens, dtype=jnp.int32)[:, None]
    )

    head_of = jnp.arange(seq_count, dtype=jnp.int32) // pieces
    qkv_heads = w_qkv.reshape(LAYERS, rows_local, 3, heads_local, HEAD_DIM)
    qkv_part = jnp.take(qkv_heads, head_of, axis=3)
    qkv_part = qkv_part.transpose(3, 0, 1, 2, 4).reshape(seq_count, LAYERS, rows_local, 3 * HEAD_DIM)
    fc1_part = w_fc1.reshape(LAYERS, rows_local, seq_count, unit_count).transpose(2, 0, 1, 3)
    message = jnp.concatenate([qkv_part, fc1_part], axis=-1)
    cols_mine = message.shape[-1]
    got_w = all_to_all(message.reshape(seq_count, LAYERS * rows_local, cols_mine), False, tp_count)
    w_mine = (
        got_w.reshape(seq_count, LAYERS, rows_local, cols_mine)
        .transpose(1, 0, 2, 3)
        .reshape(LAYERS, seq_count * rows_local, cols_mine)
    )
    for layer_index in range(LAYERS):
        normed = layer_norm(hidden_state, ln_gain[layer_index], ln_bias[layer_index]).astype(
            jnp.bfloat16
        )
        local = jnp.dot(normed, w_mine[layer_index], preferred_element_type=jnp.float32)
        q_h = rotary(local[:, None, 0:HEAD_DIM], positions)[:, 0].astype(jnp.bfloat16)
        k_h = rotary(local[:, None, HEAD_DIM : 2 * HEAD_DIM], positions)[:, 0].astype(jnp.bfloat16)
        v_h = local[:, 2 * HEAD_DIM : 3 * HEAD_DIM].astype(jnp.bfloat16)
        pre_act = local[:, 3 * HEAD_DIM :]
        pre_act = (
            pre_act
            + lax.dynamic_slice_in_dim(b_fc1[layer_index], seq_index * unit_count, unit_count, 0)[
                None, :
            ]
        )
        activated = jax.nn.gelu(pre_act, approximate=True).astype(jnp.bfloat16)
        q_piece = lax.dynamic_slice_in_dim(q_h, my_piece * sub_width, sub_width, 1).T
        q_all = all_to_all(jnp.broadcast_to(q_piece[None], (seq_count,) + q_piece.shape), False, tp_count)
        queries = (
            q_all.reshape(heads_local, pieces, sub_width, rows)
            .transpose(3, 0, 1, 2)
            .reshape(rows, heads_local, HEAD_DIM)
        )
        head_cols = (
            jnp.arange(heads_local * HEAD_DIM, dtype=jnp.int32)[None, :] // HEAD_DIM
            == jnp.arange(heads_local, dtype=jnp.int32)[:, None]
        )
        q_block = jnp.where(
            head_cols[:, None, :], queries.reshape(rows, heads_local * HEAD_DIM)[None], 0
        ).astype(jnp.bfloat16)
        scores = (
            jnp.einsum(
                "hrc,sc->hrs", q_block, k_cache[layer_index], preferred_element_type=jnp.float32
            )
            * score_scale
        )
        scores = jnp.where(allowed[None], scores, very_negative)
        part_max = jnp.max(scores, axis=2)
        weights = jnp.where(allowed[None], jnp.exp(scores - part_max[..., None]), 0.0)
        part_sum = jnp.sum(weights, axis=2)
        out_all = jnp.einsum(
            "hrs,sc->hrc",
            weights.astype(jnp.bfloat16),
            v_cache[layer_index],
            preferred_element_type=jnp.float32,
        ).reshape(heads_local, rows, heads_local, HEAD_DIM)
        part_out = jnp.sum(
            jnp.where(
                (
                    jnp.arange(heads_local, dtype=jnp.int32)[:, None]
                    == jnp.arange(heads_local, dtype=jnp.int32)[None, :]
                )[:, None, :, None],
                out_all,
                0.0,
            ),
            axis=2,
        )
        out_pieces = (
            part_out.reshape(heads_local, rows, pieces, sub_width)
            .transpose(0, 2, 3, 1)
            .reshape(heads_local * pieces, sub_width, rows)
        )
        max_rows = jnp.repeat(part_max, pieces, axis=0)[:, None, :]
        sum_rows = jnp.repeat(part_sum, pieces, axis=0)[:, None, :]
        pad_rows = jnp.zeros((heads_local * pieces, 6, rows), jnp.float32)
        message = jnp.concatenate([out_pieces, max_rows, sum_rows, pad_rows], axis=1)
        received = all_to_all(message, False, tp_count)
        got_out = received[:, :sub_width, :]
        got_max = received[:, sub_width, :]
        got_sum = received[:, sub_width + 1, :]

        q_h = q_h.reshape(requests, new_tokens, HEAD_DIM)
        k_h = k_h.reshape(requests, new_tokens, HEAD_DIM)
        v_h = lax.dynamic_slice_in_dim(v_h, my_piece * sub_width, sub_width, 1)
        v_h = v_h.reshape(requests, new_tokens, sub_width)
        fresh_scores = (
            jnp.einsum("rtd,rud->rtu", q_h, k_h, preferred_element_type=jnp.float32) * score_scale
        )
        fresh_scores = jnp.where(causal[None], fresh_scores, very_negative)
        fresh_max = jnp.max(fresh_scores, axis=2)
        fresh_weights = jnp.where(causal[None], jnp.exp(fresh_scores - fresh_max[..., None]), 0.0)
        fresh_sum = jnp.sum(fresh_weights, axis=2)
        fresh_out = jnp.einsum(
            "rtu,rud->rtd",
            fresh_weights.astype(jnp.bfloat16),
            v_h,
            preferred_element_type=jnp.float32,
        )
        fresh_max = fresh_max.reshape(rows)
        fresh_sum = fresh_sum.reshape(rows)
        fresh_out = fresh_out.reshape(rows, sub_width)

        top = jnp.maximum(jnp.max(got_max, axis=0), fresh_max)
        scale_cache = jnp.exp(got_max - top[None, :])
        scale_fresh = jnp.exp(fresh_max - top)
        denom = jnp.sum(got_sum * scale_cache, axis=0) + fresh_sum * scale_fresh
        numer = jnp.sum(got_out * scale_cache[:, None, :], axis=0).T + fresh_out * scale_fresh[:, None]
        my_cols = (numer / denom[:, None]).astype(jnp.bfloat16)

        update = jnp.dot(my_cols, w_out[layer_index], preferred_element_type=jnp.float32)
        update = update + jnp.dot(activated, w_fc2[layer_index], preferred_element_type=jnp.float32)
        update = allreduce(update.reshape(all_count, -1, 128), True, tp_count)
        hidden_state = hidden_state + update.reshape(rows, width)
    return hidden_state.reshape(requests, new_tokens, width)


def solution(mesh):
    in_specs = (
        P(),
        P(("seq", "tp"), None),
        P(),
        P(),
        P(),
        P("seq", None),
        P(None, "seq", "tp"),
        P(None, "seq", "tp"),
        P(),
        P(),
        P(None, "seq", None, "tp"),
        P(None, "seq", "tp"),
        P(None, "tp"),
        P(None, ("tp", "seq"), None),
        P(None, ("tp", "seq"), None),
    )
    out_specs = P()
    return jax.shard_map(
        per_device, mesh=mesh, in_specs=in_specs, out_specs=out_specs, check_vma=False
    )
```

```python
import functools
import math

import jax
import jax.numpy as jnp
from jax import lax
from jax.experimental import pallas as pl
from jax.experimental.pallas import tpu as pltpu
from jax.sharding import PartitionSpec as P

HEADS = 32
HEAD_DIM = 64
ROT = 32
LAYERS = 2
BLOCK = 128
SPAN = 512
MESH_IDS = pl.DeviceIdType.MESH

very_negative = -1e30


def layer_norm(values, gain_row, bias_row):
    average = jnp.mean(values, axis=-1, keepdims=True)
    centred = values - average
    variance = jnp.mean(centred * centred, axis=-1, keepdims=True)
    return centred * lax.rsqrt(variance + 1e-05) * gain_row + bias_row


def rotary(values, positions):
    half_width = ROT // 2
    frequency = jnp.exp(
        jnp.arange(half_width, dtype=jnp.float32) * (-2.0 * math.log(10000.0) / ROT)
    )
    angles = positions.astype(jnp.float32)[:, None] * frequency[None, :]
    cosine = jnp.cos(angles)[:, None, :]
    sine_part = jnp.sin(angles)[:, None, :]
    low_half = values[..., :half_width]
    high_half = values[..., half_width:ROT]
    return jnp.concatenate(
        [
            low_half * cosine - high_half * sine_part,
            high_half * cosine + low_half * sine_part,
            values[..., ROT:],
        ],
        axis=-1,
    )


def _group_ids(whole, tp_count):
    seq_index = lax.axis_index("seq")
    tp_index = lax.axis_index("tp")
    if whole:
        me = seq_index * tp_count + tp_index

        def peer(j):
            return (j // tp_count, j % tp_count)

    else:
        me = seq_index

        def peer(j):
            return (j, tp_index)

    return me, peer


_KERNEL_IDS = {}


def _kernel_id(key):
    if key not in _KERNEL_IDS:
        _KERNEL_IDS[key] = len(_KERNEL_IDS)
    return _KERNEL_IDS[key]


def _enter(n, me, peer):
    barrier = pltpu.get_barrier_semaphore()

    def greet(i, carry):
        j = lax.rem(me + i, n)
        pl.semaphore_signal(barrier, 1, device_id=peer(j), device_id_type=MESH_IDS)
        return carry

    lax.fori_loop(1, n, greet, 0)
    pl.semaphore_wait(barrier, n - 1)


def _rcopy(src, dst, send_sem, recv_sem, device):
    return pltpu.make_async_remote_copy(
        src_ref=src,
        dst_ref=dst,
        send_sem=send_sem,
        recv_sem=recv_sem,
        device_id=device,
        device_id_type=MESH_IDS,
    )


def _allreduce_kernel(n, whole, tp_count, x_ref, o_ref, rs_buf, ag_buf, s1, r1, s2, r2):
    me, peer = _group_ids(whole, tp_count)
    _enter(n, me, peer)

    def start_scatter(i, carry):
        j = lax.rem(me + i, n)
        _rcopy(x_ref.at[j], rs_buf.at[me], s1.at[j], r1.at[me], peer(j)).start()
        return carry

    lax.fori_loop(1, n, start_scatter, 0)

    def gather_sum(i, acc):
        j = lax.rem(me + i, n)
        _rcopy(x_ref.at[j], rs_buf.at[j], s1.at[j], r1.at[j], peer(j)).wait_recv()
        return acc + rs_buf[j].astype(jnp.float32)

    total = lax.fori_loop(1, n, gather_sum, x_ref[me].astype(jnp.float32))
    ag_buf[me] = total.astype(ag_buf.dtype)

    def start_gather(i, carry):
        j = lax.rem(me + i, n)
        _rcopy(ag_buf.at[me], ag_buf.at[me], s2.at[j], r2.at[me], peer(j)).start()
        return carry

    lax.fori_loop(1, n, start_gather, 0)

    def finish(i, carry):
        j = lax.rem(me + i, n)
        _rcopy(ag_buf.at[j], ag_buf.at[j], s2.at[j], r2.at[j], peer(j)).wait_recv()
        _rcopy(x_ref.at[j], rs_buf.at[me], s1.at[j], r1.at[me], peer(j)).wait_send()
        _rcopy(ag_buf.at[me], ag_buf.at[me], s2.at[j], r2.at[me], peer(j)).wait_send()
        return carry

    lax.fori_loop(1, n, finish, 0)
    o_ref[...] = ag_buf[...]


def allreduce(x, whole, tp_count):
    n = x.shape[0]
    return pl.pallas_call(
        functools.partial(_allreduce_kernel, n, whole, tp_count),
        out_shape=jax.ShapeDtypeStruct(x.shape, x.dtype),
        in_specs=[pl.BlockSpec(memory_space=pltpu.VMEM)],
        out_specs=pl.BlockSpec(memory_space=pltpu.VMEM),
        scratch_shapes=[
            pltpu.VMEM(x.shape, x.dtype),
            pltpu.VMEM(x.shape, x.dtype),
            pltpu.SemaphoreType.DMA((n,)),
            pltpu.SemaphoreType.DMA((n,)),
            pltpu.SemaphoreType.DMA((n,)),
            pltpu.SemaphoreType.DMA((n,)),
        ],
        compiler_params=pltpu.CompilerParams(
            has_side_effects=True,
            collective_id=_kernel_id(("allreduce", whole, x.shape, str(x.dtype))),
        ),
    )(x)


def _allreduce_chip_kernel(tp_count, x_ref, o_ref, pbuf, sbuf, rs_buf, ag_buf, sa, ra, s1, r1, s2, r2, sd, rd):
    seq_index = lax.axis_index("seq")
    tp_index = lax.axis_index("tp")
    n = x_ref.shape[1]
    core = seq_index % 2
    other = 1 - core
    me = (seq_index // 2) * tp_count + tp_index
    partner = (seq_index + 1 - 2 * core, tp_index)

    def peer(j):
        return ((j // tp_count) * 2 + core, j % tp_count)

    barrier = pltpu.get_barrier_semaphore()

    def greet(i, carry):
        j = lax.rem(me + i, n)
        pl.semaphore_signal(barrier, 1, device_id=peer(j), device_id_type=MESH_IDS)
        return carry

    lax.fori_loop(1, n, greet, 0)
    pl.semaphore_signal(barrier, 1, device_id=partner, device_id_type=MESH_IDS)
    pl.semaphore_wait(barrier, n)

    swap = _rcopy(x_ref.at[other], pbuf, sa, ra, partner)
    swap.start()
    swap.wait_recv()
    sbuf[...] = (x_ref[core].astype(jnp.float32) + pbuf[...].astype(jnp.float32)).astype(sbuf.dtype)

    def start_scatter(i, carry):
        j = lax.rem(me + i, n)
        _rcopy(sbuf.at[j], rs_buf.at[me], s1.at[j], r1.at[me], peer(j)).start()
        return carry

    lax.fori_loop(1, n, start_scatter, 0)

    def gather_sum(i, acc):
        j = lax.rem(me + i, n)
        _rcopy(sbuf.at[j], rs_buf.at[j], s1.at[j], r1.at[j], peer(j)).wait_recv()
        return acc + rs_buf[j].astype(jnp.float32)

    total = lax.fori_loop(1, n, gather_sum, sbuf[me].astype(jnp.float32))
    ag_buf[core, me] = total.astype(ag_buf.dtype)

    def start_gather(i, carry):
        j = lax.rem(me + i, n)
        _rcopy(ag_buf.at[core, me], ag_buf.at[core, me], s2.at[j], r2.at[me], peer(j)).start()
        return carry

    lax.fori_loop(1, n, start_gather, 0)

    def finish(i, carry):
        j = lax.rem(me + i, n)
        _rcopy(ag_buf.at[core, j], ag_buf.at[core, j], s2.at[j], r2.at[j], peer(j)).wait_recv()
        _rcopy(sbuf.at[j], rs_buf.at[me], s1.at[j], r1.at[me], peer(j)).wait_send()
        _rcopy(ag_buf.at[core, me], ag_buf.at[core, me], s2.at[j], r2.at[me], peer(j)).wait_send()
        return carry

    lax.fori_loop(1, n, finish, 0)
    swap.wait_send()
    back = _rcopy(ag_buf.at[core], ag_buf.at[core], sd, rd, partner)
    back.start()
    _rcopy(ag_buf.at[other], ag_buf.at[other], sd, rd, partner).wait_recv()
    back.wait_send()
    o_ref[...] = ag_buf[...]


def allreduce_chip(x, tp_count):
    n = x.shape[1]
    half = x.shape[1:]
    return pl.pallas_call(
        functools.partial(_allreduce_chip_kernel, tp_count),
        out_shape=jax.ShapeDtypeStruct(x.shape, x.dtype),
        in_specs=[pl.BlockSpec(memory_space=pltpu.VMEM)],
        out_specs=pl.BlockSpec(memory_space=pltpu.VMEM),
        scratch_shapes=[
            pltpu.VMEM(half, x.dtype),
            pltpu.VMEM(half, x.dtype),
            pltpu.VMEM(half, x.dtype),
            pltpu.VMEM(x.shape, x.dtype),
            pltpu.SemaphoreType.DMA(()),
            pltpu.SemaphoreType.DMA(()),
            pltpu.SemaphoreType.DMA((n,)),
            pltpu.SemaphoreType.DMA((n,)),
            pltpu.SemaphoreType.DMA((n,)),
            pltpu.SemaphoreType.DMA((n,)),
            pltpu.SemaphoreType.DMA(()),
            pltpu.SemaphoreType.DMA(()),
        ],
        compiler_params=pltpu.CompilerParams(
            has_side_effects=True,
            collective_id=_kernel_id(("allreduce_chip", x.shape, str(x.dtype))),
        ),
    )(x)


def _all_to_all_kernel(n, whole, tp_count, x_ref, o_ref, buf, s1, r1):
    me, peer = _group_ids(whole, tp_count)
    _enter(n, me, peer)

    def start(i, carry):
        j = lax.rem(me + i, n)
        _rcopy(x_ref.at[j], buf.at[me], s1.at[j], r1.at[me], peer(j)).start()
        return carry

    lax.fori_loop(1, n, start, 0)

    def finish(i, carry):
        j = lax.rem(me + i, n)
        _rcopy(x_ref.at[j], buf.at[j], s1.at[j], r1.at[j], peer(j)).wait_recv()
        _rcopy(x_ref.at[j], buf.at[me], s1.at[j], r1.at[me], peer(j)).wait_send()
        return carry

    lax.fori_loop(1, n, finish, 0)
    buf[me] = x_ref[me]
    o_ref[...] = buf[...]


def all_to_all(x, whole, tp_count):
    n = x.shape[0]
    return pl.pallas_call(
        functools.partial(_all_to_all_kernel, n, whole, tp_count),
        out_shape=jax.ShapeDtypeStruct(x.shape, x.dtype),
        in_specs=[pl.BlockSpec(memory_space=pltpu.VMEM)],
        out_specs=pl.BlockSpec(memory_space=pltpu.VMEM),
        scratch_shapes=[
            pltpu.VMEM(x.shape, x.dtype),
            pltpu.SemaphoreType.DMA((n,)),
            pltpu.SemaphoreType.DMA((n,)),
        ],
        compiler_params=pltpu.CompilerParams(
            has_side_effects=True,
            collective_id=_kernel_id(("all_to_all", whole, x.shape, str(x.dtype))),
        ),
    )(x)


def per_device(
    token_ids,
    embedding,
    group_of,
    prefix_len,
    tail_len,
    block_map,
    k_cache,
    v_cache,
    ln_gain,
    ln_bias,
    w_qkv,
    w_fc1,
    b_fc1,
    w_out,
    w_fc2,
):
    tp_count = lax.axis_size("tp")
    seq_count = lax.axis_size("seq")
    all_count = tp_count * seq_count
    seq_index = lax.axis_index("seq")
    tp_index = lax.axis_index("tp")
    requests = token_ids.shape[0]
    new_tokens = token_ids.shape[1]
    rows = requests * new_tokens
    groups = prefix_len.shape[0]
    heads_local = HEADS // tp_count
    width = embedding.shape[1]
    score_scale = 1.0 / math.sqrt(HEAD_DIM)

    vocab_rows = embedding.shape[0]
    first_row = (seq_index * tp_count + tp_index) * vocab_rows
    local_ids = token_ids.reshape(-1) - first_row
    inside = (local_ids >= 0) & (local_ids < vocab_rows)
    picked = jnp.take(embedding, jnp.clip(local_ids, 0, vocab_rows - 1), axis=0)
    picked = jnp.where(inside[:, None], picked, jnp.zeros_like(picked))
    start_states = allreduce_chip(picked.reshape(2, all_count // 2, -1, 128), tp_count)
    hidden_state = start_states.reshape(rows, width).astype(jnp.float32)

    group_hit = group_of[:, None] == jnp.arange(groups, dtype=jnp.int32)[None, :]
    shared_len = jnp.sum(jnp.where(group_hit, prefix_len[None, :], 0), axis=1)
    base_positions = shared_len + tail_len
    positions = (base_positions[:, None] + jnp.arange(new_tokens, dtype=jnp.int32)[None, :]).reshape(-1)
    seg_len = jnp.concatenate([prefix_len, tail_len])
    seg_count = seg_len.shape[0]
    blocks_local = block_map.shape[0]
    seg_blk = block_map[:, 0]
    rank_blk = block_map[:, 1]
    seg_hit = seg_blk[:, None] == jnp.arange(seg_count, dtype=jnp.int32)[None, :]
    len_blk = jnp.sum(jnp.where(seg_hit, seg_len[None, :], 0), axis=1)
    slot_positions = rank_blk[:, None] * BLOCK + jnp.arange(BLOCK, dtype=jnp.int32)[None, :]
    live_slot = ((seg_blk[:, None] >= 0) & (slot_positions < len_blk[:, None])).reshape(-1)
    seg_slot = jnp.broadcast_to(seg_blk[:, None], (blocks_local, BLOCK)).reshape(-1)
    own_tail = seg_slot[None, :] == (groups + jnp.arange(requests, dtype=jnp.int32))[:, None]
    own_prompt = seg_slot[None, :] == group_of[:, None]
    allowed = (own_tail | own_prompt) & live_slot[None, :]
    allowed = jnp.repeat(allowed, new_tokens, axis=0)

    rows_local = w_qkv.shape[1]
    unit_count = w_fc2.shape[1]
    sub_width = w_out.shape[1]
    pieces = HEAD_DIM // sub_width
    my_head = seq_index // pieces
    my_piece = seq_index % pieces
    causal = (
        jnp.arange(new_tokens, dtype=jnp.int32)[None, :]
        <= jnp.arange(new_tokens, dtype=jnp.int32)[:, None]
    )

    head_of = jnp.arange(seq_count, dtype=jnp.int32) // pieces
    qkv_heads = w_qkv.reshape(LAYERS, rows_local, 3, heads_local, HEAD_DIM)
    qkv_part = jnp.take(qkv_heads, head_of, axis=3)
    qkv_part = qkv_part.transpose(3, 0, 1, 2, 4).reshape(seq_count, LAYERS, rows_local, 3 * HEAD_DIM)
    fc1_part = w_fc1.reshape(LAYERS, rows_local, seq_count, unit_count).transpose(2, 0, 1, 3)
    message = jnp.concatenate([qkv_part, fc1_part], axis=-1)
    cols_mine = message.shape[-1]
    got_w = all_to_all(message.reshape(seq_count, LAYERS * rows_local, cols_mine), False, tp_count)
    w_mine = (
        got_w.reshape(seq_count, LAYERS, rows_local, cols_mine)
        .transpose(1, 0, 2, 3)
        .reshape(LAYERS, seq_count * rows_local, cols_mine)
    )
    for layer_index in range(LAYERS):
        normed = layer_norm(hidden_state, ln_gain[layer_index], ln_bias[layer_index]).astype(
            jnp.bfloat16
        )
        local = jnp.dot(normed, w_mine[layer_index], preferred_element_type=jnp.float32)
        q_h = rotary(local[:, None, 0:HEAD_DIM], positions)[:, 0].astype(jnp.bfloat16)
        k_h = rotary(local[:, None, HEAD_DIM : 2 * HEAD_DIM], positions)[:, 0].astype(jnp.bfloat16)
        v_h = local[:, 2 * HEAD_DIM : 3 * HEAD_DIM].astype(jnp.bfloat16)
        pre_act = local[:, 3 * HEAD_DIM :]
        pre_act = (
            pre_act
            + lax.dynamic_slice_in_dim(b_fc1[layer_index], seq_index * unit_count, unit_count, 0)[
                None, :
            ]
        )
        activated = jax.nn.gelu(pre_act, approximate=True).astype(jnp.bfloat16)
        q_piece = lax.dynamic_slice_in_dim(q_h, my_piece * sub_width, sub_width, 1).T
        q_all = all_to_all(jnp.broadcast_to(q_piece[None], (seq_count,) + q_piece.shape), False, tp_count)
        queries = (
            q_all.reshape(heads_local, pieces, sub_width, rows)
            .transpose(3, 0, 1, 2)
            .reshape(rows, heads_local, HEAD_DIM)
        )
        head_cols = (
            jnp.arange(heads_local * HEAD_DIM, dtype=jnp.int32)[None, :] // HEAD_DIM
            == jnp.arange(heads_local, dtype=jnp.int32)[:, None]
        )
        q_block = jnp.where(
            head_cols[:, None, :], queries.reshape(rows, heads_local * HEAD_DIM)[None], 0
        ).astype(jnp.bfloat16)
        scores = (
            jnp.einsum(
                "hrc,sc->hrs", q_block, k_cache[layer_index], preferred_element_type=jnp.float32
            )
            * score_scale
        )
        scores = jnp.where(allowed[None], scores, very_negative)
        part_max = jnp.max(scores, axis=2)
        weights = jnp.where(allowed[None], jnp.exp(scores - part_max[..., None]), 0.0)
        part_sum = jnp.sum(weights, axis=2)
        out_all = jnp.einsum(
            "hrs,sc->hrc",
            weights.astype(jnp.bfloat16),
            v_cache[layer_index],
            preferred_element_type=jnp.float32,
        ).reshape(heads_local, rows, heads_local, HEAD_DIM)
        part_out = jnp.sum(
            jnp.where(
                (
                    jnp.arange(heads_local, dtype=jnp.int32)[:, None]
                    == jnp.arange(heads_local, dtype=jnp.int32)[None, :]
                )[:, None, :, None],
                out_all,
                0.0,
            ),
            axis=2,
        )
        out_pieces = (
            part_out.reshape(heads_local, rows, pieces, sub_width)
            .transpose(0, 2, 3, 1)
            .reshape(heads_local * pieces, sub_width, rows)
        )
        max_rows = jnp.repeat(part_max, pieces, axis=0)[:, None, :]
        sum_rows = jnp.repeat(part_sum, pieces, axis=0)[:, None, :]
        pad_rows = jnp.zeros((heads_local * pieces, 6, rows), jnp.float32)
        message = jnp.concatenate([out_pieces, max_rows, sum_rows, pad_rows], axis=1)
        received = all_to_all(message, False, tp_count)
        got_out = received[:, :sub_width, :]
        got_max = received[:, sub_width, :]
        got_sum = received[:, sub_width + 1, :]

        q_h = q_h.reshape(requests, new_tokens, HEAD_DIM)
        k_h = k_h.reshape(requests, new_tokens, HEAD_DIM)
        v_h = lax.dynamic_slice_in_dim(v_h, my_piece * sub_width, sub_width, 1)
        v_h = v_h.reshape(requests, new_tokens, sub_width)
        fresh_scores = (
            jnp.einsum("rtd,rud->rtu", q_h, k_h, preferred_element_type=jnp.float32) * score_scale
        )
        fresh_scores = jnp.where(causal[None], fresh_scores, very_negative)
        fresh_max = jnp.max(fresh_scores, axis=2)
        fresh_weights = jnp.where(causal[None], jnp.exp(fresh_scores - fresh_max[..., None]), 0.0)
        fresh_sum = jnp.sum(fresh_weights, axis=2)
        fresh_out = jnp.einsum(
            "rtu,rud->rtd",
            fresh_weights.astype(jnp.bfloat16),
            v_h,
            preferred_element_type=jnp.float32,
        )
        fresh_max = fresh_max.reshape(rows)
        fresh_sum = fresh_sum.reshape(rows)
        fresh_out = fresh_out.reshape(rows, sub_width)

        top = jnp.maximum(jnp.max(got_max, axis=0), fresh_max)
        scale_cache = jnp.exp(got_max - top[None, :])
        scale_fresh = jnp.exp(fresh_max - top)
        denom = jnp.sum(got_sum * scale_cache, axis=0) + fresh_sum * scale_fresh
        numer = jnp.sum(got_out * scale_cache[:, None, :], axis=0).T + fresh_out * scale_fresh[:, None]
        my_cols = (numer / denom[:, None]).astype(jnp.bfloat16)

        update = jnp.dot(my_cols, w_out[layer_index], preferred_element_type=jnp.float32)
        update = update + jnp.dot(activated, w_fc2[layer_index], preferred_element_type=jnp.float32)
        update = allreduce_chip(update.reshape(2, all_count // 2, -1, 128), tp_count)
        hidden_state = hidden_state + update.reshape(rows, width)
    return hidden_state.reshape(requests, new_tokens, width)


def solution(mesh):
    in_specs = (
        P(),
        P(("seq", "tp"), None),
        P(),
        P(),
        P(),
        P("seq", None),
        P(None, "seq", "tp"),
        P(None, "seq", "tp"),
        P(),
        P(),
        P(None, "seq", None, "tp"),
        P(None, "seq", "tp"),
        P(None, "tp"),
        P(None, ("tp", "seq"), None),
        P(None, ("tp", "seq"), None),
    )
    out_specs = P()
    return jax.shard_map(
        per_device, mesh=mesh, in_specs=in_specs, out_specs=out_specs, check_vma=False
    )
```

```python
import functools
import math

import jax
import jax.numpy as jnp
from jax import lax
from jax.experimental import pallas as pl
from jax.experimental.pallas import tpu as pltpu
from jax.sharding import PartitionSpec as P

HEADS = 32
HEAD_DIM = 64
ROT = 32
LAYERS = 2
BLOCK = 128
SPAN = 512
MESH_IDS = pl.DeviceIdType.MESH

very_negative = -1e30


def layer_norm(values, gain_row, bias_row):
    average = jnp.mean(values, axis=-1, keepdims=True)
    centred = values - average
    variance = jnp.mean(centred * centred, axis=-1, keepdims=True)
    return centred * lax.rsqrt(variance + 1e-05) * gain_row + bias_row


def rotary(values, positions):
    half_width = ROT // 2
    frequency = jnp.exp(
        jnp.arange(half_width, dtype=jnp.float32) * (-2.0 * math.log(10000.0) / ROT)
    )
    angles = positions.astype(jnp.float32)[:, None] * frequency[None, :]
    cosine = jnp.cos(angles)[:, None, :]
    sine_part = jnp.sin(angles)[:, None, :]
    low_half = values[..., :half_width]
    high_half = values[..., half_width:ROT]
    return jnp.concatenate(
        [
            low_half * cosine - high_half * sine_part,
            high_half * cosine + low_half * sine_part,
            values[..., ROT:],
        ],
        axis=-1,
    )


def _group_ids(whole, tp_count):
    seq_index = lax.axis_index("seq")
    tp_index = lax.axis_index("tp")
    if whole:
        me = seq_index * tp_count + tp_index

        def peer(j):
            return (j // tp_count, j % tp_count)

    else:
        me = seq_index

        def peer(j):
            return (j, tp_index)

    return me, peer


_KERNEL_IDS = {}


def _kernel_id(key):
    if key not in _KERNEL_IDS:
        _KERNEL_IDS[key] = len(_KERNEL_IDS)
    return _KERNEL_IDS[key]


def _enter(n, me, peer):
    barrier = pltpu.get_barrier_semaphore()

    def greet(i, carry):
        j = lax.rem(me + i, n)
        pl.semaphore_signal(barrier, 1, device_id=peer(j), device_id_type=MESH_IDS)
        return carry

    lax.fori_loop(1, n, greet, 0)
    pl.semaphore_wait(barrier, n - 1)


def _rcopy(src, dst, send_sem, recv_sem, device):
    return pltpu.make_async_remote_copy(
        src_ref=src,
        dst_ref=dst,
        send_sem=send_sem,
        recv_sem=recv_sem,
        device_id=device,
        device_id_type=MESH_IDS,
    )


def _allreduce_kernel(n, whole, tp_count, x_ref, o_ref, rs_buf, ag_buf, s1, r1, s2, r2):
    me, peer = _group_ids(whole, tp_count)
    _enter(n, me, peer)

    def start_scatter(i, carry):
        j = lax.rem(me + i, n)
        _rcopy(x_ref.at[j], rs_buf.at[me], s1.at[j], r1.at[me], peer(j)).start()
        return carry

    lax.fori_loop(1, n, start_scatter, 0)

    def gather_sum(i, acc):
        j = lax.rem(me + i, n)
        _rcopy(x_ref.at[j], rs_buf.at[j], s1.at[j], r1.at[j], peer(j)).wait_recv()
        return acc + rs_buf[j].astype(jnp.float32)

    total = lax.fori_loop(1, n, gather_sum, x_ref[me].astype(jnp.float32))
    ag_buf[me] = total.astype(ag_buf.dtype)

    def start_gather(i, carry):
        j = lax.rem(me + i, n)
        _rcopy(ag_buf.at[me], ag_buf.at[me], s2.at[j], r2.at[me], peer(j)).start()
        return carry

    lax.fori_loop(1, n, start_gather, 0)

    def finish(i, carry):
        j = lax.rem(me + i, n)
        _rcopy(ag_buf.at[j], ag_buf.at[j], s2.at[j], r2.at[j], peer(j)).wait_recv()
        _rcopy(x_ref.at[j], rs_buf.at[me], s1.at[j], r1.at[me], peer(j)).wait_send()
        _rcopy(ag_buf.at[me], ag_buf.at[me], s2.at[j], r2.at[me], peer(j)).wait_send()
        return carry

    lax.fori_loop(1, n, finish, 0)
    o_ref[...] = ag_buf[...]


def allreduce(x, whole, tp_count):
    n = x.shape[0]
    return pl.pallas_call(
        functools.partial(_allreduce_kernel, n, whole, tp_count),
        out_shape=jax.ShapeDtypeStruct(x.shape, x.dtype),
        in_specs=[pl.BlockSpec(memory_space=pltpu.VMEM)],
        out_specs=pl.BlockSpec(memory_space=pltpu.VMEM),
        scratch_shapes=[
            pltpu.VMEM(x.shape, x.dtype),
            pltpu.VMEM(x.shape, x.dtype),
            pltpu.SemaphoreType.DMA((n,)),
            pltpu.SemaphoreType.DMA((n,)),
            pltpu.SemaphoreType.DMA((n,)),
            pltpu.SemaphoreType.DMA((n,)),
        ],
        compiler_params=pltpu.CompilerParams(
            has_side_effects=True,
            collective_id=_kernel_id(("allreduce", whole, x.shape, str(x.dtype))),
        ),
    )(x)


def _allreduce_chip_kernel(tp_count, x_ref, o_ref, pbuf, sbuf, rs_buf, ag_buf, sa, ra, s1, r1, s2, r2, sd, rd):
    seq_index = lax.axis_index("seq")
    tp_index = lax.axis_index("tp")
    n = x_ref.shape[1]
    core = seq_index % 2
    other = 1 - core
    me = (seq_index // 2) * tp_count + tp_index
    partner = (seq_index + 1 - 2 * core, tp_index)

    def peer(j):
        return ((j // tp_count) * 2 + core, j % tp_count)

    barrier = pltpu.get_barrier_semaphore()

    def greet(i, carry):
        j = lax.rem(me + i, n)
        pl.semaphore_signal(barrier, 1, device_id=peer(j), device_id_type=MESH_IDS)
        return carry

    lax.fori_loop(1, n, greet, 0)
    pl.semaphore_signal(barrier, 1, device_id=partner, device_id_type=MESH_IDS)
    pl.semaphore_wait(barrier, n)

    swap = _rcopy(x_ref.at[other], pbuf, sa, ra, partner)
    swap.start()
    swap.wait_recv()
    sbuf[...] = (x_ref[core].astype(jnp.float32) + pbuf[...].astype(jnp.float32)).astype(sbuf.dtype)

    def start_scatter(i, carry):
        j = lax.rem(me + i, n)
        _rcopy(sbuf.at[j], rs_buf.at[me], s1.at[j], r1.at[me], peer(j)).start()
        return carry

    lax.fori_loop(1, n, start_scatter, 0)

    def gather_sum(i, acc):
        j = lax.rem(me + i, n)
        _rcopy(sbuf.at[j], rs_buf.at[j], s1.at[j], r1.at[j], peer(j)).wait_recv()
        return acc + rs_buf[j].astype(jnp.float32)

    total = lax.fori_loop(1, n, gather_sum, sbuf[me].astype(jnp.float32))
    ag_buf[core, me] = total.astype(ag_buf.dtype)

    def start_gather(i, carry):
        j = lax.rem(me + i, n)
        _rcopy(ag_buf.at[core, me], ag_buf.at[core, me], s2.at[j], r2.at[me], peer(j)).start()
        return carry

    lax.fori_loop(1, n, start_gather, 0)

    def finish(i, carry):
        j = lax.rem(me + i, n)
        _rcopy(ag_buf.at[core, j], ag_buf.at[core, j], s2.at[j], r2.at[j], peer(j)).wait_recv()
        _rcopy(sbuf.at[j], rs_buf.at[me], s1.at[j], r1.at[me], peer(j)).wait_send()
        _rcopy(ag_buf.at[core, me], ag_buf.at[core, me], s2.at[j], r2.at[me], peer(j)).wait_send()
        return carry

    lax.fori_loop(1, n, finish, 0)
    swap.wait_send()
    back = _rcopy(ag_buf.at[core], ag_buf.at[core], sd, rd, partner)
    back.start()
    _rcopy(ag_buf.at[other], ag_buf.at[other], sd, rd, partner).wait_recv()
    back.wait_send()
    o_ref[...] = ag_buf[...]


def allreduce_chip(x, tp_count, sum_dtype=None):
    n = x.shape[1]
    half = x.shape[1:]
    sum_dtype = x.dtype if sum_dtype is None else sum_dtype
    return pl.pallas_call(
        functools.partial(_allreduce_chip_kernel, tp_count),
        out_shape=jax.ShapeDtypeStruct(x.shape, sum_dtype),
        in_specs=[pl.BlockSpec(memory_space=pltpu.VMEM)],
        out_specs=pl.BlockSpec(memory_space=pltpu.VMEM),
        scratch_shapes=[
            pltpu.VMEM(half, x.dtype),
            pltpu.VMEM(half, x.dtype),
            pltpu.VMEM(half, x.dtype),
            pltpu.VMEM(x.shape, sum_dtype),
            pltpu.SemaphoreType.DMA(()),
            pltpu.SemaphoreType.DMA(()),
            pltpu.SemaphoreType.DMA((n,)),
            pltpu.SemaphoreType.DMA((n,)),
            pltpu.SemaphoreType.DMA((n,)),
            pltpu.SemaphoreType.DMA((n,)),
            pltpu.SemaphoreType.DMA(()),
            pltpu.SemaphoreType.DMA(()),
        ],
        compiler_params=pltpu.CompilerParams(
            has_side_effects=True,
            collective_id=_kernel_id(("allreduce_chip", x.shape, str(x.dtype), str(sum_dtype))),
        ),
    )(x)


def _all_to_all_kernel(n, whole, tp_count, x_ref, o_ref, buf, s1, r1):
    me, peer = _group_ids(whole, tp_count)
    _enter(n, me, peer)

    def start(i, carry):
        j = lax.rem(me + i, n)
        _rcopy(x_ref.at[j], buf.at[me], s1.at[j], r1.at[me], peer(j)).start()
        return carry

    lax.fori_loop(1, n, start, 0)

    def finish(i, carry):
        j = lax.rem(me + i, n)
        _rcopy(x_ref.at[j], buf.at[j], s1.at[j], r1.at[j], peer(j)).wait_recv()
        _rcopy(x_ref.at[j], buf.at[me], s1.at[j], r1.at[me], peer(j)).wait_send()
        return carry

    lax.fori_loop(1, n, finish, 0)
    buf[me] = x_ref[me]
    o_ref[...] = buf[...]


def all_to_all(x, whole, tp_count):
    n = x.shape[0]
    return pl.pallas_call(
        functools.partial(_all_to_all_kernel, n, whole, tp_count),
        out_shape=jax.ShapeDtypeStruct(x.shape, x.dtype),
        in_specs=[pl.BlockSpec(memory_space=pltpu.VMEM)],
        out_specs=pl.BlockSpec(memory_space=pltpu.VMEM),
        scratch_shapes=[
            pltpu.VMEM(x.shape, x.dtype),
            pltpu.SemaphoreType.DMA((n,)),
            pltpu.SemaphoreType.DMA((n,)),
        ],
        compiler_params=pltpu.CompilerParams(
            has_side_effects=True,
            collective_id=_kernel_id(("all_to_all", whole, x.shape, str(x.dtype))),
        ),
    )(x)


def per_device(
    token_ids,
    embedding,
    group_of,
    prefix_len,
    tail_len,
    block_map,
    k_cache,
    v_cache,
    ln_gain,
    ln_bias,
    w_qkv,
    w_fc1,
    b_fc1,
    w_out,
    w_fc2,
):
    tp_count = lax.axis_size("tp")
    seq_count = lax.axis_size("seq")
    all_count = tp_count * seq_count
    seq_index = lax.axis_index("seq")
    tp_index = lax.axis_index("tp")
    requests = token_ids.shape[0]
    new_tokens = token_ids.shape[1]
    rows = requests * new_tokens
    groups = prefix_len.shape[0]
    heads_local = HEADS // tp_count
    width = embedding.shape[1]
    score_scale = 1.0 / math.sqrt(HEAD_DIM)

    vocab_rows = embedding.shape[0]
    first_row = (seq_index * tp_count + tp_index) * vocab_rows
    local_ids = token_ids.reshape(-1) - first_row
    inside = (local_ids >= 0) & (local_ids < vocab_rows)
    picked = jnp.take(embedding, jnp.clip(local_ids, 0, vocab_rows - 1), axis=0)
    picked = jnp.where(inside[:, None], picked, jnp.zeros_like(picked))
    start_states = allreduce_chip(picked.reshape(2, all_count // 2, -1, 128), tp_count)
    hidden_state = start_states.reshape(rows, width).astype(jnp.float32)

    group_hit = group_of[:, None] == jnp.arange(groups, dtype=jnp.int32)[None, :]
    shared_len = jnp.sum(jnp.where(group_hit, prefix_len[None, :], 0), axis=1)
    base_positions = shared_len + tail_len
    positions = (base_positions[:, None] + jnp.arange(new_tokens, dtype=jnp.int32)[None, :]).reshape(-1)
    seg_len = jnp.concatenate([prefix_len, tail_len])
    seg_count = seg_len.shape[0]
    blocks_local = block_map.shape[0]
    seg_blk = block_map[:, 0]
    rank_blk = block_map[:, 1]
    seg_hit = seg_blk[:, None] == jnp.arange(seg_count, dtype=jnp.int32)[None, :]
    len_blk = jnp.sum(jnp.where(seg_hit, seg_len[None, :], 0), axis=1)
    slot_positions = rank_blk[:, None] * BLOCK + jnp.arange(BLOCK, dtype=jnp.int32)[None, :]
    live_slot = ((seg_blk[:, None] >= 0) & (slot_positions < len_blk[:, None])).reshape(-1)
    seg_slot = jnp.broadcast_to(seg_blk[:, None], (blocks_local, BLOCK)).reshape(-1)
    own_tail = seg_slot[None, :] == (groups + jnp.arange(requests, dtype=jnp.int32))[:, None]
    own_prompt = seg_slot[None, :] == group_of[:, None]
    allowed = (own_tail | own_prompt) & live_slot[None, :]
    allowed = jnp.repeat(allowed, new_tokens, axis=0)

    rows_local = w_qkv.shape[1]
    unit_count = w_fc2.shape[1]
    sub_width = w_out.shape[1]
    pieces = HEAD_DIM // sub_width
    my_head = seq_index // pieces
    my_piece = seq_index % pieces
    causal = (
        jnp.arange(new_tokens, dtype=jnp.int32)[None, :]
        <= jnp.arange(new_tokens, dtype=jnp.int32)[:, None]
    )

    head_of = jnp.arange(seq_count, dtype=jnp.int32) // pieces
    qkv_heads = w_qkv.reshape(LAYERS, rows_local, 3, heads_local, HEAD_DIM)
    qkv_part = jnp.take(qkv_heads, head_of, axis=3)
    qkv_part = qkv_part.transpose(3, 0, 1, 2, 4).reshape(seq_count, LAYERS, rows_local, 3 * HEAD_DIM)
    fc1_part = w_fc1.reshape(LAYERS, rows_local, seq_count, unit_count).transpose(2, 0, 1, 3)
    message = jnp.concatenate([qkv_part, fc1_part], axis=-1)
    cols_mine = message.shape[-1]
    got_w = all_to_all(message.reshape(seq_count, LAYERS * rows_local, cols_mine), False, tp_count)
    w_mine = (
        got_w.reshape(seq_count, LAYERS, rows_local, cols_mine)
        .transpose(1, 0, 2, 3)
        .reshape(LAYERS, seq_count * rows_local, cols_mine)
    )
    for layer_index in range(LAYERS):
        normed = layer_norm(hidden_state, ln_gain[layer_index], ln_bias[layer_index]).astype(
            jnp.bfloat16
        )
        local = jnp.dot(normed, w_mine[layer_index], preferred_element_type=jnp.float32)
        q_h = rotary(local[:, None, 0:HEAD_DIM], positions)[:, 0].astype(jnp.bfloat16)
        k_h = rotary(local[:, None, HEAD_DIM : 2 * HEAD_DIM], positions)[:, 0].astype(jnp.bfloat16)
        v_h = local[:, 2 * HEAD_DIM : 3 * HEAD_DIM].astype(jnp.bfloat16)
        pre_act = local[:, 3 * HEAD_DIM :]
        pre_act = (
            pre_act
            + lax.dynamic_slice_in_dim(b_fc1[layer_index], seq_index * unit_count, unit_count, 0)[
                None, :
            ]
        )
        activated = jax.nn.gelu(pre_act, approximate=True).astype(jnp.bfloat16)
        q_piece = lax.dynamic_slice_in_dim(q_h, my_piece * sub_width, sub_width, 1).T
        q_all = all_to_all(jnp.broadcast_to(q_piece[None], (seq_count,) + q_piece.shape), False, tp_count)
        queries = (
            q_all.reshape(heads_local, pieces, sub_width, rows)
            .transpose(3, 0, 1, 2)
            .reshape(rows, heads_local, HEAD_DIM)
        )
        head_cols = (
            jnp.arange(heads_local * HEAD_DIM, dtype=jnp.int32)[None, :] // HEAD_DIM
            == jnp.arange(heads_local, dtype=jnp.int32)[:, None]
        )
        q_block = jnp.where(
            head_cols[:, None, :], queries.reshape(rows, heads_local * HEAD_DIM)[None], 0
        ).astype(jnp.bfloat16)
        scores = (
            jnp.einsum(
                "hrc,sc->hrs", q_block, k_cache[layer_index], preferred_element_type=jnp.float32
            )
            * score_scale
        )
        scores = jnp.where(allowed[None], scores, very_negative)
        part_max = jnp.max(scores, axis=2)
        weights = jnp.where(allowed[None], jnp.exp(scores - part_max[..., None]), 0.0)
        part_sum = jnp.sum(weights, axis=2)
        out_all = jnp.einsum(
            "hrs,sc->hrc",
            weights.astype(jnp.bfloat16),
            v_cache[layer_index],
            preferred_element_type=jnp.float32,
        ).reshape(heads_local, rows, heads_local, HEAD_DIM)
        part_out = jnp.sum(
            jnp.where(
                (
                    jnp.arange(heads_local, dtype=jnp.int32)[:, None]
                    == jnp.arange(heads_local, dtype=jnp.int32)[None, :]
                )[:, None, :, None],
                out_all,
                0.0,
            ),
            axis=2,
        )
        out_pieces = (
            part_out.reshape(heads_local, rows, pieces, sub_width)
            .transpose(0, 2, 3, 1)
            .reshape(heads_local * pieces, sub_width, rows)
        )
        max_rows = jnp.repeat(part_max, pieces, axis=0)[:, None, :]
        sum_rows = jnp.repeat(part_sum, pieces, axis=0)[:, None, :]
        pad_rows = jnp.zeros((heads_local * pieces, 6, rows), jnp.float32)
        message = jnp.concatenate([out_pieces, max_rows, sum_rows, pad_rows], axis=1)
        received = all_to_all(message, False, tp_count)
        got_out = received[:, :sub_width, :]
        got_max = received[:, sub_width, :]
        got_sum = received[:, sub_width + 1, :]

        q_h = q_h.reshape(requests, new_tokens, HEAD_DIM)
        k_h = k_h.reshape(requests, new_tokens, HEAD_DIM)
        v_h = lax.dynamic_slice_in_dim(v_h, my_piece * sub_width, sub_width, 1)
        v_h = v_h.reshape(requests, new_tokens, sub_width)
        fresh_scores = (
            jnp.einsum("rtd,rud->rtu", q_h, k_h, preferred_element_type=jnp.float32) * score_scale
        )
        fresh_scores = jnp.where(causal[None], fresh_scores, very_negative)
        fresh_max = jnp.max(fresh_scores, axis=2)
        fresh_weights = jnp.where(causal[None], jnp.exp(fresh_scores - fresh_max[..., None]), 0.0)
        fresh_sum = jnp.sum(fresh_weights, axis=2)
        fresh_out = jnp.einsum(
            "rtu,rud->rtd",
            fresh_weights.astype(jnp.bfloat16),
            v_h,
            preferred_element_type=jnp.float32,
        )
        fresh_max = fresh_max.reshape(rows)
        fresh_sum = fresh_sum.reshape(rows)
        fresh_out = fresh_out.reshape(rows, sub_width)

        top = jnp.maximum(jnp.max(got_max, axis=0), fresh_max)
        scale_cache = jnp.exp(got_max - top[None, :])
        scale_fresh = jnp.exp(fresh_max - top)
        denom = jnp.sum(got_sum * scale_cache, axis=0) + fresh_sum * scale_fresh
        numer = jnp.sum(got_out * scale_cache[:, None, :], axis=0).T + fresh_out * scale_fresh[:, None]
        my_cols = (numer / denom[:, None]).astype(jnp.bfloat16)

        update = jnp.dot(my_cols, w_out[layer_index], preferred_element_type=jnp.float32)
        update = update + jnp.dot(activated, w_fc2[layer_index], preferred_element_type=jnp.float32)
        update = allreduce_chip(update.reshape(2, all_count // 2, -1, 128), tp_count, jnp.bfloat16)
        hidden_state = hidden_state + update.reshape(rows, width).astype(jnp.float32)
    return hidden_state.reshape(requests, new_tokens, width)


def solution(mesh):
    in_specs = (
        P(),
        P(("seq", "tp"), None),
        P(),
        P(),
        P(),
        P("seq", None),
        P(None, "seq", "tp"),
        P(None, "seq", "tp"),
        P(),
        P(),
        P(None, "seq", None, "tp"),
        P(None, "seq", "tp"),
        P(None, "tp"),
        P(None, ("tp", "seq"), None),
        P(None, ("tp", "seq"), None),
    )
    out_specs = P()
    return jax.shard_map(
        per_device, mesh=mesh, in_specs=in_specs, out_specs=out_specs, check_vma=False
    )
```

```python
import functools
import math

import jax
import jax.numpy as jnp
from jax import lax
from jax.experimental import pallas as pl
from jax.experimental.pallas import tpu as pltpu
from jax.sharding import PartitionSpec as P

HEADS = 32
HEAD_DIM = 64
ROT = 32
LAYERS = 2
BLOCK = 128
SPAN = 512
MESH_IDS = pl.DeviceIdType.MESH

very_negative = -1e30


def layer_norm(values, gain_row, bias_row):
    average = jnp.mean(values, axis=-1, keepdims=True)
    centred = values - average
    variance = jnp.mean(centred * centred, axis=-1, keepdims=True)
    return centred * lax.rsqrt(variance + 1e-05) * gain_row + bias_row


def rotary(values, positions):
    half_width = ROT // 2
    frequency = jnp.exp(
        jnp.arange(half_width, dtype=jnp.float32) * (-2.0 * math.log(10000.0) / ROT)
    )
    angles = positions.astype(jnp.float32)[:, None] * frequency[None, :]
    cosine = jnp.cos(angles)[:, None, :]
    sine_part = jnp.sin(angles)[:, None, :]
    low_half = values[..., :half_width]
    high_half = values[..., half_width:ROT]
    return jnp.concatenate(
        [
            low_half * cosine - high_half * sine_part,
            high_half * cosine + low_half * sine_part,
            values[..., ROT:],
        ],
        axis=-1,
    )


def _group_ids(whole, tp_count):
    seq_index = lax.axis_index("seq")
    tp_index = lax.axis_index("tp")
    if whole:
        me = seq_index * tp_count + tp_index

        def peer(j):
            return (j // tp_count, j % tp_count)

    else:
        me = seq_index

        def peer(j):
            return (j, tp_index)

    return me, peer


_KERNEL_IDS = {}


def _kernel_id(key):
    if key not in _KERNEL_IDS:
        _KERNEL_IDS[key] = len(_KERNEL_IDS)
    return _KERNEL_IDS[key]


def _enter(n, me, peer):
    barrier = pltpu.get_barrier_semaphore()

    def greet(i, carry):
        j = lax.rem(me + i, n)
        pl.semaphore_signal(barrier, 1, device_id=peer(j), device_id_type=MESH_IDS)
        return carry

    lax.fori_loop(1, n, greet, 0)
    pl.semaphore_wait(barrier, n - 1)


def _rcopy(src, dst, send_sem, recv_sem, device):
    return pltpu.make_async_remote_copy(
        src_ref=src,
        dst_ref=dst,
        send_sem=send_sem,
        recv_sem=recv_sem,
        device_id=device,
        device_id_type=MESH_IDS,
    )


def _allreduce_kernel(n, whole, tp_count, x_ref, o_ref, rs_buf, ag_buf, s1, r1, s2, r2):
    me, peer = _group_ids(whole, tp_count)
    _enter(n, me, peer)

    def start_scatter(i, carry):
        j = lax.rem(me + i, n)
        _rcopy(x_ref.at[j], rs_buf.at[me], s1.at[j], r1.at[me], peer(j)).start()
        return carry

    lax.fori_loop(1, n, start_scatter, 0)

    def gather_sum(i, acc):
        j = lax.rem(me + i, n)
        _rcopy(x_ref.at[j], rs_buf.at[j], s1.at[j], r1.at[j], peer(j)).wait_recv()
        return acc + rs_buf[j].astype(jnp.float32)

    total = lax.fori_loop(1, n, gather_sum, x_ref[me].astype(jnp.float32))
    ag_buf[me] = total.astype(ag_buf.dtype)

    def start_gather(i, carry):
        j = lax.rem(me + i, n)
        _rcopy(ag_buf.at[me], ag_buf.at[me], s2.at[j], r2.at[me], peer(j)).start()
        return carry

    lax.fori_loop(1, n, start_gather, 0)

    def finish(i, carry):
        j = lax.rem(me + i, n)
        _rcopy(ag_buf.at[j], ag_buf.at[j], s2.at[j], r2.at[j], peer(j)).wait_recv()
        _rcopy(x_ref.at[j], rs_buf.at[me], s1.at[j], r1.at[me], peer(j)).wait_send()
        _rcopy(ag_buf.at[me], ag_buf.at[me], s2.at[j], r2.at[me], peer(j)).wait_send()
        return carry

    lax.fori_loop(1, n, finish, 0)
    o_ref[...] = ag_buf[...]


def allreduce(x, whole, tp_count):
    n = x.shape[0]
    return pl.pallas_call(
        functools.partial(_allreduce_kernel, n, whole, tp_count),
        out_shape=jax.ShapeDtypeStruct(x.shape, x.dtype),
        in_specs=[pl.BlockSpec(memory_space=pltpu.VMEM)],
        out_specs=pl.BlockSpec(memory_space=pltpu.VMEM),
        scratch_shapes=[
            pltpu.VMEM(x.shape, x.dtype),
            pltpu.VMEM(x.shape, x.dtype),
            pltpu.SemaphoreType.DMA((n,)),
            pltpu.SemaphoreType.DMA((n,)),
            pltpu.SemaphoreType.DMA((n,)),
            pltpu.SemaphoreType.DMA((n,)),
        ],
        compiler_params=pltpu.CompilerParams(
            has_side_effects=True,
            collective_id=_kernel_id(("allreduce", whole, x.shape, str(x.dtype))),
        ),
    )(x)


def _allreduce_chip_kernel(tp_count, x_ref, o_ref, pbuf, sbuf, rs_buf, ag_buf, sa, ra, s1, r1, s2, r2, sd, rd):
    seq_index = lax.axis_index("seq")
    tp_index = lax.axis_index("tp")
    n = x_ref.shape[1]
    core = seq_index % 2
    other = 1 - core
    me = (seq_index // 2) * tp_count + tp_index
    partner = (seq_index + 1 - 2 * core, tp_index)

    def peer(j):
        return ((j // tp_count) * 2 + core, j % tp_count)

    barrier = pltpu.get_barrier_semaphore()

    def greet(i, carry):
        j = lax.rem(me + i, n)
        pl.semaphore_signal(barrier, 1, device_id=peer(j), device_id_type=MESH_IDS)
        return carry

    lax.fori_loop(1, n, greet, 0)
    pl.semaphore_signal(barrier, 1, device_id=partner, device_id_type=MESH_IDS)
    pl.semaphore_wait(barrier, n)
    _allreduce_chip_body(tp_count, x_ref, o_ref, pbuf, sbuf, rs_buf, ag_buf, sa, ra, s1, r1, s2, r2, sd, rd)


def _allreduce_chip_body(tp_count, x_ref, o_ref, pbuf, sbuf, rs_buf, ag_buf, sa, ra, s1, r1, s2, r2, sd, rd):
    seq_index = lax.axis_index("seq")
    tp_index = lax.axis_index("tp")
    n = x_ref.shape[1]
    core = seq_index % 2
    other = 1 - core
    me = (seq_index // 2) * tp_count + tp_index
    partner = (seq_index + 1 - 2 * core, tp_index)

    def peer(j):
        return ((j // tp_count) * 2 + core, j % tp_count)

    swap = _rcopy(x_ref.at[other], pbuf, sa, ra, partner)
    swap.start()
    swap.wait_recv()
    sbuf[...] = (x_ref[core].astype(jnp.float32) + pbuf[...].astype(jnp.float32)).astype(sbuf.dtype)

    def start_scatter(i, carry):
        j = lax.rem(me + i, n)
        _rcopy(sbuf.at[j], rs_buf.at[me], s1.at[j], r1.at[me], peer(j)).start()
        return carry

    lax.fori_loop(1, n, start_scatter, 0)

    def gather_sum(i, acc):
        j = lax.rem(me + i, n)
        _rcopy(sbuf.at[j], rs_buf.at[j], s1.at[j], r1.at[j], peer(j)).wait_recv()
        return acc + rs_buf[j].astype(jnp.float32)

    total = lax.fori_loop(1, n, gather_sum, sbuf[me].astype(jnp.float32))
    ag_buf[core, me] = total.astype(ag_buf.dtype)

    def start_gather(i, carry):
        j = lax.rem(me + i, n)
        _rcopy(ag_buf.at[core, me], ag_buf.at[core, me], s2.at[j], r2.at[me], peer(j)).start()
        return carry

    lax.fori_loop(1, n, start_gather, 0)

    def finish(i, carry):
        j = lax.rem(me + i, n)
        _rcopy(ag_buf.at[core, j], ag_buf.at[core, j], s2.at[j], r2.at[j], peer(j)).wait_recv()
        _rcopy(sbuf.at[j], rs_buf.at[me], s1.at[j], r1.at[me], peer(j)).wait_send()
        _rcopy(ag_buf.at[core, me], ag_buf.at[core, me], s2.at[j], r2.at[me], peer(j)).wait_send()
        return carry

    lax.fori_loop(1, n, finish, 0)
    swap.wait_send()
    back = _rcopy(ag_buf.at[core], ag_buf.at[core], sd, rd, partner)
    back.start()
    _rcopy(ag_buf.at[other], ag_buf.at[other], sd, rd, partner).wait_recv()
    back.wait_send()
    o_ref[...] = ag_buf[...]


def allreduce_chip(x, tp_count, sum_dtype=None):
    n = x.shape[1]
    half = x.shape[1:]
    sum_dtype = x.dtype if sum_dtype is None else sum_dtype
    return pl.pallas_call(
        functools.partial(_allreduce_chip_kernel, tp_count),
        out_shape=jax.ShapeDtypeStruct(x.shape, sum_dtype),
        in_specs=[pl.BlockSpec(memory_space=pltpu.VMEM)],
        out_specs=pl.BlockSpec(memory_space=pltpu.VMEM),
        scratch_shapes=[
            pltpu.VMEM(half, x.dtype),
            pltpu.VMEM(half, x.dtype),
            pltpu.VMEM(half, x.dtype),
            pltpu.VMEM(x.shape, sum_dtype),
            pltpu.SemaphoreType.DMA(()),
            pltpu.SemaphoreType.DMA(()),
            pltpu.SemaphoreType.DMA((n,)),
            pltpu.SemaphoreType.DMA((n,)),
            pltpu.SemaphoreType.DMA((n,)),
            pltpu.SemaphoreType.DMA((n,)),
            pltpu.SemaphoreType.DMA(()),
            pltpu.SemaphoreType.DMA(()),
        ],
        compiler_params=pltpu.CompilerParams(
            has_side_effects=True,
            collective_id=_kernel_id(("allreduce_chip", x.shape, str(x.dtype), str(sum_dtype))),
        ),
    )(x)


def _opening_kernel(tp_count, x_ref, w_ref, o_ref, wo_ref, pbuf, sbuf, rs_buf, ag_buf, sa, ra, s1, r1, s2, r2, sd, rd, wbuf, ws, wr):
    seq_index = lax.axis_index("seq")
    tp_index = lax.axis_index("tp")
    count = 2 * x_ref.shape[1]
    me_all = seq_index * tp_count + tp_index
    _enter(count, me_all, lambda j: (j // tp_count, j % tp_count))
    n = w_ref.shape[0]

    def start(i, carry):
        j = lax.rem(seq_index + i, n)
        _rcopy(w_ref.at[j], wbuf.at[seq_index], ws.at[j], wr.at[seq_index], (j, tp_index)).start()
        return carry

    lax.fori_loop(1, n, start, 0)
    _allreduce_chip_body(tp_count, x_ref, o_ref, pbuf, sbuf, rs_buf, ag_buf, sa, ra, s1, r1, s2, r2, sd, rd)

    def finish(i, carry):
        j = lax.rem(seq_index + i, n)
        _rcopy(w_ref.at[j], wbuf.at[j], ws.at[j], wr.at[j], (j, tp_index)).wait_recv()
        _rcopy(w_ref.at[j], wbuf.at[seq_index], ws.at[j], wr.at[seq_index], (j, tp_index)).wait_send()
        return carry

    lax.fori_loop(1, n, finish, 0)
    wbuf[seq_index] = w_ref[seq_index]
    wo_ref[...] = wbuf[...]


def opening(x, w, tp_count):
    n = x.shape[1]
    half = x.shape[1:]
    m = w.shape[0]
    return pl.pallas_call(
        functools.partial(_opening_kernel, tp_count),
        out_shape=(jax.ShapeDtypeStruct(x.shape, x.dtype), jax.ShapeDtypeStruct(w.shape, w.dtype)),
        in_specs=[pl.BlockSpec(memory_space=pltpu.VMEM)] * 2,
        out_specs=(pl.BlockSpec(memory_space=pltpu.VMEM), pl.BlockSpec(memory_space=pltpu.VMEM)),
        scratch_shapes=[
            pltpu.VMEM(half, x.dtype),
            pltpu.VMEM(half, x.dtype),
            pltpu.VMEM(half, x.dtype),
            pltpu.VMEM(x.shape, x.dtype),
            pltpu.SemaphoreType.DMA(()),
            pltpu.SemaphoreType.DMA(()),
            pltpu.SemaphoreType.DMA((n,)),
            pltpu.SemaphoreType.DMA((n,)),
            pltpu.SemaphoreType.DMA((n,)),
            pltpu.SemaphoreType.DMA((n,)),
            pltpu.SemaphoreType.DMA(()),
            pltpu.SemaphoreType.DMA(()),
            pltpu.VMEM(w.shape, w.dtype),
            pltpu.SemaphoreType.DMA((m,)),
            pltpu.SemaphoreType.DMA((m,)),
        ],
        compiler_params=pltpu.CompilerParams(
            has_side_effects=True,
            collective_id=_kernel_id(("opening", x.shape, w.shape)),
        ),
    )(x, w)


def _all_to_all_kernel(n, whole, tp_count, x_ref, o_ref, buf, s1, r1):
    me, peer = _group_ids(whole, tp_count)
    _enter(n, me, peer)

    def start(i, carry):
        j = lax.rem(me + i, n)
        _rcopy(x_ref.at[j], buf.at[me], s1.at[j], r1.at[me], peer(j)).start()
        return carry

    lax.fori_loop(1, n, start, 0)

    def finish(i, carry):
        j = lax.rem(me + i, n)
        _rcopy(x_ref.at[j], buf.at[j], s1.at[j], r1.at[j], peer(j)).wait_recv()
        _rcopy(x_ref.at[j], buf.at[me], s1.at[j], r1.at[me], peer(j)).wait_send()
        return carry

    lax.fori_loop(1, n, finish, 0)
    buf[me] = x_ref[me]
    o_ref[...] = buf[...]


def all_to_all(x, whole, tp_count):
    n = x.shape[0]
    return pl.pallas_call(
        functools.partial(_all_to_all_kernel, n, whole, tp_count),
        out_shape=jax.ShapeDtypeStruct(x.shape, x.dtype),
        in_specs=[pl.BlockSpec(memory_space=pltpu.VMEM)],
        out_specs=pl.BlockSpec(memory_space=pltpu.VMEM),
        scratch_shapes=[
            pltpu.VMEM(x.shape, x.dtype),
            pltpu.SemaphoreType.DMA((n,)),
            pltpu.SemaphoreType.DMA((n,)),
        ],
        compiler_params=pltpu.CompilerParams(
            has_side_effects=True,
            collective_id=_kernel_id(("all_to_all", whole, x.shape, str(x.dtype))),
        ),
    )(x)


def per_device(
    token_ids,
    embedding,
    group_of,
    prefix_len,
    tail_len,
    block_map,
    k_cache,
    v_cache,
    ln_gain,
    ln_bias,
    w_qkv,
    w_fc1,
    b_fc1,
    w_out,
    w_fc2,
):
    tp_count = lax.axis_size("tp")
    seq_count = lax.axis_size("seq")
    all_count = tp_count * seq_count
    seq_index = lax.axis_index("seq")
    tp_index = lax.axis_index("tp")
    requests = token_ids.shape[0]
    new_tokens = token_ids.shape[1]
    rows = requests * new_tokens
    groups = prefix_len.shape[0]
    heads_local = HEADS // tp_count
    width = embedding.shape[1]
    score_scale = 1.0 / math.sqrt(HEAD_DIM)

    vocab_rows = embedding.shape[0]
    first_row = (seq_index * tp_count + tp_index) * vocab_rows
    local_ids = token_ids.reshape(-1) - first_row
    inside = (local_ids >= 0) & (local_ids < vocab_rows)
    picked = jnp.take(embedding, jnp.clip(local_ids, 0, vocab_rows - 1), axis=0)
    picked = jnp.where(inside[:, None], picked, jnp.zeros_like(picked))

    group_hit = group_of[:, None] == jnp.arange(groups, dtype=jnp.int32)[None, :]
    shared_len = jnp.sum(jnp.where(group_hit, prefix_len[None, :], 0), axis=1)
    base_positions = shared_len + tail_len
    positions = (base_positions[:, None] + jnp.arange(new_tokens, dtype=jnp.int32)[None, :]).reshape(-1)
    seg_len = jnp.concatenate([prefix_len, tail_len])
    seg_count = seg_len.shape[0]
    blocks_local = block_map.shape[0]
    seg_blk = block_map[:, 0]
    rank_blk = block_map[:, 1]
    seg_hit = seg_blk[:, None] == jnp.arange(seg_count, dtype=jnp.int32)[None, :]
    len_blk = jnp.sum(jnp.where(seg_hit, seg_len[None, :], 0), axis=1)
    slot_positions = rank_blk[:, None] * BLOCK + jnp.arange(BLOCK, dtype=jnp.int32)[None, :]
    live_slot = ((seg_blk[:, None] >= 0) & (slot_positions < len_blk[:, None])).reshape(-1)
    seg_slot = jnp.broadcast_to(seg_blk[:, None], (blocks_local, BLOCK)).reshape(-1)
    own_tail = seg_slot[None, :] == (groups + jnp.arange(requests, dtype=jnp.int32))[:, None]
    own_prompt = seg_slot[None, :] == group_of[:, None]
    allowed = (own_tail | own_prompt) & live_slot[None, :]
    allowed = jnp.repeat(allowed, new_tokens, axis=0)

    rows_local = w_qkv.shape[1]
    unit_count = w_fc2.shape[1]
    sub_width = w_out.shape[1]
    pieces = HEAD_DIM // sub_width
    my_head = seq_index // pieces
    my_piece = seq_index % pieces
    causal = (
        jnp.arange(new_tokens, dtype=jnp.int32)[None, :]
        <= jnp.arange(new_tokens, dtype=jnp.int32)[:, None]
    )

    head_of = jnp.arange(seq_count, dtype=jnp.int32) // pieces
    qkv_heads = w_qkv.reshape(LAYERS, rows_local, 3, heads_local, HEAD_DIM)
    qkv_part = jnp.take(qkv_heads, head_of, axis=3)
    qkv_part = qkv_part.transpose(3, 0, 1, 2, 4).reshape(seq_count, LAYERS, rows_local, 3 * HEAD_DIM)
    fc1_part = w_fc1.reshape(LAYERS, rows_local, seq_count, unit_count).transpose(2, 0, 1, 3)
    message = jnp.concatenate([qkv_part, fc1_part], axis=-1)
    cols_mine = message.shape[-1]
    start_states, got_w = opening(
        picked.reshape(2, all_count // 2, -1, 128),
        message.reshape(seq_count, LAYERS * rows_local, cols_mine),
        tp_count,
    )
    hidden_state = start_states.reshape(rows, width).astype(jnp.float32)
    w_mine = (
        got_w.reshape(seq_count, LAYERS, rows_local, cols_mine)
        .transpose(1, 0, 2, 3)
        .reshape(LAYERS, seq_count * rows_local, cols_mine)
    )
    for layer_index in range(LAYERS):
        normed = layer_norm(hidden_state, ln_gain[layer_index], ln_bias[layer_index]).astype(
            jnp.bfloat16
        )
        local = jnp.dot(normed, w_mine[layer_index], preferred_element_type=jnp.float32)
        q_h = rotary(local[:, None, 0:HEAD_DIM], positions)[:, 0].astype(jnp.bfloat16)
        k_h = rotary(local[:, None, HEAD_DIM : 2 * HEAD_DIM], positions)[:, 0].astype(jnp.bfloat16)
        v_h = local[:, 2 * HEAD_DIM : 3 * HEAD_DIM].astype(jnp.bfloat16)
        pre_act = local[:, 3 * HEAD_DIM :]
        pre_act = (
            pre_act
            + lax.dynamic_slice_in_dim(b_fc1[layer_index], seq_index * unit_count, unit_count, 0)[
                None, :
            ]
        )
        activated = jax.nn.gelu(pre_act, approximate=True).astype(jnp.bfloat16)
        q_piece = lax.dynamic_slice_in_dim(q_h, my_piece * sub_width, sub_width, 1).T
        q_all = all_to_all(jnp.broadcast_to(q_piece[None], (seq_count,) + q_piece.shape), False, tp_count)
        queries = (
            q_all.reshape(heads_local, pieces, sub_width, rows)
            .transpose(3, 0, 1, 2)
            .reshape(rows, heads_local, HEAD_DIM)
        )
        head_cols = (
            jnp.arange(heads_local * HEAD_DIM, dtype=jnp.int32)[None, :] // HEAD_DIM
            == jnp.arange(heads_local, dtype=jnp.int32)[:, None]
        )
        q_block = jnp.where(
            head_cols[:, None, :], queries.reshape(rows, heads_local * HEAD_DIM)[None], 0
        ).astype(jnp.bfloat16)
        scores = (
            jnp.einsum(
                "hrc,sc->hrs", q_block, k_cache[layer_index], preferred_element_type=jnp.float32
            )
            * score_scale
        )
        scores = jnp.where(allowed[None], scores, very_negative)
        part_max = jnp.max(scores, axis=2)
        weights = jnp.where(allowed[None], jnp.exp(scores - part_max[..., None]), 0.0)
        part_sum = jnp.sum(weights, axis=2)
        out_all = jnp.einsum(
            "hrs,sc->hrc",
            weights.astype(jnp.bfloat16),
            v_cache[layer_index],
            preferred_element_type=jnp.float32,
        ).reshape(heads_local, rows, heads_local, HEAD_DIM)
        part_out = jnp.sum(
            jnp.where(
                (
                    jnp.arange(heads_local, dtype=jnp.int32)[:, None]
                    == jnp.arange(heads_local, dtype=jnp.int32)[None, :]
                )[:, None, :, None],
                out_all,
                0.0,
            ),
            axis=2,
        )
        out_pieces = (
            part_out.reshape(heads_local, rows, pieces, sub_width)
            .transpose(0, 2, 3, 1)
            .reshape(heads_local * pieces, sub_width, rows)
        )
        max_rows = jnp.repeat(part_max, pieces, axis=0)[:, None, :]
        sum_rows = jnp.repeat(part_sum, pieces, axis=0)[:, None, :]
        pad_rows = jnp.zeros((heads_local * pieces, 6, rows), jnp.float32)
        message = jnp.concatenate([out_pieces, max_rows, sum_rows, pad_rows], axis=1)
        received = all_to_all(message, False, tp_count)
        got_out = received[:, :sub_width, :]
        got_max = received[:, sub_width, :]
        got_sum = received[:, sub_width + 1, :]

        q_h = q_h.reshape(requests, new_tokens, HEAD_DIM)
        k_h = k_h.reshape(requests, new_tokens, HEAD_DIM)
        v_h = lax.dynamic_slice_in_dim(v_h, my_piece * sub_width, sub_width, 1)
        v_h = v_h.reshape(requests, new_tokens, sub_width)
        fresh_scores = (
            jnp.einsum("rtd,rud->rtu", q_h, k_h, preferred_element_type=jnp.float32) * score_scale
        )
        fresh_scores = jnp.where(causal[None], fresh_scores, very_negative)
        fresh_max = jnp.max(fresh_scores, axis=2)
        fresh_weights = jnp.where(causal[None], jnp.exp(fresh_scores - fresh_max[..., None]), 0.0)
        fresh_sum = jnp.sum(fresh_weights, axis=2)
        fresh_out = jnp.einsum(
            "rtu,rud->rtd",
            fresh_weights.astype(jnp.bfloat16),
            v_h,
            preferred_element_type=jnp.float32,
        )
        fresh_max = fresh_max.reshape(rows)
        fresh_sum = fresh_sum.reshape(rows)
        fresh_out = fresh_out.reshape(rows, sub_width)

        top = jnp.maximum(jnp.max(got_max, axis=0), fresh_max)
        scale_cache = jnp.exp(got_max - top[None, :])
        scale_fresh = jnp.exp(fresh_max - top)
        denom = jnp.sum(got_sum * scale_cache, axis=0) + fresh_sum * scale_fresh
        numer = jnp.sum(got_out * scale_cache[:, None, :], axis=0).T + fresh_out * scale_fresh[:, None]
        my_cols = (numer / denom[:, None]).astype(jnp.bfloat16)

        update = jnp.dot(my_cols, w_out[layer_index], preferred_element_type=jnp.float32)
        update = update + jnp.dot(activated, w_fc2[layer_index], preferred_element_type=jnp.float32)
        update = allreduce_chip(update.reshape(2, all_count // 2, -1, 128), tp_count, jnp.bfloat16)
        hidden_state = hidden_state + update.reshape(rows, width).astype(jnp.float32)
    return hidden_state.reshape(requests, new_tokens, width)


def solution(mesh):
    in_specs = (
        P(),
        P(("seq", "tp"), None),
        P(),
        P(),
        P(),
        P("seq", None),
        P(None, "seq", "tp"),
        P(None, "seq", "tp"),
        P(),
        P(),
        P(None, "seq", None, "tp"),
        P(None, "seq", "tp"),
        P(None, "tp"),
        P(None, ("tp", "seq"), None),
        P(None, ("tp", "seq"), None),
    )
    out_specs = P()
    return jax.shard_map(
        per_device, mesh=mesh, in_specs=in_specs, out_specs=out_specs, check_vma=False
    )
```

```python
import functools
import math

import jax
import numpy as np
import jax.numpy as jnp
from jax import lax
from jax.experimental import pallas as pl
from jax.experimental.pallas import tpu as pltpu
from jax.sharding import PartitionSpec as P

HEADS = 32
HEAD_DIM = 64
ROT = 32
LAYERS = 2
BLOCK = 128
SPAN = 512
MESH_IDS = pl.DeviceIdType.MESH

very_negative = -1e30


def layer_norm(values, gain_row, bias_row):
    average = jnp.mean(values, axis=-1, keepdims=True)
    centred = values - average
    variance = jnp.mean(centred * centred, axis=-1, keepdims=True)
    return centred * lax.rsqrt(variance + 1e-05) * gain_row + bias_row


def rotary(values, positions):
    half_width = ROT // 2
    frequency = jnp.exp(
        jnp.arange(half_width, dtype=jnp.float32) * (-2.0 * math.log(10000.0) / ROT)
    )
    angles = positions.astype(jnp.float32)[:, None] * frequency[None, :]
    cosine = jnp.cos(angles)[:, None, :]
    sine_part = jnp.sin(angles)[:, None, :]
    low_half = values[..., :half_width]
    high_half = values[..., half_width:ROT]
    return jnp.concatenate(
        [
            low_half * cosine - high_half * sine_part,
            high_half * cosine + low_half * sine_part,
            values[..., ROT:],
        ],
        axis=-1,
    )


def _group_ids(whole, tp_count):
    seq_index = lax.axis_index("seq")
    tp_index = lax.axis_index("tp")
    if whole:
        me = seq_index * tp_count + tp_index

        def peer(j):
            return (j // tp_count, j % tp_count)

    else:
        me = seq_index

        def peer(j):
            return (j, tp_index)

    return me, peer


_KERNEL_IDS = {}


def _kernel_id(key):
    if key not in _KERNEL_IDS:
        _KERNEL_IDS[key] = len(_KERNEL_IDS)
    return _KERNEL_IDS[key]


def _enter(n, me, peer):
    barrier = pltpu.get_barrier_semaphore()

    def greet(i, carry):
        j = lax.rem(me + i, n)
        pl.semaphore_signal(barrier, 1, device_id=peer(j), device_id_type=MESH_IDS)
        return carry

    lax.fori_loop(1, n, greet, 0)
    pl.semaphore_wait(barrier, n - 1)


def _rcopy(src, dst, send_sem, recv_sem, device):
    return pltpu.make_async_remote_copy(
        src_ref=src,
        dst_ref=dst,
        send_sem=send_sem,
        recv_sem=recv_sem,
        device_id=device,
        device_id_type=MESH_IDS,
    )


def _allreduce_kernel(n, whole, tp_count, x_ref, o_ref, rs_buf, ag_buf, s1, r1, s2, r2):
    me, peer = _group_ids(whole, tp_count)
    _enter(n, me, peer)

    def start_scatter(i, carry):
        j = lax.rem(me + i, n)
        _rcopy(x_ref.at[j], rs_buf.at[me], s1.at[j], r1.at[me], peer(j)).start()
        return carry

    lax.fori_loop(1, n, start_scatter, 0)

    def gather_sum(i, acc):
        j = lax.rem(me + i, n)
        _rcopy(x_ref.at[j], rs_buf.at[j], s1.at[j], r1.at[j], peer(j)).wait_recv()
        return acc + rs_buf[j].astype(jnp.float32)

    total = lax.fori_loop(1, n, gather_sum, x_ref[me].astype(jnp.float32))
    ag_buf[me] = total.astype(ag_buf.dtype)

    def start_gather(i, carry):
        j = lax.rem(me + i, n)
        _rcopy(ag_buf.at[me], ag_buf.at[me], s2.at[j], r2.at[me], peer(j)).start()
        return carry

    lax.fori_loop(1, n, start_gather, 0)

    def finish(i, carry):
        j = lax.rem(me + i, n)
        _rcopy(ag_buf.at[j], ag_buf.at[j], s2.at[j], r2.at[j], peer(j)).wait_recv()
        _rcopy(x_ref.at[j], rs_buf.at[me], s1.at[j], r1.at[me], peer(j)).wait_send()
        _rcopy(ag_buf.at[me], ag_buf.at[me], s2.at[j], r2.at[me], peer(j)).wait_send()
        return carry

    lax.fori_loop(1, n, finish, 0)
    o_ref[...] = ag_buf[...]


def allreduce(x, whole, tp_count):
    n = x.shape[0]
    return pl.pallas_call(
        functools.partial(_allreduce_kernel, n, whole, tp_count),
        out_shape=jax.ShapeDtypeStruct(x.shape, x.dtype),
        in_specs=[pl.BlockSpec(memory_space=pltpu.VMEM)],
        out_specs=pl.BlockSpec(memory_space=pltpu.VMEM),
        scratch_shapes=[
            pltpu.VMEM(x.shape, x.dtype),
            pltpu.VMEM(x.shape, x.dtype),
            pltpu.SemaphoreType.DMA((n,)),
            pltpu.SemaphoreType.DMA((n,)),
            pltpu.SemaphoreType.DMA((n,)),
            pltpu.SemaphoreType.DMA((n,)),
        ],
        compiler_params=pltpu.CompilerParams(
            has_side_effects=True,
            collective_id=_kernel_id(("allreduce", whole, x.shape, str(x.dtype))),
        ),
    )(x)


def _allreduce_chip_kernel(tp_count, x_ref, o_ref, pbuf, sbuf, rs_buf, ag_buf, sa, ra, s1, r1, s2, r2, sd, rd):
    seq_index = lax.axis_index("seq")
    tp_index = lax.axis_index("tp")
    n = x_ref.shape[1]
    core = seq_index % 2
    other = 1 - core
    me = (seq_index // 2) * tp_count + tp_index
    partner = (seq_index + 1 - 2 * core, tp_index)

    def peer(j):
        return ((j // tp_count) * 2 + core, j % tp_count)

    barrier = pltpu.get_barrier_semaphore()

    def greet(i, carry):
        j = lax.rem(me + i, n)
        pl.semaphore_signal(barrier, 1, device_id=peer(j), device_id_type=MESH_IDS)
        return carry

    lax.fori_loop(1, n, greet, 0)
    pl.semaphore_signal(barrier, 1, device_id=partner, device_id_type=MESH_IDS)
    pl.semaphore_wait(barrier, n)
    _allreduce_chip_body(tp_count, x_ref, o_ref, pbuf, sbuf, rs_buf, ag_buf, sa, ra, s1, r1, s2, r2, sd, rd)


def _allreduce_chip_body(tp_count, x_ref, o_ref, pbuf, sbuf, rs_buf, ag_buf, sa, ra, s1, r1, s2, r2, sd, rd):
    seq_index = lax.axis_index("seq")
    tp_index = lax.axis_index("tp")
    n = x_ref.shape[1]
    core = seq_index % 2
    other = 1 - core
    me = (seq_index // 2) * tp_count + tp_index
    partner = (seq_index + 1 - 2 * core, tp_index)

    def peer(j):
        return ((j // tp_count) * 2 + core, j % tp_count)

    swap = _rcopy(x_ref.at[other], pbuf, sa, ra, partner)
    swap.start()
    swap.wait_recv()
    sbuf[...] = (x_ref[core].astype(jnp.float32) + pbuf[...].astype(jnp.float32)).astype(sbuf.dtype)

    def start_scatter(i, carry):
        j = lax.rem(me + i, n)
        _rcopy(sbuf.at[j], rs_buf.at[me], s1.at[j], r1.at[me], peer(j)).start()
        return carry

    lax.fori_loop(1, n, start_scatter, 0)

    def gather_sum(i, acc):
        j = lax.rem(me + i, n)
        _rcopy(sbuf.at[j], rs_buf.at[j], s1.at[j], r1.at[j], peer(j)).wait_recv()
        return acc + rs_buf[j].astype(jnp.float32)

    total = lax.fori_loop(1, n, gather_sum, sbuf[me].astype(jnp.float32))
    ag_buf[core, me] = total.astype(ag_buf.dtype)

    def start_gather(i, carry):
        j = lax.rem(me + i, n)
        _rcopy(ag_buf.at[core, me], ag_buf.at[core, me], s2.at[j], r2.at[me], peer(j)).start()
        return carry

    lax.fori_loop(1, n, start_gather, 0)

    def finish(i, carry):
        j = lax.rem(me + i, n)
        _rcopy(ag_buf.at[core, j], ag_buf.at[core, j], s2.at[j], r2.at[j], peer(j)).wait_recv()
        _rcopy(sbuf.at[j], rs_buf.at[me], s1.at[j], r1.at[me], peer(j)).wait_send()
        _rcopy(ag_buf.at[core, me], ag_buf.at[core, me], s2.at[j], r2.at[me], peer(j)).wait_send()
        return carry

    lax.fori_loop(1, n, finish, 0)
    swap.wait_send()
    back = _rcopy(ag_buf.at[core], ag_buf.at[core], sd, rd, partner)
    back.start()
    _rcopy(ag_buf.at[other], ag_buf.at[other], sd, rd, partner).wait_recv()
    back.wait_send()
    o_ref[...] = ag_buf[...]


def allreduce_chip(x, tp_count, sum_dtype=None):
    n = x.shape[1]
    half = x.shape[1:]
    sum_dtype = x.dtype if sum_dtype is None else sum_dtype
    return pl.pallas_call(
        functools.partial(_allreduce_chip_kernel, tp_count),
        out_shape=jax.ShapeDtypeStruct(x.shape, sum_dtype),
        in_specs=[pl.BlockSpec(memory_space=pltpu.VMEM)],
        out_specs=pl.BlockSpec(memory_space=pltpu.VMEM),
        scratch_shapes=[
            pltpu.VMEM(half, x.dtype),
            pltpu.VMEM(half, x.dtype),
            pltpu.VMEM(half, x.dtype),
            pltpu.VMEM(x.shape, sum_dtype),
            pltpu.SemaphoreType.DMA(()),
            pltpu.SemaphoreType.DMA(()),
            pltpu.SemaphoreType.DMA((n,)),
            pltpu.SemaphoreType.DMA((n,)),
            pltpu.SemaphoreType.DMA((n,)),
            pltpu.SemaphoreType.DMA((n,)),
            pltpu.SemaphoreType.DMA(()),
            pltpu.SemaphoreType.DMA(()),
        ],
        compiler_params=pltpu.CompilerParams(
            has_side_effects=True,
            collective_id=_kernel_id(("allreduce_chip", x.shape, str(x.dtype), str(sum_dtype))),
        ),
    )(x)


def _opening_kernel(tp_count, x_ref, w_ref, o_ref, wo_ref, pbuf, sbuf, rs_buf, ag_buf, sa, ra, s1, r1, s2, r2, sd, rd, wbuf, ws, wr):
    seq_index = lax.axis_index("seq")
    tp_index = lax.axis_index("tp")
    count = 2 * x_ref.shape[1]
    me_all = seq_index * tp_count + tp_index
    _enter(count, me_all, lambda j: (j // tp_count, j % tp_count))
    n = w_ref.shape[0]

    def start(i, carry):
        j = lax.rem(seq_index + i, n)
        _rcopy(w_ref.at[j], wbuf.at[seq_index], ws.at[j], wr.at[seq_index], (j, tp_index)).start()
        return carry

    lax.fori_loop(1, n, start, 0)
    _allreduce_chip_body(tp_count, x_ref, o_ref, pbuf, sbuf, rs_buf, ag_buf, sa, ra, s1, r1, s2, r2, sd, rd)

    def finish(i, carry):
        j = lax.rem(seq_index + i, n)
        _rcopy(w_ref.at[j], wbuf.at[j], ws.at[j], wr.at[j], (j, tp_index)).wait_recv()
        _rcopy(w_ref.at[j], wbuf.at[seq_index], ws.at[j], wr.at[seq_index], (j, tp_index)).wait_send()
        return carry

    lax.fori_loop(1, n, finish, 0)
    wbuf[seq_index] = w_ref[seq_index]
    wo_ref[...] = wbuf[...]


def opening(x, w, tp_count):
    n = x.shape[1]
    half = x.shape[1:]
    m = w.shape[0]
    return pl.pallas_call(
        functools.partial(_opening_kernel, tp_count),
        out_shape=(jax.ShapeDtypeStruct(x.shape, x.dtype), jax.ShapeDtypeStruct(w.shape, w.dtype)),
        in_specs=[pl.BlockSpec(memory_space=pltpu.VMEM)] * 2,
        out_specs=(pl.BlockSpec(memory_space=pltpu.VMEM), pl.BlockSpec(memory_space=pltpu.VMEM)),
        scratch_shapes=[
            pltpu.VMEM(half, x.dtype),
            pltpu.VMEM(half, x.dtype),
            pltpu.VMEM(half, x.dtype),
            pltpu.VMEM(x.shape, x.dtype),
            pltpu.SemaphoreType.DMA(()),
            pltpu.SemaphoreType.DMA(()),
            pltpu.SemaphoreType.DMA((n,)),
            pltpu.SemaphoreType.DMA((n,)),
            pltpu.SemaphoreType.DMA((n,)),
            pltpu.SemaphoreType.DMA((n,)),
            pltpu.SemaphoreType.DMA(()),
            pltpu.SemaphoreType.DMA(()),
            pltpu.VMEM(w.shape, w.dtype),
            pltpu.SemaphoreType.DMA((m,)),
            pltpu.SemaphoreType.DMA((m,)),
        ],
        compiler_params=pltpu.CompilerParams(
            has_side_effects=True,
            collective_id=_kernel_id(("opening", x.shape, w.shape)),
        ),
    )(x, w)


def _all_to_all_kernel(n, whole, tp_count, x_ref, o_ref, buf, s1, r1):
    me, peer = _group_ids(whole, tp_count)
    _enter(n, me, peer)

    def start(i, carry):
        j = lax.rem(me + i, n)
        _rcopy(x_ref.at[j], buf.at[me], s1.at[j], r1.at[me], peer(j)).start()
        return carry

    lax.fori_loop(1, n, start, 0)

    def finish(i, carry):
        j = lax.rem(me + i, n)
        _rcopy(x_ref.at[j], buf.at[j], s1.at[j], r1.at[j], peer(j)).wait_recv()
        _rcopy(x_ref.at[j], buf.at[me], s1.at[j], r1.at[me], peer(j)).wait_send()
        return carry

    lax.fori_loop(1, n, finish, 0)
    buf[me] = x_ref[me]
    o_ref[...] = buf[...]


def all_to_all(x, whole, tp_count):
    n = x.shape[0]
    return pl.pallas_call(
        functools.partial(_all_to_all_kernel, n, whole, tp_count),
        out_shape=jax.ShapeDtypeStruct(x.shape, x.dtype),
        in_specs=[pl.BlockSpec(memory_space=pltpu.VMEM)],
        out_specs=pl.BlockSpec(memory_space=pltpu.VMEM),
        scratch_shapes=[
            pltpu.VMEM(x.shape, x.dtype),
            pltpu.SemaphoreType.DMA((n,)),
            pltpu.SemaphoreType.DMA((n,)),
        ],
        compiler_params=pltpu.CompilerParams(
            has_side_effects=True,
            collective_id=_kernel_id(("all_to_all", whole, x.shape, str(x.dtype))),
        ),
    )(x)


def per_device(
    token_ids,
    embedding,
    group_of,
    prefix_len,
    tail_len,
    block_map,
    k_cache,
    v_cache,
    ln_gain,
    ln_bias,
    w_qkv,
    w_fc1,
    b_fc1,
    w_out,
    w_fc2,
):
    tp_count = lax.axis_size("tp")
    seq_count = lax.axis_size("seq")
    all_count = tp_count * seq_count
    seq_index = lax.axis_index("seq")
    tp_index = lax.axis_index("tp")
    requests = token_ids.shape[0]
    new_tokens = token_ids.shape[1]
    rows = requests * new_tokens
    groups = prefix_len.shape[0]
    heads_local = HEADS // tp_count
    width = embedding.shape[1]
    score_scale = 1.0 / math.sqrt(HEAD_DIM)

    vocab_rows = embedding.shape[0]
    first_row = (seq_index * tp_count + tp_index) * vocab_rows
    local_ids = token_ids.reshape(-1) - first_row
    inside = (local_ids >= 0) & (local_ids < vocab_rows)
    picked = jnp.take(embedding, jnp.clip(local_ids, 0, vocab_rows - 1), axis=0)
    picked = jnp.where(inside[:, None], picked, jnp.zeros_like(picked))

    group_hit = group_of[:, None] == jnp.arange(groups, dtype=jnp.int32)[None, :]
    shared_len = jnp.sum(jnp.where(group_hit, prefix_len[None, :], 0), axis=1)
    base_positions = shared_len + tail_len
    positions = (base_positions[:, None] + jnp.arange(new_tokens, dtype=jnp.int32)[None, :]).reshape(-1)
    seg_len = jnp.concatenate([prefix_len, tail_len])
    seg_count = seg_len.shape[0]
    blocks_local = block_map.shape[0]
    seg_blk = block_map[:, 0]
    rank_blk = block_map[:, 1]
    seg_hit = seg_blk[:, None] == jnp.arange(seg_count, dtype=jnp.int32)[None, :]
    len_blk = jnp.sum(jnp.where(seg_hit, seg_len[None, :], 0), axis=1)
    slot_positions = rank_blk[:, None] * BLOCK + jnp.arange(BLOCK, dtype=jnp.int32)[None, :]
    live_slot = ((seg_blk[:, None] >= 0) & (slot_positions < len_blk[:, None])).reshape(-1)
    seg_slot = jnp.broadcast_to(seg_blk[:, None], (blocks_local, BLOCK)).reshape(-1)
    own_tail = seg_slot[None, :] == (groups + jnp.arange(requests, dtype=jnp.int32))[:, None]
    own_prompt = seg_slot[None, :] == group_of[:, None]
    allowed = (own_tail | own_prompt) & live_slot[None, :]
    allowed = jnp.repeat(allowed, new_tokens, axis=0)

    rows_local = w_qkv.shape[1]
    unit_count = w_fc2.shape[1]
    sub_width = w_out.shape[1]
    pieces = HEAD_DIM // sub_width
    my_head = seq_index // pieces
    my_piece = seq_index % pieces
    causal = (
        jnp.arange(new_tokens, dtype=jnp.int32)[None, :]
        <= jnp.arange(new_tokens, dtype=jnp.int32)[:, None]
    )

    half_rot = ROT // 2
    member = np.arange(seq_count)
    head_np, piece_np = member // pieces, member % pieces
    pair_width = 2 * sub_width
    q_idx = (head_np * HEAD_DIM + (piece_np // 2) * pair_width)[:, None] + np.arange(pair_width)[None, :]
    k_idx = heads_local * HEAD_DIM + (head_np * HEAD_DIM)[:, None] + np.arange(HEAD_DIM)[None, :]
    v_idx = (
        2 * heads_local * HEAD_DIM
        + (head_np * HEAD_DIM + piece_np * sub_width)[:, None]
        + np.arange(sub_width)[None, :]
    )
    f_idx = 3 * heads_local * HEAD_DIM + (member * unit_count)[:, None] + np.arange(unit_count)[None, :]
    pick = np.concatenate([q_idx, k_idx, v_idx, f_idx], axis=1).astype(np.int32)
    cols_mine = pick.shape[1]
    weights_t = jnp.concatenate(
        [
            w_qkv.transpose(2, 3, 0, 1).reshape(3 * heads_local * HEAD_DIM, LAYERS * rows_local),
            w_fc1.transpose(2, 0, 1).reshape(-1, LAYERS * rows_local),
        ],
        axis=0,
    )
    message = jnp.take(weights_t, jnp.asarray(pick), axis=0)
    start_states, got_w = opening(
        picked.reshape(2, all_count // 2, -1, 128),
        message,
        tp_count,
    )
    hidden_state = start_states.reshape(rows, width).astype(jnp.float32)
    w_mine = (
        got_w.reshape(seq_count, cols_mine, LAYERS, rows_local)
        .transpose(2, 1, 0, 3)
        .reshape(LAYERS, cols_mine, seq_count * rows_local)
    )
    q_end = pair_width
    k_end = q_end + HEAD_DIM
    v_end = k_end + sub_width
    angles = positions.astype(jnp.float32)[:, None] * jnp.exp(
        jnp.arange(half_rot, dtype=jnp.float32) * (-2.0 * math.log(10000.0) / ROT)
    )[None, :]
    cosine = jnp.cos(angles)
    sine_part = jnp.sin(angles)
    for layer_index in range(LAYERS):
        normed = layer_norm(hidden_state, ln_gain[layer_index], ln_bias[layer_index]).astype(
            jnp.bfloat16
        )
        local = jnp.einsum(
            "rc,kc->rk", normed, w_mine[layer_index], preferred_element_type=jnp.float32
        )
        q_pair = local[:, :q_end]
        low_half = q_pair[:, :half_rot]
        high_half = q_pair[:, half_rot:]
        q_rot = jnp.concatenate(
            [low_half * cosine - high_half * sine_part, high_half * cosine + low_half * sine_part],
            axis=1,
        )
        q_pair = jnp.where(my_piece < 2, q_rot, q_pair)
        q_piece = lax.dynamic_slice_in_dim(q_pair, (my_piece % 2) * sub_width, sub_width, 1)
        q_piece = q_piece.astype(jnp.bfloat16).T
        k_h = rotary(local[:, None, q_end:k_end], positions)[:, 0].astype(jnp.bfloat16)
        v_h = local[:, k_end:v_end].astype(jnp.bfloat16)
        pre_act = local[:, v_end:]
        pre_act = (
            pre_act
            + lax.dynamic_slice_in_dim(b_fc1[layer_index], seq_index * unit_count, unit_count, 0)[
                None, :
            ]
        )
        activated = jax.nn.gelu(pre_act, approximate=True).astype(jnp.bfloat16)
        q_all = all_to_all(jnp.broadcast_to(q_piece[None], (seq_count,) + q_piece.shape), False, tp_count)
        queries = (
            q_all.reshape(heads_local, pieces, sub_width, rows)
            .transpose(3, 0, 1, 2)
            .reshape(rows, heads_local, HEAD_DIM)
        )
        head_cols = (
            jnp.arange(heads_local * HEAD_DIM, dtype=jnp.int32)[None, :] // HEAD_DIM
            == jnp.arange(heads_local, dtype=jnp.int32)[:, None]
        )
        q_block = jnp.where(
            head_cols[:, None, :], queries.reshape(rows, heads_local * HEAD_DIM)[None], 0
        ).astype(jnp.bfloat16)
        scores = (
            jnp.einsum(
                "hrc,sc->hrs", q_block, k_cache[layer_index], preferred_element_type=jnp.float32
            )
            * score_scale
        )
        scores = jnp.where(allowed[None], scores, very_negative)
        part_max = jnp.max(scores, axis=2)
        weights = jnp.where(allowed[None], jnp.exp(scores - part_max[..., None]), 0.0)
        part_sum = jnp.sum(weights, axis=2)
        out_all = jnp.einsum(
            "hrs,sc->hrc",
            weights.astype(jnp.bfloat16),
            v_cache[layer_index],
            preferred_element_type=jnp.float32,
        ).reshape(heads_local, rows, heads_local, HEAD_DIM)
        part_out = jnp.sum(
            jnp.where(
                (
                    jnp.arange(heads_local, dtype=jnp.int32)[:, None]
                    == jnp.arange(heads_local, dtype=jnp.int32)[None, :]
                )[:, None, :, None],
                out_all,
                0.0,
            ),
            axis=2,
        )
        out_pieces = (
            part_out.reshape(heads_local, rows, pieces, sub_width)
            .transpose(0, 2, 3, 1)
            .reshape(heads_local * pieces, sub_width, rows)
        )
        max_rows = jnp.repeat(part_max, pieces, axis=0)[:, None, :]
        sum_rows = jnp.repeat(part_sum, pieces, axis=0)[:, None, :]
        pad_rows = jnp.zeros((heads_local * pieces, 6, rows), jnp.float32)
        message = jnp.concatenate([out_pieces, max_rows, sum_rows, pad_rows], axis=1)
        received = all_to_all(message, False, tp_count)
        got_out = received[:, :sub_width, :]
        got_max = received[:, sub_width, :]
        got_sum = received[:, sub_width + 1, :]

        q_h = lax.dynamic_index_in_dim(queries, my_head, 1, keepdims=False)
        q_h = q_h.reshape(requests, new_tokens, HEAD_DIM)
        k_h = k_h.reshape(requests, new_tokens, HEAD_DIM)
        v_h = v_h.reshape(requests, new_tokens, sub_width)
        fresh_scores = (
            jnp.einsum("rtd,rud->rtu", q_h, k_h, preferred_element_type=jnp.float32) * score_scale
        )
        fresh_scores = jnp.where(causal[None], fresh_scores, very_negative)
        fresh_max = jnp.max(fresh_scores, axis=2)
        fresh_weights = jnp.where(causal[None], jnp.exp(fresh_scores - fresh_max[..., None]), 0.0)
        fresh_sum = jnp.sum(fresh_weights, axis=2)
        fresh_out = jnp.einsum(
            "rtu,rud->rtd",
            fresh_weights.astype(jnp.bfloat16),
            v_h,
            preferred_element_type=jnp.float32,
        )
        fresh_max = fresh_max.reshape(rows)
        fresh_sum = fresh_sum.reshape(rows)
        fresh_out = fresh_out.reshape(rows, sub_width)

        top = jnp.maximum(jnp.max(got_max, axis=0), fresh_max)
        scale_cache = jnp.exp(got_max - top[None, :])
        scale_fresh = jnp.exp(fresh_max - top)
        denom = jnp.sum(got_sum * scale_cache, axis=0) + fresh_sum * scale_fresh
        numer = jnp.sum(got_out * scale_cache[:, None, :], axis=0).T + fresh_out * scale_fresh[:, None]
        my_cols = (numer / denom[:, None]).astype(jnp.bfloat16)

        update = jnp.dot(my_cols, w_out[layer_index], preferred_element_type=jnp.float32)
        update = update + jnp.dot(activated, w_fc2[layer_index], preferred_element_type=jnp.float32)
        update = allreduce_chip(update.reshape(2, all_count // 2, -1, 128), tp_count, jnp.bfloat16)
        hidden_state = hidden_state + update.reshape(rows, width).astype(jnp.float32)
    return hidden_state.reshape(requests, new_tokens, width)


def solution(mesh):
    in_specs = (
        P(),
        P(("seq", "tp"), None),
        P(),
        P(),
        P(),
        P("seq", None),
        P(None, "seq", "tp"),
        P(None, "seq", "tp"),
        P(),
        P(),
        P(None, "seq", None, "tp"),
        P(None, "seq", "tp"),
        P(None, "tp"),
        P(None, ("tp", "seq"), None),
        P(None, ("tp", "seq"), None),
    )
    out_specs = P()
    return jax.shard_map(
        per_device, mesh=mesh, in_specs=in_specs, out_specs=out_specs, check_vma=False
    )
```

```python
import functools
import math

import jax
import numpy as np
import jax.numpy as jnp
from jax import lax
from jax.experimental import pallas as pl
from jax.experimental.pallas import tpu as pltpu
from jax.sharding import PartitionSpec as P

HEADS = 32
HEAD_DIM = 64
ROT = 32
LAYERS = 2
BLOCK = 128
SPAN = 512
MESH_IDS = pl.DeviceIdType.MESH

very_negative = -1e30


def layer_norm(values, gain_row, bias_row):
    average = jnp.mean(values, axis=-1, keepdims=True)
    centred = values - average
    variance = jnp.mean(centred * centred, axis=-1, keepdims=True)
    return centred * lax.rsqrt(variance + 1e-05) * gain_row + bias_row


def rotary(values, positions):
    half_width = ROT // 2
    frequency = jnp.exp(
        jnp.arange(half_width, dtype=jnp.float32) * (-2.0 * math.log(10000.0) / ROT)
    )
    angles = positions.astype(jnp.float32)[:, None] * frequency[None, :]
    cosine = jnp.cos(angles)[:, None, :]
    sine_part = jnp.sin(angles)[:, None, :]
    low_half = values[..., :half_width]
    high_half = values[..., half_width:ROT]
    return jnp.concatenate(
        [
            low_half * cosine - high_half * sine_part,
            high_half * cosine + low_half * sine_part,
            values[..., ROT:],
        ],
        axis=-1,
    )


def _group_ids(whole, tp_count):
    seq_index = lax.axis_index("seq")
    tp_index = lax.axis_index("tp")
    if whole:
        me = seq_index * tp_count + tp_index

        def peer(j):
            return (j // tp_count, j % tp_count)

    else:
        me = seq_index

        def peer(j):
            return (j, tp_index)

    return me, peer


_KERNEL_IDS = {}


def _kernel_id(key):
    if key not in _KERNEL_IDS:
        _KERNEL_IDS[key] = len(_KERNEL_IDS)
    return _KERNEL_IDS[key]


def _enter(n, me, peer):
    barrier = pltpu.get_barrier_semaphore()

    def greet(i, carry):
        j = lax.rem(me + i, n)
        pl.semaphore_signal(barrier, 1, device_id=peer(j), device_id_type=MESH_IDS)
        return carry

    lax.fori_loop(1, n, greet, 0)
    pl.semaphore_wait(barrier, n - 1)


def _rcopy(src, dst, send_sem, recv_sem, device):
    return pltpu.make_async_remote_copy(
        src_ref=src,
        dst_ref=dst,
        send_sem=send_sem,
        recv_sem=recv_sem,
        device_id=device,
        device_id_type=MESH_IDS,
    )


def _allreduce_kernel(n, whole, tp_count, x_ref, o_ref, rs_buf, ag_buf, s1, r1, s2, r2):
    me, peer = _group_ids(whole, tp_count)
    _enter(n, me, peer)

    def start_scatter(i, carry):
        j = lax.rem(me + i, n)
        _rcopy(x_ref.at[j], rs_buf.at[me], s1.at[j], r1.at[me], peer(j)).start()
        return carry

    lax.fori_loop(1, n, start_scatter, 0)

    def gather_sum(i, acc):
        j = lax.rem(me + i, n)
        _rcopy(x_ref.at[j], rs_buf.at[j], s1.at[j], r1.at[j], peer(j)).wait_recv()
        return acc + rs_buf[j].astype(jnp.float32)

    total = lax.fori_loop(1, n, gather_sum, x_ref[me].astype(jnp.float32))
    ag_buf[me] = total.astype(ag_buf.dtype)

    def start_gather(i, carry):
        j = lax.rem(me + i, n)
        _rcopy(ag_buf.at[me], ag_buf.at[me], s2.at[j], r2.at[me], peer(j)).start()
        return carry

    lax.fori_loop(1, n, start_gather, 0)

    def finish(i, carry):
        j = lax.rem(me + i, n)
        _rcopy(ag_buf.at[j], ag_buf.at[j], s2.at[j], r2.at[j], peer(j)).wait_recv()
        _rcopy(x_ref.at[j], rs_buf.at[me], s1.at[j], r1.at[me], peer(j)).wait_send()
        _rcopy(ag_buf.at[me], ag_buf.at[me], s2.at[j], r2.at[me], peer(j)).wait_send()
        return carry

    lax.fori_loop(1, n, finish, 0)
    o_ref[...] = ag_buf[...]


def allreduce(x, whole, tp_count):
    n = x.shape[0]
    return pl.pallas_call(
        functools.partial(_allreduce_kernel, n, whole, tp_count),
        out_shape=jax.ShapeDtypeStruct(x.shape, x.dtype),
        in_specs=[pl.BlockSpec(memory_space=pltpu.VMEM)],
        out_specs=pl.BlockSpec(memory_space=pltpu.VMEM),
        scratch_shapes=[
            pltpu.VMEM(x.shape, x.dtype),
            pltpu.VMEM(x.shape, x.dtype),
            pltpu.SemaphoreType.DMA((n,)),
            pltpu.SemaphoreType.DMA((n,)),
            pltpu.SemaphoreType.DMA((n,)),
            pltpu.SemaphoreType.DMA((n,)),
        ],
        compiler_params=pltpu.CompilerParams(
            has_side_effects=True,
            collective_id=_kernel_id(("allreduce", whole, x.shape, str(x.dtype))),
        ),
    )(x)


def _allreduce_chip_kernel(tp_count, x_ref, o_ref, pbuf, sbuf, rs_buf, ag_buf, sa, ra, s1, r1, s2, r2, sd, rd):
    seq_index = lax.axis_index("seq")
    tp_index = lax.axis_index("tp")
    n = x_ref.shape[1]
    core = seq_index % 2
    other = 1 - core
    me = (seq_index // 2) * tp_count + tp_index
    partner = (seq_index + 1 - 2 * core, tp_index)

    def peer(j):
        return ((j // tp_count) * 2 + core, j % tp_count)

    barrier = pltpu.get_barrier_semaphore()

    def greet(i, carry):
        j = lax.rem(me + i, n)
        pl.semaphore_signal(barrier, 1, device_id=peer(j), device_id_type=MESH_IDS)
        return carry

    lax.fori_loop(1, n, greet, 0)
    pl.semaphore_signal(barrier, 1, device_id=partner, device_id_type=MESH_IDS)
    pl.semaphore_wait(barrier, n)
    _allreduce_chip_body(tp_count, x_ref, o_ref, pbuf, sbuf, rs_buf, ag_buf, sa, ra, s1, r1, s2, r2, sd, rd)


def _allreduce_chip_body(tp_count, x_ref, o_ref, pbuf, sbuf, rs_buf, ag_buf, sa, ra, s1, r1, s2, r2, sd, rd):
    seq_index = lax.axis_index("seq")
    tp_index = lax.axis_index("tp")
    n = x_ref.shape[1]
    core = seq_index % 2
    other = 1 - core
    me = (seq_index // 2) * tp_count + tp_index
    partner = (seq_index + 1 - 2 * core, tp_index)

    def peer(j):
        return ((j // tp_count) * 2 + core, j % tp_count)

    swap = _rcopy(x_ref.at[other], pbuf, sa, ra, partner)
    swap.start()
    swap.wait_recv()
    sbuf[...] = (x_ref[core].astype(jnp.float32) + pbuf[...].astype(jnp.float32)).astype(sbuf.dtype)

    def start_scatter(i, carry):
        j = lax.rem(me + i, n)
        _rcopy(sbuf.at[j], rs_buf.at[me], s1.at[j], r1.at[me], peer(j)).start()
        return carry

    lax.fori_loop(1, n, start_scatter, 0)

    def gather_sum(i, acc):
        j = lax.rem(me + i, n)
        _rcopy(sbuf.at[j], rs_buf.at[j], s1.at[j], r1.at[j], peer(j)).wait_recv()
        return acc + rs_buf[j].astype(jnp.float32)

    total = lax.fori_loop(1, n, gather_sum, sbuf[me].astype(jnp.float32))
    ag_buf[core, me] = total.astype(ag_buf.dtype)

    def start_gather(i, carry):
        j = lax.rem(me + i, n)
        _rcopy(ag_buf.at[core, me], ag_buf.at[core, me], s2.at[j], r2.at[me], peer(j)).start()
        return carry

    lax.fori_loop(1, n, start_gather, 0)

    def finish(i, carry):
        j = lax.rem(me + i, n)
        _rcopy(ag_buf.at[core, j], ag_buf.at[core, j], s2.at[j], r2.at[j], peer(j)).wait_recv()
        _rcopy(sbuf.at[j], rs_buf.at[me], s1.at[j], r1.at[me], peer(j)).wait_send()
        _rcopy(ag_buf.at[core, me], ag_buf.at[core, me], s2.at[j], r2.at[me], peer(j)).wait_send()
        return carry

    lax.fori_loop(1, n, finish, 0)
    swap.wait_send()
    back = _rcopy(ag_buf.at[core], ag_buf.at[core], sd, rd, partner)
    back.start()
    _rcopy(ag_buf.at[other], ag_buf.at[other], sd, rd, partner).wait_recv()
    back.wait_send()
    o_ref[...] = ag_buf[...]


def allreduce_chip(x, tp_count, sum_dtype=None):
    n = x.shape[1]
    half = x.shape[1:]
    sum_dtype = x.dtype if sum_dtype is None else sum_dtype
    return pl.pallas_call(
        functools.partial(_allreduce_chip_kernel, tp_count),
        out_shape=jax.ShapeDtypeStruct(x.shape, sum_dtype),
        in_specs=[pl.BlockSpec(memory_space=pltpu.VMEM)],
        out_specs=pl.BlockSpec(memory_space=pltpu.VMEM),
        scratch_shapes=[
            pltpu.VMEM(half, x.dtype),
            pltpu.VMEM(half, x.dtype),
            pltpu.VMEM(half, x.dtype),
            pltpu.VMEM(x.shape, sum_dtype),
            pltpu.SemaphoreType.DMA(()),
            pltpu.SemaphoreType.DMA(()),
            pltpu.SemaphoreType.DMA((n,)),
            pltpu.SemaphoreType.DMA((n,)),
            pltpu.SemaphoreType.DMA((n,)),
            pltpu.SemaphoreType.DMA((n,)),
            pltpu.SemaphoreType.DMA(()),
            pltpu.SemaphoreType.DMA(()),
        ],
        compiler_params=pltpu.CompilerParams(
            has_side_effects=True,
            collective_id=_kernel_id(("allreduce_chip", x.shape, str(x.dtype), str(sum_dtype))),
        ),
    )(x)


def _opening_kernel(tp_count, x_ref, w_ref, o_ref, wo_ref, pbuf, sbuf, rs_buf, ag_buf, sa, ra, s1, r1, s2, r2, sd, rd, wbuf, ws, wr):
    seq_index = lax.axis_index("seq")
    tp_index = lax.axis_index("tp")
    count = 2 * x_ref.shape[1]
    me_all = seq_index * tp_count + tp_index
    _enter(count, me_all, lambda j: (j // tp_count, j % tp_count))
    n = w_ref.shape[0]

    def start(i, carry):
        j = lax.rem(seq_index + i, n)
        _rcopy(w_ref.at[j], wbuf.at[seq_index], ws.at[j], wr.at[seq_index], (j, tp_index)).start()
        return carry

    lax.fori_loop(1, n, start, 0)
    _allreduce_chip_body(tp_count, x_ref, o_ref, pbuf, sbuf, rs_buf, ag_buf, sa, ra, s1, r1, s2, r2, sd, rd)

    def finish(i, carry):
        j = lax.rem(seq_index + i, n)
        _rcopy(w_ref.at[j], wbuf.at[j], ws.at[j], wr.at[j], (j, tp_index)).wait_recv()
        _rcopy(w_ref.at[j], wbuf.at[seq_index], ws.at[j], wr.at[seq_index], (j, tp_index)).wait_send()
        return carry

    lax.fori_loop(1, n, finish, 0)
    wbuf[seq_index] = w_ref[seq_index]
    wo_ref[...] = wbuf[...]


def opening(x, w, tp_count):
    n = x.shape[1]
    half = x.shape[1:]
    m = w.shape[0]
    return pl.pallas_call(
        functools.partial(_opening_kernel, tp_count),
        out_shape=(jax.ShapeDtypeStruct(x.shape, x.dtype), jax.ShapeDtypeStruct(w.shape, w.dtype)),
        in_specs=[pl.BlockSpec(memory_space=pltpu.VMEM)] * 2,
        out_specs=(pl.BlockSpec(memory_space=pltpu.VMEM), pl.BlockSpec(memory_space=pltpu.VMEM)),
        scratch_shapes=[
            pltpu.VMEM(half, x.dtype),
            pltpu.VMEM(half, x.dtype),
            pltpu.VMEM(half, x.dtype),
            pltpu.VMEM(x.shape, x.dtype),
            pltpu.SemaphoreType.DMA(()),
            pltpu.SemaphoreType.DMA(()),
            pltpu.SemaphoreType.DMA((n,)),
            pltpu.SemaphoreType.DMA((n,)),
            pltpu.SemaphoreType.DMA((n,)),
            pltpu.SemaphoreType.DMA((n,)),
            pltpu.SemaphoreType.DMA(()),
            pltpu.SemaphoreType.DMA(()),
            pltpu.VMEM(w.shape, w.dtype),
            pltpu.SemaphoreType.DMA((m,)),
            pltpu.SemaphoreType.DMA((m,)),
        ],
        compiler_params=pltpu.CompilerParams(
            has_side_effects=True,
            collective_id=_kernel_id(("opening", x.shape, w.shape)),
        ),
    )(x, w)


def _all_to_all_kernel(n, whole, tp_count, x_ref, o_ref, buf, s1, r1):
    me, peer = _group_ids(whole, tp_count)
    _enter(n, me, peer)

    def start(i, carry):
        j = lax.rem(me + i, n)
        _rcopy(x_ref.at[j], buf.at[me], s1.at[j], r1.at[me], peer(j)).start()
        return carry

    lax.fori_loop(1, n, start, 0)

    def finish(i, carry):
        j = lax.rem(me + i, n)
        _rcopy(x_ref.at[j], buf.at[j], s1.at[j], r1.at[j], peer(j)).wait_recv()
        _rcopy(x_ref.at[j], buf.at[me], s1.at[j], r1.at[me], peer(j)).wait_send()
        return carry

    lax.fori_loop(1, n, finish, 0)
    buf[me] = x_ref[me]
    o_ref[...] = buf[...]


def all_to_all(x, whole, tp_count):
    n = x.shape[0]
    return pl.pallas_call(
        functools.partial(_all_to_all_kernel, n, whole, tp_count),
        out_shape=jax.ShapeDtypeStruct(x.shape, x.dtype),
        in_specs=[pl.BlockSpec(memory_space=pltpu.VMEM)],
        out_specs=pl.BlockSpec(memory_space=pltpu.VMEM),
        scratch_shapes=[
            pltpu.VMEM(x.shape, x.dtype),
            pltpu.SemaphoreType.DMA((n,)),
            pltpu.SemaphoreType.DMA((n,)),
        ],
        compiler_params=pltpu.CompilerParams(
            has_side_effects=True,
            collective_id=_kernel_id(("all_to_all", whole, x.shape, str(x.dtype))),
        ),
    )(x)


def per_device(
    token_ids,
    embedding,
    group_of,
    prefix_len,
    tail_len,
    block_map,
    k_cache,
    v_cache,
    ln_gain,
    ln_bias,
    w_qkv,
    w_fc1,
    b_fc1,
    w_out,
    w_fc2,
):
    tp_count = lax.axis_size("tp")
    seq_count = lax.axis_size("seq")
    all_count = tp_count * seq_count
    seq_index = lax.axis_index("seq")
    tp_index = lax.axis_index("tp")
    requests = token_ids.shape[0]
    new_tokens = token_ids.shape[1]
    rows = requests * new_tokens
    groups = prefix_len.shape[0]
    heads_local = HEADS // tp_count
    width = embedding.shape[1]
    score_scale = 1.0 / math.sqrt(HEAD_DIM)

    vocab_rows = embedding.shape[0]
    first_row = (seq_index * tp_count + tp_index) * vocab_rows
    local_ids = token_ids.reshape(-1) - first_row
    inside = (local_ids >= 0) & (local_ids < vocab_rows)
    picked = jnp.take(embedding, jnp.clip(local_ids, 0, vocab_rows - 1), axis=0)
    picked = jnp.where(inside[:, None], picked, jnp.zeros_like(picked))

    group_hit = group_of[:, None] == jnp.arange(groups, dtype=jnp.int32)[None, :]
    shared_len = jnp.sum(jnp.where(group_hit, prefix_len[None, :], 0), axis=1)
    base_positions = shared_len + tail_len
    positions = (base_positions[:, None] + jnp.arange(new_tokens, dtype=jnp.int32)[None, :]).reshape(-1)
    seg_len = jnp.concatenate([prefix_len, tail_len])
    seg_count = seg_len.shape[0]
    blocks_local = block_map.shape[0]
    seg_blk = block_map[:, 0]
    rank_blk = block_map[:, 1]
    seg_hit = seg_blk[:, None] == jnp.arange(seg_count, dtype=jnp.int32)[None, :]
    len_blk = jnp.sum(jnp.where(seg_hit, seg_len[None, :], 0), axis=1)
    slot_positions = rank_blk[:, None] * BLOCK + jnp.arange(BLOCK, dtype=jnp.int32)[None, :]
    live_slot = ((seg_blk[:, None] >= 0) & (slot_positions < len_blk[:, None])).reshape(-1)
    seg_slot = jnp.broadcast_to(seg_blk[:, None], (blocks_local, BLOCK)).reshape(-1)
    own_tail = seg_slot[None, :] == (groups + jnp.arange(requests, dtype=jnp.int32))[:, None]
    own_prompt = seg_slot[None, :] == group_of[:, None]
    allowed = (own_tail | own_prompt) & live_slot[None, :]
    allowed = jnp.repeat(allowed, new_tokens, axis=0)

    rows_local = w_qkv.shape[1]
    unit_count = w_fc2.shape[1]
    sub_width = w_out.shape[1]
    pieces = HEAD_DIM // sub_width
    my_head = seq_index // pieces
    my_piece = seq_index % pieces
    causal = (
        jnp.arange(new_tokens, dtype=jnp.int32)[None, :]
        <= jnp.arange(new_tokens, dtype=jnp.int32)[:, None]
    )

    half_rot = ROT // 2
    pair_width = 2 * sub_width
    qkv_t = w_qkv.transpose(2, 3, 0, 1).reshape(3, heads_local, HEAD_DIM, LAYERS * rows_local)
    q_t = qkv_t[0].reshape(heads_local, 1, HEAD_DIM // pair_width, 1, pair_width, LAYERS * rows_local)
    q_t = jnp.broadcast_to(
        q_t, (heads_local, 1, HEAD_DIM // pair_width, pieces // 2, pair_width, LAYERS * rows_local)
    )
    k_t = jnp.broadcast_to(
        qkv_t[1][:, None], (heads_local, pieces, HEAD_DIM, LAYERS * rows_local)
    )
    v_t = qkv_t[2].reshape(seq_count, sub_width, LAYERS * rows_local)
    f_t = w_fc1.transpose(2, 0, 1).reshape(seq_count, unit_count, LAYERS * rows_local)
    message = jnp.concatenate(
        [
            q_t.reshape(seq_count, pair_width, LAYERS * rows_local),
            k_t.reshape(seq_count, HEAD_DIM, LAYERS * rows_local),
            v_t,
            f_t,
        ],
        axis=1,
    )
    cols_mine = message.shape[1]
    start_states, got_w = opening(
        picked.reshape(2, all_count // 2, -1, 128),
        message,
        tp_count,
    )
    hidden_state = start_states.reshape(rows, width).astype(jnp.float32)
    w_mine = (
        got_w.reshape(seq_count, cols_mine, LAYERS, rows_local)
        .transpose(2, 1, 0, 3)
        .reshape(LAYERS, cols_mine, seq_count * rows_local)
    )
    q_end = pair_width
    k_end = q_end + HEAD_DIM
    v_end = k_end + sub_width
    angles = positions.astype(jnp.float32)[:, None] * jnp.exp(
        jnp.arange(half_rot, dtype=jnp.float32) * (-2.0 * math.log(10000.0) / ROT)
    )[None, :]
    cosine = jnp.cos(angles)
    sine_part = jnp.sin(angles)
    for layer_index in range(LAYERS):
        normed = layer_norm(hidden_state, ln_gain[layer_index], ln_bias[layer_index]).astype(
            jnp.bfloat16
        )
        local = jnp.einsum(
            "rc,kc->rk", normed, w_mine[layer_index], preferred_element_type=jnp.float32
        )
        q_pair = local[:, :q_end]
        low_half = q_pair[:, :half_rot]
        high_half = q_pair[:, half_rot:]
        q_rot = jnp.concatenate(
            [low_half * cosine - high_half * sine_part, high_half * cosine + low_half * sine_part],
            axis=1,
        )
        q_pair = jnp.where(my_piece < 2, q_rot, q_pair)
        q_piece = lax.dynamic_slice_in_dim(q_pair, (my_piece % 2) * sub_width, sub_width, 1)
        q_piece = q_piece.astype(jnp.bfloat16).T
        k_h = rotary(local[:, None, q_end:k_end], positions)[:, 0].astype(jnp.bfloat16)
        v_h = local[:, k_end:v_end].astype(jnp.bfloat16)
        pre_act = local[:, v_end:]
        pre_act = (
            pre_act
            + lax.dynamic_slice_in_dim(b_fc1[layer_index], seq_index * unit_count, unit_count, 0)[
                None, :
            ]
        )
        activated = jax.nn.gelu(pre_act, approximate=True).astype(jnp.bfloat16)
        q_all = all_to_all(jnp.broadcast_to(q_piece[None], (seq_count,) + q_piece.shape), False, tp_count)
        queries = (
            q_all.reshape(heads_local, pieces, sub_width, rows)
            .transpose(3, 0, 1, 2)
            .reshape(rows, heads_local, HEAD_DIM)
        )
        head_cols = (
            jnp.arange(heads_local * HEAD_DIM, dtype=jnp.int32)[None, :] // HEAD_DIM
            == jnp.arange(heads_local, dtype=jnp.int32)[:, None]
        )
        q_block = jnp.where(
            head_cols[:, None, :], queries.reshape(rows, heads_local * HEAD_DIM)[None], 0
        ).astype(jnp.bfloat16)
        scores = (
            jnp.einsum(
                "hrc,sc->hrs", q_block, k_cache[layer_index], preferred_element_type=jnp.float32
            )
            * score_scale
        )
        scores = jnp.where(allowed[None], scores, very_negative)
        part_max = jnp.max(scores, axis=2)
        weights = jnp.where(allowed[None], jnp.exp(scores - part_max[..., None]), 0.0)
        part_sum = jnp.sum(weights, axis=2)
        out_all = jnp.einsum(
            "hrs,sc->hrc",
            weights.astype(jnp.bfloat16),
            v_cache[layer_index],
            preferred_element_type=jnp.float32,
        ).reshape(heads_local, rows, heads_local, HEAD_DIM)
        part_out = jnp.sum(
            jnp.where(
                (
                    jnp.arange(heads_local, dtype=jnp.int32)[:, None]
                    == jnp.arange(heads_local, dtype=jnp.int32)[None, :]
                )[:, None, :, None],
                out_all,
                0.0,
            ),
            axis=2,
        )
        out_pieces = (
            part_out.reshape(heads_local, rows, pieces, sub_width)
            .transpose(0, 2, 3, 1)
            .reshape(heads_local * pieces, sub_width, rows)
        )
        max_rows = jnp.repeat(part_max, pieces, axis=0)[:, None, :]
        sum_rows = jnp.repeat(part_sum, pieces, axis=0)[:, None, :]
        pad_rows = jnp.zeros((heads_local * pieces, 6, rows), jnp.float32)
        message = jnp.concatenate([out_pieces, max_rows, sum_rows, pad_rows], axis=1)
        received = all_to_all(message, False, tp_count)
        got_out = received[:, :sub_width, :]
        got_max = received[:, sub_width, :]
        got_sum = received[:, sub_width + 1, :]

        q_h = lax.dynamic_index_in_dim(queries, my_head, 1, keepdims=False)
        q_h = q_h.reshape(requests, new_tokens, HEAD_DIM)
        k_h = k_h.reshape(requests, new_tokens, HEAD_DIM)
        v_h = v_h.reshape(requests, new_tokens, sub_width)
        fresh_scores = (
            jnp.einsum("rtd,rud->rtu", q_h, k_h, preferred_element_type=jnp.float32) * score_scale
        )
        fresh_scores = jnp.where(causal[None], fresh_scores, very_negative)
        fresh_max = jnp.max(fresh_scores, axis=2)
        fresh_weights = jnp.where(causal[None], jnp.exp(fresh_scores - fresh_max[..., None]), 0.0)
        fresh_sum = jnp.sum(fresh_weights, axis=2)
        fresh_out = jnp.einsum(
            "rtu,rud->rtd",
            fresh_weights.astype(jnp.bfloat16),
            v_h,
            preferred_element_type=jnp.float32,
        )
        fresh_max = fresh_max.reshape(rows)
        fresh_sum = fresh_sum.reshape(rows)
        fresh_out = fresh_out.reshape(rows, sub_width)

        top = jnp.maximum(jnp.max(got_max, axis=0), fresh_max)
        scale_cache = jnp.exp(got_max - top[None, :])
        scale_fresh = jnp.exp(fresh_max - top)
        denom = jnp.sum(got_sum * scale_cache, axis=0) + fresh_sum * scale_fresh
        numer = jnp.sum(got_out * scale_cache[:, None, :], axis=0).T + fresh_out * scale_fresh[:, None]
        my_cols = (numer / denom[:, None]).astype(jnp.bfloat16)

        update = jnp.dot(my_cols, w_out[layer_index], preferred_element_type=jnp.float32)
        update = update + jnp.dot(activated, w_fc2[layer_index], preferred_element_type=jnp.float32)
        update = allreduce_chip(update.reshape(2, all_count // 2, -1, 128), tp_count, jnp.bfloat16)
        hidden_state = hidden_state + update.reshape(rows, width).astype(jnp.float32)
    return hidden_state.reshape(requests, new_tokens, width)


def solution(mesh):
    in_specs = (
        P(),
        P(("seq", "tp"), None),
        P(),
        P(),
        P(),
        P("seq", None),
        P(None, "seq", "tp"),
        P(None, "seq", "tp"),
        P(),
        P(),
        P(None, "seq", None, "tp"),
        P(None, "seq", "tp"),
        P(None, "tp"),
        P(None, ("tp", "seq"), None),
        P(None, ("tp", "seq"), None),
    )
    out_specs = P()
    return jax.shard_map(
        per_device, mesh=mesh, in_specs=in_specs, out_specs=out_specs, check_vma=False
    )
```

```python
import functools
import math

import jax
import numpy as np
import jax.numpy as jnp
from jax import lax
from jax.experimental import pallas as pl
from jax.experimental.pallas import tpu as pltpu
from jax.sharding import PartitionSpec as P

HEADS = 32
HEAD_DIM = 64
ROT = 32
LAYERS = 2
BLOCK = 128
SPAN = 512
MESH_IDS = pl.DeviceIdType.MESH

very_negative = -1e30


def layer_norm(values, gain_row, bias_row):
    average = jnp.mean(values, axis=-1, keepdims=True)
    centred = values - average
    variance = jnp.mean(centred * centred, axis=-1, keepdims=True)
    return centred * lax.rsqrt(variance + 1e-05) * gain_row + bias_row


def rotary(values, positions):
    half_width = ROT // 2
    frequency = jnp.exp(
        jnp.arange(half_width, dtype=jnp.float32) * (-2.0 * math.log(10000.0) / ROT)
    )
    angles = positions.astype(jnp.float32)[:, None] * frequency[None, :]
    cosine = jnp.cos(angles)[:, None, :]
    sine_part = jnp.sin(angles)[:, None, :]
    low_half = values[..., :half_width]
    high_half = values[..., half_width:ROT]
    return jnp.concatenate(
        [
            low_half * cosine - high_half * sine_part,
            high_half * cosine + low_half * sine_part,
            values[..., ROT:],
        ],
        axis=-1,
    )


def _group_ids(whole, tp_count):
    seq_index = lax.axis_index("seq")
    tp_index = lax.axis_index("tp")
    if whole:
        me = seq_index * tp_count + tp_index

        def peer(j):
            return (j // tp_count, j % tp_count)

    else:
        me = seq_index

        def peer(j):
            return (j, tp_index)

    return me, peer


_KERNEL_IDS = {}


def _kernel_id(key):
    if key not in _KERNEL_IDS:
        _KERNEL_IDS[key] = len(_KERNEL_IDS)
    return _KERNEL_IDS[key]


def _enter(n, me, peer):
    barrier = pltpu.get_barrier_semaphore()

    def greet(i, carry):
        j = lax.rem(me + i, n)
        pl.semaphore_signal(barrier, 1, device_id=peer(j), device_id_type=MESH_IDS)
        return carry

    lax.fori_loop(1, n, greet, 0)
    pl.semaphore_wait(barrier, n - 1)


def _rcopy(src, dst, send_sem, recv_sem, device):
    return pltpu.make_async_remote_copy(
        src_ref=src,
        dst_ref=dst,
        send_sem=send_sem,
        recv_sem=recv_sem,
        device_id=device,
        device_id_type=MESH_IDS,
    )


def _allreduce_kernel(n, whole, tp_count, x_ref, o_ref, rs_buf, ag_buf, s1, r1, s2, r2):
    me, peer = _group_ids(whole, tp_count)
    _enter(n, me, peer)

    def start_scatter(i, carry):
        j = lax.rem(me + i, n)
        _rcopy(x_ref.at[j], rs_buf.at[me], s1.at[j], r1.at[me], peer(j)).start()
        return carry

    lax.fori_loop(1, n, start_scatter, 0)

    def gather_sum(i, acc):
        j = lax.rem(me + i, n)
        _rcopy(x_ref.at[j], rs_buf.at[j], s1.at[j], r1.at[j], peer(j)).wait_recv()
        return acc + rs_buf[j].astype(jnp.float32)

    total = lax.fori_loop(1, n, gather_sum, x_ref[me].astype(jnp.float32))
    ag_buf[me] = total.astype(ag_buf.dtype)

    def start_gather(i, carry):
        j = lax.rem(me + i, n)
        _rcopy(ag_buf.at[me], ag_buf.at[me], s2.at[j], r2.at[me], peer(j)).start()
        return carry

    lax.fori_loop(1, n, start_gather, 0)

    def finish(i, carry):
        j = lax.rem(me + i, n)
        _rcopy(ag_buf.at[j], ag_buf.at[j], s2.at[j], r2.at[j], peer(j)).wait_recv()
        _rcopy(x_ref.at[j], rs_buf.at[me], s1.at[j], r1.at[me], peer(j)).wait_send()
        _rcopy(ag_buf.at[me], ag_buf.at[me], s2.at[j], r2.at[me], peer(j)).wait_send()
        return carry

    lax.fori_loop(1, n, finish, 0)
    o_ref[...] = ag_buf[...]


def allreduce(x, whole, tp_count):
    n = x.shape[0]
    return pl.pallas_call(
        functools.partial(_allreduce_kernel, n, whole, tp_count),
        out_shape=jax.ShapeDtypeStruct(x.shape, x.dtype),
        in_specs=[pl.BlockSpec(memory_space=pltpu.VMEM)],
        out_specs=pl.BlockSpec(memory_space=pltpu.VMEM),
        scratch_shapes=[
            pltpu.VMEM(x.shape, x.dtype),
            pltpu.VMEM(x.shape, x.dtype),
            pltpu.SemaphoreType.DMA((n,)),
            pltpu.SemaphoreType.DMA((n,)),
            pltpu.SemaphoreType.DMA((n,)),
            pltpu.SemaphoreType.DMA((n,)),
        ],
        compiler_params=pltpu.CompilerParams(
            has_side_effects=True,
            collective_id=_kernel_id(("allreduce", whole, x.shape, str(x.dtype))),
        ),
    )(x)


def _allreduce_chip_kernel(tp_count, x_ref, o_ref, pbuf, sbuf, rs_buf, ag_buf, sa, ra, s1, r1, s2, r2, sd, rd):
    seq_index = lax.axis_index("seq")
    tp_index = lax.axis_index("tp")
    n = x_ref.shape[1]
    core = seq_index % 2
    other = 1 - core
    me = (seq_index // 2) * tp_count + tp_index
    partner = (seq_index + 1 - 2 * core, tp_index)

    def peer(j):
        return ((j // tp_count) * 2 + core, j % tp_count)

    barrier = pltpu.get_barrier_semaphore()

    def greet(i, carry):
        j = lax.rem(me + i, n)
        pl.semaphore_signal(barrier, 1, device_id=peer(j), device_id_type=MESH_IDS)
        return carry

    lax.fori_loop(1, n, greet, 0)
    pl.semaphore_signal(barrier, 1, device_id=partner, device_id_type=MESH_IDS)
    pl.semaphore_wait(barrier, n)
    _allreduce_chip_body(tp_count, x_ref, o_ref, pbuf, sbuf, rs_buf, ag_buf, sa, ra, s1, r1, s2, r2, sd, rd)


def _allreduce_chip_body(tp_count, x_ref, o_ref, pbuf, sbuf, rs_buf, ag_buf, sa, ra, s1, r1, s2, r2, sd, rd):
    seq_index = lax.axis_index("seq")
    tp_index = lax.axis_index("tp")
    n = x_ref.shape[1]
    core = seq_index % 2
    other = 1 - core
    me = (seq_index // 2) * tp_count + tp_index
    partner = (seq_index + 1 - 2 * core, tp_index)

    def peer(j):
        return ((j // tp_count) * 2 + core, j % tp_count)

    swap = _rcopy(x_ref.at[other], pbuf, sa, ra, partner)
    swap.start()
    swap.wait_recv()
    sbuf[...] = (x_ref[core].astype(jnp.float32) + pbuf[...].astype(jnp.float32)).astype(sbuf.dtype)

    def start_scatter(i, carry):
        j = lax.rem(me + i, n)
        _rcopy(sbuf.at[j], rs_buf.at[me], s1.at[j], r1.at[me], peer(j)).start()
        return carry

    lax.fori_loop(1, n, start_scatter, 0)

    def gather_sum(i, acc):
        j = lax.rem(me + i, n)
        _rcopy(sbuf.at[j], rs_buf.at[j], s1.at[j], r1.at[j], peer(j)).wait_recv()
        return acc + rs_buf[j].astype(jnp.float32)

    total = lax.fori_loop(1, n, gather_sum, sbuf[me].astype(jnp.float32))
    ag_buf[core, me] = total.astype(ag_buf.dtype)

    def start_gather(i, carry):
        j = lax.rem(me + i, n)
        _rcopy(ag_buf.at[core, me], ag_buf.at[core, me], s2.at[j], r2.at[me], peer(j)).start()
        return carry

    lax.fori_loop(1, n, start_gather, 0)

    def finish(i, carry):
        j = lax.rem(me + i, n)
        _rcopy(ag_buf.at[core, j], ag_buf.at[core, j], s2.at[j], r2.at[j], peer(j)).wait_recv()
        _rcopy(sbuf.at[j], rs_buf.at[me], s1.at[j], r1.at[me], peer(j)).wait_send()
        _rcopy(ag_buf.at[core, me], ag_buf.at[core, me], s2.at[j], r2.at[me], peer(j)).wait_send()
        return carry

    lax.fori_loop(1, n, finish, 0)
    swap.wait_send()
    back = _rcopy(ag_buf.at[core], ag_buf.at[core], sd, rd, partner)
    back.start()
    _rcopy(ag_buf.at[other], ag_buf.at[other], sd, rd, partner).wait_recv()
    back.wait_send()
    o_ref[...] = ag_buf[...]


def allreduce_chip(x, tp_count, sum_dtype=None):
    n = x.shape[1]
    half = x.shape[1:]
    sum_dtype = x.dtype if sum_dtype is None else sum_dtype
    return pl.pallas_call(
        functools.partial(_allreduce_chip_kernel, tp_count),
        out_shape=jax.ShapeDtypeStruct(x.shape, sum_dtype),
        in_specs=[pl.BlockSpec(memory_space=pltpu.VMEM)],
        out_specs=pl.BlockSpec(memory_space=pltpu.VMEM),
        scratch_shapes=[
            pltpu.VMEM(half, x.dtype),
            pltpu.VMEM(half, sum_dtype),
            pltpu.VMEM(half, sum_dtype),
            pltpu.VMEM(x.shape, sum_dtype),
            pltpu.SemaphoreType.DMA(()),
            pltpu.SemaphoreType.DMA(()),
            pltpu.SemaphoreType.DMA((n,)),
            pltpu.SemaphoreType.DMA((n,)),
            pltpu.SemaphoreType.DMA((n,)),
            pltpu.SemaphoreType.DMA((n,)),
            pltpu.SemaphoreType.DMA(()),
            pltpu.SemaphoreType.DMA(()),
        ],
        compiler_params=pltpu.CompilerParams(
            has_side_effects=True,
            collective_id=_kernel_id(("allreduce_chip", x.shape, str(x.dtype), str(sum_dtype))),
        ),
    )(x)


def _opening_kernel(tp_count, x_ref, w_ref, o_ref, wo_ref, pbuf, sbuf, rs_buf, ag_buf, sa, ra, s1, r1, s2, r2, sd, rd, wbuf, ws, wr):
    seq_index = lax.axis_index("seq")
    tp_index = lax.axis_index("tp")
    count = 2 * x_ref.shape[1]
    me_all = seq_index * tp_count + tp_index
    _enter(count, me_all, lambda j: (j // tp_count, j % tp_count))
    n = w_ref.shape[0]

    def start(i, carry):
        j = lax.rem(seq_index + i, n)
        _rcopy(w_ref.at[j], wbuf.at[seq_index], ws.at[j], wr.at[seq_index], (j, tp_index)).start()
        return carry

    lax.fori_loop(1, n, start, 0)
    _allreduce_chip_body(tp_count, x_ref, o_ref, pbuf, sbuf, rs_buf, ag_buf, sa, ra, s1, r1, s2, r2, sd, rd)

    def finish(i, carry):
        j = lax.rem(seq_index + i, n)
        _rcopy(w_ref.at[j], wbuf.at[j], ws.at[j], wr.at[j], (j, tp_index)).wait_recv()
        _rcopy(w_ref.at[j], wbuf.at[seq_index], ws.at[j], wr.at[seq_index], (j, tp_index)).wait_send()
        return carry

    lax.fori_loop(1, n, finish, 0)
    wbuf[seq_index] = w_ref[seq_index]
    wo_ref[...] = wbuf[...]


def opening(x, w, tp_count):
    n = x.shape[1]
    half = x.shape[1:]
    m = w.shape[0]
    return pl.pallas_call(
        functools.partial(_opening_kernel, tp_count),
        out_shape=(jax.ShapeDtypeStruct(x.shape, x.dtype), jax.ShapeDtypeStruct(w.shape, w.dtype)),
        in_specs=[pl.BlockSpec(memory_space=pltpu.VMEM)] * 2,
        out_specs=(pl.BlockSpec(memory_space=pltpu.VMEM), pl.BlockSpec(memory_space=pltpu.VMEM)),
        scratch_shapes=[
            pltpu.VMEM(half, x.dtype),
            pltpu.VMEM(half, x.dtype),
            pltpu.VMEM(half, x.dtype),
            pltpu.VMEM(x.shape, x.dtype),
            pltpu.SemaphoreType.DMA(()),
            pltpu.SemaphoreType.DMA(()),
            pltpu.SemaphoreType.DMA((n,)),
            pltpu.SemaphoreType.DMA((n,)),
            pltpu.SemaphoreType.DMA((n,)),
            pltpu.SemaphoreType.DMA((n,)),
            pltpu.SemaphoreType.DMA(()),
            pltpu.SemaphoreType.DMA(()),
            pltpu.VMEM(w.shape, w.dtype),
            pltpu.SemaphoreType.DMA((m,)),
            pltpu.SemaphoreType.DMA((m,)),
        ],
        compiler_params=pltpu.CompilerParams(
            has_side_effects=True,
            collective_id=_kernel_id(("opening", x.shape, w.shape)),
        ),
    )(x, w)


def _all_to_all_kernel(n, whole, tp_count, x_ref, o_ref, buf, s1, r1):
    me, peer = _group_ids(whole, tp_count)
    _enter(n, me, peer)

    def start(i, carry):
        j = lax.rem(me + i, n)
        _rcopy(x_ref.at[j], buf.at[me], s1.at[j], r1.at[me], peer(j)).start()
        return carry

    lax.fori_loop(1, n, start, 0)

    def finish(i, carry):
        j = lax.rem(me + i, n)
        _rcopy(x_ref.at[j], buf.at[j], s1.at[j], r1.at[j], peer(j)).wait_recv()
        _rcopy(x_ref.at[j], buf.at[me], s1.at[j], r1.at[me], peer(j)).wait_send()
        return carry

    lax.fori_loop(1, n, finish, 0)
    buf[me] = x_ref[me]
    o_ref[...] = buf[...]


def all_to_all(x, whole, tp_count):
    n = x.shape[0]
    return pl.pallas_call(
        functools.partial(_all_to_all_kernel, n, whole, tp_count),
        out_shape=jax.ShapeDtypeStruct(x.shape, x.dtype),
        in_specs=[pl.BlockSpec(memory_space=pltpu.VMEM)],
        out_specs=pl.BlockSpec(memory_space=pltpu.VMEM),
        scratch_shapes=[
            pltpu.VMEM(x.shape, x.dtype),
            pltpu.SemaphoreType.DMA((n,)),
            pltpu.SemaphoreType.DMA((n,)),
        ],
        compiler_params=pltpu.CompilerParams(
            has_side_effects=True,
            collective_id=_kernel_id(("all_to_all", whole, x.shape, str(x.dtype))),
        ),
    )(x)


def per_device(
    token_ids,
    embedding,
    group_of,
    prefix_len,
    tail_len,
    block_map,
    k_cache,
    v_cache,
    ln_gain,
    ln_bias,
    w_qkv,
    w_fc1,
    b_fc1,
    w_out,
    w_fc2,
):
    tp_count = lax.axis_size("tp")
    seq_count = lax.axis_size("seq")
    all_count = tp_count * seq_count
    seq_index = lax.axis_index("seq")
    tp_index = lax.axis_index("tp")
    requests = token_ids.shape[0]
    new_tokens = token_ids.shape[1]
    rows = requests * new_tokens
    groups = prefix_len.shape[0]
    heads_local = HEADS // tp_count
    width = embedding.shape[1]
    score_scale = 1.0 / math.sqrt(HEAD_DIM)

    vocab_rows = embedding.shape[0]
    first_row = (seq_index * tp_count + tp_index) * vocab_rows
    local_ids = token_ids.reshape(-1) - first_row
    inside = (local_ids >= 0) & (local_ids < vocab_rows)
    picked = jnp.take(embedding, jnp.clip(local_ids, 0, vocab_rows - 1), axis=0)
    picked = jnp.where(inside[:, None], picked, jnp.zeros_like(picked))

    group_hit = group_of[:, None] == jnp.arange(groups, dtype=jnp.int32)[None, :]
    shared_len = jnp.sum(jnp.where(group_hit, prefix_len[None, :], 0), axis=1)
    base_positions = shared_len + tail_len
    positions = (base_positions[:, None] + jnp.arange(new_tokens, dtype=jnp.int32)[None, :]).reshape(-1)
    seg_len = jnp.concatenate([prefix_len, tail_len])
    seg_count = seg_len.shape[0]
    blocks_local = block_map.shape[0]
    seg_blk = block_map[:, 0]
    rank_blk = block_map[:, 1]
    seg_hit = seg_blk[:, None] == jnp.arange(seg_count, dtype=jnp.int32)[None, :]
    len_blk = jnp.sum(jnp.where(seg_hit, seg_len[None, :], 0), axis=1)
    slot_positions = rank_blk[:, None] * BLOCK + jnp.arange(BLOCK, dtype=jnp.int32)[None, :]
    live_slot = ((seg_blk[:, None] >= 0) & (slot_positions < len_blk[:, None])).reshape(-1)
    seg_slot = jnp.broadcast_to(seg_blk[:, None], (blocks_local, BLOCK)).reshape(-1)
    own_tail = seg_slot[None, :] == (groups + jnp.arange(requests, dtype=jnp.int32))[:, None]
    own_prompt = seg_slot[None, :] == group_of[:, None]
    allowed = (own_tail | own_prompt) & live_slot[None, :]
    allowed = jnp.repeat(allowed, new_tokens, axis=0)

    rows_local = w_qkv.shape[1]
    unit_count = w_fc2.shape[1]
    sub_width = w_out.shape[1]
    pieces = HEAD_DIM // sub_width
    my_head = seq_index // pieces
    my_piece = seq_index % pieces
    causal = (
        jnp.arange(new_tokens, dtype=jnp.int32)[None, :]
        <= jnp.arange(new_tokens, dtype=jnp.int32)[:, None]
    )

    half_rot = ROT // 2
    pair_width = 2 * sub_width
    qkv_t = w_qkv.transpose(2, 3, 0, 1).reshape(3, heads_local, HEAD_DIM, LAYERS * rows_local)
    q_t = qkv_t[0].reshape(heads_local, 1, HEAD_DIM // pair_width, 1, pair_width, LAYERS * rows_local)
    q_t = jnp.broadcast_to(
        q_t, (heads_local, 1, HEAD_DIM // pair_width, pieces // 2, pair_width, LAYERS * rows_local)
    )
    k_t = jnp.broadcast_to(
        qkv_t[1][:, None], (heads_local, pieces, HEAD_DIM, LAYERS * rows_local)
    )
    v_t = qkv_t[2].reshape(seq_count, sub_width, LAYERS * rows_local)
    f_t = w_fc1.transpose(2, 0, 1).reshape(seq_count, unit_count, LAYERS * rows_local)
    message = jnp.concatenate(
        [
            q_t.reshape(seq_count, pair_width, LAYERS * rows_local),
            k_t.reshape(seq_count, HEAD_DIM, LAYERS * rows_local),
            v_t,
            f_t,
        ],
        axis=1,
    )
    cols_mine = message.shape[1]
    start_states, got_w = opening(
        picked.reshape(2, all_count // 2, -1, 128),
        message,
        tp_count,
    )
    hidden_state = start_states.reshape(rows, width).astype(jnp.float32)
    w_mine = (
        got_w.reshape(seq_count, cols_mine, LAYERS, rows_local)
        .transpose(2, 1, 0, 3)
        .reshape(LAYERS, cols_mine, seq_count * rows_local)
    )
    q_end = pair_width
    k_end = q_end + HEAD_DIM
    v_end = k_end + sub_width
    angles = positions.astype(jnp.float32)[:, None] * jnp.exp(
        jnp.arange(half_rot, dtype=jnp.float32) * (-2.0 * math.log(10000.0) / ROT)
    )[None, :]
    cosine = jnp.cos(angles)
    sine_part = jnp.sin(angles)
    for layer_index in range(LAYERS):
        normed = layer_norm(hidden_state, ln_gain[layer_index], ln_bias[layer_index]).astype(
            jnp.bfloat16
        )
        local = jnp.einsum(
            "rc,kc->rk", normed, w_mine[layer_index], preferred_element_type=jnp.float32
        )
        q_pair = local[:, :q_end]
        low_half = q_pair[:, :half_rot]
        high_half = q_pair[:, half_rot:]
        q_rot = jnp.concatenate(
            [low_half * cosine - high_half * sine_part, high_half * cosine + low_half * sine_part],
            axis=1,
        )
        q_pair = jnp.where(my_piece < 2, q_rot, q_pair)
        q_piece = lax.dynamic_slice_in_dim(q_pair, (my_piece % 2) * sub_width, sub_width, 1)
        q_piece = q_piece.astype(jnp.bfloat16).T
        k_h = rotary(local[:, None, q_end:k_end], positions)[:, 0].astype(jnp.bfloat16)
        v_h = local[:, k_end:v_end].astype(jnp.bfloat16)
        pre_act = local[:, v_end:]
        pre_act = (
            pre_act
            + lax.dynamic_slice_in_dim(b_fc1[layer_index], seq_index * unit_count, unit_count, 0)[
                None, :
            ]
        )
        activated = jax.nn.gelu(pre_act, approximate=True).astype(jnp.bfloat16)
        q_all = all_to_all(jnp.broadcast_to(q_piece[None], (seq_count,) + q_piece.shape), False, tp_count)
        queries = (
            q_all.reshape(heads_local, pieces, sub_width, rows)
            .transpose(3, 0, 1, 2)
            .reshape(rows, heads_local, HEAD_DIM)
        )
        head_cols = (
            jnp.arange(heads_local * HEAD_DIM, dtype=jnp.int32)[None, :] // HEAD_DIM
            == jnp.arange(heads_local, dtype=jnp.int32)[:, None]
        )
        q_block = jnp.where(
            head_cols[:, None, :], queries.reshape(rows, heads_local * HEAD_DIM)[None], 0
        ).astype(jnp.bfloat16)
        scores = (
            jnp.einsum(
                "hrc,sc->hrs", q_block, k_cache[layer_index], preferred_element_type=jnp.float32
            )
            * score_scale
        )
        scores = jnp.where(allowed[None], scores, very_negative)
        part_max = jnp.max(scores, axis=2)
        weights = jnp.where(allowed[None], jnp.exp(scores - part_max[..., None]), 0.0)
        part_sum = jnp.sum(weights, axis=2)
        out_all = jnp.einsum(
            "hrs,sc->hrc",
            weights.astype(jnp.bfloat16),
            v_cache[layer_index],
            preferred_element_type=jnp.float32,
        ).reshape(heads_local, rows, heads_local, HEAD_DIM)
        part_out = jnp.sum(
            jnp.where(
                (
                    jnp.arange(heads_local, dtype=jnp.int32)[:, None]
                    == jnp.arange(heads_local, dtype=jnp.int32)[None, :]
                )[:, None, :, None],
                out_all,
                0.0,
            ),
            axis=2,
        )
        out_pieces = (
            part_out.reshape(heads_local, rows, pieces, sub_width)
            .transpose(0, 2, 3, 1)
            .reshape(heads_local * pieces, sub_width, rows)
        )
        max_rows = jnp.repeat(part_max, pieces, axis=0)[:, None, :]
        sum_rows = jnp.repeat(part_sum, pieces, axis=0)[:, None, :]
        pad_rows = jnp.zeros((heads_local * pieces, 6, rows), jnp.float32)
        message = jnp.concatenate([out_pieces, max_rows, sum_rows, pad_rows], axis=1)
        received = all_to_all(message, False, tp_count)
        got_out = received[:, :sub_width, :]
        got_max = received[:, sub_width, :]
        got_sum = received[:, sub_width + 1, :]

        q_h = lax.dynamic_index_in_dim(queries, my_head, 1, keepdims=False)
        q_h = q_h.reshape(requests, new_tokens, HEAD_DIM)
        k_h = k_h.reshape(requests, new_tokens, HEAD_DIM)
        v_h = v_h.reshape(requests, new_tokens, sub_width)
        fresh_scores = (
            jnp.einsum("rtd,rud->rtu", q_h, k_h, preferred_element_type=jnp.float32) * score_scale
        )
        fresh_scores = jnp.where(causal[None], fresh_scores, very_negative)
        fresh_max = jnp.max(fresh_scores, axis=2)
        fresh_weights = jnp.where(causal[None], jnp.exp(fresh_scores - fresh_max[..., None]), 0.0)
        fresh_sum = jnp.sum(fresh_weights, axis=2)
        fresh_out = jnp.einsum(
            "rtu,rud->rtd",
            fresh_weights.astype(jnp.bfloat16),
            v_h,
            preferred_element_type=jnp.float32,
        )
        fresh_max = fresh_max.reshape(rows)
        fresh_sum = fresh_sum.reshape(rows)
        fresh_out = fresh_out.reshape(rows, sub_width)

        top = jnp.maximum(jnp.max(got_max, axis=0), fresh_max)
        scale_cache = jnp.exp(got_max - top[None, :])
        scale_fresh = jnp.exp(fresh_max - top)
        denom = jnp.sum(got_sum * scale_cache, axis=0) + fresh_sum * scale_fresh
        numer = jnp.sum(got_out * scale_cache[:, None, :], axis=0).T + fresh_out * scale_fresh[:, None]
        my_cols = (numer / denom[:, None]).astype(jnp.bfloat16)

        update = jnp.dot(my_cols, w_out[layer_index], preferred_element_type=jnp.float32)
        update = update + jnp.dot(activated, w_fc2[layer_index], preferred_element_type=jnp.float32)
        update = allreduce_chip(update.reshape(2, all_count // 2, -1, 128), tp_count, jnp.bfloat16)
        hidden_state = hidden_state + update.reshape(rows, width).astype(jnp.float32)
    return hidden_state.reshape(requests, new_tokens, width)


def solution(mesh):
    in_specs = (
        P(),
        P(("seq", "tp"), None),
        P(),
        P(),
        P(),
        P("seq", None),
        P(None, "seq", "tp"),
        P(None, "seq", "tp"),
        P(),
        P(),
        P(None, "seq", None, "tp"),
        P(None, "seq", "tp"),
        P(None, "tp"),
        P(None, ("tp", "seq"), None),
        P(None, ("tp", "seq"), None),
    )
    out_specs = P()
    return jax.shard_map(
        per_device, mesh=mesh, in_specs=in_specs, out_specs=out_specs, check_vma=False
    )
```

```python
import functools
import math

import jax
import numpy as np
import jax.numpy as jnp
from jax import lax
from jax.experimental import pallas as pl
from jax.experimental.pallas import tpu as pltpu
from jax.sharding import PartitionSpec as P

HEADS = 32
HEAD_DIM = 64
ROT = 32
LAYERS = 2
BLOCK = 128
SPAN = 512
MESH_IDS = pl.DeviceIdType.MESH

very_negative = -1e30


def layer_norm(values, gain_row, bias_row):
    average = jnp.mean(values, axis=-1, keepdims=True)
    centred = values - average
    variance = jnp.mean(centred * centred, axis=-1, keepdims=True)
    return centred * lax.rsqrt(variance + 1e-05) * gain_row + bias_row


def rotary(values, positions):
    half_width = ROT // 2
    frequency = jnp.exp(
        jnp.arange(half_width, dtype=jnp.float32) * (-2.0 * math.log(10000.0) / ROT)
    )
    angles = positions.astype(jnp.float32)[:, None] * frequency[None, :]
    cosine = jnp.cos(angles)[:, None, :]
    sine_part = jnp.sin(angles)[:, None, :]
    low_half = values[..., :half_width]
    high_half = values[..., half_width:ROT]
    return jnp.concatenate(
        [
            low_half * cosine - high_half * sine_part,
            high_half * cosine + low_half * sine_part,
            values[..., ROT:],
        ],
        axis=-1,
    )


def _group_ids(whole, tp_count):
    seq_index = lax.axis_index("seq")
    tp_index = lax.axis_index("tp")
    if whole:
        me = seq_index * tp_count + tp_index

        def peer(j):
            return (j // tp_count, j % tp_count)

    else:
        me = seq_index

        def peer(j):
            return (j, tp_index)

    return me, peer


_KERNEL_IDS = {}


def _kernel_id(key):
    if key not in _KERNEL_IDS:
        _KERNEL_IDS[key] = len(_KERNEL_IDS)
    return _KERNEL_IDS[key]


def _enter(n, me, peer):
    barrier = pltpu.get_barrier_semaphore()

    def greet(i, carry):
        j = lax.rem(me + i, n)
        pl.semaphore_signal(barrier, 1, device_id=peer(j), device_id_type=MESH_IDS)
        return carry

    lax.fori_loop(1, n, greet, 0)
    pl.semaphore_wait(barrier, n - 1)


def _rcopy(src, dst, send_sem, recv_sem, device):
    return pltpu.make_async_remote_copy(
        src_ref=src,
        dst_ref=dst,
        send_sem=send_sem,
        recv_sem=recv_sem,
        device_id=device,
        device_id_type=MESH_IDS,
    )


def _allreduce_kernel(n, whole, tp_count, x_ref, o_ref, rs_buf, ag_buf, s1, r1, s2, r2):
    me, peer = _group_ids(whole, tp_count)
    _enter(n, me, peer)

    def start_scatter(i, carry):
        j = lax.rem(me + i, n)
        _rcopy(x_ref.at[j], rs_buf.at[me], s1.at[j], r1.at[me], peer(j)).start()
        return carry

    lax.fori_loop(1, n, start_scatter, 0)

    def gather_sum(i, acc):
        j = lax.rem(me + i, n)
        _rcopy(x_ref.at[j], rs_buf.at[j], s1.at[j], r1.at[j], peer(j)).wait_recv()
        return acc + rs_buf[j].astype(jnp.float32)

    total = lax.fori_loop(1, n, gather_sum, x_ref[me].astype(jnp.float32))
    ag_buf[me] = total.astype(ag_buf.dtype)

    def start_gather(i, carry):
        j = lax.rem(me + i, n)
        _rcopy(ag_buf.at[me], ag_buf.at[me], s2.at[j], r2.at[me], peer(j)).start()
        return carry

    lax.fori_loop(1, n, start_gather, 0)

    def finish(i, carry):
        j = lax.rem(me + i, n)
        _rcopy(ag_buf.at[j], ag_buf.at[j], s2.at[j], r2.at[j], peer(j)).wait_recv()
        _rcopy(x_ref.at[j], rs_buf.at[me], s1.at[j], r1.at[me], peer(j)).wait_send()
        _rcopy(ag_buf.at[me], ag_buf.at[me], s2.at[j], r2.at[me], peer(j)).wait_send()
        return carry

    lax.fori_loop(1, n, finish, 0)
    o_ref[...] = ag_buf[...]


def allreduce(x, whole, tp_count):
    n = x.shape[0]
    return pl.pallas_call(
        functools.partial(_allreduce_kernel, n, whole, tp_count),
        out_shape=jax.ShapeDtypeStruct(x.shape, x.dtype),
        in_specs=[pl.BlockSpec(memory_space=pltpu.VMEM)],
        out_specs=pl.BlockSpec(memory_space=pltpu.VMEM),
        scratch_shapes=[
            pltpu.VMEM(x.shape, x.dtype),
            pltpu.VMEM(x.shape, x.dtype),
            pltpu.SemaphoreType.DMA((n,)),
            pltpu.SemaphoreType.DMA((n,)),
            pltpu.SemaphoreType.DMA((n,)),
            pltpu.SemaphoreType.DMA((n,)),
        ],
        compiler_params=pltpu.CompilerParams(
            has_side_effects=True,
            collective_id=_kernel_id(("allreduce", whole, x.shape, str(x.dtype))),
        ),
    )(x)


def _allreduce_chip_kernel(tp_count, x_ref, o_ref, pbuf, sbuf, rs_buf, ag_buf, sa, ra, s1, r1, s2, r2, sd, rd):
    seq_index = lax.axis_index("seq")
    tp_index = lax.axis_index("tp")
    n = x_ref.shape[1]
    core = seq_index % 2
    other = 1 - core
    me = (seq_index // 2) * tp_count + tp_index
    partner = (seq_index + 1 - 2 * core, tp_index)

    def peer(j):
        return ((j // tp_count) * 2 + core, j % tp_count)

    barrier = pltpu.get_barrier_semaphore()

    def greet(i, carry):
        j = lax.rem(me + i, n)
        pl.semaphore_signal(barrier, 1, device_id=peer(j), device_id_type=MESH_IDS)
        return carry

    lax.fori_loop(1, n, greet, 0)
    pl.semaphore_signal(barrier, 1, device_id=partner, device_id_type=MESH_IDS)
    pl.semaphore_wait(barrier, n)
    _allreduce_chip_body(tp_count, x_ref, o_ref, pbuf, sbuf, rs_buf, ag_buf, sa, ra, s1, r1, s2, r2, sd, rd)


def _allreduce_chip_body(tp_count, x_ref, o_ref, pbuf, sbuf, rs_buf, ag_buf, sa, ra, s1, r1, s2, r2, sd, rd):
    seq_index = lax.axis_index("seq")
    tp_index = lax.axis_index("tp")
    n = x_ref.shape[1]
    core = seq_index % 2
    other = 1 - core
    me = (seq_index // 2) * tp_count + tp_index
    partner = (seq_index + 1 - 2 * core, tp_index)

    def peer(j):
        return ((j // tp_count) * 2 + core, j % tp_count)

    swap = _rcopy(x_ref.at[other], pbuf, sa, ra, partner)
    swap.start()
    swap.wait_recv()
    sbuf[...] = (x_ref[core].astype(jnp.float32) + pbuf[...].astype(jnp.float32)).astype(sbuf.dtype)

    def start_scatter(i, carry):
        j = lax.rem(me + i, n)
        _rcopy(sbuf.at[j], rs_buf.at[me], s1.at[j], r1.at[me], peer(j)).start()
        return carry

    lax.fori_loop(1, n, start_scatter, 0)

    def gather_sum(i, acc):
        j = lax.rem(me + i, n)
        _rcopy(sbuf.at[j], rs_buf.at[j], s1.at[j], r1.at[j], peer(j)).wait_recv()
        return acc + rs_buf[j].astype(jnp.float32)

    total = lax.fori_loop(1, n, gather_sum, sbuf[me].astype(jnp.float32))
    ag_buf[core, me] = total.astype(ag_buf.dtype)

    def start_gather(i, carry):
        j = lax.rem(me + i, n)
        _rcopy(ag_buf.at[core, me], ag_buf.at[core, me], s2.at[j], r2.at[me], peer(j)).start()
        return carry

    lax.fori_loop(1, n, start_gather, 0)

    def finish(i, carry):
        j = lax.rem(me + i, n)
        _rcopy(ag_buf.at[core, j], ag_buf.at[core, j], s2.at[j], r2.at[j], peer(j)).wait_recv()
        _rcopy(sbuf.at[j], rs_buf.at[me], s1.at[j], r1.at[me], peer(j)).wait_send()
        _rcopy(ag_buf.at[core, me], ag_buf.at[core, me], s2.at[j], r2.at[me], peer(j)).wait_send()
        return carry

    lax.fori_loop(1, n, finish, 0)
    swap.wait_send()
    back = _rcopy(ag_buf.at[core], ag_buf.at[core], sd, rd, partner)
    back.start()
    _rcopy(ag_buf.at[other], ag_buf.at[other], sd, rd, partner).wait_recv()
    back.wait_send()
    o_ref[...] = ag_buf[...]


def allreduce_chip(x, tp_count, sum_dtype=None):
    n = x.shape[1]
    half = x.shape[1:]
    sum_dtype = x.dtype if sum_dtype is None else sum_dtype
    return pl.pallas_call(
        functools.partial(_allreduce_chip_kernel, tp_count),
        out_shape=jax.ShapeDtypeStruct(x.shape, sum_dtype),
        in_specs=[pl.BlockSpec(memory_space=pltpu.VMEM)],
        out_specs=pl.BlockSpec(memory_space=pltpu.VMEM),
        scratch_shapes=[
            pltpu.VMEM(half, x.dtype),
            pltpu.VMEM(half, sum_dtype),
            pltpu.VMEM(half, sum_dtype),
            pltpu.VMEM(x.shape, sum_dtype),
            pltpu.SemaphoreType.DMA(()),
            pltpu.SemaphoreType.DMA(()),
            pltpu.SemaphoreType.DMA((n,)),
            pltpu.SemaphoreType.DMA((n,)),
            pltpu.SemaphoreType.DMA((n,)),
            pltpu.SemaphoreType.DMA((n,)),
            pltpu.SemaphoreType.DMA(()),
            pltpu.SemaphoreType.DMA(()),
        ],
        compiler_params=pltpu.CompilerParams(
            has_side_effects=True,
            collective_id=_kernel_id(("allreduce_chip", x.shape, str(x.dtype), str(sum_dtype))),
        ),
    )(x)


def _opening_kernel(tp_count, x_ref, w_ref, o_ref, wo_ref, pbuf, sbuf, rs_buf, ag_buf, sa, ra, s1, r1, s2, r2, sd, rd, wbuf, ws, wr):
    seq_index = lax.axis_index("seq")
    tp_index = lax.axis_index("tp")
    count = 2 * x_ref.shape[1]
    me_all = seq_index * tp_count + tp_index
    _enter(count, me_all, lambda j: (j // tp_count, j % tp_count))
    n = w_ref.shape[0]

    def start(i, carry):
        j = lax.rem(seq_index + i, n)
        _rcopy(w_ref.at[j], wbuf.at[seq_index], ws.at[j], wr.at[seq_index], (j, tp_index)).start()
        return carry

    lax.fori_loop(1, n, start, 0)
    _allreduce_chip_body(tp_count, x_ref, o_ref, pbuf, sbuf, rs_buf, ag_buf, sa, ra, s1, r1, s2, r2, sd, rd)

    def finish(i, carry):
        j = lax.rem(seq_index + i, n)
        _rcopy(w_ref.at[j], wbuf.at[j], ws.at[j], wr.at[j], (j, tp_index)).wait_recv()
        _rcopy(w_ref.at[j], wbuf.at[seq_index], ws.at[j], wr.at[seq_index], (j, tp_index)).wait_send()
        return carry

    lax.fori_loop(1, n, finish, 0)
    wbuf[seq_index] = w_ref[seq_index]
    wo_ref[...] = wbuf[...]


def opening(x, w, tp_count):
    n = x.shape[1]
    half = x.shape[1:]
    m = w.shape[0]
    return pl.pallas_call(
        functools.partial(_opening_kernel, tp_count),
        out_shape=(jax.ShapeDtypeStruct(x.shape, x.dtype), jax.ShapeDtypeStruct(w.shape, w.dtype)),
        in_specs=[pl.BlockSpec(memory_space=pltpu.VMEM)] * 2,
        out_specs=(pl.BlockSpec(memory_space=pltpu.VMEM), pl.BlockSpec(memory_space=pltpu.VMEM)),
        scratch_shapes=[
            pltpu.VMEM(half, x.dtype),
            pltpu.VMEM(half, x.dtype),
            pltpu.VMEM(half, x.dtype),
            pltpu.VMEM(x.shape, x.dtype),
            pltpu.SemaphoreType.DMA(()),
            pltpu.SemaphoreType.DMA(()),
            pltpu.SemaphoreType.DMA((n,)),
            pltpu.SemaphoreType.DMA((n,)),
            pltpu.SemaphoreType.DMA((n,)),
            pltpu.SemaphoreType.DMA((n,)),
            pltpu.SemaphoreType.DMA(()),
            pltpu.SemaphoreType.DMA(()),
            pltpu.VMEM(w.shape, w.dtype),
            pltpu.SemaphoreType.DMA((m,)),
            pltpu.SemaphoreType.DMA((m,)),
        ],
        compiler_params=pltpu.CompilerParams(
            has_side_effects=True,
            collective_id=_kernel_id(("opening", x.shape, w.shape)),
        ),
    )(x, w)


def _all_to_all_kernel(n, whole, tp_count, x_ref, o_ref, buf, s1, r1):
    me, peer = _group_ids(whole, tp_count)
    _enter(n, me, peer)

    def start(i, carry):
        j = lax.rem(me + i, n)
        _rcopy(x_ref.at[j], buf.at[me], s1.at[j], r1.at[me], peer(j)).start()
        return carry

    lax.fori_loop(1, n, start, 0)

    def finish(i, carry):
        j = lax.rem(me + i, n)
        _rcopy(x_ref.at[j], buf.at[j], s1.at[j], r1.at[j], peer(j)).wait_recv()
        _rcopy(x_ref.at[j], buf.at[me], s1.at[j], r1.at[me], peer(j)).wait_send()
        return carry

    lax.fori_loop(1, n, finish, 0)
    buf[me] = x_ref[me]
    o_ref[...] = buf[...]


def all_to_all(x, whole, tp_count):
    n = x.shape[0]
    return pl.pallas_call(
        functools.partial(_all_to_all_kernel, n, whole, tp_count),
        out_shape=jax.ShapeDtypeStruct(x.shape, x.dtype),
        in_specs=[pl.BlockSpec(memory_space=pltpu.VMEM)],
        out_specs=pl.BlockSpec(memory_space=pltpu.VMEM),
        scratch_shapes=[
            pltpu.VMEM(x.shape, x.dtype),
            pltpu.SemaphoreType.DMA((n,)),
            pltpu.SemaphoreType.DMA((n,)),
        ],
        compiler_params=pltpu.CompilerParams(
            has_side_effects=True,
            collective_id=_kernel_id(("all_to_all", whole, x.shape, str(x.dtype))),
        ),
    )(x)


def _attention_kernel(scale, q_ref, k_ref, v_ref, mask_ref, o_ref, m_ref, l_ref):
    valid = mask_ref[...] > 0.5
    scores = lax.dot_general(
        q_ref[0], k_ref[...], (((1,), (1,)), ((), ())), preferred_element_type=jnp.float32
    )
    scores = jnp.where(valid, scores * scale, very_negative)
    top = jnp.max(scores, axis=1, keepdims=True)
    weights = jnp.where(valid, jnp.exp(scores - top), 0.0)
    total = jnp.sum(weights, axis=1, keepdims=True)
    o_ref[0] = jnp.dot(weights.astype(jnp.bfloat16), v_ref[...], preferred_element_type=jnp.float32)
    m_ref[0] = jnp.broadcast_to(top, m_ref.shape[1:])
    l_ref[0] = jnp.broadcast_to(total, l_ref.shape[1:])


def cache_attention(q_pad, k_cache, v_cache, mask, layer_index, scale):
    heads, rows, lanes = q_pad.shape
    slots = k_cache.shape[1]
    per_block = lanes // HEAD_DIM
    out_spec = pl.BlockSpec((1, rows, lanes), lambda h: (h, 0, 0))
    return pl.pallas_call(
        functools.partial(_attention_kernel, scale),
        grid=(heads,),
        out_shape=[jax.ShapeDtypeStruct((heads, rows, lanes), jnp.float32)] * 3,
        in_specs=[
            pl.BlockSpec((1, rows, lanes), lambda h: (h, 0, 0)),
            pl.BlockSpec((None, slots, lanes), lambda h: (layer_index, 0, h // per_block)),
            pl.BlockSpec((None, slots, lanes), lambda h: (layer_index, 0, h // per_block)),
            pl.BlockSpec((rows, slots), lambda h: (0, 0)),
        ],
        out_specs=[out_spec] * 3,
    )(q_pad, k_cache, v_cache, mask)


def per_device(
    token_ids,
    embedding,
    group_of,
    prefix_len,
    tail_len,
    block_map,
    k_cache,
    v_cache,
    ln_gain,
    ln_bias,
    w_qkv,
    w_fc1,
    b_fc1,
    w_out,
    w_fc2,
):
    tp_count = lax.axis_size("tp")
    seq_count = lax.axis_size("seq")
    all_count = tp_count * seq_count
    seq_index = lax.axis_index("seq")
    tp_index = lax.axis_index("tp")
    requests = token_ids.shape[0]
    new_tokens = token_ids.shape[1]
    rows = requests * new_tokens
    groups = prefix_len.shape[0]
    heads_local = HEADS // tp_count
    width = embedding.shape[1]
    score_scale = 1.0 / math.sqrt(HEAD_DIM)

    vocab_rows = embedding.shape[0]
    first_row = (seq_index * tp_count + tp_index) * vocab_rows
    local_ids = token_ids.reshape(-1) - first_row
    inside = (local_ids >= 0) & (local_ids < vocab_rows)
    picked = jnp.take(embedding, jnp.clip(local_ids, 0, vocab_rows - 1), axis=0)
    picked = jnp.where(inside[:, None], picked, jnp.zeros_like(picked))

    group_hit = group_of[:, None] == jnp.arange(groups, dtype=jnp.int32)[None, :]
    shared_len = jnp.sum(jnp.where(group_hit, prefix_len[None, :], 0), axis=1)
    base_positions = shared_len + tail_len
    positions = (base_positions[:, None] + jnp.arange(new_tokens, dtype=jnp.int32)[None, :]).reshape(-1)
    seg_len = jnp.concatenate([prefix_len, tail_len])
    seg_count = seg_len.shape[0]
    blocks_local = block_map.shape[0]
    seg_blk = block_map[:, 0]
    rank_blk = block_map[:, 1]
    seg_hit = seg_blk[:, None] == jnp.arange(seg_count, dtype=jnp.int32)[None, :]
    len_blk = jnp.sum(jnp.where(seg_hit, seg_len[None, :], 0), axis=1)
    slot_positions = rank_blk[:, None] * BLOCK + jnp.arange(BLOCK, dtype=jnp.int32)[None, :]
    live_slot = ((seg_blk[:, None] >= 0) & (slot_positions < len_blk[:, None])).reshape(-1)
    seg_slot = jnp.broadcast_to(seg_blk[:, None], (blocks_local, BLOCK)).reshape(-1)
    own_tail = seg_slot[None, :] == (groups + jnp.arange(requests, dtype=jnp.int32))[:, None]
    own_prompt = seg_slot[None, :] == group_of[:, None]
    allowed = (own_tail | own_prompt) & live_slot[None, :]
    allowed = jnp.repeat(allowed, new_tokens, axis=0)
    mask_f = allowed.astype(jnp.float32)

    rows_local = w_qkv.shape[1]
    unit_count = w_fc2.shape[1]
    sub_width = w_out.shape[1]
    pieces = HEAD_DIM // sub_width
    my_head = seq_index // pieces
    my_piece = seq_index % pieces
    causal = (
        jnp.arange(new_tokens, dtype=jnp.int32)[None, :]
        <= jnp.arange(new_tokens, dtype=jnp.int32)[:, None]
    )

    half_rot = ROT // 2
    pair_width = 2 * sub_width
    qkv_t = w_qkv.transpose(2, 3, 0, 1).reshape(3, heads_local, HEAD_DIM, LAYERS * rows_local)
    q_t = qkv_t[0].reshape(heads_local, 1, HEAD_DIM // pair_width, 1, pair_width, LAYERS * rows_local)
    q_t = jnp.broadcast_to(
        q_t, (heads_local, 1, HEAD_DIM // pair_width, pieces // 2, pair_width, LAYERS * rows_local)
    )
    k_t = jnp.broadcast_to(
        qkv_t[1][:, None], (heads_local, pieces, HEAD_DIM, LAYERS * rows_local)
    )
    v_t = qkv_t[2].reshape(seq_count, sub_width, LAYERS * rows_local)
    f_t = w_fc1.transpose(2, 0, 1).reshape(seq_count, unit_count, LAYERS * rows_local)
    message = jnp.concatenate(
        [
            q_t.reshape(seq_count, pair_width, LAYERS * rows_local),
            k_t.reshape(seq_count, HEAD_DIM, LAYERS * rows_local),
            v_t,
            f_t,
        ],
        axis=1,
    )
    cols_mine = message.shape[1]
    start_states, got_w = opening(
        picked.reshape(2, all_count // 2, -1, 128),
        message,
        tp_count,
    )
    hidden_state = start_states.reshape(rows, width).astype(jnp.float32)
    w_mine = (
        got_w.reshape(seq_count, cols_mine, LAYERS, rows_local)
        .transpose(2, 1, 0, 3)
        .reshape(LAYERS, cols_mine, seq_count * rows_local)
    )
    q_end = pair_width
    k_end = q_end + HEAD_DIM
    v_end = k_end + sub_width
    angles = positions.astype(jnp.float32)[:, None] * jnp.exp(
        jnp.arange(half_rot, dtype=jnp.float32) * (-2.0 * math.log(10000.0) / ROT)
    )[None, :]
    cosine = jnp.cos(angles)
    sine_part = jnp.sin(angles)
    for layer_index in range(LAYERS):
        normed = layer_norm(hidden_state, ln_gain[layer_index], ln_bias[layer_index]).astype(
            jnp.bfloat16
        )
        local = jnp.einsum(
            "rc,kc->rk", normed, w_mine[layer_index], preferred_element_type=jnp.float32
        )
        q_pair = local[:, :q_end]
        low_half = q_pair[:, :half_rot]
        high_half = q_pair[:, half_rot:]
        q_rot = jnp.concatenate(
            [low_half * cosine - high_half * sine_part, high_half * cosine + low_half * sine_part],
            axis=1,
        )
        q_pair = jnp.where(my_piece < 2, q_rot, q_pair)
        q_piece = lax.dynamic_slice_in_dim(q_pair, (my_piece % 2) * sub_width, sub_width, 1)
        q_piece = q_piece.astype(jnp.bfloat16).T
        k_h = rotary(local[:, None, q_end:k_end], positions)[:, 0].astype(jnp.bfloat16)
        v_h = local[:, k_end:v_end].astype(jnp.bfloat16)
        pre_act = local[:, v_end:]
        pre_act = (
            pre_act
            + lax.dynamic_slice_in_dim(b_fc1[layer_index], seq_index * unit_count, unit_count, 0)[
                None, :
            ]
        )
        activated = jax.nn.gelu(pre_act, approximate=True).astype(jnp.bfloat16)
        q_all = all_to_all(jnp.broadcast_to(q_piece[None], (seq_count,) + q_piece.shape), False, tp_count)
        queries = (
            q_all.reshape(heads_local, pieces, sub_width, rows)
            .transpose(3, 0, 1, 2)
            .reshape(rows, heads_local, HEAD_DIM)
        )
        per_block = 128 // HEAD_DIM
        same_half = (
            jnp.arange(per_block, dtype=jnp.int32)[:, None]
            == jnp.arange(per_block, dtype=jnp.int32)[None, :]
        )
        q_pairs = queries.reshape(rows, heads_local // per_block, per_block, HEAD_DIM).transpose(1, 2, 0, 3)
        q_pad = jnp.where(
            same_half[None, :, None, :, None], q_pairs[:, :, :, None, :], jnp.zeros((), jnp.bfloat16)
        ).reshape(heads_local, rows, 128)
        out_pad, max_pad, sum_pad = cache_attention(
            q_pad, k_cache, v_cache, mask_f, layer_index, score_scale
        )
        part_out = jnp.sum(
            jnp.where(
                same_half[None, :, None, :, None],
                out_pad.reshape(heads_local // per_block, per_block, rows, per_block, HEAD_DIM),
                0.0,
            ),
            axis=3,
        ).reshape(heads_local, rows, HEAD_DIM)
        part_max = max_pad[:, :, 0]
        part_sum = sum_pad[:, :, 0]
        out_pieces = (
            part_out.reshape(heads_local, rows, pieces, sub_width)
            .transpose(0, 2, 3, 1)
            .reshape(heads_local * pieces, sub_width, rows)
        )
        max_rows = jnp.repeat(part_max, pieces, axis=0)[:, None, :]
        sum_rows = jnp.repeat(part_sum, pieces, axis=0)[:, None, :]
        pad_rows = jnp.zeros((heads_local * pieces, 6, rows), jnp.float32)
        message = jnp.concatenate([out_pieces, max_rows, sum_rows, pad_rows], axis=1)
        received = all_to_all(message, False, tp_count)
        got_out = received[:, :sub_width, :]
        got_max = received[:, sub_width, :]
        got_sum = received[:, sub_width + 1, :]

        q_h = lax.dynamic_index_in_dim(queries, my_head, 1, keepdims=False)
        q_h = q_h.reshape(requests, new_tokens, HEAD_DIM)
        k_h = k_h.reshape(requests, new_tokens, HEAD_DIM)
        v_h = v_h.reshape(requests, new_tokens, sub_width)
        fresh_scores = (
            jnp.einsum("rtd,rud->rtu", q_h, k_h, preferred_element_type=jnp.float32) * score_scale
        )
        fresh_scores = jnp.where(causal[None], fresh_scores, very_negative)
        fresh_max = jnp.max(fresh_scores, axis=2)
        fresh_weights = jnp.where(causal[None], jnp.exp(fresh_scores - fresh_max[..., None]), 0.0)
        fresh_sum = jnp.sum(fresh_weights, axis=2)
        fresh_out = jnp.einsum(
            "rtu,rud->rtd",
            fresh_weights.astype(jnp.bfloat16),
            v_h,
            preferred_element_type=jnp.float32,
        )
        fresh_max = fresh_max.reshape(rows)
        fresh_sum = fresh_sum.reshape(rows)
        fresh_out = fresh_out.reshape(rows, sub_width)

        top = jnp.maximum(jnp.max(got_max, axis=0), fresh_max)
        scale_cache = jnp.exp(got_max - top[None, :])
        scale_fresh = jnp.exp(fresh_max - top)
        denom = jnp.sum(got_sum * scale_cache, axis=0) + fresh_sum * scale_fresh
        numer = jnp.sum(got_out * scale_cache[:, None, :], axis=0).T + fresh_out * scale_fresh[:, None]
        my_cols = (numer / denom[:, None]).astype(jnp.bfloat16)

        update = jnp.dot(my_cols, w_out[layer_index], preferred_element_type=jnp.float32)
        update = update + jnp.dot(activated, w_fc2[layer_index], preferred_element_type=jnp.float32)
        update = allreduce_chip(update.reshape(2, all_count // 2, -1, 128), tp_count, jnp.bfloat16)
        hidden_state = hidden_state + update.reshape(rows, width).astype(jnp.float32)
    return hidden_state.reshape(requests, new_tokens, width)


def solution(mesh):
    in_specs = (
        P(),
        P(("seq", "tp"), None),
        P(),
        P(),
        P(),
        P("seq", None),
        P(None, "seq", "tp"),
        P(None, "seq", "tp"),
        P(),
        P(),
        P(None, "seq", None, "tp"),
        P(None, "seq", "tp"),
        P(None, "tp"),
        P(None, ("tp", "seq"), None),
        P(None, ("tp", "seq"), None),
    )
    out_specs = P()
    return jax.shard_map(
        per_device, mesh=mesh, in_specs=in_specs, out_specs=out_specs, check_vma=False
    )
```

```python
import functools
import math

import jax
import numpy as np
import jax.numpy as jnp
from jax import lax
from jax.experimental import pallas as pl
from jax.experimental.pallas import tpu as pltpu
from jax.sharding import PartitionSpec as P

HEADS = 32
HEAD_DIM = 64
ROT = 32
LAYERS = 2
BLOCK = 128
SPAN = 512
MESH_IDS = pl.DeviceIdType.MESH

very_negative = -1e30


def layer_norm(values, gain_row, bias_row):
    average = jnp.mean(values, axis=-1, keepdims=True)
    centred = values - average
    variance = jnp.mean(centred * centred, axis=-1, keepdims=True)
    return centred * lax.rsqrt(variance + 1e-05) * gain_row + bias_row


def rotary(values, positions):
    half_width = ROT // 2
    frequency = jnp.exp(
        jnp.arange(half_width, dtype=jnp.float32) * (-2.0 * math.log(10000.0) / ROT)
    )
    angles = positions.astype(jnp.float32)[:, None] * frequency[None, :]
    cosine = jnp.cos(angles)[:, None, :]
    sine_part = jnp.sin(angles)[:, None, :]
    low_half = values[..., :half_width]
    high_half = values[..., half_width:ROT]
    return jnp.concatenate(
        [
            low_half * cosine - high_half * sine_part,
            high_half * cosine + low_half * sine_part,
            values[..., ROT:],
        ],
        axis=-1,
    )


def _group_ids(whole, tp_count):
    seq_index = lax.axis_index("seq")
    tp_index = lax.axis_index("tp")
    if whole:
        me = seq_index * tp_count + tp_index

        def peer(j):
            return (j // tp_count, j % tp_count)

    else:
        me = seq_index

        def peer(j):
            return (j, tp_index)

    return me, peer


_KERNEL_IDS = {}


def _kernel_id(key):
    if key not in _KERNEL_IDS:
        _KERNEL_IDS[key] = len(_KERNEL_IDS)
    return _KERNEL_IDS[key]


def _enter(n, me, peer):
    barrier = pltpu.get_barrier_semaphore()

    def greet(i, carry):
        j = lax.rem(me + i, n)
        pl.semaphore_signal(barrier, 1, device_id=peer(j), device_id_type=MESH_IDS)
        return carry

    lax.fori_loop(1, n, greet, 0)
    pl.semaphore_wait(barrier, n - 1)


def _rcopy(src, dst, send_sem, recv_sem, device):
    return pltpu.make_async_remote_copy(
        src_ref=src,
        dst_ref=dst,
        send_sem=send_sem,
        recv_sem=recv_sem,
        device_id=device,
        device_id_type=MESH_IDS,
    )


def _allreduce_kernel(n, whole, tp_count, x_ref, o_ref, rs_buf, ag_buf, s1, r1, s2, r2):
    me, peer = _group_ids(whole, tp_count)
    _enter(n, me, peer)

    def start_scatter(i, carry):
        j = lax.rem(me + i, n)
        _rcopy(x_ref.at[j], rs_buf.at[me], s1.at[j], r1.at[me], peer(j)).start()
        return carry

    lax.fori_loop(1, n, start_scatter, 0)

    def gather_sum(i, acc):
        j = lax.rem(me + i, n)
        _rcopy(x_ref.at[j], rs_buf.at[j], s1.at[j], r1.at[j], peer(j)).wait_recv()
        return acc + rs_buf[j].astype(jnp.float32)

    total = lax.fori_loop(1, n, gather_sum, x_ref[me].astype(jnp.float32))
    ag_buf[me] = total.astype(ag_buf.dtype)

    def start_gather(i, carry):
        j = lax.rem(me + i, n)
        _rcopy(ag_buf.at[me], ag_buf.at[me], s2.at[j], r2.at[me], peer(j)).start()
        return carry

    lax.fori_loop(1, n, start_gather, 0)

    def finish(i, carry):
        j = lax.rem(me + i, n)
        _rcopy(ag_buf.at[j], ag_buf.at[j], s2.at[j], r2.at[j], peer(j)).wait_recv()
        _rcopy(x_ref.at[j], rs_buf.at[me], s1.at[j], r1.at[me], peer(j)).wait_send()
        _rcopy(ag_buf.at[me], ag_buf.at[me], s2.at[j], r2.at[me], peer(j)).wait_send()
        return carry

    lax.fori_loop(1, n, finish, 0)
    o_ref[...] = ag_buf[...]


def allreduce(x, whole, tp_count):
    n = x.shape[0]
    return pl.pallas_call(
        functools.partial(_allreduce_kernel, n, whole, tp_count),
        out_shape=jax.ShapeDtypeStruct(x.shape, x.dtype),
        in_specs=[pl.BlockSpec(memory_space=pltpu.VMEM)],
        out_specs=pl.BlockSpec(memory_space=pltpu.VMEM),
        scratch_shapes=[
            pltpu.VMEM(x.shape, x.dtype),
            pltpu.VMEM(x.shape, x.dtype),
            pltpu.SemaphoreType.DMA((n,)),
            pltpu.SemaphoreType.DMA((n,)),
            pltpu.SemaphoreType.DMA((n,)),
            pltpu.SemaphoreType.DMA((n,)),
        ],
        compiler_params=pltpu.CompilerParams(
            has_side_effects=True,
            collective_id=_kernel_id(("allreduce", whole, x.shape, str(x.dtype))),
        ),
    )(x)


def _allreduce_chip_kernel(tp_count, x_ref, o_ref, pbuf, sbuf, rs_buf, ag_buf, sa, ra, s1, r1, s2, r2, sd, rd):
    seq_index = lax.axis_index("seq")
    tp_index = lax.axis_index("tp")
    n = x_ref.shape[1]
    core = seq_index % 2
    other = 1 - core
    me = (seq_index // 2) * tp_count + tp_index
    partner = (seq_index + 1 - 2 * core, tp_index)

    def peer(j):
        return ((j // tp_count) * 2 + core, j % tp_count)

    barrier = pltpu.get_barrier_semaphore()

    def greet(i, carry):
        j = lax.rem(me + i, n)
        pl.semaphore_signal(barrier, 1, device_id=peer(j), device_id_type=MESH_IDS)
        return carry

    lax.fori_loop(1, n, greet, 0)
    pl.semaphore_signal(barrier, 1, device_id=partner, device_id_type=MESH_IDS)
    pl.semaphore_wait(barrier, n)
    _allreduce_chip_body(tp_count, x_ref, o_ref, pbuf, sbuf, rs_buf, ag_buf, sa, ra, s1, r1, s2, r2, sd, rd)


def _allreduce_chip_body(tp_count, x_ref, o_ref, pbuf, sbuf, rs_buf, ag_buf, sa, ra, s1, r1, s2, r2, sd, rd):
    seq_index = lax.axis_index("seq")
    tp_index = lax.axis_index("tp")
    n = x_ref.shape[1]
    core = seq_index % 2
    other = 1 - core
    me = (seq_index // 2) * tp_count + tp_index
    partner = (seq_index + 1 - 2 * core, tp_index)

    def peer(j):
        return ((j // tp_count) * 2 + core, j % tp_count)

    swap = _rcopy(x_ref.at[other], pbuf, sa, ra, partner)
    swap.start()
    swap.wait_recv()
    sbuf[...] = (x_ref[core].astype(jnp.float32) + pbuf[...].astype(jnp.float32)).astype(sbuf.dtype)

    def start_scatter(i, carry):
        j = lax.rem(me + i, n)
        _rcopy(sbuf.at[j], rs_buf.at[me], s1.at[j], r1.at[me], peer(j)).start()
        return carry

    lax.fori_loop(1, n, start_scatter, 0)

    def gather_sum(i, acc):
        j = lax.rem(me + i, n)
        _rcopy(sbuf.at[j], rs_buf.at[j], s1.at[j], r1.at[j], peer(j)).wait_recv()
        return acc + rs_buf[j].astype(jnp.float32)

    total = lax.fori_loop(1, n, gather_sum, sbuf[me].astype(jnp.float32))
    ag_buf[core, me] = total.astype(ag_buf.dtype)

    def start_gather(i, carry):
        j = lax.rem(me + i, n)
        _rcopy(ag_buf.at[core, me], ag_buf.at[core, me], s2.at[j], r2.at[me], peer(j)).start()
        return carry

    lax.fori_loop(1, n, start_gather, 0)

    def finish(i, carry):
        j = lax.rem(me + i, n)
        _rcopy(ag_buf.at[core, j], ag_buf.at[core, j], s2.at[j], r2.at[j], peer(j)).wait_recv()
        _rcopy(sbuf.at[j], rs_buf.at[me], s1.at[j], r1.at[me], peer(j)).wait_send()
        _rcopy(ag_buf.at[core, me], ag_buf.at[core, me], s2.at[j], r2.at[me], peer(j)).wait_send()
        return carry

    lax.fori_loop(1, n, finish, 0)
    swap.wait_send()
    back = _rcopy(ag_buf.at[core], ag_buf.at[core], sd, rd, partner)
    back.start()
    _rcopy(ag_buf.at[other], ag_buf.at[other], sd, rd, partner).wait_recv()
    back.wait_send()
    o_ref[...] = ag_buf[...]


def allreduce_chip(x, tp_count, sum_dtype=None):
    n = x.shape[1]
    half = x.shape[1:]
    sum_dtype = x.dtype if sum_dtype is None else sum_dtype
    return pl.pallas_call(
        functools.partial(_allreduce_chip_kernel, tp_count),
        out_shape=jax.ShapeDtypeStruct(x.shape, sum_dtype),
        in_specs=[pl.BlockSpec(memory_space=pltpu.VMEM)],
        out_specs=pl.BlockSpec(memory_space=pltpu.VMEM),
        scratch_shapes=[
            pltpu.VMEM(half, x.dtype),
            pltpu.VMEM(half, sum_dtype),
            pltpu.VMEM(half, sum_dtype),
            pltpu.VMEM(x.shape, sum_dtype),
            pltpu.SemaphoreType.DMA(()),
            pltpu.SemaphoreType.DMA(()),
            pltpu.SemaphoreType.DMA((n,)),
            pltpu.SemaphoreType.DMA((n,)),
            pltpu.SemaphoreType.DMA((n,)),
            pltpu.SemaphoreType.DMA((n,)),
            pltpu.SemaphoreType.DMA(()),
            pltpu.SemaphoreType.DMA(()),
        ],
        compiler_params=pltpu.CompilerParams(
            has_side_effects=True,
            collective_id=_kernel_id(("allreduce_chip", x.shape, str(x.dtype), str(sum_dtype))),
        ),
    )(x)


def _opening_kernel(tp_count, x_ref, w_ref, o_ref, wo_ref, pbuf, sbuf, rs_buf, ag_buf, sa, ra, s1, r1, s2, r2, sd, rd, wbuf, ws, wr):
    seq_index = lax.axis_index("seq")
    tp_index = lax.axis_index("tp")
    count = 2 * x_ref.shape[1]
    me_all = seq_index * tp_count + tp_index
    _enter(count, me_all, lambda j: (j // tp_count, j % tp_count))
    n = w_ref.shape[0]

    def start(i, carry):
        j = lax.rem(seq_index + i, n)
        _rcopy(w_ref.at[j], wbuf.at[seq_index], ws.at[j], wr.at[seq_index], (j, tp_index)).start()
        return carry

    lax.fori_loop(1, n, start, 0)
    _allreduce_chip_body(tp_count, x_ref, o_ref, pbuf, sbuf, rs_buf, ag_buf, sa, ra, s1, r1, s2, r2, sd, rd)

    def finish(i, carry):
        j = lax.rem(seq_index + i, n)
        _rcopy(w_ref.at[j], wbuf.at[j], ws.at[j], wr.at[j], (j, tp_index)).wait_recv()
        _rcopy(w_ref.at[j], wbuf.at[seq_index], ws.at[j], wr.at[seq_index], (j, tp_index)).wait_send()
        return carry

    lax.fori_loop(1, n, finish, 0)
    wbuf[seq_index] = w_ref[seq_index]
    wo_ref[...] = wbuf[...]


def opening(x, w, tp_count):
    n = x.shape[1]
    half = x.shape[1:]
    m = w.shape[0]
    return pl.pallas_call(
        functools.partial(_opening_kernel, tp_count),
        out_shape=(jax.ShapeDtypeStruct(x.shape, x.dtype), jax.ShapeDtypeStruct(w.shape, w.dtype)),
        in_specs=[pl.BlockSpec(memory_space=pltpu.VMEM)] * 2,
        out_specs=(pl.BlockSpec(memory_space=pltpu.VMEM), pl.BlockSpec(memory_space=pltpu.VMEM)),
        scratch_shapes=[
            pltpu.VMEM(half, x.dtype),
            pltpu.VMEM(half, x.dtype),
            pltpu.VMEM(half, x.dtype),
            pltpu.VMEM(x.shape, x.dtype),
            pltpu.SemaphoreType.DMA(()),
            pltpu.SemaphoreType.DMA(()),
            pltpu.SemaphoreType.DMA((n,)),
            pltpu.SemaphoreType.DMA((n,)),
            pltpu.SemaphoreType.DMA((n,)),
            pltpu.SemaphoreType.DMA((n,)),
            pltpu.SemaphoreType.DMA(()),
            pltpu.SemaphoreType.DMA(()),
            pltpu.VMEM(w.shape, w.dtype),
            pltpu.SemaphoreType.DMA((m,)),
            pltpu.SemaphoreType.DMA((m,)),
        ],
        compiler_params=pltpu.CompilerParams(
            has_side_effects=True,
            collective_id=_kernel_id(("opening", x.shape, w.shape)),
        ),
    )(x, w)


def _all_to_all_kernel(n, whole, tp_count, x_ref, o_ref, buf, s1, r1):
    me, peer = _group_ids(whole, tp_count)
    _enter(n, me, peer)

    def start(i, carry):
        j = lax.rem(me + i, n)
        _rcopy(x_ref.at[j], buf.at[me], s1.at[j], r1.at[me], peer(j)).start()
        return carry

    lax.fori_loop(1, n, start, 0)

    def finish(i, carry):
        j = lax.rem(me + i, n)
        _rcopy(x_ref.at[j], buf.at[j], s1.at[j], r1.at[j], peer(j)).wait_recv()
        _rcopy(x_ref.at[j], buf.at[me], s1.at[j], r1.at[me], peer(j)).wait_send()
        return carry

    lax.fori_loop(1, n, finish, 0)
    buf[me] = x_ref[me]
    o_ref[...] = buf[...]


def all_to_all(x, whole, tp_count):
    n = x.shape[0]
    return pl.pallas_call(
        functools.partial(_all_to_all_kernel, n, whole, tp_count),
        out_shape=jax.ShapeDtypeStruct(x.shape, x.dtype),
        in_specs=[pl.BlockSpec(memory_space=pltpu.VMEM)],
        out_specs=pl.BlockSpec(memory_space=pltpu.VMEM),
        scratch_shapes=[
            pltpu.VMEM(x.shape, x.dtype),
            pltpu.SemaphoreType.DMA((n,)),
            pltpu.SemaphoreType.DMA((n,)),
        ],
        compiler_params=pltpu.CompilerParams(
            has_side_effects=True,
            collective_id=_kernel_id(("all_to_all", whole, x.shape, str(x.dtype))),
        ),
    )(x)


def _all_to_all_pair_kernel(n, whole, tp_count, xa_ref, xb_ref, oa_ref, ob_ref, bufa, bufb, sa, ra, sb, rb):
    me, peer = _group_ids(whole, tp_count)
    _enter(n, me, peer)

    def start(i, carry):
        j = lax.rem(me + i, n)
        _rcopy(xa_ref.at[j], bufa.at[me], sa.at[j], ra.at[me], peer(j)).start()
        _rcopy(xb_ref.at[j], bufb.at[me], sb.at[j], rb.at[me], peer(j)).start()
        return carry

    lax.fori_loop(1, n, start, 0)

    def finish(i, carry):
        j = lax.rem(me + i, n)
        _rcopy(xa_ref.at[j], bufa.at[j], sa.at[j], ra.at[j], peer(j)).wait_recv()
        _rcopy(xb_ref.at[j], bufb.at[j], sb.at[j], rb.at[j], peer(j)).wait_recv()
        _rcopy(xa_ref.at[j], bufa.at[me], sa.at[j], ra.at[me], peer(j)).wait_send()
        _rcopy(xb_ref.at[j], bufb.at[me], sb.at[j], rb.at[me], peer(j)).wait_send()
        return carry

    lax.fori_loop(1, n, finish, 0)
    bufa[me] = xa_ref[me]
    bufb[me] = xb_ref[me]
    oa_ref[...] = bufa[...]
    ob_ref[...] = bufb[...]


def all_to_all_pair(xa, xb, whole, tp_count):
    n = xa.shape[0]
    return pl.pallas_call(
        functools.partial(_all_to_all_pair_kernel, n, whole, tp_count),
        out_shape=(jax.ShapeDtypeStruct(xa.shape, xa.dtype), jax.ShapeDtypeStruct(xb.shape, xb.dtype)),
        in_specs=[pl.BlockSpec(memory_space=pltpu.VMEM)] * 2,
        out_specs=(pl.BlockSpec(memory_space=pltpu.VMEM), pl.BlockSpec(memory_space=pltpu.VMEM)),
        scratch_shapes=[
            pltpu.VMEM(xa.shape, xa.dtype),
            pltpu.VMEM(xb.shape, xb.dtype),
            pltpu.SemaphoreType.DMA((n,)),
            pltpu.SemaphoreType.DMA((n,)),
            pltpu.SemaphoreType.DMA((n,)),
            pltpu.SemaphoreType.DMA((n,)),
        ],
        compiler_params=pltpu.CompilerParams(
            has_side_effects=True,
            collective_id=_kernel_id(("all_to_all_pair", whole, xa.shape, xb.shape)),
        ),
    )(xa, xb)


def _attention_kernel(scale, q_ref, k_ref, v_ref, mask_ref, o_ref, m_ref, l_ref):
    valid = mask_ref[...] > 0.5
    scores = lax.dot_general(
        q_ref[0], k_ref[...], (((1,), (1,)), ((), ())), preferred_element_type=jnp.float32
    )
    scores = jnp.where(valid, scores * scale, very_negative)
    top = jnp.max(scores, axis=1, keepdims=True)
    weights = jnp.where(valid, jnp.exp(scores - top), 0.0)
    total = jnp.sum(weights, axis=1, keepdims=True)
    o_ref[0] = jnp.dot(weights.astype(jnp.bfloat16), v_ref[...], preferred_element_type=jnp.float32)
    m_ref[0] = jnp.broadcast_to(top, m_ref.shape[1:])
    l_ref[0] = jnp.broadcast_to(total, l_ref.shape[1:])


def cache_attention(q_pad, k_cache, v_cache, mask, layer_index, scale):
    heads, rows, lanes = q_pad.shape
    slots = k_cache.shape[1]
    per_block = lanes // HEAD_DIM
    out_spec = pl.BlockSpec((1, rows, lanes), lambda h: (h, 0, 0))
    return pl.pallas_call(
        functools.partial(_attention_kernel, scale),
        grid=(heads,),
        out_shape=[jax.ShapeDtypeStruct((heads, rows, lanes), jnp.float32)] * 3,
        in_specs=[
            pl.BlockSpec((1, rows, lanes), lambda h: (h, 0, 0)),
            pl.BlockSpec((None, slots, lanes), lambda h: (layer_index, 0, h // per_block)),
            pl.BlockSpec((None, slots, lanes), lambda h: (layer_index, 0, h // per_block)),
            pl.BlockSpec((rows, slots), lambda h: (0, 0)),
        ],
        out_specs=[out_spec] * 3,
    )(q_pad, k_cache, v_cache, mask)


def per_device(
    token_ids,
    embedding,
    group_of,
    prefix_len,
    tail_len,
    block_map,
    k_cache,
    v_cache,
    ln_gain,
    ln_bias,
    w_qkv,
    w_fc1,
    b_fc1,
    w_out,
    w_fc2,
):
    tp_count = lax.axis_size("tp")
    seq_count = lax.axis_size("seq")
    all_count = tp_count * seq_count
    seq_index = lax.axis_index("seq")
    tp_index = lax.axis_index("tp")
    requests = token_ids.shape[0]
    new_tokens = token_ids.shape[1]
    rows = requests * new_tokens
    groups = prefix_len.shape[0]
    heads_local = HEADS // tp_count
    width = embedding.shape[1]
    score_scale = 1.0 / math.sqrt(HEAD_DIM)

    vocab_rows = embedding.shape[0]
    first_row = (seq_index * tp_count + tp_index) * vocab_rows
    local_ids = token_ids.reshape(-1) - first_row
    inside = (local_ids >= 0) & (local_ids < vocab_rows)
    picked = jnp.take(embedding, jnp.clip(local_ids, 0, vocab_rows - 1), axis=0)
    picked = jnp.where(inside[:, None], picked, jnp.zeros_like(picked))

    group_hit = group_of[:, None] == jnp.arange(groups, dtype=jnp.int32)[None, :]
    shared_len = jnp.sum(jnp.where(group_hit, prefix_len[None, :], 0), axis=1)
    base_positions = shared_len + tail_len
    positions = (base_positions[:, None] + jnp.arange(new_tokens, dtype=jnp.int32)[None, :]).reshape(-1)
    seg_len = jnp.concatenate([prefix_len, tail_len])
    seg_count = seg_len.shape[0]
    blocks_local = block_map.shape[0]
    seg_blk = block_map[:, 0]
    rank_blk = block_map[:, 1]
    seg_hit = seg_blk[:, None] == jnp.arange(seg_count, dtype=jnp.int32)[None, :]
    len_blk = jnp.sum(jnp.where(seg_hit, seg_len[None, :], 0), axis=1)
    slot_positions = rank_blk[:, None] * BLOCK + jnp.arange(BLOCK, dtype=jnp.int32)[None, :]
    live_slot = ((seg_blk[:, None] >= 0) & (slot_positions < len_blk[:, None])).reshape(-1)
    seg_slot = jnp.broadcast_to(seg_blk[:, None], (blocks_local, BLOCK)).reshape(-1)
    own_tail = seg_slot[None, :] == (groups + jnp.arange(requests, dtype=jnp.int32))[:, None]
    own_prompt = seg_slot[None, :] == group_of[:, None]
    allowed = (own_tail | own_prompt) & live_slot[None, :]
    allowed = jnp.repeat(allowed, new_tokens, axis=0)
    mask_f = allowed.astype(jnp.float32)

    rows_local = w_qkv.shape[1]
    unit_count = w_fc2.shape[1]
    sub_width = w_out.shape[1]
    pieces = HEAD_DIM // sub_width
    my_head = seq_index // pieces
    my_piece = seq_index % pieces
    causal = (
        jnp.arange(new_tokens, dtype=jnp.int32)[None, :]
        <= jnp.arange(new_tokens, dtype=jnp.int32)[:, None]
    )

    half_rot = ROT // 2
    pair_width = 2 * sub_width
    qkv_t = w_qkv.transpose(2, 3, 0, 1).reshape(3, heads_local, HEAD_DIM, LAYERS * rows_local)
    q_t = qkv_t[0].reshape(heads_local, 1, HEAD_DIM // pair_width, 1, pair_width, LAYERS * rows_local)
    q_t = jnp.broadcast_to(
        q_t, (heads_local, 1, HEAD_DIM // pair_width, pieces // 2, pair_width, LAYERS * rows_local)
    )
    k_t = jnp.broadcast_to(
        qkv_t[1][:, None], (heads_local, pieces, HEAD_DIM, LAYERS * rows_local)
    )
    v_t = qkv_t[2].reshape(seq_count, sub_width, LAYERS * rows_local)
    f_t = w_fc1.transpose(2, 0, 1).reshape(seq_count, unit_count, LAYERS * rows_local)
    message = jnp.concatenate(
        [
            q_t.reshape(seq_count, pair_width, LAYERS * rows_local),
            k_t.reshape(seq_count, HEAD_DIM, LAYERS * rows_local),
            v_t,
            f_t,
        ],
        axis=1,
    )
    cols_mine = message.shape[1]
    start_states, got_w = opening(
        picked.reshape(2, all_count // 2, -1, 128),
        message,
        tp_count,
    )
    hidden_state = start_states.reshape(rows, width).astype(jnp.float32)
    w_mine = (
        got_w.reshape(seq_count, cols_mine, LAYERS, rows_local)
        .transpose(2, 1, 0, 3)
        .reshape(LAYERS, cols_mine, seq_count * rows_local)
    )
    q_end = pair_width
    k_end = q_end + HEAD_DIM
    v_end = k_end + sub_width
    angles = positions.astype(jnp.float32)[:, None] * jnp.exp(
        jnp.arange(half_rot, dtype=jnp.float32) * (-2.0 * math.log(10000.0) / ROT)
    )[None, :]
    cosine = jnp.cos(angles)
    sine_part = jnp.sin(angles)
    for layer_index in range(LAYERS):
        normed = layer_norm(hidden_state, ln_gain[layer_index], ln_bias[layer_index]).astype(
            jnp.bfloat16
        )
        local = jnp.einsum(
            "rc,kc->rk", normed, w_mine[layer_index], preferred_element_type=jnp.float32
        )
        q_pair = local[:, :q_end]
        low_half = q_pair[:, :half_rot]
        high_half = q_pair[:, half_rot:]
        q_rot = jnp.concatenate(
            [low_half * cosine - high_half * sine_part, high_half * cosine + low_half * sine_part],
            axis=1,
        )
        q_pair = jnp.where(my_piece < 2, q_rot, q_pair)
        q_piece = lax.dynamic_slice_in_dim(q_pair, (my_piece % 2) * sub_width, sub_width, 1)
        q_piece = q_piece.astype(jnp.bfloat16).T
        k_h = rotary(local[:, None, q_end:k_end], positions)[:, 0].astype(jnp.bfloat16)
        v_h = local[:, k_end:v_end].astype(jnp.bfloat16)
        pre_act = local[:, v_end:]
        pre_act = (
            pre_act
            + lax.dynamic_slice_in_dim(b_fc1[layer_index], seq_index * unit_count, unit_count, 0)[
                None, :
            ]
        )
        activated = jax.nn.gelu(pre_act, approximate=True).astype(jnp.bfloat16)
        q_all = all_to_all(jnp.broadcast_to(q_piece[None], (seq_count,) + q_piece.shape), False, tp_count)
        queries = (
            q_all.reshape(heads_local, pieces, sub_width, rows)
            .transpose(3, 0, 1, 2)
            .reshape(rows, heads_local, HEAD_DIM)
        )
        per_block = 128 // HEAD_DIM
        same_half = (
            jnp.arange(per_block, dtype=jnp.int32)[:, None]
            == jnp.arange(per_block, dtype=jnp.int32)[None, :]
        )
        q_pairs = queries.reshape(rows, heads_local // per_block, per_block, HEAD_DIM).transpose(1, 2, 0, 3)
        q_pad = jnp.where(
            same_half[None, :, None, :, None], q_pairs[:, :, :, None, :], jnp.zeros((), jnp.bfloat16)
        ).reshape(heads_local, rows, 128)
        out_pad, max_pad, sum_pad = cache_attention(
            q_pad, k_cache, v_cache, mask_f, layer_index, score_scale
        )
        part_out = jnp.sum(
            jnp.where(
                same_half[None, :, None, :, None],
                out_pad.reshape(heads_local // per_block, per_block, rows, per_block, HEAD_DIM),
                0.0,
            ),
            axis=3,
        ).reshape(heads_local, rows, HEAD_DIM)
        part_max = max_pad[:, :, 0]
        part_sum = sum_pad[:, :, 0]
        out_pieces = (
            part_out.reshape(heads_local, rows, pieces, sub_width)
            .transpose(0, 2, 3, 1)
            .reshape(heads_local * pieces, sub_width, rows)
        )
        max_rows = jnp.repeat(part_max, pieces, axis=0)[:, None, :]
        sum_rows = jnp.repeat(part_sum, pieces, axis=0)[:, None, :]
        pad_rows = jnp.zeros((heads_local * pieces, 6, rows), jnp.float32)
        stats = jnp.concatenate([max_rows, sum_rows, pad_rows], axis=1)
        got_out, got_stats = all_to_all_pair(out_pieces.astype(jnp.bfloat16), stats, False, tp_count)
        got_out = got_out.astype(jnp.float32)
        got_max = got_stats[:, 0, :]
        got_sum = got_stats[:, 1, :]

        q_h = lax.dynamic_index_in_dim(queries, my_head, 1, keepdims=False)
        q_h = q_h.reshape(requests, new_tokens, HEAD_DIM)
        k_h = k_h.reshape(requests, new_tokens, HEAD_DIM)
        v_h = v_h.reshape(requests, new_tokens, sub_width)
        fresh_scores = (
            jnp.einsum("rtd,rud->rtu", q_h, k_h, preferred_element_type=jnp.float32) * score_scale
        )
        fresh_scores = jnp.where(causal[None], fresh_scores, very_negative)
        fresh_max = jnp.max(fresh_scores, axis=2)
        fresh_weights = jnp.where(causal[None], jnp.exp(fresh_scores - fresh_max[..., None]), 0.0)
        fresh_sum = jnp.sum(fresh_weights, axis=2)
        fresh_out = jnp.einsum(
            "rtu,rud->rtd",
            fresh_weights.astype(jnp.bfloat16),
            v_h,
            preferred_element_type=jnp.float32,
        )
        fresh_max = fresh_max.reshape(rows)
        fresh_sum = fresh_sum.reshape(rows)
        fresh_out = fresh_out.reshape(rows, sub_width)

        top = jnp.maximum(jnp.max(got_max, axis=0), fresh_max)
        scale_cache = jnp.exp(got_max - top[None, :])
        scale_fresh = jnp.exp(fresh_max - top)
        denom = jnp.sum(got_sum * scale_cache, axis=0) + fresh_sum * scale_fresh
        numer = jnp.sum(got_out * scale_cache[:, None, :], axis=0).T + fresh_out * scale_fresh[:, None]
        my_cols = (numer / denom[:, None]).astype(jnp.bfloat16)

        update = jnp.dot(my_cols, w_out[layer_index], preferred_element_type=jnp.float32)
        update = update + jnp.dot(activated, w_fc2[layer_index], preferred_element_type=jnp.float32)
        update = allreduce_chip(update.reshape(2, all_count // 2, -1, 128), tp_count, jnp.bfloat16)
        hidden_state = hidden_state + update.reshape(rows, width).astype(jnp.float32)
    return hidden_state.reshape(requests, new_tokens, width)


def solution(mesh):
    in_specs = (
        P(),
        P(("seq", "tp"), None),
        P(),
        P(),
        P(),
        P("seq", None),
        P(None, "seq", "tp"),
        P(None, "seq", "tp"),
        P(),
        P(),
        P(None, "seq", None, "tp"),
        P(None, "seq", "tp"),
        P(None, "tp"),
        P(None, ("tp", "seq"), None),
        P(None, ("tp", "seq"), None),
    )
    out_specs = P()
    return jax.shard_map(
        per_device, mesh=mesh, in_specs=in_specs, out_specs=out_specs, check_vma=False
    )
```

```python
import functools
import math

import jax
import numpy as np
import jax.numpy as jnp
from jax import lax
from jax.experimental import pallas as pl
from jax.experimental.pallas import tpu as pltpu
from jax.sharding import PartitionSpec as P

HEADS = 32
HEAD_DIM = 64
ROT = 32
LAYERS = 2
BLOCK = 128
SPAN = 512
MESH_IDS = pl.DeviceIdType.MESH

very_negative = -1e30


def layer_norm(values, gain_row, bias_row):
    average = jnp.mean(values, axis=-1, keepdims=True)
    centred = values - average
    variance = jnp.mean(centred * centred, axis=-1, keepdims=True)
    return centred * lax.rsqrt(variance + 1e-05) * gain_row + bias_row


def rotary(values, positions):
    half_width = ROT // 2
    frequency = jnp.exp(
        jnp.arange(half_width, dtype=jnp.float32) * (-2.0 * math.log(10000.0) / ROT)
    )
    angles = positions.astype(jnp.float32)[:, None] * frequency[None, :]
    cosine = jnp.cos(angles)[:, None, :]
    sine_part = jnp.sin(angles)[:, None, :]
    low_half = values[..., :half_width]
    high_half = values[..., half_width:ROT]
    return jnp.concatenate(
        [
            low_half * cosine - high_half * sine_part,
            high_half * cosine + low_half * sine_part,
            values[..., ROT:],
        ],
        axis=-1,
    )


def _group_ids(whole, tp_count):
    seq_index = lax.axis_index("seq")
    tp_index = lax.axis_index("tp")
    if whole:
        me = seq_index * tp_count + tp_index

        def peer(j):
            return (j // tp_count, j % tp_count)

    else:
        me = seq_index

        def peer(j):
            return (j, tp_index)

    return me, peer


_KERNEL_IDS = {}


def _kernel_id(key):
    if key not in _KERNEL_IDS:
        _KERNEL_IDS[key] = len(_KERNEL_IDS)
    return _KERNEL_IDS[key]


def _enter(n, me, peer):
    barrier = pltpu.get_barrier_semaphore()

    def greet(i, carry):
        j = lax.rem(me + i, n)
        pl.semaphore_signal(barrier, 1, device_id=peer(j), device_id_type=MESH_IDS)
        return carry

    lax.fori_loop(1, n, greet, 0)
    pl.semaphore_wait(barrier, n - 1)


def _rcopy(src, dst, send_sem, recv_sem, device):
    return pltpu.make_async_remote_copy(
        src_ref=src,
        dst_ref=dst,
        send_sem=send_sem,
        recv_sem=recv_sem,
        device_id=device,
        device_id_type=MESH_IDS,
    )


def _allreduce_kernel(n, whole, tp_count, x_ref, o_ref, rs_buf, ag_buf, s1, r1, s2, r2):
    me, peer = _group_ids(whole, tp_count)
    _enter(n, me, peer)

    def start_scatter(i, carry):
        j = lax.rem(me + i, n)
        _rcopy(x_ref.at[j], rs_buf.at[me], s1.at[j], r1.at[me], peer(j)).start()
        return carry

    lax.fori_loop(1, n, start_scatter, 0)

    def gather_sum(i, acc):
        j = lax.rem(me + i, n)
        _rcopy(x_ref.at[j], rs_buf.at[j], s1.at[j], r1.at[j], peer(j)).wait_recv()
        return acc + rs_buf[j].astype(jnp.float32)

    total = lax.fori_loop(1, n, gather_sum, x_ref[me].astype(jnp.float32))
    ag_buf[me] = total.astype(ag_buf.dtype)

    def start_gather(i, carry):
        j = lax.rem(me + i, n)
        _rcopy(ag_buf.at[me], ag_buf.at[me], s2.at[j], r2.at[me], peer(j)).start()
        return carry

    lax.fori_loop(1, n, start_gather, 0)

    def finish(i, carry):
        j = lax.rem(me + i, n)
        _rcopy(ag_buf.at[j], ag_buf.at[j], s2.at[j], r2.at[j], peer(j)).wait_recv()
        _rcopy(x_ref.at[j], rs_buf.at[me], s1.at[j], r1.at[me], peer(j)).wait_send()
        _rcopy(ag_buf.at[me], ag_buf.at[me], s2.at[j], r2.at[me], peer(j)).wait_send()
        return carry

    lax.fori_loop(1, n, finish, 0)
    o_ref[...] = ag_buf[...]


def allreduce(x, whole, tp_count):
    n = x.shape[0]
    return pl.pallas_call(
        functools.partial(_allreduce_kernel, n, whole, tp_count),
        out_shape=jax.ShapeDtypeStruct(x.shape, x.dtype),
        in_specs=[pl.BlockSpec(memory_space=pltpu.VMEM)],
        out_specs=pl.BlockSpec(memory_space=pltpu.VMEM),
        scratch_shapes=[
            pltpu.VMEM(x.shape, x.dtype),
            pltpu.VMEM(x.shape, x.dtype),
            pltpu.SemaphoreType.DMA((n,)),
            pltpu.SemaphoreType.DMA((n,)),
            pltpu.SemaphoreType.DMA((n,)),
            pltpu.SemaphoreType.DMA((n,)),
        ],
        compiler_params=pltpu.CompilerParams(
            has_side_effects=True,
            collective_id=_kernel_id(("allreduce", whole, x.shape, str(x.dtype))),
        ),
    )(x)


def _allreduce_chip_kernel(tp_count, x_ref, o_ref, pbuf, sbuf, rs_buf, ag_buf, sa, ra, s1, r1, s2, r2, sd, rd):
    seq_index = lax.axis_index("seq")
    tp_index = lax.axis_index("tp")
    n = x_ref.shape[1]
    core = seq_index % 2
    other = 1 - core
    me = (seq_index // 2) * tp_count + tp_index
    partner = (seq_index + 1 - 2 * core, tp_index)

    def peer(j):
        return ((j // tp_count) * 2 + core, j % tp_count)

    barrier = pltpu.get_barrier_semaphore()

    def greet(i, carry):
        j = lax.rem(me + i, n)
        pl.semaphore_signal(barrier, 1, device_id=peer(j), device_id_type=MESH_IDS)
        return carry

    lax.fori_loop(1, n, greet, 0)
    pl.semaphore_signal(barrier, 1, device_id=partner, device_id_type=MESH_IDS)
    pl.semaphore_wait(barrier, n)
    _allreduce_chip_body(tp_count, x_ref, o_ref, pbuf, sbuf, rs_buf, ag_buf, sa, ra, s1, r1, s2, r2, sd, rd)


def _allreduce_chip_body(tp_count, x_ref, o_ref, pbuf, sbuf, rs_buf, ag_buf, sa, ra, s1, r1, s2, r2, sd, rd):
    seq_index = lax.axis_index("seq")
    tp_index = lax.axis_index("tp")
    n = x_ref.shape[1]
    core = seq_index % 2
    other = 1 - core
    me = (seq_index // 2) * tp_count + tp_index
    partner = (seq_index + 1 - 2 * core, tp_index)

    def peer(j):
        return ((j // tp_count) * 2 + core, j % tp_count)

    swap = _rcopy(x_ref.at[other], pbuf, sa, ra, partner)
    swap.start()
    swap.wait_recv()
    sbuf[...] = (x_ref[core].astype(jnp.float32) + pbuf[...].astype(jnp.float32)).astype(sbuf.dtype)

    def start_scatter(i, carry):
        j = lax.rem(me + i, n)
        _rcopy(sbuf.at[j], rs_buf.at[me], s1.at[j], r1.at[me], peer(j)).start()
        return carry

    lax.fori_loop(1, n, start_scatter, 0)

    def gather_sum(i, acc):
        j = lax.rem(me + i, n)
        _rcopy(sbuf.at[j], rs_buf.at[j], s1.at[j], r1.at[j], peer(j)).wait_recv()
        return acc + rs_buf[j].astype(jnp.float32)

    total = lax.fori_loop(1, n, gather_sum, sbuf[me].astype(jnp.float32))
    ag_buf[core, me] = total.astype(ag_buf.dtype)

    def start_gather(i, carry):
        j = lax.rem(me + i, n)
        _rcopy(ag_buf.at[core, me], ag_buf.at[core, me], s2.at[j], r2.at[me], peer(j)).start()
        return carry

    lax.fori_loop(1, n, start_gather, 0)

    def finish(i, carry):
        j = lax.rem(me + i, n)
        _rcopy(ag_buf.at[core, j], ag_buf.at[core, j], s2.at[j], r2.at[j], peer(j)).wait_recv()
        _rcopy(sbuf.at[j], rs_buf.at[me], s1.at[j], r1.at[me], peer(j)).wait_send()
        _rcopy(ag_buf.at[core, me], ag_buf.at[core, me], s2.at[j], r2.at[me], peer(j)).wait_send()
        return carry

    lax.fori_loop(1, n, finish, 0)
    swap.wait_send()
    back = _rcopy(ag_buf.at[core], ag_buf.at[core], sd, rd, partner)
    back.start()
    _rcopy(ag_buf.at[other], ag_buf.at[other], sd, rd, partner).wait_recv()
    back.wait_send()
    o_ref[...] = ag_buf[...]


def allreduce_chip(x, tp_count, sum_dtype=None):
    n = x.shape[1]
    half = x.shape[1:]
    sum_dtype = x.dtype if sum_dtype is None else sum_dtype
    return pl.pallas_call(
        functools.partial(_allreduce_chip_kernel, tp_count),
        out_shape=jax.ShapeDtypeStruct(x.shape, sum_dtype),
        in_specs=[pl.BlockSpec(memory_space=pltpu.VMEM)],
        out_specs=pl.BlockSpec(memory_space=pltpu.VMEM),
        scratch_shapes=[
            pltpu.VMEM(half, x.dtype),
            pltpu.VMEM(half, sum_dtype),
            pltpu.VMEM(half, sum_dtype),
            pltpu.VMEM(x.shape, sum_dtype),
            pltpu.SemaphoreType.DMA(()),
            pltpu.SemaphoreType.DMA(()),
            pltpu.SemaphoreType.DMA((n,)),
            pltpu.SemaphoreType.DMA((n,)),
            pltpu.SemaphoreType.DMA((n,)),
            pltpu.SemaphoreType.DMA((n,)),
            pltpu.SemaphoreType.DMA(()),
            pltpu.SemaphoreType.DMA(()),
        ],
        compiler_params=pltpu.CompilerParams(
            has_side_effects=True,
            collective_id=_kernel_id(("allreduce_chip", x.shape, str(x.dtype), str(sum_dtype))),
        ),
    )(x)


def _opening_kernel(tp_count, x_ref, w_ref, o_ref, wo_ref, pbuf, sbuf, rs_buf, ag_buf, sa, ra, s1, r1, s2, r2, sd, rd, wbuf, ws, wr):
    seq_index = lax.axis_index("seq")
    tp_index = lax.axis_index("tp")
    count = 2 * x_ref.shape[1]
    me_all = seq_index * tp_count + tp_index
    _enter(count, me_all, lambda j: (j // tp_count, j % tp_count))
    n = w_ref.shape[0]

    def start(i, carry):
        j = lax.rem(seq_index + i, n)
        _rcopy(w_ref.at[j], wbuf.at[seq_index], ws.at[j], wr.at[seq_index], (j, tp_index)).start()
        return carry

    lax.fori_loop(1, n, start, 0)
    _allreduce_chip_body(tp_count, x_ref, o_ref, pbuf, sbuf, rs_buf, ag_buf, sa, ra, s1, r1, s2, r2, sd, rd)

    def finish(i, carry):
        j = lax.rem(seq_index + i, n)
        _rcopy(w_ref.at[j], wbuf.at[j], ws.at[j], wr.at[j], (j, tp_index)).wait_recv()
        _rcopy(w_ref.at[j], wbuf.at[seq_index], ws.at[j], wr.at[seq_index], (j, tp_index)).wait_send()
        return carry

    lax.fori_loop(1, n, finish, 0)
    wbuf[seq_index] = w_ref[seq_index]
    wo_ref[...] = wbuf[...]


def opening(x, w, tp_count):
    n = x.shape[1]
    half = x.shape[1:]
    m = w.shape[0]
    return pl.pallas_call(
        functools.partial(_opening_kernel, tp_count),
        out_shape=(jax.ShapeDtypeStruct(x.shape, x.dtype), jax.ShapeDtypeStruct(w.shape, w.dtype)),
        in_specs=[pl.BlockSpec(memory_space=pltpu.VMEM)] * 2,
        out_specs=(pl.BlockSpec(memory_space=pltpu.VMEM), pl.BlockSpec(memory_space=pltpu.VMEM)),
        scratch_shapes=[
            pltpu.VMEM(half, x.dtype),
            pltpu.VMEM(half, x.dtype),
            pltpu.VMEM(half, x.dtype),
            pltpu.VMEM(x.shape, x.dtype),
            pltpu.SemaphoreType.DMA(()),
            pltpu.SemaphoreType.DMA(()),
            pltpu.SemaphoreType.DMA((n,)),
            pltpu.SemaphoreType.DMA((n,)),
            pltpu.SemaphoreType.DMA((n,)),
            pltpu.SemaphoreType.DMA((n,)),
            pltpu.SemaphoreType.DMA(()),
            pltpu.SemaphoreType.DMA(()),
            pltpu.VMEM(w.shape, w.dtype),
            pltpu.SemaphoreType.DMA((m,)),
            pltpu.SemaphoreType.DMA((m,)),
        ],
        compiler_params=pltpu.CompilerParams(
            has_side_effects=True,
            collective_id=_kernel_id(("opening", x.shape, w.shape)),
        ),
    )(x, w)


def _all_to_all_kernel(n, whole, tp_count, x_ref, o_ref, buf, s1, r1):
    me, peer = _group_ids(whole, tp_count)
    _enter(n, me, peer)

    def start(i, carry):
        j = lax.rem(me + i, n)
        _rcopy(x_ref.at[j], buf.at[me], s1.at[j], r1.at[me], peer(j)).start()
        return carry

    lax.fori_loop(1, n, start, 0)

    def finish(i, carry):
        j = lax.rem(me + i, n)
        _rcopy(x_ref.at[j], buf.at[j], s1.at[j], r1.at[j], peer(j)).wait_recv()
        _rcopy(x_ref.at[j], buf.at[me], s1.at[j], r1.at[me], peer(j)).wait_send()
        return carry

    lax.fori_loop(1, n, finish, 0)
    buf[me] = x_ref[me]
    o_ref[...] = buf[...]


def all_to_all(x, whole, tp_count):
    n = x.shape[0]
    return pl.pallas_call(
        functools.partial(_all_to_all_kernel, n, whole, tp_count),
        out_shape=jax.ShapeDtypeStruct(x.shape, x.dtype),
        in_specs=[pl.BlockSpec(memory_space=pltpu.VMEM)],
        out_specs=pl.BlockSpec(memory_space=pltpu.VMEM),
        scratch_shapes=[
            pltpu.VMEM(x.shape, x.dtype),
            pltpu.SemaphoreType.DMA((n,)),
            pltpu.SemaphoreType.DMA((n,)),
        ],
        compiler_params=pltpu.CompilerParams(
            has_side_effects=True,
            collective_id=_kernel_id(("all_to_all", whole, x.shape, str(x.dtype))),
        ),
    )(x)


def _all_to_all_pair_kernel(n, whole, tp_count, xa_ref, xb_ref, oa_ref, ob_ref, bufa, bufb, sa, ra, sb, rb):
    me, peer = _group_ids(whole, tp_count)
    _enter(n, me, peer)

    def start(i, carry):
        j = lax.rem(me + i, n)
        _rcopy(xa_ref.at[j], bufa.at[me], sa.at[j], ra.at[me], peer(j)).start()
        _rcopy(xb_ref.at[j], bufb.at[me], sb.at[j], rb.at[me], peer(j)).start()
        return carry

    lax.fori_loop(1, n, start, 0)

    def finish(i, carry):
        j = lax.rem(me + i, n)
        _rcopy(xa_ref.at[j], bufa.at[j], sa.at[j], ra.at[j], peer(j)).wait_recv()
        _rcopy(xb_ref.at[j], bufb.at[j], sb.at[j], rb.at[j], peer(j)).wait_recv()
        _rcopy(xa_ref.at[j], bufa.at[me], sa.at[j], ra.at[me], peer(j)).wait_send()
        _rcopy(xb_ref.at[j], bufb.at[me], sb.at[j], rb.at[me], peer(j)).wait_send()
        return carry

    lax.fori_loop(1, n, finish, 0)
    bufa[me] = xa_ref[me]
    bufb[me] = xb_ref[me]
    oa_ref[...] = bufa[...]
    ob_ref[...] = bufb[...]


def all_to_all_pair(xa, xb, whole, tp_count):
    n = xa.shape[0]
    return pl.pallas_call(
        functools.partial(_all_to_all_pair_kernel, n, whole, tp_count),
        out_shape=(jax.ShapeDtypeStruct(xa.shape, xa.dtype), jax.ShapeDtypeStruct(xb.shape, xb.dtype)),
        in_specs=[pl.BlockSpec(memory_space=pltpu.VMEM)] * 2,
        out_specs=(pl.BlockSpec(memory_space=pltpu.VMEM), pl.BlockSpec(memory_space=pltpu.VMEM)),
        scratch_shapes=[
            pltpu.VMEM(xa.shape, xa.dtype),
            pltpu.VMEM(xb.shape, xb.dtype),
            pltpu.SemaphoreType.DMA((n,)),
            pltpu.SemaphoreType.DMA((n,)),
            pltpu.SemaphoreType.DMA((n,)),
            pltpu.SemaphoreType.DMA((n,)),
        ],
        compiler_params=pltpu.CompilerParams(
            has_side_effects=True,
            collective_id=_kernel_id(("all_to_all_pair", whole, xa.shape, xb.shape)),
        ),
    )(xa, xb)


def _attention_kernel(scale, q_ref, k_ref, v_ref, mask_ref, o_ref, m_ref, l_ref):
    valid = mask_ref[...] > 0.5
    scores = lax.dot_general(
        q_ref[0], k_ref[...], (((1,), (1,)), ((), ())), preferred_element_type=jnp.float32
    )
    scores = jnp.where(valid, scores * scale, very_negative)
    top = jnp.max(scores, axis=1, keepdims=True)
    weights = jnp.where(valid, jnp.exp(scores - top), 0.0)
    total = jnp.sum(weights, axis=1, keepdims=True)
    o_ref[0] = jnp.dot(weights.astype(jnp.bfloat16), v_ref[...], preferred_element_type=jnp.float32)
    m_ref[0] = jnp.broadcast_to(top, m_ref.shape[1:])
    l_ref[0] = jnp.broadcast_to(total, l_ref.shape[1:])


def cache_attention(q_pad, k_cache, v_cache, mask, layer_index, scale):
    heads, rows, lanes = q_pad.shape
    slots = k_cache.shape[1]
    per_block = lanes // HEAD_DIM
    out_spec = pl.BlockSpec((1, rows, lanes), lambda h: (h, 0, 0))
    return pl.pallas_call(
        functools.partial(_attention_kernel, scale),
        grid=(heads,),
        out_shape=[jax.ShapeDtypeStruct((heads, rows, lanes), jnp.float32)] * 3,
        in_specs=[
            pl.BlockSpec((1, rows, lanes), lambda h: (h, 0, 0)),
            pl.BlockSpec((None, slots, lanes), lambda h: (layer_index, 0, h // per_block)),
            pl.BlockSpec((None, slots, lanes), lambda h: (layer_index, 0, h // per_block)),
            pl.BlockSpec((rows, slots), lambda h: (0, 0)),
        ],
        out_specs=[out_spec] * 3,
    )(q_pad, k_cache, v_cache, mask)


def per_device(
    token_ids,
    embedding,
    group_of,
    prefix_len,
    tail_len,
    block_map,
    k_cache,
    v_cache,
    ln_gain,
    ln_bias,
    w_qkv,
    w_fc1,
    b_fc1,
    w_out,
    w_fc2,
):
    tp_count = lax.axis_size("tp")
    seq_count = lax.axis_size("seq")
    all_count = tp_count * seq_count
    seq_index = lax.axis_index("seq")
    tp_index = lax.axis_index("tp")
    requests = token_ids.shape[0]
    new_tokens = token_ids.shape[1]
    rows = requests * new_tokens
    groups = prefix_len.shape[0]
    heads_local = HEADS // tp_count
    width = embedding.shape[1]
    score_scale = 1.0 / math.sqrt(HEAD_DIM)

    vocab_rows = embedding.shape[0]
    first_row = (seq_index * tp_count + tp_index) * vocab_rows
    local_ids = token_ids.reshape(-1) - first_row
    inside = (local_ids >= 0) & (local_ids < vocab_rows)
    picked = jnp.take(embedding, jnp.clip(local_ids, 0, vocab_rows - 1), axis=0)
    picked = jnp.where(inside[:, None], picked, jnp.zeros_like(picked))

    group_hit = group_of[:, None] == jnp.arange(groups, dtype=jnp.int32)[None, :]
    shared_len = jnp.sum(jnp.where(group_hit, prefix_len[None, :], 0), axis=1)
    base_positions = shared_len + tail_len
    positions = (base_positions[:, None] + jnp.arange(new_tokens, dtype=jnp.int32)[None, :]).reshape(-1)
    seg_len = jnp.concatenate([prefix_len, tail_len])
    seg_count = seg_len.shape[0]
    blocks_local = block_map.shape[0]
    seg_blk = block_map[:, 0]
    rank_blk = block_map[:, 1]
    seg_hit = seg_blk[:, None] == jnp.arange(seg_count, dtype=jnp.int32)[None, :]
    len_blk = jnp.sum(jnp.where(seg_hit, seg_len[None, :], 0), axis=1)
    slot_positions = rank_blk[:, None] * BLOCK + jnp.arange(BLOCK, dtype=jnp.int32)[None, :]
    live_slot = ((seg_blk[:, None] >= 0) & (slot_positions < len_blk[:, None])).reshape(-1)
    seg_slot = jnp.broadcast_to(seg_blk[:, None], (blocks_local, BLOCK)).reshape(-1)
    own_tail = seg_slot[None, :] == (groups + jnp.arange(requests, dtype=jnp.int32))[:, None]
    own_prompt = seg_slot[None, :] == group_of[:, None]
    allowed = (own_tail | own_prompt) & live_slot[None, :]
    allowed = jnp.repeat(allowed, new_tokens, axis=0)
    mask_f = allowed.astype(jnp.float32)

    rows_local = w_qkv.shape[1]
    unit_count = w_fc2.shape[1]
    sub_width = w_out.shape[1]
    pieces = HEAD_DIM // sub_width
    my_head = seq_index // pieces
    my_piece = seq_index % pieces
    causal = (
        jnp.arange(new_tokens, dtype=jnp.int32)[None, :]
        <= jnp.arange(new_tokens, dtype=jnp.int32)[:, None]
    )

    half_rot = ROT // 2
    pair_width = 2 * sub_width
    qkv_t = w_qkv.transpose(2, 3, 0, 1).reshape(3, heads_local, HEAD_DIM, LAYERS * rows_local)
    q_t = qkv_t[0].reshape(heads_local, 1, HEAD_DIM // pair_width, 1, pair_width, LAYERS * rows_local)
    q_t = jnp.broadcast_to(
        q_t, (heads_local, 1, HEAD_DIM // pair_width, pieces // 2, pair_width, LAYERS * rows_local)
    )
    k_t = jnp.broadcast_to(
        qkv_t[1][:, None], (heads_local, pieces, HEAD_DIM, LAYERS * rows_local)
    )
    v_t = qkv_t[2].reshape(seq_count, sub_width, LAYERS * rows_local)
    f_t = w_fc1.transpose(2, 0, 1).reshape(seq_count, unit_count, LAYERS * rows_local)
    message = jnp.concatenate(
        [
            q_t.reshape(seq_count, pair_width, LAYERS * rows_local),
            k_t.reshape(seq_count, HEAD_DIM, LAYERS * rows_local),
            v_t,
            f_t,
        ],
        axis=1,
    )
    cols_mine = message.shape[1]
    start_states, got_w = opening(
        picked.reshape(2, all_count // 2, -1, 128),
        message,
        tp_count,
    )
    hidden_state = start_states.reshape(rows, width).astype(jnp.float32)
    w_mine = (
        got_w.reshape(seq_count, cols_mine, LAYERS, rows_local)
        .transpose(2, 1, 0, 3)
        .reshape(LAYERS, cols_mine, seq_count * rows_local)
    )
    q_end = pair_width
    k_end = q_end + HEAD_DIM
    v_end = k_end + sub_width
    angles = positions.astype(jnp.float32)[:, None] * jnp.exp(
        jnp.arange(half_rot, dtype=jnp.float32) * (-2.0 * math.log(10000.0) / ROT)
    )[None, :]
    cosine = jnp.cos(angles)
    sine_part = jnp.sin(angles)
    for layer_index in range(LAYERS):
        normed = layer_norm(hidden_state, ln_gain[layer_index], ln_bias[layer_index]).astype(
            jnp.bfloat16
        )
        local = jnp.einsum(
            "rc,kc->rk", normed, w_mine[layer_index], preferred_element_type=jnp.float32
        )
        q_pair = local[:, :q_end]
        low_half = q_pair[:, :half_rot]
        high_half = q_pair[:, half_rot:]
        q_rot = jnp.concatenate(
            [low_half * cosine - high_half * sine_part, high_half * cosine + low_half * sine_part],
            axis=1,
        )
        q_pair = jnp.where(my_piece < 2, q_rot, q_pair)
        q_piece = lax.dynamic_slice_in_dim(q_pair, (my_piece % 2) * sub_width, sub_width, 1)
        q_piece = q_piece.astype(jnp.bfloat16).T
        k_h = rotary(local[:, None, q_end:k_end], positions)[:, 0].astype(jnp.bfloat16)
        v_h = local[:, k_end:v_end].astype(jnp.bfloat16)
        pre_act = local[:, v_end:]
        pre_act = (
            pre_act
            + lax.dynamic_slice_in_dim(b_fc1[layer_index], seq_index * unit_count, unit_count, 0)[
                None, :
            ]
        )
        activated = jax.nn.gelu(pre_act, approximate=True).astype(jnp.bfloat16)
        q_all = all_to_all(jnp.broadcast_to(q_piece[None], (seq_count,) + q_piece.shape), False, tp_count)
        queries = (
            q_all.reshape(heads_local, pieces, sub_width, rows)
            .transpose(3, 0, 1, 2)
            .reshape(rows, heads_local, HEAD_DIM)
        )
        per_block = 128 // HEAD_DIM
        same_half = (
            jnp.arange(per_block, dtype=jnp.int32)[:, None]
            == jnp.arange(per_block, dtype=jnp.int32)[None, :]
        )
        q_pairs = queries.reshape(rows, heads_local // per_block, per_block, HEAD_DIM).transpose(1, 2, 0, 3)
        q_pad = jnp.where(
            same_half[None, :, None, :, None], q_pairs[:, :, :, None, :], jnp.zeros((), jnp.bfloat16)
        ).reshape(heads_local, rows, 128)
        out_pad, max_pad, sum_pad = cache_attention(
            q_pad, k_cache, v_cache, mask_f, layer_index, score_scale
        )
        part_out = jnp.sum(
            jnp.where(
                same_half[None, :, None, :, None],
                out_pad.reshape(heads_local // per_block, per_block, rows, per_block, HEAD_DIM),
                0.0,
            ),
            axis=3,
        ).reshape(heads_local, rows, HEAD_DIM)
        part_max = max_pad[:, :, 0]
        part_sum = sum_pad[:, :, 0]
        out_pieces = (
            part_out.reshape(heads_local, rows, pieces, sub_width)
            .transpose(0, 2, 3, 1)
            .reshape(heads_local * pieces, sub_width, rows)
        )
        max_rows = jnp.repeat(part_max, pieces, axis=0)[:, None, :]
        sum_rows = jnp.repeat(part_sum, pieces, axis=0)[:, None, :]
        pad_rows = jnp.zeros((heads_local * pieces, 6, rows), jnp.float32)
        stats = jnp.concatenate([max_rows, sum_rows, pad_rows], axis=1)
        got_out, got_stats = all_to_all_pair(out_pieces.astype(jnp.bfloat16), stats, False, tp_count)
        got_out = got_out.astype(jnp.float32)
        got_max = got_stats[:, 0, :]
        got_sum = got_stats[:, 1, :]

        q_h = lax.dynamic_index_in_dim(queries, my_head, 1, keepdims=False)
        q_h = q_h.reshape(requests, new_tokens, HEAD_DIM)
        k_h = k_h.reshape(requests, new_tokens, HEAD_DIM)
        v_h = v_h.reshape(requests, new_tokens, sub_width)
        fresh_scores = (
            jnp.einsum("rtd,rud->rtu", q_h, k_h, preferred_element_type=jnp.float32) * score_scale
        )
        fresh_scores = jnp.where(causal[None], fresh_scores, very_negative)
        fresh_max = jnp.max(fresh_scores, axis=2)
        fresh_weights = jnp.where(causal[None], jnp.exp(fresh_scores - fresh_max[..., None]), 0.0)
        fresh_sum = jnp.sum(fresh_weights, axis=2)
        fresh_out = jnp.einsum(
            "rtu,rud->rtd",
            fresh_weights.astype(jnp.bfloat16),
            v_h,
            preferred_element_type=jnp.float32,
        )
        fresh_max = fresh_max.reshape(rows)
        fresh_sum = fresh_sum.reshape(rows)
        fresh_out = fresh_out.reshape(rows, sub_width)

        top = jnp.maximum(jnp.max(got_max, axis=0), fresh_max)
        scale_cache = jnp.exp(got_max - top[None, :])
        scale_fresh = jnp.exp(fresh_max - top)
        denom = jnp.sum(got_sum * scale_cache, axis=0) + fresh_sum * scale_fresh
        numer = jnp.sum(got_out * scale_cache[:, None, :], axis=0).T + fresh_out * scale_fresh[:, None]
        my_cols = (numer / denom[:, None]).astype(jnp.bfloat16)

        update = jnp.dot(my_cols, w_out[layer_index], preferred_element_type=jnp.float32)
        update = update + jnp.dot(activated, w_fc2[layer_index], preferred_element_type=jnp.float32)
        update = allreduce_chip(
            update.astype(jnp.bfloat16).reshape(2, all_count // 2, -1, 128), tp_count
        )
        hidden_state = hidden_state + update.reshape(rows, width).astype(jnp.float32)
    return hidden_state.reshape(requests, new_tokens, width)


def solution(mesh):
    in_specs = (
        P(),
        P(("seq", "tp"), None),
        P(),
        P(),
        P(),
        P("seq", None),
        P(None, "seq", "tp"),
        P(None, "seq", "tp"),
        P(),
        P(),
        P(None, "seq", None, "tp"),
        P(None, "seq", "tp"),
        P(None, "tp"),
        P(None, ("tp", "seq"), None),
        P(None, ("tp", "seq"), None),
    )
    out_specs = P()
    return jax.shard_map(
        per_device, mesh=mesh, in_specs=in_specs, out_specs=out_specs, check_vma=False
    )
```

```python
import functools
import math

import jax
import numpy as np
import jax.numpy as jnp
from jax import lax
from jax.experimental import pallas as pl
from jax.experimental.pallas import tpu as pltpu
from jax.sharding import PartitionSpec as P

HEADS = 32
HEAD_DIM = 64
ROT = 32
LAYERS = 2
BLOCK = 128
SPAN = 512
MESH_IDS = pl.DeviceIdType.MESH

very_negative = -1e30


def layer_norm(values, gain_row, bias_row):
    average = jnp.mean(values, axis=-1, keepdims=True)
    centred = values - average
    variance = jnp.mean(centred * centred, axis=-1, keepdims=True)
    return centred * lax.rsqrt(variance + 1e-05) * gain_row + bias_row


def rotary(values, positions):
    half_width = ROT // 2
    frequency = jnp.exp(
        jnp.arange(half_width, dtype=jnp.float32) * (-2.0 * math.log(10000.0) / ROT)
    )
    angles = positions.astype(jnp.float32)[:, None] * frequency[None, :]
    cosine = jnp.cos(angles)[:, None, :]
    sine_part = jnp.sin(angles)[:, None, :]
    low_half = values[..., :half_width]
    high_half = values[..., half_width:ROT]
    return jnp.concatenate(
        [
            low_half * cosine - high_half * sine_part,
            high_half * cosine + low_half * sine_part,
            values[..., ROT:],
        ],
        axis=-1,
    )


def _group_ids(whole, tp_count):
    seq_index = lax.axis_index("seq")
    tp_index = lax.axis_index("tp")
    if whole:
        me = seq_index * tp_count + tp_index

        def peer(j):
            return (j // tp_count, j % tp_count)

    else:
        me = seq_index

        def peer(j):
            return (j, tp_index)

    return me, peer


_KERNEL_IDS = {}


def _kernel_id(key):
    if key not in _KERNEL_IDS:
        _KERNEL_IDS[key] = len(_KERNEL_IDS)
    return _KERNEL_IDS[key]


def _enter(n, me, peer):
    barrier = pltpu.get_barrier_semaphore()

    def greet(i, carry):
        j = lax.rem(me + i, n)
        pl.semaphore_signal(barrier, 1, device_id=peer(j), device_id_type=MESH_IDS)
        return carry

    lax.fori_loop(1, n, greet, 0)
    pl.semaphore_wait(barrier, n - 1)


def _rcopy(src, dst, send_sem, recv_sem, device):
    return pltpu.make_async_remote_copy(
        src_ref=src,
        dst_ref=dst,
        send_sem=send_sem,
        recv_sem=recv_sem,
        device_id=device,
        device_id_type=MESH_IDS,
    )


def _allreduce_kernel(n, whole, tp_count, x_ref, o_ref, rs_buf, ag_buf, s1, r1, s2, r2):
    me, peer = _group_ids(whole, tp_count)
    _enter(n, me, peer)

    def start_scatter(i, carry):
        j = lax.rem(me + i, n)
        _rcopy(x_ref.at[j], rs_buf.at[me], s1.at[j], r1.at[me], peer(j)).start()
        return carry

    lax.fori_loop(1, n, start_scatter, 0)

    def gather_sum(i, acc):
        j = lax.rem(me + i, n)
        _rcopy(x_ref.at[j], rs_buf.at[j], s1.at[j], r1.at[j], peer(j)).wait_recv()
        return acc + rs_buf[j].astype(jnp.float32)

    total = lax.fori_loop(1, n, gather_sum, x_ref[me].astype(jnp.float32))
    ag_buf[me] = total.astype(ag_buf.dtype)

    def start_gather(i, carry):
        j = lax.rem(me + i, n)
        _rcopy(ag_buf.at[me], ag_buf.at[me], s2.at[j], r2.at[me], peer(j)).start()
        return carry

    lax.fori_loop(1, n, start_gather, 0)

    def finish(i, carry):
        j = lax.rem(me + i, n)
        _rcopy(ag_buf.at[j], ag_buf.at[j], s2.at[j], r2.at[j], peer(j)).wait_recv()
        _rcopy(x_ref.at[j], rs_buf.at[me], s1.at[j], r1.at[me], peer(j)).wait_send()
        _rcopy(ag_buf.at[me], ag_buf.at[me], s2.at[j], r2.at[me], peer(j)).wait_send()
        return carry

    lax.fori_loop(1, n, finish, 0)
    o_ref[...] = ag_buf[...]


def allreduce(x, whole, tp_count):
    n = x.shape[0]
    return pl.pallas_call(
        functools.partial(_allreduce_kernel, n, whole, tp_count),
        out_shape=jax.ShapeDtypeStruct(x.shape, x.dtype),
        in_specs=[pl.BlockSpec(memory_space=pltpu.VMEM)],
        out_specs=pl.BlockSpec(memory_space=pltpu.VMEM),
        scratch_shapes=[
            pltpu.VMEM(x.shape, x.dtype),
            pltpu.VMEM(x.shape, x.dtype),
            pltpu.SemaphoreType.DMA((n,)),
            pltpu.SemaphoreType.DMA((n,)),
            pltpu.SemaphoreType.DMA((n,)),
            pltpu.SemaphoreType.DMA((n,)),
        ],
        compiler_params=pltpu.CompilerParams(
            has_side_effects=True,
            collective_id=_kernel_id(("allreduce", whole, x.shape, str(x.dtype))),
        ),
    )(x)


def _allreduce_chip_kernel(tp_count, x_ref, o_ref, pbuf, sbuf, rs_buf, ag_buf, sa, ra, s1, r1, s2, r2, sd, rd):
    seq_index = lax.axis_index("seq")
    tp_index = lax.axis_index("tp")
    n = x_ref.shape[1]
    core = seq_index % 2
    other = 1 - core
    me = (seq_index // 2) * tp_count + tp_index
    partner = (seq_index + 1 - 2 * core, tp_index)

    def peer(j):
        return ((j // tp_count) * 2 + core, j % tp_count)

    barrier = pltpu.get_barrier_semaphore()

    def greet(i, carry):
        j = lax.rem(me + i, n)
        pl.semaphore_signal(barrier, 1, device_id=peer(j), device_id_type=MESH_IDS)
        return carry

    lax.fori_loop(1, n, greet, 0)
    pl.semaphore_signal(barrier, 1, device_id=partner, device_id_type=MESH_IDS)
    pl.semaphore_wait(barrier, n)
    _allreduce_chip_body(tp_count, x_ref, o_ref, pbuf, sbuf, rs_buf, ag_buf, sa, ra, s1, r1, s2, r2, sd, rd)


def _allreduce_chip_body(tp_count, x_ref, o_ref, pbuf, sbuf, rs_buf, ag_buf, sa, ra, s1, r1, s2, r2, sd, rd):
    seq_index = lax.axis_index("seq")
    tp_index = lax.axis_index("tp")
    n = x_ref.shape[1]
    core = seq_index % 2
    other = 1 - core
    me = (seq_index // 2) * tp_count + tp_index
    partner = (seq_index + 1 - 2 * core, tp_index)

    def peer(j):
        return ((j // tp_count) * 2 + core, j % tp_count)

    swap = _rcopy(x_ref.at[other], pbuf, sa, ra, partner)
    swap.start()
    swap.wait_recv()
    sbuf[...] = (x_ref[core].astype(jnp.float32) + pbuf[...].astype(jnp.float32)).astype(sbuf.dtype)

    def start_scatter(i, carry):
        j = lax.rem(me + i, n)
        _rcopy(sbuf.at[j], rs_buf.at[me], s1.at[j], r1.at[me], peer(j)).start()
        return carry

    lax.fori_loop(1, n, start_scatter, 0)

    def gather_sum(i, acc):
        j = lax.rem(me + i, n)
        _rcopy(sbuf.at[j], rs_buf.at[j], s1.at[j], r1.at[j], peer(j)).wait_recv()
        return acc + rs_buf[j].astype(jnp.float32)

    total = lax.fori_loop(1, n, gather_sum, sbuf[me].astype(jnp.float32))
    ag_buf[core, me] = total.astype(ag_buf.dtype)

    def start_gather(i, carry):
        j = lax.rem(me + i, n)
        _rcopy(ag_buf.at[core, me], ag_buf.at[core, me], s2.at[j], r2.at[me], peer(j)).start()
        return carry

    lax.fori_loop(1, n, start_gather, 0)

    def finish(i, carry):
        j = lax.rem(me + i, n)
        _rcopy(ag_buf.at[core, j], ag_buf.at[core, j], s2.at[j], r2.at[j], peer(j)).wait_recv()
        _rcopy(sbuf.at[j], rs_buf.at[me], s1.at[j], r1.at[me], peer(j)).wait_send()
        _rcopy(ag_buf.at[core, me], ag_buf.at[core, me], s2.at[j], r2.at[me], peer(j)).wait_send()
        return carry

    lax.fori_loop(1, n, finish, 0)
    swap.wait_send()
    back = _rcopy(ag_buf.at[core], ag_buf.at[core], sd, rd, partner)
    back.start()
    _rcopy(ag_buf.at[other], ag_buf.at[other], sd, rd, partner).wait_recv()
    back.wait_send()
    o_ref[...] = ag_buf[...]


def allreduce_chip(x, tp_count, sum_dtype=None):
    n = x.shape[1]
    half = x.shape[1:]
    sum_dtype = x.dtype if sum_dtype is None else sum_dtype
    return pl.pallas_call(
        functools.partial(_allreduce_chip_kernel, tp_count),
        out_shape=jax.ShapeDtypeStruct(x.shape, sum_dtype),
        in_specs=[pl.BlockSpec(memory_space=pltpu.VMEM)],
        out_specs=pl.BlockSpec(memory_space=pltpu.VMEM),
        scratch_shapes=[
            pltpu.VMEM(half, x.dtype),
            pltpu.VMEM(half, sum_dtype),
            pltpu.VMEM(half, sum_dtype),
            pltpu.VMEM(x.shape, sum_dtype),
            pltpu.SemaphoreType.DMA(()),
            pltpu.SemaphoreType.DMA(()),
            pltpu.SemaphoreType.DMA((n,)),
            pltpu.SemaphoreType.DMA((n,)),
            pltpu.SemaphoreType.DMA((n,)),
            pltpu.SemaphoreType.DMA((n,)),
            pltpu.SemaphoreType.DMA(()),
            pltpu.SemaphoreType.DMA(()),
        ],
        compiler_params=pltpu.CompilerParams(
            has_side_effects=True,
            collective_id=_kernel_id(("allreduce_chip", x.shape, str(x.dtype), str(sum_dtype))),
        ),
    )(x)


def _opening_kernel(tp_count, x_ref, w_ref, o_ref, wo_ref, pbuf, sbuf, rs_buf, ag_buf, sa, ra, s1, r1, s2, r2, sd, rd, wbuf, ws, wr):
    seq_index = lax.axis_index("seq")
    tp_index = lax.axis_index("tp")
    count = 2 * x_ref.shape[1]
    me_all = seq_index * tp_count + tp_index
    _enter(count, me_all, lambda j: (j // tp_count, j % tp_count))
    n = w_ref.shape[0]

    def start(i, carry):
        j = lax.rem(seq_index + i, n)
        _rcopy(w_ref.at[j], wbuf.at[seq_index], ws.at[j], wr.at[seq_index], (j, tp_index)).start()
        return carry

    lax.fori_loop(1, n, start, 0)
    _allreduce_chip_body(tp_count, x_ref, o_ref, pbuf, sbuf, rs_buf, ag_buf, sa, ra, s1, r1, s2, r2, sd, rd)

    def finish(i, carry):
        j = lax.rem(seq_index + i, n)
        _rcopy(w_ref.at[j], wbuf.at[j], ws.at[j], wr.at[j], (j, tp_index)).wait_recv()
        _rcopy(w_ref.at[j], wbuf.at[seq_index], ws.at[j], wr.at[seq_index], (j, tp_index)).wait_send()
        return carry

    lax.fori_loop(1, n, finish, 0)
    wbuf[seq_index] = w_ref[seq_index]
    wo_ref[...] = wbuf[...]


def opening(x, w, tp_count):
    n = x.shape[1]
    half = x.shape[1:]
    m = w.shape[0]
    return pl.pallas_call(
        functools.partial(_opening_kernel, tp_count),
        out_shape=(jax.ShapeDtypeStruct(x.shape, x.dtype), jax.ShapeDtypeStruct(w.shape, w.dtype)),
        in_specs=[pl.BlockSpec(memory_space=pltpu.VMEM)] * 2,
        out_specs=(pl.BlockSpec(memory_space=pltpu.VMEM), pl.BlockSpec(memory_space=pltpu.VMEM)),
        scratch_shapes=[
            pltpu.VMEM(half, x.dtype),
            pltpu.VMEM(half, x.dtype),
            pltpu.VMEM(half, x.dtype),
            pltpu.VMEM(x.shape, x.dtype),
            pltpu.SemaphoreType.DMA(()),
            pltpu.SemaphoreType.DMA(()),
            pltpu.SemaphoreType.DMA((n,)),
            pltpu.SemaphoreType.DMA((n,)),
            pltpu.SemaphoreType.DMA((n,)),
            pltpu.SemaphoreType.DMA((n,)),
            pltpu.SemaphoreType.DMA(()),
            pltpu.SemaphoreType.DMA(()),
            pltpu.VMEM(w.shape, w.dtype),
            pltpu.SemaphoreType.DMA((m,)),
            pltpu.SemaphoreType.DMA((m,)),
        ],
        compiler_params=pltpu.CompilerParams(
            has_side_effects=True,
            collective_id=_kernel_id(("opening", x.shape, w.shape)),
        ),
    )(x, w)


def _all_to_all_kernel(n, whole, tp_count, x_ref, o_ref, buf, s1, r1):
    me, peer = _group_ids(whole, tp_count)
    _enter(n, me, peer)

    def start(i, carry):
        j = lax.rem(me + i, n)
        _rcopy(x_ref.at[j], buf.at[me], s1.at[j], r1.at[me], peer(j)).start()
        return carry

    lax.fori_loop(1, n, start, 0)

    def finish(i, carry):
        j = lax.rem(me + i, n)
        _rcopy(x_ref.at[j], buf.at[j], s1.at[j], r1.at[j], peer(j)).wait_recv()
        _rcopy(x_ref.at[j], buf.at[me], s1.at[j], r1.at[me], peer(j)).wait_send()
        return carry

    lax.fori_loop(1, n, finish, 0)
    buf[me] = x_ref[me]
    o_ref[...] = buf[...]


def all_to_all(x, whole, tp_count):
    n = x.shape[0]
    return pl.pallas_call(
        functools.partial(_all_to_all_kernel, n, whole, tp_count),
        out_shape=jax.ShapeDtypeStruct(x.shape, x.dtype),
        in_specs=[pl.BlockSpec(memory_space=pltpu.VMEM)],
        out_specs=pl.BlockSpec(memory_space=pltpu.VMEM),
        scratch_shapes=[
            pltpu.VMEM(x.shape, x.dtype),
            pltpu.SemaphoreType.DMA((n,)),
            pltpu.SemaphoreType.DMA((n,)),
        ],
        compiler_params=pltpu.CompilerParams(
            has_side_effects=True,
            collective_id=_kernel_id(("all_to_all", whole, x.shape, str(x.dtype))),
        ),
    )(x)


def _all_to_all_pair_kernel(n, whole, tp_count, xa_ref, xb_ref, oa_ref, ob_ref, bufa, bufb, sa, ra, sb, rb):
    me, peer = _group_ids(whole, tp_count)
    _enter(n, me, peer)

    def start(i, carry):
        j = lax.rem(me + i, n)
        _rcopy(xa_ref.at[j], bufa.at[me], sa.at[j], ra.at[me], peer(j)).start()
        _rcopy(xb_ref.at[j], bufb.at[me], sb.at[j], rb.at[me], peer(j)).start()
        return carry

    lax.fori_loop(1, n, start, 0)

    def finish(i, carry):
        j = lax.rem(me + i, n)
        _rcopy(xa_ref.at[j], bufa.at[j], sa.at[j], ra.at[j], peer(j)).wait_recv()
        _rcopy(xb_ref.at[j], bufb.at[j], sb.at[j], rb.at[j], peer(j)).wait_recv()
        _rcopy(xa_ref.at[j], bufa.at[me], sa.at[j], ra.at[me], peer(j)).wait_send()
        _rcopy(xb_ref.at[j], bufb.at[me], sb.at[j], rb.at[me], peer(j)).wait_send()
        return carry

    lax.fori_loop(1, n, finish, 0)
    bufa[me] = xa_ref[me]
    bufb[me] = xb_ref[me]
    oa_ref[...] = bufa[...]
    ob_ref[...] = bufb[...]


def all_to_all_pair(xa, xb, whole, tp_count):
    n = xa.shape[0]
    return pl.pallas_call(
        functools.partial(_all_to_all_pair_kernel, n, whole, tp_count),
        out_shape=(jax.ShapeDtypeStruct(xa.shape, xa.dtype), jax.ShapeDtypeStruct(xb.shape, xb.dtype)),
        in_specs=[pl.BlockSpec(memory_space=pltpu.VMEM)] * 2,
        out_specs=(pl.BlockSpec(memory_space=pltpu.VMEM), pl.BlockSpec(memory_space=pltpu.VMEM)),
        scratch_shapes=[
            pltpu.VMEM(xa.shape, xa.dtype),
            pltpu.VMEM(xb.shape, xb.dtype),
            pltpu.SemaphoreType.DMA((n,)),
            pltpu.SemaphoreType.DMA((n,)),
            pltpu.SemaphoreType.DMA((n,)),
            pltpu.SemaphoreType.DMA((n,)),
        ],
        compiler_params=pltpu.CompilerParams(
            has_side_effects=True,
            collective_id=_kernel_id(("all_to_all_pair", whole, xa.shape, xb.shape)),
        ),
    )(xa, xb)


def _attention_kernel(scale, q_ref, k_ref, v_ref, mask_ref, o_ref, m_ref, l_ref):
    valid = mask_ref[...] > 0.5
    for half in range(q_ref.shape[0]):
        scores = lax.dot_general(
            q_ref[half], k_ref[...], (((1,), (1,)), ((), ())), preferred_element_type=jnp.float32
        )
        scores = jnp.where(valid, scores * scale, very_negative)
        top = jnp.max(scores, axis=1, keepdims=True)
        weights = jnp.where(valid, jnp.exp(scores - top), 0.0)
        total = jnp.sum(weights, axis=1, keepdims=True)
        o_ref[half] = jnp.dot(
            weights.astype(jnp.bfloat16), v_ref[...], preferred_element_type=jnp.float32
        )
        m_ref[half] = jnp.broadcast_to(top, m_ref.shape[1:])
        l_ref[half] = jnp.broadcast_to(total, l_ref.shape[1:])


def cache_attention(q_pad, k_cache, v_cache, mask, layer_index, scale):
    heads, rows, lanes = q_pad.shape
    slots = k_cache.shape[1]
    per_block = lanes // HEAD_DIM
    out_spec = pl.BlockSpec((per_block, rows, lanes), lambda b: (b, 0, 0))
    return pl.pallas_call(
        functools.partial(_attention_kernel, scale),
        grid=(heads // per_block,),
        out_shape=[jax.ShapeDtypeStruct((heads, rows, lanes), jnp.float32)] * 3,
        in_specs=[
            pl.BlockSpec((per_block, rows, lanes), lambda b: (b, 0, 0)),
            pl.BlockSpec((None, slots, lanes), lambda b: (layer_index, 0, b)),
            pl.BlockSpec((None, slots, lanes), lambda b: (layer_index, 0, b)),
            pl.BlockSpec((rows, slots), lambda b: (0, 0)),
        ],
        out_specs=[out_spec] * 3,
    )(q_pad, k_cache, v_cache, mask)


def per_device(
    token_ids,
    embedding,
    group_of,
    prefix_len,
    tail_len,
    block_map,
    k_cache,
    v_cache,
    ln_gain,
    ln_bias,
    w_qkv,
    w_fc1,
    b_fc1,
    w_out,
    w_fc2,
):
    tp_count = lax.axis_size("tp")
    seq_count = lax.axis_size("seq")
    all_count = tp_count * seq_count
    seq_index = lax.axis_index("seq")
    tp_index = lax.axis_index("tp")
    requests = token_ids.shape[0]
    new_tokens = token_ids.shape[1]
    rows = requests * new_tokens
    groups = prefix_len.shape[0]
    heads_local = HEADS // tp_count
    width = embedding.shape[1]
    score_scale = 1.0 / math.sqrt(HEAD_DIM)

    vocab_rows = embedding.shape[0]
    first_row = (seq_index * tp_count + tp_index) * vocab_rows
    local_ids = token_ids.reshape(-1) - first_row
    inside = (local_ids >= 0) & (local_ids < vocab_rows)
    picked = jnp.take(embedding, jnp.clip(local_ids, 0, vocab_rows - 1), axis=0)
    picked = jnp.where(inside[:, None], picked, jnp.zeros_like(picked))

    group_hit = group_of[:, None] == jnp.arange(groups, dtype=jnp.int32)[None, :]
    shared_len = jnp.sum(jnp.where(group_hit, prefix_len[None, :], 0), axis=1)
    base_positions = shared_len + tail_len
    positions = (base_positions[:, None] + jnp.arange(new_tokens, dtype=jnp.int32)[None, :]).reshape(-1)
    seg_len = jnp.concatenate([prefix_len, tail_len])
    seg_count = seg_len.shape[0]
    blocks_local = block_map.shape[0]
    seg_blk = block_map[:, 0]
    rank_blk = block_map[:, 1]
    seg_hit = seg_blk[:, None] == jnp.arange(seg_count, dtype=jnp.int32)[None, :]
    len_blk = jnp.sum(jnp.where(seg_hit, seg_len[None, :], 0), axis=1)
    slot_positions = rank_blk[:, None] * BLOCK + jnp.arange(BLOCK, dtype=jnp.int32)[None, :]
    live_slot = ((seg_blk[:, None] >= 0) & (slot_positions < len_blk[:, None])).reshape(-1)
    seg_slot = jnp.broadcast_to(seg_blk[:, None], (blocks_local, BLOCK)).reshape(-1)
    own_tail = seg_slot[None, :] == (groups + jnp.arange(requests, dtype=jnp.int32))[:, None]
    own_prompt = seg_slot[None, :] == group_of[:, None]
    allowed = (own_tail | own_prompt) & live_slot[None, :]
    allowed = jnp.repeat(allowed, new_tokens, axis=0)
    mask_f = allowed.astype(jnp.float32)

    rows_local = w_qkv.shape[1]
    unit_count = w_fc2.shape[1]
    sub_width = w_out.shape[1]
    pieces = HEAD_DIM // sub_width
    my_head = seq_index // pieces
    my_piece = seq_index % pieces
    causal = (
        jnp.arange(new_tokens, dtype=jnp.int32)[None, :]
        <= jnp.arange(new_tokens, dtype=jnp.int32)[:, None]
    )

    half_rot = ROT // 2
    pair_width = 2 * sub_width
    qkv_t = w_qkv.transpose(2, 3, 0, 1).reshape(3, heads_local, HEAD_DIM, LAYERS * rows_local)
    q_t = qkv_t[0].reshape(heads_local, 1, HEAD_DIM // pair_width, 1, pair_width, LAYERS * rows_local)
    q_t = jnp.broadcast_to(
        q_t, (heads_local, 1, HEAD_DIM // pair_width, pieces // 2, pair_width, LAYERS * rows_local)
    )
    k_t = jnp.broadcast_to(
        qkv_t[1][:, None], (heads_local, pieces, HEAD_DIM, LAYERS * rows_local)
    )
    v_t = qkv_t[2].reshape(seq_count, sub_width, LAYERS * rows_local)
    f_t = w_fc1.transpose(2, 0, 1).reshape(seq_count, unit_count, LAYERS * rows_local)
    message = jnp.concatenate(
        [
            q_t.reshape(seq_count, pair_width, LAYERS * rows_local),
            k_t.reshape(seq_count, HEAD_DIM, LAYERS * rows_local),
            v_t,
            f_t,
        ],
        axis=1,
    )
    cols_mine = message.shape[1]
    start_states, got_w = opening(
        picked.reshape(2, all_count // 2, -1, 128),
        message,
        tp_count,
    )
    hidden_state = start_states.reshape(rows, width).astype(jnp.float32)
    w_mine = (
        got_w.reshape(seq_count, cols_mine, LAYERS, rows_local)
        .transpose(2, 1, 0, 3)
        .reshape(LAYERS, cols_mine, seq_count * rows_local)
    )
    q_end = pair_width
    k_end = q_end + HEAD_DIM
    v_end = k_end + sub_width
    angles = positions.astype(jnp.float32)[:, None] * jnp.exp(
        jnp.arange(half_rot, dtype=jnp.float32) * (-2.0 * math.log(10000.0) / ROT)
    )[None, :]
    cosine = jnp.cos(angles)
    sine_part = jnp.sin(angles)
    for layer_index in range(LAYERS):
        normed = layer_norm(hidden_state, ln_gain[layer_index], ln_bias[layer_index]).astype(
            jnp.bfloat16
        )
        local = jnp.einsum(
            "rc,kc->rk", normed, w_mine[layer_index], preferred_element_type=jnp.float32
        )
        q_pair = local[:, :q_end]
        low_half = q_pair[:, :half_rot]
        high_half = q_pair[:, half_rot:]
        q_rot = jnp.concatenate(
            [low_half * cosine - high_half * sine_part, high_half * cosine + low_half * sine_part],
            axis=1,
        )
        q_pair = jnp.where(my_piece < 2, q_rot, q_pair)
        q_piece = lax.dynamic_slice_in_dim(q_pair, (my_piece % 2) * sub_width, sub_width, 1)
        q_piece = q_piece.astype(jnp.bfloat16).T
        k_h = rotary(local[:, None, q_end:k_end], positions)[:, 0].astype(jnp.bfloat16)
        v_h = local[:, k_end:v_end].astype(jnp.bfloat16)
        pre_act = local[:, v_end:]
        pre_act = (
            pre_act
            + lax.dynamic_slice_in_dim(b_fc1[layer_index], seq_index * unit_count, unit_count, 0)[
                None, :
            ]
        )
        activated = jax.nn.gelu(pre_act, approximate=True).astype(jnp.bfloat16)
        q_all = all_to_all(jnp.broadcast_to(q_piece[None], (seq_count,) + q_piece.shape), False, tp_count)
        queries = (
            q_all.reshape(heads_local, pieces, sub_width, rows)
            .transpose(3, 0, 1, 2)
            .reshape(rows, heads_local, HEAD_DIM)
        )
        per_block = 128 // HEAD_DIM
        same_half = (
            jnp.arange(per_block, dtype=jnp.int32)[:, None]
            == jnp.arange(per_block, dtype=jnp.int32)[None, :]
        )
        q_pairs = queries.reshape(rows, heads_local // per_block, per_block, HEAD_DIM).transpose(1, 2, 0, 3)
        q_pad = jnp.where(
            same_half[None, :, None, :, None], q_pairs[:, :, :, None, :], jnp.zeros((), jnp.bfloat16)
        ).reshape(heads_local, rows, 128)
        out_pad, max_pad, sum_pad = cache_attention(
            q_pad, k_cache, v_cache, mask_f, layer_index, score_scale
        )
        part_out = jnp.sum(
            jnp.where(
                same_half[None, :, None, :, None],
                out_pad.reshape(heads_local // per_block, per_block, rows, per_block, HEAD_DIM),
                0.0,
            ),
            axis=3,
        ).reshape(heads_local, rows, HEAD_DIM)
        part_max = max_pad[:, :, 0]
        part_sum = sum_pad[:, :, 0]
        out_pieces = (
            part_out.reshape(heads_local, rows, pieces, sub_width)
            .transpose(0, 2, 3, 1)
            .reshape(heads_local * pieces, sub_width, rows)
        )
        max_rows = jnp.repeat(part_max, pieces, axis=0)[:, None, :]
        sum_rows = jnp.repeat(part_sum, pieces, axis=0)[:, None, :]
        pad_rows = jnp.zeros((heads_local * pieces, 6, rows), jnp.float32)
        stats = jnp.concatenate([max_rows, sum_rows, pad_rows], axis=1)
        got_out, got_stats = all_to_all_pair(out_pieces.astype(jnp.bfloat16), stats, False, tp_count)
        got_out = got_out.astype(jnp.float32)
        got_max = got_stats[:, 0, :]
        got_sum = got_stats[:, 1, :]

        q_h = lax.dynamic_index_in_dim(queries, my_head, 1, keepdims=False)
        q_h = q_h.reshape(requests, new_tokens, HEAD_DIM)
        k_h = k_h.reshape(requests, new_tokens, HEAD_DIM)
        v_h = v_h.reshape(requests, new_tokens, sub_width)
        fresh_scores = (
            jnp.einsum("rtd,rud->rtu", q_h, k_h, preferred_element_type=jnp.float32) * score_scale
        )
        fresh_scores = jnp.where(causal[None], fresh_scores, very_negative)
        fresh_max = jnp.max(fresh_scores, axis=2)
        fresh_weights = jnp.where(causal[None], jnp.exp(fresh_scores - fresh_max[..., None]), 0.0)
        fresh_sum = jnp.sum(fresh_weights, axis=2)
        fresh_out = jnp.einsum(
            "rtu,rud->rtd",
            fresh_weights.astype(jnp.bfloat16),
            v_h,
            preferred_element_type=jnp.float32,
        )
        fresh_max = fresh_max.reshape(rows)
        fresh_sum = fresh_sum.reshape(rows)
        fresh_out = fresh_out.reshape(rows, sub_width)

        top = jnp.maximum(jnp.max(got_max, axis=0), fresh_max)
        scale_cache = jnp.exp(got_max - top[None, :])
        scale_fresh = jnp.exp(fresh_max - top)
        denom = jnp.sum(got_sum * scale_cache, axis=0) + fresh_sum * scale_fresh
        numer = jnp.sum(got_out * scale_cache[:, None, :], axis=0).T + fresh_out * scale_fresh[:, None]
        my_cols = (numer / denom[:, None]).astype(jnp.bfloat16)

        update = jnp.dot(my_cols, w_out[layer_index], preferred_element_type=jnp.float32)
        update = update + jnp.dot(activated, w_fc2[layer_index], preferred_element_type=jnp.float32)
        update = allreduce_chip(
            update.astype(jnp.bfloat16).reshape(2, all_count // 2, -1, 128), tp_count
        )
        hidden_state = hidden_state + update.reshape(rows, width).astype(jnp.float32)
    return hidden_state.reshape(requests, new_tokens, width)


def solution(mesh):
    in_specs = (
        P(),
        P(("seq", "tp"), None),
        P(),
        P(),
        P(),
        P("seq", None),
        P(None, "seq", "tp"),
        P(None, "seq", "tp"),
        P(),
        P(),
        P(None, "seq", None, "tp"),
        P(None, "seq", "tp"),
        P(None, "tp"),
        P(None, ("tp", "seq"), None),
        P(None, ("tp", "seq"), None),
    )
    out_specs = P()
    return jax.shard_map(
        per_device, mesh=mesh, in_specs=in_specs, out_specs=out_specs, check_vma=False
    )
```

```python
import functools
import math

import jax
import numpy as np
import jax.numpy as jnp
from jax import lax
from jax.experimental import pallas as pl
from jax.experimental.pallas import tpu as pltpu
from jax.sharding import PartitionSpec as P

HEADS = 32
HEAD_DIM = 64
ROT = 32
LAYERS = 2
BLOCK = 128
SPAN = 512
MESH_IDS = pl.DeviceIdType.MESH

very_negative = -1e30


def layer_norm(values, gain_row, bias_row):
    average = jnp.mean(values, axis=-1, keepdims=True)
    centred = values - average
    variance = jnp.mean(centred * centred, axis=-1, keepdims=True)
    return centred * lax.rsqrt(variance + 1e-05) * gain_row + bias_row


def rotary(values, positions):
    half_width = ROT // 2
    frequency = jnp.exp(
        jnp.arange(half_width, dtype=jnp.float32) * (-2.0 * math.log(10000.0) / ROT)
    )
    angles = positions.astype(jnp.float32)[:, None] * frequency[None, :]
    cosine = jnp.cos(angles)[:, None, :]
    sine_part = jnp.sin(angles)[:, None, :]
    low_half = values[..., :half_width]
    high_half = values[..., half_width:ROT]
    return jnp.concatenate(
        [
            low_half * cosine - high_half * sine_part,
            high_half * cosine + low_half * sine_part,
            values[..., ROT:],
        ],
        axis=-1,
    )


def _group_ids(whole, tp_count):
    seq_index = lax.axis_index("seq")
    tp_index = lax.axis_index("tp")
    if whole:
        me = seq_index * tp_count + tp_index

        def peer(j):
            return (j // tp_count, j % tp_count)

    else:
        me = seq_index

        def peer(j):
            return (j, tp_index)

    return me, peer


_KERNEL_IDS = {}


def _kernel_id(key):
    if key not in _KERNEL_IDS:
        _KERNEL_IDS[key] = len(_KERNEL_IDS)
    return _KERNEL_IDS[key]


def _enter(n, me, peer):
    barrier = pltpu.get_barrier_semaphore()

    def greet(i, carry):
        j = lax.rem(me + i, n)
        pl.semaphore_signal(barrier, 1, device_id=peer(j), device_id_type=MESH_IDS)
        return carry

    lax.fori_loop(1, n, greet, 0)
    pl.semaphore_wait(barrier, n - 1)


def _rcopy(src, dst, send_sem, recv_sem, device):
    return pltpu.make_async_remote_copy(
        src_ref=src,
        dst_ref=dst,
        send_sem=send_sem,
        recv_sem=recv_sem,
        device_id=device,
        device_id_type=MESH_IDS,
    )


def _allreduce_kernel(n, whole, tp_count, x_ref, o_ref, rs_buf, ag_buf, s1, r1, s2, r2):
    me, peer = _group_ids(whole, tp_count)
    _enter(n, me, peer)

    def start_scatter(i, carry):
        j = lax.rem(me + i, n)
        _rcopy(x_ref.at[j], rs_buf.at[me], s1.at[j], r1.at[me], peer(j)).start()
        return carry

    lax.fori_loop(1, n, start_scatter, 0)

    def gather_sum(i, acc):
        j = lax.rem(me + i, n)
        _rcopy(x_ref.at[j], rs_buf.at[j], s1.at[j], r1.at[j], peer(j)).wait_recv()
        return acc + rs_buf[j].astype(jnp.float32)

    total = lax.fori_loop(1, n, gather_sum, x_ref[me].astype(jnp.float32))
    ag_buf[me] = total.astype(ag_buf.dtype)

    def start_gather(i, carry):
        j = lax.rem(me + i, n)
        _rcopy(ag_buf.at[me], ag_buf.at[me], s2.at[j], r2.at[me], peer(j)).start()
        return carry

    lax.fori_loop(1, n, start_gather, 0)

    def finish(i, carry):
        j = lax.rem(me + i, n)
        _rcopy(ag_buf.at[j], ag_buf.at[j], s2.at[j], r2.at[j], peer(j)).wait_recv()
        _rcopy(x_ref.at[j], rs_buf.at[me], s1.at[j], r1.at[me], peer(j)).wait_send()
        _rcopy(ag_buf.at[me], ag_buf.at[me], s2.at[j], r2.at[me], peer(j)).wait_send()
        return carry

    lax.fori_loop(1, n, finish, 0)
    o_ref[...] = ag_buf[...]


def allreduce(x, whole, tp_count):
    n = x.shape[0]
    return pl.pallas_call(
        functools.partial(_allreduce_kernel, n, whole, tp_count),
        out_shape=jax.ShapeDtypeStruct(x.shape, x.dtype),
        in_specs=[pl.BlockSpec(memory_space=pltpu.VMEM)],
        out_specs=pl.BlockSpec(memory_space=pltpu.VMEM),
        scratch_shapes=[
            pltpu.VMEM(x.shape, x.dtype),
            pltpu.VMEM(x.shape, x.dtype),
            pltpu.SemaphoreType.DMA((n,)),
            pltpu.SemaphoreType.DMA((n,)),
            pltpu.SemaphoreType.DMA((n,)),
            pltpu.SemaphoreType.DMA((n,)),
        ],
        compiler_params=pltpu.CompilerParams(
            has_side_effects=True,
            collective_id=_kernel_id(("allreduce", whole, x.shape, str(x.dtype))),
        ),
    )(x)


def _allreduce_chip_kernel(tp_count, x_ref, o_ref, pbuf, sbuf, rs_buf, ag_buf, sa, ra, s1, r1, s2, r2, sd, rd):
    seq_index = lax.axis_index("seq")
    tp_index = lax.axis_index("tp")
    n = x_ref.shape[1]
    core = seq_index % 2
    other = 1 - core
    me = (seq_index // 2) * tp_count + tp_index
    partner = (seq_index + 1 - 2 * core, tp_index)

    def peer(j):
        return ((j // tp_count) * 2 + core, j % tp_count)

    barrier = pltpu.get_barrier_semaphore()

    def greet(i, carry):
        j = lax.rem(me + i, n)
        pl.semaphore_signal(barrier, 1, device_id=peer(j), device_id_type=MESH_IDS)
        return carry

    lax.fori_loop(1, n, greet, 0)
    pl.semaphore_signal(barrier, 1, device_id=partner, device_id_type=MESH_IDS)
    pl.semaphore_wait(barrier, n)
    _allreduce_chip_body(tp_count, x_ref, o_ref, pbuf, sbuf, rs_buf, ag_buf, sa, ra, s1, r1, s2, r2, sd, rd)


def _allreduce_chip_body(tp_count, x_ref, o_ref, pbuf, sbuf, rs_buf, ag_buf, sa, ra, s1, r1, s2, r2, sd, rd):
    seq_index = lax.axis_index("seq")
    tp_index = lax.axis_index("tp")
    n = x_ref.shape[1]
    core = seq_index % 2
    other = 1 - core
    me = (seq_index // 2) * tp_count + tp_index
    partner = (seq_index + 1 - 2 * core, tp_index)

    def peer(j):
        return ((j // tp_count) * 2 + core, j % tp_count)

    swap = _rcopy(x_ref.at[other], pbuf, sa, ra, partner)
    swap.start()
    swap.wait_recv()
    sbuf[...] = (x_ref[core].astype(jnp.float32) + pbuf[...].astype(jnp.float32)).astype(sbuf.dtype)

    def start_scatter(i, carry):
        j = lax.rem(me + i, n)
        _rcopy(sbuf.at[j], rs_buf.at[me], s1.at[j], r1.at[me], peer(j)).start()
        return carry

    lax.fori_loop(1, n, start_scatter, 0)

    def gather_sum(i, acc):
        j = lax.rem(me + i, n)
        _rcopy(sbuf.at[j], rs_buf.at[j], s1.at[j], r1.at[j], peer(j)).wait_recv()
        return acc + rs_buf[j].astype(jnp.float32)

    total = lax.fori_loop(1, n, gather_sum, sbuf[me].astype(jnp.float32))
    ag_buf[core, me] = total.astype(ag_buf.dtype)

    def start_gather(i, carry):
        j = lax.rem(me + i, n)
        _rcopy(ag_buf.at[core, me], ag_buf.at[core, me], s2.at[j], r2.at[me], peer(j)).start()
        return carry

    lax.fori_loop(1, n, start_gather, 0)

    def finish(i, carry):
        j = lax.rem(me + i, n)
        _rcopy(ag_buf.at[core, j], ag_buf.at[core, j], s2.at[j], r2.at[j], peer(j)).wait_recv()
        _rcopy(sbuf.at[j], rs_buf.at[me], s1.at[j], r1.at[me], peer(j)).wait_send()
        _rcopy(ag_buf.at[core, me], ag_buf.at[core, me], s2.at[j], r2.at[me], peer(j)).wait_send()
        return carry

    lax.fori_loop(1, n, finish, 0)
    swap.wait_send()
    back = _rcopy(ag_buf.at[core], ag_buf.at[core], sd, rd, partner)
    back.start()
    _rcopy(ag_buf.at[other], ag_buf.at[other], sd, rd, partner).wait_recv()
    back.wait_send()
    o_ref[...] = ag_buf[...]


def allreduce_chip(x, tp_count, sum_dtype=None):
    n = x.shape[1]
    half = x.shape[1:]
    sum_dtype = x.dtype if sum_dtype is None else sum_dtype
    return pl.pallas_call(
        functools.partial(_allreduce_chip_kernel, tp_count),
        out_shape=jax.ShapeDtypeStruct(x.shape, sum_dtype),
        in_specs=[pl.BlockSpec(memory_space=pltpu.VMEM)],
        out_specs=pl.BlockSpec(memory_space=pltpu.VMEM),
        scratch_shapes=[
            pltpu.VMEM(half, x.dtype),
            pltpu.VMEM(half, sum_dtype),
            pltpu.VMEM(half, sum_dtype),
            pltpu.VMEM(x.shape, sum_dtype),
            pltpu.SemaphoreType.DMA(()),
            pltpu.SemaphoreType.DMA(()),
            pltpu.SemaphoreType.DMA((n,)),
            pltpu.SemaphoreType.DMA((n,)),
            pltpu.SemaphoreType.DMA((n,)),
            pltpu.SemaphoreType.DMA((n,)),
            pltpu.SemaphoreType.DMA(()),
            pltpu.SemaphoreType.DMA(()),
        ],
        compiler_params=pltpu.CompilerParams(
            has_side_effects=True,
            collective_id=_kernel_id(("allreduce_chip", x.shape, str(x.dtype), str(sum_dtype))),
        ),
    )(x)


def _opening_kernel(tp_count, x_ref, w_ref, o_ref, wo_ref, pbuf, sbuf, rs_buf, ag_buf, sa, ra, s1, r1, s2, r2, sd, rd, wbuf, ws, wr):
    seq_index = lax.axis_index("seq")
    tp_index = lax.axis_index("tp")
    count = 2 * x_ref.shape[1]
    me_all = seq_index * tp_count + tp_index
    _enter(count, me_all, lambda j: (j // tp_count, j % tp_count))
    n = w_ref.shape[0]

    def start(i, carry):
        j = lax.rem(seq_index + i, n)
        _rcopy(w_ref.at[j], wbuf.at[seq_index], ws.at[j], wr.at[seq_index], (j, tp_index)).start()
        return carry

    lax.fori_loop(1, n, start, 0)
    _allreduce_chip_body(tp_count, x_ref, o_ref, pbuf, sbuf, rs_buf, ag_buf, sa, ra, s1, r1, s2, r2, sd, rd)

    def finish(i, carry):
        j = lax.rem(seq_index + i, n)
        _rcopy(w_ref.at[j], wbuf.at[j], ws.at[j], wr.at[j], (j, tp_index)).wait_recv()
        _rcopy(w_ref.at[j], wbuf.at[seq_index], ws.at[j], wr.at[seq_index], (j, tp_index)).wait_send()
        return carry

    lax.fori_loop(1, n, finish, 0)
    wbuf[seq_index] = w_ref[seq_index]
    wo_ref[...] = wbuf[...]


def opening(x, w, tp_count):
    n = x.shape[1]
    half = x.shape[1:]
    m = w.shape[0]
    return pl.pallas_call(
        functools.partial(_opening_kernel, tp_count),
        out_shape=(jax.ShapeDtypeStruct(x.shape, x.dtype), jax.ShapeDtypeStruct(w.shape, w.dtype)),
        in_specs=[pl.BlockSpec(memory_space=pltpu.VMEM)] * 2,
        out_specs=(pl.BlockSpec(memory_space=pltpu.VMEM), pl.BlockSpec(memory_space=pltpu.VMEM)),
        scratch_shapes=[
            pltpu.VMEM(half, x.dtype),
            pltpu.VMEM(half, x.dtype),
            pltpu.VMEM(half, x.dtype),
            pltpu.VMEM(x.shape, x.dtype),
            pltpu.SemaphoreType.DMA(()),
            pltpu.SemaphoreType.DMA(()),
            pltpu.SemaphoreType.DMA((n,)),
            pltpu.SemaphoreType.DMA((n,)),
            pltpu.SemaphoreType.DMA((n,)),
            pltpu.SemaphoreType.DMA((n,)),
            pltpu.SemaphoreType.DMA(()),
            pltpu.SemaphoreType.DMA(()),
            pltpu.VMEM(w.shape, w.dtype),
            pltpu.SemaphoreType.DMA((m,)),
            pltpu.SemaphoreType.DMA((m,)),
        ],
        compiler_params=pltpu.CompilerParams(
            has_side_effects=True,
            collective_id=_kernel_id(("opening", x.shape, w.shape)),
        ),
    )(x, w)


def _all_to_all_kernel(n, whole, tp_count, x_ref, o_ref, buf, s1, r1):
    me, peer = _group_ids(whole, tp_count)
    _enter(n, me, peer)

    def start(i, carry):
        j = lax.rem(me + i, n)
        _rcopy(x_ref.at[j], buf.at[me], s1.at[j], r1.at[me], peer(j)).start()
        return carry

    lax.fori_loop(1, n, start, 0)

    def finish(i, carry):
        j = lax.rem(me + i, n)
        _rcopy(x_ref.at[j], buf.at[j], s1.at[j], r1.at[j], peer(j)).wait_recv()
        _rcopy(x_ref.at[j], buf.at[me], s1.at[j], r1.at[me], peer(j)).wait_send()
        return carry

    lax.fori_loop(1, n, finish, 0)
    buf[me] = x_ref[me]
    o_ref[...] = buf[...]


def all_to_all(x, whole, tp_count):
    n = x.shape[0]
    return pl.pallas_call(
        functools.partial(_all_to_all_kernel, n, whole, tp_count),
        out_shape=jax.ShapeDtypeStruct(x.shape, x.dtype),
        in_specs=[pl.BlockSpec(memory_space=pltpu.VMEM)],
        out_specs=pl.BlockSpec(memory_space=pltpu.VMEM),
        scratch_shapes=[
            pltpu.VMEM(x.shape, x.dtype),
            pltpu.SemaphoreType.DMA((n,)),
            pltpu.SemaphoreType.DMA((n,)),
        ],
        compiler_params=pltpu.CompilerParams(
            has_side_effects=True,
            collective_id=_kernel_id(("all_to_all", whole, x.shape, str(x.dtype))),
        ),
    )(x)


def _all_to_all_pair_kernel(n, whole, tp_count, xa_ref, xb_ref, oa_ref, ob_ref, bufa, bufb, sa, ra, sb, rb):
    me, peer = _group_ids(whole, tp_count)
    _enter(n, me, peer)

    def start(i, carry):
        j = lax.rem(me + i, n)
        _rcopy(xa_ref.at[j], bufa.at[me], sa.at[j], ra.at[me], peer(j)).start()
        _rcopy(xb_ref.at[j], bufb.at[me], sb.at[j], rb.at[me], peer(j)).start()
        return carry

    lax.fori_loop(1, n, start, 0)

    def finish(i, carry):
        j = lax.rem(me + i, n)
        _rcopy(xa_ref.at[j], bufa.at[j], sa.at[j], ra.at[j], peer(j)).wait_recv()
        _rcopy(xb_ref.at[j], bufb.at[j], sb.at[j], rb.at[j], peer(j)).wait_recv()
        _rcopy(xa_ref.at[j], bufa.at[me], sa.at[j], ra.at[me], peer(j)).wait_send()
        _rcopy(xb_ref.at[j], bufb.at[me], sb.at[j], rb.at[me], peer(j)).wait_send()
        return carry

    lax.fori_loop(1, n, finish, 0)
    bufa[me] = xa_ref[me]
    bufb[me] = xb_ref[me]
    oa_ref[...] = bufa[...]
    ob_ref[...] = bufb[...]


def all_to_all_pair(xa, xb, whole, tp_count):
    n = xa.shape[0]
    return pl.pallas_call(
        functools.partial(_all_to_all_pair_kernel, n, whole, tp_count),
        out_shape=(jax.ShapeDtypeStruct(xa.shape, xa.dtype), jax.ShapeDtypeStruct(xb.shape, xb.dtype)),
        in_specs=[pl.BlockSpec(memory_space=pltpu.VMEM)] * 2,
        out_specs=(pl.BlockSpec(memory_space=pltpu.VMEM), pl.BlockSpec(memory_space=pltpu.VMEM)),
        scratch_shapes=[
            pltpu.VMEM(xa.shape, xa.dtype),
            pltpu.VMEM(xb.shape, xb.dtype),
            pltpu.SemaphoreType.DMA((n,)),
            pltpu.SemaphoreType.DMA((n,)),
            pltpu.SemaphoreType.DMA((n,)),
            pltpu.SemaphoreType.DMA((n,)),
        ],
        compiler_params=pltpu.CompilerParams(
            has_side_effects=True,
            collective_id=_kernel_id(("all_to_all_pair", whole, xa.shape, xb.shape)),
        ),
    )(xa, xb)


def _gather_chip_kernel(x_ref, o_ref, buf, sx, sp, rr, sa):
    seq_index = lax.axis_index("seq")
    tp_index = lax.axis_index("tp")
    count = buf.shape[0]
    core = seq_index % 2
    mate = seq_index + 1 - 2 * core
    n = count // 2
    me = seq_index // 2

    def peer(m):
        return (m * 2 + core, tp_index)

    barrier = pltpu.get_barrier_semaphore()

    def greet(i, carry):
        m = lax.rem(me + i, n)
        pl.semaphore_signal(barrier, 1, device_id=peer(m), device_id_type=MESH_IDS)
        return carry

    lax.fori_loop(1, n, greet, 0)
    pl.semaphore_signal(barrier, 1, device_id=(mate, tp_index), device_id_type=MESH_IDS)
    pl.semaphore_wait(barrier, n)

    swap = _rcopy(x_ref, buf.at[seq_index], sa, rr.at[seq_index], (mate, tp_index))
    swap.start()

    def start_own(i, carry):
        m = lax.rem(me + i, n)
        _rcopy(x_ref, buf.at[seq_index], sx.at[m], rr.at[seq_index], peer(m)).start()
        return carry

    lax.fori_loop(1, n, start_own, 0)
    _rcopy(x_ref, buf.at[mate], sa, rr.at[mate], (mate, tp_index)).wait_recv()

    def start_mate(i, carry):
        m = lax.rem(me + i, n)
        _rcopy(buf.at[mate], buf.at[mate], sp.at[m], rr.at[mate], peer(m)).start()
        return carry

    lax.fori_loop(1, n, start_mate, 0)

    def finish(i, carry):
        m = lax.rem(me + i, n)
        j = m * 2 + core
        k = m * 2 + 1 - core
        _rcopy(x_ref, buf.at[j], sx.at[m], rr.at[j], peer(m)).wait_recv()
        _rcopy(x_ref, buf.at[k], sp.at[m], rr.at[k], peer(m)).wait_recv()
        _rcopy(x_ref, buf.at[seq_index], sx.at[m], rr.at[seq_index], peer(m)).wait_send()
        _rcopy(buf.at[mate], buf.at[mate], sp.at[m], rr.at[mate], peer(m)).wait_send()
        return carry

    lax.fori_loop(1, n, finish, 0)
    swap.wait_send()
    buf[seq_index] = x_ref[...]
    o_ref[...] = buf[...]


def gather_chip(x, count):
    shape = (count,) + x.shape
    n = count // 2
    return pl.pallas_call(
        _gather_chip_kernel,
        out_shape=jax.ShapeDtypeStruct(shape, x.dtype),
        in_specs=[pl.BlockSpec(memory_space=pltpu.VMEM)],
        out_specs=pl.BlockSpec(memory_space=pltpu.VMEM),
        scratch_shapes=[
            pltpu.VMEM(shape, x.dtype),
            pltpu.SemaphoreType.DMA((n,)),
            pltpu.SemaphoreType.DMA((n,)),
            pltpu.SemaphoreType.DMA((count,)),
            pltpu.SemaphoreType.DMA(()),
        ],
        compiler_params=pltpu.CompilerParams(
            has_side_effects=True,
            collective_id=_kernel_id(("gather_chip", shape, str(x.dtype))),
        ),
    )(x)


def _attention_kernel(scale, q_ref, k_ref, v_ref, mask_ref, o_ref, m_ref, l_ref):
    valid = mask_ref[...] > 0.5
    for half in range(q_ref.shape[0]):
        scores = lax.dot_general(
            q_ref[half], k_ref[...], (((1,), (1,)), ((), ())), preferred_element_type=jnp.float32
        )
        scores = jnp.where(valid, scores * scale, very_negative)
        top = jnp.max(scores, axis=1, keepdims=True)
        weights = jnp.where(valid, jnp.exp(scores - top), 0.0)
        total = jnp.sum(weights, axis=1, keepdims=True)
        o_ref[half] = jnp.dot(
            weights.astype(jnp.bfloat16), v_ref[...], preferred_element_type=jnp.float32
        )
        m_ref[half] = jnp.broadcast_to(top, m_ref.shape[1:])
        l_ref[half] = jnp.broadcast_to(total, l_ref.shape[1:])


def cache_attention(q_pad, k_cache, v_cache, mask, layer_index, scale):
    heads, rows, lanes = q_pad.shape
    slots = k_cache.shape[1]
    per_block = lanes // HEAD_DIM
    out_spec = pl.BlockSpec((per_block, rows, lanes), lambda b: (b, 0, 0))
    return pl.pallas_call(
        functools.partial(_attention_kernel, scale),
        grid=(heads // per_block,),
        out_shape=[jax.ShapeDtypeStruct((heads, rows, lanes), jnp.float32)] * 3,
        in_specs=[
            pl.BlockSpec((per_block, rows, lanes), lambda b: (b, 0, 0)),
            pl.BlockSpec((None, slots, lanes), lambda b: (layer_index, 0, b)),
            pl.BlockSpec((None, slots, lanes), lambda b: (layer_index, 0, b)),
            pl.BlockSpec((rows, slots), lambda b: (0, 0)),
        ],
        out_specs=[out_spec] * 3,
    )(q_pad, k_cache, v_cache, mask)


def per_device(
    token_ids,
    embedding,
    group_of,
    prefix_len,
    tail_len,
    block_map,
    k_cache,
    v_cache,
    ln_gain,
    ln_bias,
    w_qkv,
    w_fc1,
    b_fc1,
    w_out,
    w_fc2,
):
    tp_count = lax.axis_size("tp")
    seq_count = lax.axis_size("seq")
    all_count = tp_count * seq_count
    seq_index = lax.axis_index("seq")
    tp_index = lax.axis_index("tp")
    requests = token_ids.shape[0]
    new_tokens = token_ids.shape[1]
    rows = requests * new_tokens
    groups = prefix_len.shape[0]
    heads_local = HEADS // tp_count
    width = embedding.shape[1]
    score_scale = 1.0 / math.sqrt(HEAD_DIM)

    vocab_rows = embedding.shape[0]
    first_row = (seq_index * tp_count + tp_index) * vocab_rows
    local_ids = token_ids.reshape(-1) - first_row
    inside = (local_ids >= 0) & (local_ids < vocab_rows)
    picked = jnp.take(embedding, jnp.clip(local_ids, 0, vocab_rows - 1), axis=0)
    picked = jnp.where(inside[:, None], picked, jnp.zeros_like(picked))

    group_hit = group_of[:, None] == jnp.arange(groups, dtype=jnp.int32)[None, :]
    shared_len = jnp.sum(jnp.where(group_hit, prefix_len[None, :], 0), axis=1)
    base_positions = shared_len + tail_len
    positions = (base_positions[:, None] + jnp.arange(new_tokens, dtype=jnp.int32)[None, :]).reshape(-1)
    seg_len = jnp.concatenate([prefix_len, tail_len])
    seg_count = seg_len.shape[0]
    blocks_local = block_map.shape[0]
    seg_blk = block_map[:, 0]
    rank_blk = block_map[:, 1]
    seg_hit = seg_blk[:, None] == jnp.arange(seg_count, dtype=jnp.int32)[None, :]
    len_blk = jnp.sum(jnp.where(seg_hit, seg_len[None, :], 0), axis=1)
    slot_positions = rank_blk[:, None] * BLOCK + jnp.arange(BLOCK, dtype=jnp.int32)[None, :]
    live_slot = ((seg_blk[:, None] >= 0) & (slot_positions < len_blk[:, None])).reshape(-1)
    seg_slot = jnp.broadcast_to(seg_blk[:, None], (blocks_local, BLOCK)).reshape(-1)
    own_tail = seg_slot[None, :] == (groups + jnp.arange(requests, dtype=jnp.int32))[:, None]
    own_prompt = seg_slot[None, :] == group_of[:, None]
    allowed = (own_tail | own_prompt) & live_slot[None, :]
    allowed = jnp.repeat(allowed, new_tokens, axis=0)
    mask_f = allowed.astype(jnp.float32)

    rows_local = w_qkv.shape[1]
    unit_count = w_fc2.shape[1]
    sub_width = w_out.shape[1]
    pieces = HEAD_DIM // sub_width
    my_head = seq_index // pieces
    my_piece = seq_index % pieces
    causal = (
        jnp.arange(new_tokens, dtype=jnp.int32)[None, :]
        <= jnp.arange(new_tokens, dtype=jnp.int32)[:, None]
    )

    half_rot = ROT // 2
    pair_width = 2 * sub_width
    qkv_t = w_qkv.transpose(2, 3, 0, 1).reshape(3, heads_local, HEAD_DIM, LAYERS * rows_local)
    q_t = qkv_t[0].reshape(heads_local, 1, HEAD_DIM // pair_width, 1, pair_width, LAYERS * rows_local)
    q_t = jnp.broadcast_to(
        q_t, (heads_local, 1, HEAD_DIM // pair_width, pieces // 2, pair_width, LAYERS * rows_local)
    )
    k_t = jnp.broadcast_to(
        qkv_t[1][:, None], (heads_local, pieces, HEAD_DIM, LAYERS * rows_local)
    )
    v_t = qkv_t[2].reshape(seq_count, sub_width, LAYERS * rows_local)
    f_t = w_fc1.transpose(2, 0, 1).reshape(seq_count, unit_count, LAYERS * rows_local)
    message = jnp.concatenate(
        [
            q_t.reshape(seq_count, pair_width, LAYERS * rows_local),
            k_t.reshape(seq_count, HEAD_DIM, LAYERS * rows_local),
            v_t,
            f_t,
        ],
        axis=1,
    )
    cols_mine = message.shape[1]
    start_states, got_w = opening(
        picked.reshape(2, all_count // 2, -1, 128),
        message,
        tp_count,
    )
    hidden_state = start_states.reshape(rows, width).astype(jnp.float32)
    w_mine = (
        got_w.reshape(seq_count, cols_mine, LAYERS, rows_local)
        .transpose(2, 1, 0, 3)
        .reshape(LAYERS, cols_mine, seq_count * rows_local)
    )
    q_end = pair_width
    k_end = q_end + HEAD_DIM
    v_end = k_end + sub_width
    angles = positions.astype(jnp.float32)[:, None] * jnp.exp(
        jnp.arange(half_rot, dtype=jnp.float32) * (-2.0 * math.log(10000.0) / ROT)
    )[None, :]
    cosine = jnp.cos(angles)
    sine_part = jnp.sin(angles)
    for layer_index in range(LAYERS):
        normed = layer_norm(hidden_state, ln_gain[layer_index], ln_bias[layer_index]).astype(
            jnp.bfloat16
        )
        local = jnp.einsum(
            "rc,kc->rk", normed, w_mine[layer_index], preferred_element_type=jnp.float32
        )
        q_pair = local[:, :q_end]
        low_half = q_pair[:, :half_rot]
        high_half = q_pair[:, half_rot:]
        q_rot = jnp.concatenate(
            [low_half * cosine - high_half * sine_part, high_half * cosine + low_half * sine_part],
            axis=1,
        )
        q_pair = jnp.where(my_piece < 2, q_rot, q_pair)
        q_piece = lax.dynamic_slice_in_dim(q_pair, (my_piece % 2) * sub_width, sub_width, 1)
        q_piece = q_piece.astype(jnp.bfloat16).T
        k_h = rotary(local[:, None, q_end:k_end], positions)[:, 0].astype(jnp.bfloat16)
        v_h = local[:, k_end:v_end].astype(jnp.bfloat16)
        pre_act = local[:, v_end:]
        pre_act = (
            pre_act
            + lax.dynamic_slice_in_dim(b_fc1[layer_index], seq_index * unit_count, unit_count, 0)[
                None, :
            ]
        )
        activated = jax.nn.gelu(pre_act, approximate=True).astype(jnp.bfloat16)
        q_all = gather_chip(q_piece, seq_count)
        queries = (
            q_all.reshape(heads_local, pieces, sub_width, rows)
            .transpose(3, 0, 1, 2)
            .reshape(rows, heads_local, HEAD_DIM)
        )
        per_block = 128 // HEAD_DIM
        same_half = (
            jnp.arange(per_block, dtype=jnp.int32)[:, None]
            == jnp.arange(per_block, dtype=jnp.int32)[None, :]
        )
        q_pairs = queries.reshape(rows, heads_local // per_block, per_block, HEAD_DIM).transpose(1, 2, 0, 3)
        q_pad = jnp.where(
            same_half[None, :, None, :, None], q_pairs[:, :, :, None, :], jnp.zeros((), jnp.bfloat16)
        ).reshape(heads_local, rows, 128)
        out_pad, max_pad, sum_pad = cache_attention(
            q_pad, k_cache, v_cache, mask_f, layer_index, score_scale
        )
        part_out = jnp.sum(
            jnp.where(
                same_half[None, :, None, :, None],
                out_pad.reshape(heads_local // per_block, per_block, rows, per_block, HEAD_DIM),
                0.0,
            ),
            axis=3,
        ).reshape(heads_local, rows, HEAD_DIM)
        part_max = max_pad[:, :, 0]
        part_sum = sum_pad[:, :, 0]
        out_pieces = (
            part_out.reshape(heads_local, rows, pieces, sub_width)
            .transpose(0, 2, 3, 1)
            .reshape(heads_local * pieces, sub_width, rows)
        )
        max_rows = jnp.repeat(part_max, pieces, axis=0)[:, None, :]
        sum_rows = jnp.repeat(part_sum, pieces, axis=0)[:, None, :]
        pad_rows = jnp.zeros((heads_local * pieces, 6, rows), jnp.float32)
        stats = jnp.concatenate([max_rows, sum_rows, pad_rows], axis=1)
        got_out, got_stats = all_to_all_pair(out_pieces.astype(jnp.bfloat16), stats, False, tp_count)
        got_out = got_out.astype(jnp.float32)
        got_max = got_stats[:, 0, :]
        got_sum = got_stats[:, 1, :]

        q_h = lax.dynamic_index_in_dim(queries, my_head, 1, keepdims=False)
        q_h = q_h.reshape(requests, new_tokens, HEAD_DIM)
        k_h = k_h.reshape(requests, new_tokens, HEAD_DIM)
        v_h = v_h.reshape(requests, new_tokens, sub_width)
        fresh_scores = (
            jnp.einsum("rtd,rud->rtu", q_h, k_h, preferred_element_type=jnp.float32) * score_scale
        )
        fresh_scores = jnp.where(causal[None], fresh_scores, very_negative)
        fresh_max = jnp.max(fresh_scores, axis=2)
        fresh_weights = jnp.where(causal[None], jnp.exp(fresh_scores - fresh_max[..., None]), 0.0)
        fresh_sum = jnp.sum(fresh_weights, axis=2)
        fresh_out = jnp.einsum(
            "rtu,rud->rtd",
            fresh_weights.astype(jnp.bfloat16),
            v_h,
            preferred_element_type=jnp.float32,
        )
        fresh_max = fresh_max.reshape(rows)
        fresh_sum = fresh_sum.reshape(rows)
        fresh_out = fresh_out.reshape(rows, sub_width)

        top = jnp.maximum(jnp.max(got_max, axis=0), fresh_max)
        scale_cache = jnp.exp(got_max - top[None, :])
        scale_fresh = jnp.exp(fresh_max - top)
        denom = jnp.sum(got_sum * scale_cache, axis=0) + fresh_sum * scale_fresh
        numer = jnp.sum(got_out * scale_cache[:, None, :], axis=0).T + fresh_out * scale_fresh[:, None]
        my_cols = (numer / denom[:, None]).astype(jnp.bfloat16)

        update = jnp.dot(my_cols, w_out[layer_index], preferred_element_type=jnp.float32)
        update = update + jnp.dot(activated, w_fc2[layer_index], preferred_element_type=jnp.float32)
        update = allreduce_chip(
            update.astype(jnp.bfloat16).reshape(2, all_count // 2, -1, 128), tp_count
        )
        hidden_state = hidden_state + update.reshape(rows, width).astype(jnp.float32)
    return hidden_state.reshape(requests, new_tokens, width)


def solution(mesh):
    in_specs = (
        P(),
        P(("seq", "tp"), None),
        P(),
        P(),
        P(),
        P("seq", None),
        P(None, "seq", "tp"),
        P(None, "seq", "tp"),
        P(),
        P(),
        P(None, "seq", None, "tp"),
        P(None, "seq", "tp"),
        P(None, "tp"),
        P(None, ("tp", "seq"), None),
        P(None, ("tp", "seq"), None),
    )
    out_specs = P()
    return jax.shard_map(
        per_device, mesh=mesh, in_specs=in_specs, out_specs=out_specs, check_vma=False
    )
```

```python
import functools
import math

import jax
import numpy as np
import jax.numpy as jnp
from jax import lax
from jax.experimental import pallas as pl
from jax.experimental.pallas import tpu as pltpu
from jax.sharding import PartitionSpec as P

HEADS = 32
HEAD_DIM = 64
ROT = 32
LAYERS = 2
BLOCK = 128
SPAN = 512
MESH_IDS = pl.DeviceIdType.MESH

very_negative = -1e30


def layer_norm(values, gain_row, bias_row):
    average = jnp.mean(values, axis=-1, keepdims=True)
    centred = values - average
    variance = jnp.mean(centred * centred, axis=-1, keepdims=True)
    return centred * lax.rsqrt(variance + 1e-05) * gain_row + bias_row


def rotary(values, positions):
    half_width = ROT // 2
    frequency = jnp.exp(
        jnp.arange(half_width, dtype=jnp.float32) * (-2.0 * math.log(10000.0) / ROT)
    )
    angles = positions.astype(jnp.float32)[:, None] * frequency[None, :]
    cosine = jnp.cos(angles)[:, None, :]
    sine_part = jnp.sin(angles)[:, None, :]
    low_half = values[..., :half_width]
    high_half = values[..., half_width:ROT]
    return jnp.concatenate(
        [
            low_half * cosine - high_half * sine_part,
            high_half * cosine + low_half * sine_part,
            values[..., ROT:],
        ],
        axis=-1,
    )


def _group_ids(whole, tp_count):
    seq_index = lax.axis_index("seq")
    tp_index = lax.axis_index("tp")
    if whole:
        me = seq_index * tp_count + tp_index

        def peer(j):
            return (j // tp_count, j % tp_count)

    else:
        me = seq_index

        def peer(j):
            return (j, tp_index)

    return me, peer


_KERNEL_IDS = {}


def _kernel_id(key):
    if key not in _KERNEL_IDS:
        _KERNEL_IDS[key] = len(_KERNEL_IDS)
    return _KERNEL_IDS[key]


def _enter(n, me, peer):
    barrier = pltpu.get_barrier_semaphore()

    def greet(i, carry):
        j = lax.rem(me + i, n)
        pl.semaphore_signal(barrier, 1, device_id=peer(j), device_id_type=MESH_IDS)
        return carry

    lax.fori_loop(1, n, greet, 0)
    pl.semaphore_wait(barrier, n - 1)


def _rcopy(src, dst, send_sem, recv_sem, device):
    return pltpu.make_async_remote_copy(
        src_ref=src,
        dst_ref=dst,
        send_sem=send_sem,
        recv_sem=recv_sem,
        device_id=device,
        device_id_type=MESH_IDS,
    )


def _allreduce_kernel(n, whole, tp_count, x_ref, o_ref, rs_buf, ag_buf, s1, r1, s2, r2):
    me, peer = _group_ids(whole, tp_count)
    _enter(n, me, peer)

    def start_scatter(i, carry):
        j = lax.rem(me + i, n)
        _rcopy(x_ref.at[j], rs_buf.at[me], s1.at[j], r1.at[me], peer(j)).start()
        return carry

    lax.fori_loop(1, n, start_scatter, 0)

    def gather_sum(i, acc):
        j = lax.rem(me + i, n)
        _rcopy(x_ref.at[j], rs_buf.at[j], s1.at[j], r1.at[j], peer(j)).wait_recv()
        return acc + rs_buf[j].astype(jnp.float32)

    total = lax.fori_loop(1, n, gather_sum, x_ref[me].astype(jnp.float32))
    ag_buf[me] = total.astype(ag_buf.dtype)

    def start_gather(i, carry):
        j = lax.rem(me + i, n)
        _rcopy(ag_buf.at[me], ag_buf.at[me], s2.at[j], r2.at[me], peer(j)).start()
        return carry

    lax.fori_loop(1, n, start_gather, 0)

    def finish(i, carry):
        j = lax.rem(me + i, n)
        _rcopy(ag_buf.at[j], ag_buf.at[j], s2.at[j], r2.at[j], peer(j)).wait_recv()
        _rcopy(x_ref.at[j], rs_buf.at[me], s1.at[j], r1.at[me], peer(j)).wait_send()
        _rcopy(ag_buf.at[me], ag_buf.at[me], s2.at[j], r2.at[me], peer(j)).wait_send()
        return carry

    lax.fori_loop(1, n, finish, 0)
    o_ref[...] = ag_buf[...]


def allreduce(x, whole, tp_count):
    n = x.shape[0]
    return pl.pallas_call(
        functools.partial(_allreduce_kernel, n, whole, tp_count),
        out_shape=jax.ShapeDtypeStruct(x.shape, x.dtype),
        in_specs=[pl.BlockSpec(memory_space=pltpu.VMEM)],
        out_specs=pl.BlockSpec(memory_space=pltpu.VMEM),
        scratch_shapes=[
            pltpu.VMEM(x.shape, x.dtype),
            pltpu.VMEM(x.shape, x.dtype),
            pltpu.SemaphoreType.DMA((n,)),
            pltpu.SemaphoreType.DMA((n,)),
            pltpu.SemaphoreType.DMA((n,)),
            pltpu.SemaphoreType.DMA((n,)),
        ],
        compiler_params=pltpu.CompilerParams(
            has_side_effects=True,
            collective_id=_kernel_id(("allreduce", whole, x.shape, str(x.dtype))),
        ),
    )(x)


def _allreduce_chip_kernel(tp_count, x_ref, o_ref, pbuf, sbuf, rs_buf, ag_buf, sa, ra, s1, r1, s2, r2, sd, rd):
    seq_index = lax.axis_index("seq")
    tp_index = lax.axis_index("tp")
    n = x_ref.shape[1]
    core = seq_index % 2
    other = 1 - core
    me = (seq_index // 2) * tp_count + tp_index
    partner = (seq_index + 1 - 2 * core, tp_index)

    def peer(j):
        return ((j // tp_count) * 2 + core, j % tp_count)

    barrier = pltpu.get_barrier_semaphore()

    def greet(i, carry):
        j = lax.rem(me + i, n)
        pl.semaphore_signal(barrier, 1, device_id=peer(j), device_id_type=MESH_IDS)
        return carry

    lax.fori_loop(1, n, greet, 0)
    pl.semaphore_signal(barrier, 1, device_id=partner, device_id_type=MESH_IDS)
    pl.semaphore_wait(barrier, n)
    _allreduce_chip_body(tp_count, x_ref, o_ref, pbuf, sbuf, rs_buf, ag_buf, sa, ra, s1, r1, s2, r2, sd, rd)


def _allreduce_chip_body(tp_count, x_ref, o_ref, pbuf, sbuf, rs_buf, ag_buf, sa, ra, s1, r1, s2, r2, sd, rd):
    seq_index = lax.axis_index("seq")
    tp_index = lax.axis_index("tp")
    n = x_ref.shape[1]
    core = seq_index % 2
    other = 1 - core
    me = (seq_index // 2) * tp_count + tp_index
    partner = (seq_index + 1 - 2 * core, tp_index)

    def peer(j):
        return ((j // tp_count) * 2 + core, j % tp_count)

    swap = _rcopy(x_ref.at[other], pbuf, sa, ra, partner)
    swap.start()
    swap.wait_recv()
    sbuf[...] = (x_ref[core].astype(jnp.float32) + pbuf[...].astype(jnp.float32)).astype(sbuf.dtype)

    def start_scatter(i, carry):
        j = lax.rem(me + i, n)
        _rcopy(sbuf.at[j], rs_buf.at[me], s1.at[j], r1.at[me], peer(j)).start()
        return carry

    lax.fori_loop(1, n, start_scatter, 0)

    def gather_sum(i, acc):
        j = lax.rem(me + i, n)
        _rcopy(sbuf.at[j], rs_buf.at[j], s1.at[j], r1.at[j], peer(j)).wait_recv()
        return acc + rs_buf[j].astype(jnp.float32)

    total = lax.fori_loop(1, n, gather_sum, sbuf[me].astype(jnp.float32))
    ag_buf[core, me] = total.astype(ag_buf.dtype)

    def start_gather(i, carry):
        j = lax.rem(me + i, n)
        _rcopy(ag_buf.at[core, me], ag_buf.at[core, me], s2.at[j], r2.at[me], peer(j)).start()
        return carry

    lax.fori_loop(1, n, start_gather, 0)

    def finish(i, carry):
        j = lax.rem(me + i, n)
        _rcopy(ag_buf.at[core, j], ag_buf.at[core, j], s2.at[j], r2.at[j], peer(j)).wait_recv()
        _rcopy(sbuf.at[j], rs_buf.at[me], s1.at[j], r1.at[me], peer(j)).wait_send()
        _rcopy(ag_buf.at[core, me], ag_buf.at[core, me], s2.at[j], r2.at[me], peer(j)).wait_send()
        return carry

    lax.fori_loop(1, n, finish, 0)
    swap.wait_send()
    back = _rcopy(ag_buf.at[core], ag_buf.at[core], sd, rd, partner)
    back.start()
    _rcopy(ag_buf.at[other], ag_buf.at[other], sd, rd, partner).wait_recv()
    back.wait_send()
    o_ref[...] = ag_buf[...]


def allreduce_chip(x, tp_count, sum_dtype=None):
    n = x.shape[1]
    half = x.shape[1:]
    sum_dtype = x.dtype if sum_dtype is None else sum_dtype
    return pl.pallas_call(
        functools.partial(_allreduce_chip_kernel, tp_count),
        out_shape=jax.ShapeDtypeStruct(x.shape, sum_dtype),
        in_specs=[pl.BlockSpec(memory_space=pltpu.VMEM)],
        out_specs=pl.BlockSpec(memory_space=pltpu.VMEM),
        scratch_shapes=[
            pltpu.VMEM(half, x.dtype),
            pltpu.VMEM(half, sum_dtype),
            pltpu.VMEM(half, sum_dtype),
            pltpu.VMEM(x.shape, sum_dtype),
            pltpu.SemaphoreType.DMA(()),
            pltpu.SemaphoreType.DMA(()),
            pltpu.SemaphoreType.DMA((n,)),
            pltpu.SemaphoreType.DMA((n,)),
            pltpu.SemaphoreType.DMA((n,)),
            pltpu.SemaphoreType.DMA((n,)),
            pltpu.SemaphoreType.DMA(()),
            pltpu.SemaphoreType.DMA(()),
        ],
        compiler_params=pltpu.CompilerParams(
            has_side_effects=True,
            collective_id=_kernel_id(("allreduce_chip", x.shape, str(x.dtype), str(sum_dtype))),
        ),
    )(x)


def _opening_kernel(tp_count, x_ref, w_ref, o_ref, wo_ref, pbuf, sbuf, rs_buf, ag_buf, sa, ra, s1, r1, s2, r2, sd, rd, wbuf, ws, wr):
    seq_index = lax.axis_index("seq")
    tp_index = lax.axis_index("tp")
    count = 2 * x_ref.shape[1]
    me_all = seq_index * tp_count + tp_index
    _enter(count, me_all, lambda j: (j // tp_count, j % tp_count))
    n = w_ref.shape[0]

    def start(i, carry):
        j = lax.rem(seq_index + i, n)
        _rcopy(w_ref.at[j], wbuf.at[seq_index], ws.at[j], wr.at[seq_index], (j, tp_index)).start()
        return carry

    lax.fori_loop(1, n, start, 0)
    _allreduce_chip_body(tp_count, x_ref, o_ref, pbuf, sbuf, rs_buf, ag_buf, sa, ra, s1, r1, s2, r2, sd, rd)

    def finish(i, carry):
        j = lax.rem(seq_index + i, n)
        _rcopy(w_ref.at[j], wbuf.at[j], ws.at[j], wr.at[j], (j, tp_index)).wait_recv()
        _rcopy(w_ref.at[j], wbuf.at[seq_index], ws.at[j], wr.at[seq_index], (j, tp_index)).wait_send()
        return carry

    lax.fori_loop(1, n, finish, 0)
    wbuf[seq_index] = w_ref[seq_index]
    wo_ref[...] = wbuf[...]


def opening(x, w, tp_count):
    n = x.shape[1]
    half = x.shape[1:]
    m = w.shape[0]
    return pl.pallas_call(
        functools.partial(_opening_kernel, tp_count),
        out_shape=(jax.ShapeDtypeStruct(x.shape, x.dtype), jax.ShapeDtypeStruct(w.shape, w.dtype)),
        in_specs=[pl.BlockSpec(memory_space=pltpu.VMEM)] * 2,
        out_specs=(pl.BlockSpec(memory_space=pltpu.VMEM), pl.BlockSpec(memory_space=pltpu.VMEM)),
        scratch_shapes=[
            pltpu.VMEM(half, x.dtype),
            pltpu.VMEM(half, x.dtype),
            pltpu.VMEM(half, x.dtype),
            pltpu.VMEM(x.shape, x.dtype),
            pltpu.SemaphoreType.DMA(()),
            pltpu.SemaphoreType.DMA(()),
            pltpu.SemaphoreType.DMA((n,)),
            pltpu.SemaphoreType.DMA((n,)),
            pltpu.SemaphoreType.DMA((n,)),
            pltpu.SemaphoreType.DMA((n,)),
            pltpu.SemaphoreType.DMA(()),
            pltpu.SemaphoreType.DMA(()),
            pltpu.VMEM(w.shape, w.dtype),
            pltpu.SemaphoreType.DMA((m,)),
            pltpu.SemaphoreType.DMA((m,)),
        ],
        compiler_params=pltpu.CompilerParams(
            has_side_effects=True,
            collective_id=_kernel_id(("opening", x.shape, w.shape)),
        ),
    )(x, w)


def _all_to_all_kernel(n, whole, tp_count, x_ref, o_ref, buf, s1, r1):
    me, peer = _group_ids(whole, tp_count)
    _enter(n, me, peer)

    def start(i, carry):
        j = lax.rem(me + i, n)
        _rcopy(x_ref.at[j], buf.at[me], s1.at[j], r1.at[me], peer(j)).start()
        return carry

    lax.fori_loop(1, n, start, 0)

    def finish(i, carry):
        j = lax.rem(me + i, n)
        _rcopy(x_ref.at[j], buf.at[j], s1.at[j], r1.at[j], peer(j)).wait_recv()
        _rcopy(x_ref.at[j], buf.at[me], s1.at[j], r1.at[me], peer(j)).wait_send()
        return carry

    lax.fori_loop(1, n, finish, 0)
    buf[me] = x_ref[me]
    o_ref[...] = buf[...]


def all_to_all(x, whole, tp_count):
    n = x.shape[0]
    return pl.pallas_call(
        functools.partial(_all_to_all_kernel, n, whole, tp_count),
        out_shape=jax.ShapeDtypeStruct(x.shape, x.dtype),
        in_specs=[pl.BlockSpec(memory_space=pltpu.VMEM)],
        out_specs=pl.BlockSpec(memory_space=pltpu.VMEM),
        scratch_shapes=[
            pltpu.VMEM(x.shape, x.dtype),
            pltpu.SemaphoreType.DMA((n,)),
            pltpu.SemaphoreType.DMA((n,)),
        ],
        compiler_params=pltpu.CompilerParams(
            has_side_effects=True,
            collective_id=_kernel_id(("all_to_all", whole, x.shape, str(x.dtype))),
        ),
    )(x)


def _all_to_all_pair_kernel(n, whole, tp_count, xa_ref, xb_ref, oa_ref, ob_ref, bufa, bufb, sa, ra, sb, rb):
    me, peer = _group_ids(whole, tp_count)
    _enter(n, me, peer)

    def start(i, carry):
        j = lax.rem(me + i, n)
        _rcopy(xa_ref.at[j], bufa.at[me], sa.at[j], ra.at[me], peer(j)).start()
        _rcopy(xb_ref.at[j], bufb.at[me], sb.at[j], rb.at[me], peer(j)).start()
        return carry

    lax.fori_loop(1, n, start, 0)

    def finish(i, carry):
        j = lax.rem(me + i, n)
        _rcopy(xa_ref.at[j], bufa.at[j], sa.at[j], ra.at[j], peer(j)).wait_recv()
        _rcopy(xb_ref.at[j], bufb.at[j], sb.at[j], rb.at[j], peer(j)).wait_recv()
        _rcopy(xa_ref.at[j], bufa.at[me], sa.at[j], ra.at[me], peer(j)).wait_send()
        _rcopy(xb_ref.at[j], bufb.at[me], sb.at[j], rb.at[me], peer(j)).wait_send()
        return carry

    lax.fori_loop(1, n, finish, 0)
    bufa[me] = xa_ref[me]
    bufb[me] = xb_ref[me]
    oa_ref[...] = bufa[...]
    ob_ref[...] = bufb[...]


def all_to_all_pair(xa, xb, whole, tp_count):
    n = xa.shape[0]
    return pl.pallas_call(
        functools.partial(_all_to_all_pair_kernel, n, whole, tp_count),
        out_shape=(jax.ShapeDtypeStruct(xa.shape, xa.dtype), jax.ShapeDtypeStruct(xb.shape, xb.dtype)),
        in_specs=[pl.BlockSpec(memory_space=pltpu.VMEM)] * 2,
        out_specs=(pl.BlockSpec(memory_space=pltpu.VMEM), pl.BlockSpec(memory_space=pltpu.VMEM)),
        scratch_shapes=[
            pltpu.VMEM(xa.shape, xa.dtype),
            pltpu.VMEM(xb.shape, xb.dtype),
            pltpu.SemaphoreType.DMA((n,)),
            pltpu.SemaphoreType.DMA((n,)),
            pltpu.SemaphoreType.DMA((n,)),
            pltpu.SemaphoreType.DMA((n,)),
        ],
        compiler_params=pltpu.CompilerParams(
            has_side_effects=True,
            collective_id=_kernel_id(("all_to_all_pair", whole, xa.shape, xb.shape)),
        ),
    )(xa, xb)


def _gather_chip_kernel(x_ref, o_ref, buf, sx, sp, rr, sa):
    seq_index = lax.axis_index("seq")
    tp_index = lax.axis_index("tp")
    count = buf.shape[0]
    core = seq_index % 2
    mate = seq_index + 1 - 2 * core
    n = count // 2
    me = seq_index // 2

    def peer(m):
        return (m * 2 + core, tp_index)

    barrier = pltpu.get_barrier_semaphore()

    def greet(i, carry):
        m = lax.rem(me + i, n)
        pl.semaphore_signal(barrier, 1, device_id=peer(m), device_id_type=MESH_IDS)
        return carry

    lax.fori_loop(1, n, greet, 0)
    pl.semaphore_signal(barrier, 1, device_id=(mate, tp_index), device_id_type=MESH_IDS)
    pl.semaphore_wait(barrier, n)

    swap = _rcopy(x_ref, buf.at[seq_index], sa, rr.at[seq_index], (mate, tp_index))
    swap.start()

    def start_own(i, carry):
        m = lax.rem(me + i, n)
        _rcopy(x_ref, buf.at[seq_index], sx.at[m], rr.at[seq_index], peer(m)).start()
        return carry

    lax.fori_loop(1, n, start_own, 0)
    _rcopy(x_ref, buf.at[mate], sa, rr.at[mate], (mate, tp_index)).wait_recv()

    def start_mate(i, carry):
        m = lax.rem(me + i, n)
        _rcopy(buf.at[mate], buf.at[mate], sp.at[m], rr.at[mate], peer(m)).start()
        return carry

    lax.fori_loop(1, n, start_mate, 0)

    def finish(i, carry):
        m = lax.rem(me + i, n)
        j = m * 2 + core
        k = m * 2 + 1 - core
        _rcopy(x_ref, buf.at[j], sx.at[m], rr.at[j], peer(m)).wait_recv()
        _rcopy(x_ref, buf.at[k], sp.at[m], rr.at[k], peer(m)).wait_recv()
        _rcopy(x_ref, buf.at[seq_index], sx.at[m], rr.at[seq_index], peer(m)).wait_send()
        _rcopy(buf.at[mate], buf.at[mate], sp.at[m], rr.at[mate], peer(m)).wait_send()
        return carry

    lax.fori_loop(1, n, finish, 0)
    swap.wait_send()
    buf[seq_index] = x_ref[...]
    o_ref[...] = buf[...]


def gather_chip(x, count):
    shape = (count,) + x.shape
    n = count // 2
    return pl.pallas_call(
        _gather_chip_kernel,
        out_shape=jax.ShapeDtypeStruct(shape, x.dtype),
        in_specs=[pl.BlockSpec(memory_space=pltpu.VMEM)],
        out_specs=pl.BlockSpec(memory_space=pltpu.VMEM),
        scratch_shapes=[
            pltpu.VMEM(shape, x.dtype),
            pltpu.SemaphoreType.DMA((n,)),
            pltpu.SemaphoreType.DMA((n,)),
            pltpu.SemaphoreType.DMA((count,)),
            pltpu.SemaphoreType.DMA(()),
        ],
        compiler_params=pltpu.CompilerParams(
            has_side_effects=True,
            collective_id=_kernel_id(("gather_chip", shape, str(x.dtype))),
        ),
    )(x)


def _attention_kernel(scale, q_ref, k_ref, v_ref, mask_ref, o_ref, m_ref, l_ref):
    valid = mask_ref[...] > 0.5
    for half in range(q_ref.shape[0]):
        scores = lax.dot_general(
            q_ref[half], k_ref[...], (((1,), (1,)), ((), ())), preferred_element_type=jnp.float32
        )
        scores = jnp.where(valid, scores * scale, very_negative)
        top = jnp.max(scores, axis=1, keepdims=True)
        weights = jnp.where(valid, jnp.exp(scores - top), 0.0)
        total = jnp.sum(weights, axis=1, keepdims=True)
        o_ref[half] = jnp.dot(
            weights.astype(jnp.bfloat16), v_ref[...], preferred_element_type=jnp.float32
        )
        m_ref[half] = jnp.broadcast_to(top, m_ref.shape[1:])
        l_ref[half] = jnp.broadcast_to(total, l_ref.shape[1:])


def cache_attention(q_pad, k_cache, v_cache, mask, layer_index, scale):
    heads, rows, lanes = q_pad.shape
    slots = k_cache.shape[1]
    per_block = lanes // HEAD_DIM
    out_spec = pl.BlockSpec((per_block, rows, lanes), lambda b: (b, 0, 0))
    return pl.pallas_call(
        functools.partial(_attention_kernel, scale),
        grid=(heads // per_block,),
        out_shape=[jax.ShapeDtypeStruct((heads, rows, lanes), jnp.float32)] * 3,
        in_specs=[
            pl.BlockSpec((per_block, rows, lanes), lambda b: (b, 0, 0)),
            pl.BlockSpec((None, slots, lanes), lambda b: (layer_index, 0, b)),
            pl.BlockSpec((None, slots, lanes), lambda b: (layer_index, 0, b)),
            pl.BlockSpec((rows, slots), lambda b: (0, 0)),
        ],
        out_specs=[out_spec] * 3,
    )(q_pad, k_cache, v_cache, mask)


def per_device(
    token_ids,
    embedding,
    group_of,
    prefix_len,
    tail_len,
    block_map,
    k_cache,
    v_cache,
    ln_gain,
    ln_bias,
    w_qkv,
    w_fc1,
    b_fc1,
    w_out,
    w_fc2,
):
    tp_count = lax.axis_size("tp")
    seq_count = lax.axis_size("seq")
    all_count = tp_count * seq_count
    seq_index = lax.axis_index("seq")
    tp_index = lax.axis_index("tp")
    requests = token_ids.shape[0]
    new_tokens = token_ids.shape[1]
    rows = requests * new_tokens
    groups = prefix_len.shape[0]
    heads_local = HEADS // tp_count
    width = embedding.shape[1]
    score_scale = 1.0 / math.sqrt(HEAD_DIM)

    vocab_rows = embedding.shape[0]
    first_row = (seq_index * tp_count + tp_index) * vocab_rows
    local_ids = token_ids.reshape(-1) - first_row
    inside = (local_ids >= 0) & (local_ids < vocab_rows)
    picked = jnp.take(embedding, jnp.clip(local_ids, 0, vocab_rows - 1), axis=0)
    picked = jnp.where(inside[:, None], picked, jnp.zeros_like(picked))

    group_hit = group_of[:, None] == jnp.arange(groups, dtype=jnp.int32)[None, :]
    shared_len = jnp.sum(jnp.where(group_hit, prefix_len[None, :], 0), axis=1)
    base_positions = shared_len + tail_len
    positions = (base_positions[:, None] + jnp.arange(new_tokens, dtype=jnp.int32)[None, :]).reshape(-1)
    seg_len = jnp.concatenate([prefix_len, tail_len])
    seg_count = seg_len.shape[0]
    blocks_local = block_map.shape[0]
    seg_blk = block_map[:, 0]
    rank_blk = block_map[:, 1]
    seg_hit = seg_blk[:, None] == jnp.arange(seg_count, dtype=jnp.int32)[None, :]
    len_blk = jnp.sum(jnp.where(seg_hit, seg_len[None, :], 0), axis=1)
    slot_positions = rank_blk[:, None] * BLOCK + jnp.arange(BLOCK, dtype=jnp.int32)[None, :]
    live_slot = ((seg_blk[:, None] >= 0) & (slot_positions < len_blk[:, None])).reshape(-1)
    seg_slot = jnp.broadcast_to(seg_blk[:, None], (blocks_local, BLOCK)).reshape(-1)
    own_tail = seg_slot[None, :] == (groups + jnp.arange(requests, dtype=jnp.int32))[:, None]
    own_prompt = seg_slot[None, :] == group_of[:, None]
    allowed = (own_tail | own_prompt) & live_slot[None, :]
    allowed = jnp.repeat(allowed, new_tokens, axis=0)
    mask_f = allowed.astype(jnp.bfloat16)

    rows_local = w_qkv.shape[1]
    unit_count = w_fc2.shape[1]
    sub_width = w_out.shape[1]
    pieces = HEAD_DIM // sub_width
    my_head = seq_index // pieces
    my_piece = seq_index % pieces
    causal = (
        jnp.arange(new_tokens, dtype=jnp.int32)[None, :]
        <= jnp.arange(new_tokens, dtype=jnp.int32)[:, None]
    )

    half_rot = ROT // 2
    pair_width = 2 * sub_width
    qkv_t = w_qkv.transpose(2, 3, 0, 1).reshape(3, heads_local, HEAD_DIM, LAYERS * rows_local)
    q_t = qkv_t[0].reshape(heads_local, 1, HEAD_DIM // pair_width, 1, pair_width, LAYERS * rows_local)
    q_t = jnp.broadcast_to(
        q_t, (heads_local, 1, HEAD_DIM // pair_width, pieces // 2, pair_width, LAYERS * rows_local)
    )
    k_t = jnp.broadcast_to(
        qkv_t[1][:, None], (heads_local, pieces, HEAD_DIM, LAYERS * rows_local)
    )
    v_t = qkv_t[2].reshape(seq_count, sub_width, LAYERS * rows_local)
    f_t = w_fc1.transpose(2, 0, 1).reshape(seq_count, unit_count, LAYERS * rows_local)
    message = jnp.concatenate(
        [
            q_t.reshape(seq_count, pair_width, LAYERS * rows_local),
            k_t.reshape(seq_count, HEAD_DIM, LAYERS * rows_local),
            v_t,
            f_t,
        ],
        axis=1,
    )
    cols_mine = message.shape[1]
    start_states, got_w = opening(
        picked.reshape(2, all_count // 2, -1, 128),
        message,
        tp_count,
    )
    hidden_state = start_states.reshape(rows, width).astype(jnp.float32)
    w_mine = (
        got_w.reshape(seq_count, cols_mine, LAYERS, rows_local)
        .transpose(2, 1, 0, 3)
        .reshape(LAYERS, cols_mine, seq_count * rows_local)
    )
    q_end = pair_width
    k_end = q_end + HEAD_DIM
    v_end = k_end + sub_width
    angles = positions.astype(jnp.float32)[:, None] * jnp.exp(
        jnp.arange(half_rot, dtype=jnp.float32) * (-2.0 * math.log(10000.0) / ROT)
    )[None, :]
    cosine = jnp.cos(angles)
    sine_part = jnp.sin(angles)
    for layer_index in range(LAYERS):
        normed = layer_norm(hidden_state, ln_gain[layer_index], ln_bias[layer_index]).astype(
            jnp.bfloat16
        )
        local = jnp.einsum(
            "rc,kc->rk", normed, w_mine[layer_index], preferred_element_type=jnp.float32
        )
        q_pair = local[:, :q_end]
        low_half = q_pair[:, :half_rot]
        high_half = q_pair[:, half_rot:]
        q_rot = jnp.concatenate(
            [low_half * cosine - high_half * sine_part, high_half * cosine + low_half * sine_part],
            axis=1,
        )
        q_pair = jnp.where(my_piece < 2, q_rot, q_pair)
        q_piece = lax.dynamic_slice_in_dim(q_pair, (my_piece % 2) * sub_width, sub_width, 1)
        q_piece = q_piece.astype(jnp.bfloat16).T
        k_h = rotary(local[:, None, q_end:k_end], positions)[:, 0].astype(jnp.bfloat16)
        v_h = local[:, k_end:v_end].astype(jnp.bfloat16)
        pre_act = local[:, v_end:]
        pre_act = (
            pre_act
            + lax.dynamic_slice_in_dim(b_fc1[layer_index], seq_index * unit_count, unit_count, 0)[
                None, :
            ]
        )
        activated = jax.nn.gelu(pre_act, approximate=True).astype(jnp.bfloat16)
        q_all = gather_chip(q_piece, seq_count)
        queries = (
            q_all.reshape(heads_local, pieces, sub_width, rows)
            .transpose(3, 0, 1, 2)
            .reshape(rows, heads_local, HEAD_DIM)
        )
        per_block = 128 // HEAD_DIM
        same_half = (
            jnp.arange(per_block, dtype=jnp.int32)[:, None]
            == jnp.arange(per_block, dtype=jnp.int32)[None, :]
        )
        q_pairs = queries.reshape(rows, heads_local // per_block, per_block, HEAD_DIM).transpose(1, 2, 0, 3)
        q_pad = jnp.where(
            same_half[None, :, None, :, None], q_pairs[:, :, :, None, :], jnp.zeros((), jnp.bfloat16)
        ).reshape(heads_local, rows, 128)
        out_pad, max_pad, sum_pad = cache_attention(
            q_pad, k_cache, v_cache, mask_f, layer_index, score_scale
        )
        part_out = jnp.sum(
            jnp.where(
                same_half[None, :, None, :, None],
                out_pad.reshape(heads_local // per_block, per_block, rows, per_block, HEAD_DIM),
                0.0,
            ),
            axis=3,
        ).reshape(heads_local, rows, HEAD_DIM)
        part_max = max_pad[:, :, 0]
        part_sum = sum_pad[:, :, 0]
        out_pieces = (
            part_out.reshape(heads_local, rows, pieces, sub_width)
            .transpose(0, 2, 3, 1)
            .reshape(heads_local * pieces, sub_width, rows)
        )
        max_rows = jnp.repeat(part_max, pieces, axis=0)[:, None, :]
        sum_rows = jnp.repeat(part_sum, pieces, axis=0)[:, None, :]
        pad_rows = jnp.zeros((heads_local * pieces, 6, rows), jnp.float32)
        stats = jnp.concatenate([max_rows, sum_rows, pad_rows], axis=1)
        got_out, got_stats = all_to_all_pair(out_pieces.astype(jnp.bfloat16), stats, False, tp_count)
        got_out = got_out.astype(jnp.float32)
        got_max = got_stats[:, 0, :]
        got_sum = got_stats[:, 1, :]

        q_h = lax.dynamic_index_in_dim(queries, my_head, 1, keepdims=False)
        q_h = q_h.reshape(requests, new_tokens, HEAD_DIM)
        k_h = k_h.reshape(requests, new_tokens, HEAD_DIM)
        v_h = v_h.reshape(requests, new_tokens, sub_width)
        fresh_scores = (
            jnp.einsum("rtd,rud->rtu", q_h, k_h, preferred_element_type=jnp.float32) * score_scale
        )
        fresh_scores = jnp.where(causal[None], fresh_scores, very_negative)
        fresh_max = jnp.max(fresh_scores, axis=2)
        fresh_weights = jnp.where(causal[None], jnp.exp(fresh_scores - fresh_max[..., None]), 0.0)
        fresh_sum = jnp.sum(fresh_weights, axis=2)
        fresh_out = jnp.einsum(
            "rtu,rud->rtd",
            fresh_weights.astype(jnp.bfloat16),
            v_h,
            preferred_element_type=jnp.float32,
        )
        fresh_max = fresh_max.reshape(rows)
        fresh_sum = fresh_sum.reshape(rows)
        fresh_out = fresh_out.reshape(rows, sub_width)

        top = jnp.maximum(jnp.max(got_max, axis=0), fresh_max)
        scale_cache = jnp.exp(got_max - top[None, :])
        scale_fresh = jnp.exp(fresh_max - top)
        denom = jnp.sum(got_sum * scale_cache, axis=0) + fresh_sum * scale_fresh
        numer = jnp.sum(got_out * scale_cache[:, None, :], axis=0).T + fresh_out * scale_fresh[:, None]
        my_cols = (numer / denom[:, None]).astype(jnp.bfloat16)

        update = jnp.dot(my_cols, w_out[layer_index], preferred_element_type=jnp.float32)
        update = update + jnp.dot(activated, w_fc2[layer_index], preferred_element_type=jnp.float32)
        update = allreduce_chip(
            update.astype(jnp.bfloat16).reshape(2, all_count // 2, -1, 128), tp_count
        )
        hidden_state = hidden_state + update.reshape(rows, width).astype(jnp.float32)
    return hidden_state.reshape(requests, new_tokens, width)


def solution(mesh):
    in_specs = (
        P(),
        P(("seq", "tp"), None),
        P(),
        P(),
        P(),
        P("seq", None),
        P(None, "seq", "tp"),
        P(None, "seq", "tp"),
        P(),
        P(),
        P(None, "seq", None, "tp"),
        P(None, "seq", "tp"),
        P(None, "tp"),
        P(None, ("tp", "seq"), None),
        P(None, ("tp", "seq"), None),
    )
    out_specs = P()
    return jax.shard_map(
        per_device, mesh=mesh, in_specs=in_specs, out_specs=out_specs, check_vma=False
    )
```

```python
import functools
import math

import jax
import numpy as np
import jax.numpy as jnp
from jax import lax
from jax.experimental import pallas as pl
from jax.experimental.pallas import tpu as pltpu
from jax.sharding import PartitionSpec as P

HEADS = 32
HEAD_DIM = 64
ROT = 32
LAYERS = 2
BLOCK = 128
SPAN = 512
MESH_IDS = pl.DeviceIdType.MESH

very_negative = -1e30


def layer_norm(values, gain_row, bias_row):
    average = jnp.mean(values, axis=-1, keepdims=True)
    centred = values - average
    variance = jnp.mean(centred * centred, axis=-1, keepdims=True)
    return centred * lax.rsqrt(variance + 1e-05) * gain_row + bias_row


def rotary(values, positions):
    half_width = ROT // 2
    frequency = jnp.exp(
        jnp.arange(half_width, dtype=jnp.float32) * (-2.0 * math.log(10000.0) / ROT)
    )
    angles = positions.astype(jnp.float32)[:, None] * frequency[None, :]
    cosine = jnp.cos(angles)[:, None, :]
    sine_part = jnp.sin(angles)[:, None, :]
    low_half = values[..., :half_width]
    high_half = values[..., half_width:ROT]
    return jnp.concatenate(
        [
            low_half * cosine - high_half * sine_part,
            high_half * cosine + low_half * sine_part,
            values[..., ROT:],
        ],
        axis=-1,
    )


def _group_ids(whole, tp_count):
    seq_index = lax.axis_index("seq")
    tp_index = lax.axis_index("tp")
    if whole:
        me = seq_index * tp_count + tp_index

        def peer(j):
            return (j // tp_count, j % tp_count)

    else:
        me = seq_index

        def peer(j):
            return (j, tp_index)

    return me, peer


_KERNEL_IDS = {}


def _kernel_id(key):
    if key not in _KERNEL_IDS:
        _KERNEL_IDS[key] = len(_KERNEL_IDS)
    return _KERNEL_IDS[key]


def _enter(n, me, peer):
    barrier = pltpu.get_barrier_semaphore()

    def greet(i, carry):
        j = lax.rem(me + i, n)
        pl.semaphore_signal(barrier, 1, device_id=peer(j), device_id_type=MESH_IDS)
        return carry

    lax.fori_loop(1, n, greet, 0)
    pl.semaphore_wait(barrier, n - 1)


def _rcopy(src, dst, send_sem, recv_sem, device):
    return pltpu.make_async_remote_copy(
        src_ref=src,
        dst_ref=dst,
        send_sem=send_sem,
        recv_sem=recv_sem,
        device_id=device,
        device_id_type=MESH_IDS,
    )


def _allreduce_kernel(n, whole, tp_count, x_ref, o_ref, rs_buf, ag_buf, s1, r1, s2, r2):
    me, peer = _group_ids(whole, tp_count)
    _enter(n, me, peer)

    def start_scatter(i, carry):
        j = lax.rem(me + i, n)
        _rcopy(x_ref.at[j], rs_buf.at[me], s1.at[j], r1.at[me], peer(j)).start()
        return carry

    lax.fori_loop(1, n, start_scatter, 0)

    def gather_sum(i, acc):
        j = lax.rem(me + i, n)
        _rcopy(x_ref.at[j], rs_buf.at[j], s1.at[j], r1.at[j], peer(j)).wait_recv()
        return acc + rs_buf[j].astype(jnp.float32)

    total = lax.fori_loop(1, n, gather_sum, x_ref[me].astype(jnp.float32))
    ag_buf[me] = total.astype(ag_buf.dtype)

    def start_gather(i, carry):
        j = lax.rem(me + i, n)
        _rcopy(ag_buf.at[me], ag_buf.at[me], s2.at[j], r2.at[me], peer(j)).start()
        return carry

    lax.fori_loop(1, n, start_gather, 0)

    def finish(i, carry):
        j = lax.rem(me + i, n)
        _rcopy(ag_buf.at[j], ag_buf.at[j], s2.at[j], r2.at[j], peer(j)).wait_recv()
        _rcopy(x_ref.at[j], rs_buf.at[me], s1.at[j], r1.at[me], peer(j)).wait_send()
        _rcopy(ag_buf.at[me], ag_buf.at[me], s2.at[j], r2.at[me], peer(j)).wait_send()
        return carry

    lax.fori_loop(1, n, finish, 0)
    o_ref[...] = ag_buf[...]


def allreduce(x, whole, tp_count):
    n = x.shape[0]
    return pl.pallas_call(
        functools.partial(_allreduce_kernel, n, whole, tp_count),
        out_shape=jax.ShapeDtypeStruct(x.shape, x.dtype),
        in_specs=[pl.BlockSpec(memory_space=pltpu.VMEM)],
        out_specs=pl.BlockSpec(memory_space=pltpu.VMEM),
        scratch_shapes=[
            pltpu.VMEM(x.shape, x.dtype),
            pltpu.VMEM(x.shape, x.dtype),
            pltpu.SemaphoreType.DMA((n,)),
            pltpu.SemaphoreType.DMA((n,)),
            pltpu.SemaphoreType.DMA((n,)),
            pltpu.SemaphoreType.DMA((n,)),
        ],
        compiler_params=pltpu.CompilerParams(
            has_side_effects=True,
            collective_id=_kernel_id(("allreduce", whole, x.shape, str(x.dtype))),
        ),
    )(x)


def _allreduce_chip_kernel(tp_count, x_ref, o_ref, pbuf, sbuf, rs_buf, ag_buf, sa, ra, s1, r1, s2, r2, sd, rd):
    seq_index = lax.axis_index("seq")
    tp_index = lax.axis_index("tp")
    n = x_ref.shape[1]
    core = seq_index % 2
    other = 1 - core
    me = (seq_index // 2) * tp_count + tp_index
    partner = (seq_index + 1 - 2 * core, tp_index)

    def peer(j):
        return ((j // tp_count) * 2 + core, j % tp_count)

    barrier = pltpu.get_barrier_semaphore()

    def greet(i, carry):
        j = lax.rem(me + i, n)
        pl.semaphore_signal(barrier, 1, device_id=peer(j), device_id_type=MESH_IDS)
        return carry

    lax.fori_loop(1, n, greet, 0)
    pl.semaphore_signal(barrier, 1, device_id=partner, device_id_type=MESH_IDS)
    pl.semaphore_wait(barrier, n)
    _allreduce_chip_body(tp_count, x_ref, o_ref, pbuf, sbuf, rs_buf, ag_buf, sa, ra, s1, r1, s2, r2, sd, rd)


def _allreduce_chip_body(tp_count, x_ref, o_ref, pbuf, sbuf, rs_buf, ag_buf, sa, ra, s1, r1, s2, r2, sd, rd):
    seq_index = lax.axis_index("seq")
    tp_index = lax.axis_index("tp")
    n = x_ref.shape[1]
    core = seq_index % 2
    other = 1 - core
    me = (seq_index // 2) * tp_count + tp_index
    partner = (seq_index + 1 - 2 * core, tp_index)

    def peer(j):
        return ((j // tp_count) * 2 + core, j % tp_count)

    swap = _rcopy(x_ref.at[other], pbuf, sa, ra, partner)
    swap.start()
    swap.wait_recv()
    sbuf[...] = (x_ref[core].astype(jnp.float32) + pbuf[...].astype(jnp.float32)).astype(sbuf.dtype)

    def start_scatter(i, carry):
        j = lax.rem(me + i, n)
        _rcopy(sbuf.at[j], rs_buf.at[me], s1.at[j], r1.at[me], peer(j)).start()
        return carry

    lax.fori_loop(1, n, start_scatter, 0)

    def gather_sum(i, acc):
        j = lax.rem(me + i, n)
        _rcopy(sbuf.at[j], rs_buf.at[j], s1.at[j], r1.at[j], peer(j)).wait_recv()
        return acc + rs_buf[j].astype(jnp.float32)

    total = lax.fori_loop(1, n, gather_sum, sbuf[me].astype(jnp.float32))
    ag_buf[core, me] = total.astype(ag_buf.dtype)

    def start_gather(i, carry):
        j = lax.rem(me + i, n)
        _rcopy(ag_buf.at[core, me], ag_buf.at[core, me], s2.at[j], r2.at[me], peer(j)).start()
        return carry

    lax.fori_loop(1, n, start_gather, 0)

    def finish(i, carry):
        j = lax.rem(me + i, n)
        _rcopy(ag_buf.at[core, j], ag_buf.at[core, j], s2.at[j], r2.at[j], peer(j)).wait_recv()
        _rcopy(sbuf.at[j], rs_buf.at[me], s1.at[j], r1.at[me], peer(j)).wait_send()
        _rcopy(ag_buf.at[core, me], ag_buf.at[core, me], s2.at[j], r2.at[me], peer(j)).wait_send()
        return carry

    lax.fori_loop(1, n, finish, 0)
    swap.wait_send()
    back = _rcopy(ag_buf.at[core], ag_buf.at[core], sd, rd, partner)
    back.start()
    _rcopy(ag_buf.at[other], ag_buf.at[other], sd, rd, partner).wait_recv()
    back.wait_send()
    o_ref[...] = ag_buf[...]


def allreduce_chip(x, tp_count, sum_dtype=None):
    n = x.shape[1]
    half = x.shape[1:]
    sum_dtype = x.dtype if sum_dtype is None else sum_dtype
    return pl.pallas_call(
        functools.partial(_allreduce_chip_kernel, tp_count),
        out_shape=jax.ShapeDtypeStruct(x.shape, sum_dtype),
        in_specs=[pl.BlockSpec(memory_space=pltpu.VMEM)],
        out_specs=pl.BlockSpec(memory_space=pltpu.VMEM),
        scratch_shapes=[
            pltpu.VMEM(half, x.dtype),
            pltpu.VMEM(half, sum_dtype),
            pltpu.VMEM(half, sum_dtype),
            pltpu.VMEM(x.shape, sum_dtype),
            pltpu.SemaphoreType.DMA(()),
            pltpu.SemaphoreType.DMA(()),
            pltpu.SemaphoreType.DMA((n,)),
            pltpu.SemaphoreType.DMA((n,)),
            pltpu.SemaphoreType.DMA((n,)),
            pltpu.SemaphoreType.DMA((n,)),
            pltpu.SemaphoreType.DMA(()),
            pltpu.SemaphoreType.DMA(()),
        ],
        compiler_params=pltpu.CompilerParams(
            has_side_effects=True,
            collective_id=_kernel_id(("allreduce_chip", x.shape, str(x.dtype), str(sum_dtype))),
        ),
    )(x)


def _opening_kernel(tp_count, x_ref, w_ref, o_ref, wo_ref, pbuf, sbuf, rs_buf, ag_buf, sa, ra, s1, r1, s2, r2, sd, rd, wbuf, ws, wr):
    seq_index = lax.axis_index("seq")
    tp_index = lax.axis_index("tp")
    count = 2 * x_ref.shape[1]
    me_all = seq_index * tp_count + tp_index
    _enter(count, me_all, lambda j: (j // tp_count, j % tp_count))
    n = w_ref.shape[0]

    def start(i, carry):
        j = lax.rem(seq_index + i, n)
        _rcopy(w_ref.at[j], wbuf.at[seq_index], ws.at[j], wr.at[seq_index], (j, tp_index)).start()
        return carry

    lax.fori_loop(1, n, start, 0)
    _allreduce_chip_body(tp_count, x_ref, o_ref, pbuf, sbuf, rs_buf, ag_buf, sa, ra, s1, r1, s2, r2, sd, rd)

    def finish(i, carry):
        j = lax.rem(seq_index + i, n)
        _rcopy(w_ref.at[j], wbuf.at[j], ws.at[j], wr.at[j], (j, tp_index)).wait_recv()
        _rcopy(w_ref.at[j], wbuf.at[seq_index], ws.at[j], wr.at[seq_index], (j, tp_index)).wait_send()
        return carry

    lax.fori_loop(1, n, finish, 0)
    wbuf[seq_index] = w_ref[seq_index]
    wo_ref[...] = wbuf[...]


def opening(x, w, tp_count):
    n = x.shape[1]
    half = x.shape[1:]
    m = w.shape[0]
    return pl.pallas_call(
        functools.partial(_opening_kernel, tp_count),
        out_shape=(jax.ShapeDtypeStruct(x.shape, x.dtype), jax.ShapeDtypeStruct(w.shape, w.dtype)),
        in_specs=[pl.BlockSpec(memory_space=pltpu.VMEM)] * 2,
        out_specs=(pl.BlockSpec(memory_space=pltpu.VMEM), pl.BlockSpec(memory_space=pltpu.VMEM)),
        scratch_shapes=[
            pltpu.VMEM(half, x.dtype),
            pltpu.VMEM(half, x.dtype),
            pltpu.VMEM(half, x.dtype),
            pltpu.VMEM(x.shape, x.dtype),
            pltpu.SemaphoreType.DMA(()),
            pltpu.SemaphoreType.DMA(()),
            pltpu.SemaphoreType.DMA((n,)),
            pltpu.SemaphoreType.DMA((n,)),
            pltpu.SemaphoreType.DMA((n,)),
            pltpu.SemaphoreType.DMA((n,)),
            pltpu.SemaphoreType.DMA(()),
            pltpu.SemaphoreType.DMA(()),
            pltpu.VMEM(w.shape, w.dtype),
            pltpu.SemaphoreType.DMA((m,)),
            pltpu.SemaphoreType.DMA((m,)),
        ],
        compiler_params=pltpu.CompilerParams(
            has_side_effects=True,
            collective_id=_kernel_id(("opening", x.shape, w.shape)),
        ),
    )(x, w)


def _all_to_all_kernel(n, whole, tp_count, x_ref, o_ref, buf, s1, r1):
    me, peer = _group_ids(whole, tp_count)
    _enter(n, me, peer)

    def start(i, carry):
        j = lax.rem(me + i, n)
        _rcopy(x_ref.at[j], buf.at[me], s1.at[j], r1.at[me], peer(j)).start()
        return carry

    lax.fori_loop(1, n, start, 0)

    def finish(i, carry):
        j = lax.rem(me + i, n)
        _rcopy(x_ref.at[j], buf.at[j], s1.at[j], r1.at[j], peer(j)).wait_recv()
        _rcopy(x_ref.at[j], buf.at[me], s1.at[j], r1.at[me], peer(j)).wait_send()
        return carry

    lax.fori_loop(1, n, finish, 0)
    buf[me] = x_ref[me]
    o_ref[...] = buf[...]


def all_to_all(x, whole, tp_count):
    n = x.shape[0]
    return pl.pallas_call(
        functools.partial(_all_to_all_kernel, n, whole, tp_count),
        out_shape=jax.ShapeDtypeStruct(x.shape, x.dtype),
        in_specs=[pl.BlockSpec(memory_space=pltpu.VMEM)],
        out_specs=pl.BlockSpec(memory_space=pltpu.VMEM),
        scratch_shapes=[
            pltpu.VMEM(x.shape, x.dtype),
            pltpu.SemaphoreType.DMA((n,)),
            pltpu.SemaphoreType.DMA((n,)),
        ],
        compiler_params=pltpu.CompilerParams(
            has_side_effects=True,
            collective_id=_kernel_id(("all_to_all", whole, x.shape, str(x.dtype))),
        ),
    )(x)


def _all_to_all_pair_kernel(n, whole, tp_count, xa_ref, xb_ref, oa_ref, ob_ref, bufa, bufb, sa, ra, sb, rb):
    me, peer = _group_ids(whole, tp_count)
    _enter(n, me, peer)

    def start(i, carry):
        j = lax.rem(me + i, n)
        _rcopy(xa_ref.at[j], bufa.at[me], sa.at[j], ra.at[me], peer(j)).start()
        _rcopy(xb_ref.at[j], bufb.at[me], sb.at[j], rb.at[me], peer(j)).start()
        return carry

    lax.fori_loop(1, n, start, 0)

    def finish(i, carry):
        j = lax.rem(me + i, n)
        _rcopy(xa_ref.at[j], bufa.at[j], sa.at[j], ra.at[j], peer(j)).wait_recv()
        _rcopy(xb_ref.at[j], bufb.at[j], sb.at[j], rb.at[j], peer(j)).wait_recv()
        _rcopy(xa_ref.at[j], bufa.at[me], sa.at[j], ra.at[me], peer(j)).wait_send()
        _rcopy(xb_ref.at[j], bufb.at[me], sb.at[j], rb.at[me], peer(j)).wait_send()
        return carry

    lax.fori_loop(1, n, finish, 0)
    bufa[me] = xa_ref[me]
    bufb[me] = xb_ref[me]
    oa_ref[...] = bufa[...]
    ob_ref[...] = bufb[...]


def all_to_all_pair(xa, xb, whole, tp_count):
    n = xa.shape[0]
    return pl.pallas_call(
        functools.partial(_all_to_all_pair_kernel, n, whole, tp_count),
        out_shape=(jax.ShapeDtypeStruct(xa.shape, xa.dtype), jax.ShapeDtypeStruct(xb.shape, xb.dtype)),
        in_specs=[pl.BlockSpec(memory_space=pltpu.VMEM)] * 2,
        out_specs=(pl.BlockSpec(memory_space=pltpu.VMEM), pl.BlockSpec(memory_space=pltpu.VMEM)),
        scratch_shapes=[
            pltpu.VMEM(xa.shape, xa.dtype),
            pltpu.VMEM(xb.shape, xb.dtype),
            pltpu.SemaphoreType.DMA((n,)),
            pltpu.SemaphoreType.DMA((n,)),
            pltpu.SemaphoreType.DMA((n,)),
            pltpu.SemaphoreType.DMA((n,)),
        ],
        compiler_params=pltpu.CompilerParams(
            has_side_effects=True,
            collective_id=_kernel_id(("all_to_all_pair", whole, xa.shape, xb.shape)),
        ),
    )(xa, xb)


def _gather_chip_kernel(x_ref, o_ref, buf, sx, sp, rr, sa):
    seq_index = lax.axis_index("seq")
    tp_index = lax.axis_index("tp")
    count = buf.shape[0]
    core = seq_index % 2
    mate = seq_index + 1 - 2 * core
    n = count // 2
    me = seq_index // 2

    def peer(m):
        return (m * 2 + core, tp_index)

    barrier = pltpu.get_barrier_semaphore()

    def greet(i, carry):
        m = lax.rem(me + i, n)
        pl.semaphore_signal(barrier, 1, device_id=peer(m), device_id_type=MESH_IDS)
        return carry

    lax.fori_loop(1, n, greet, 0)
    pl.semaphore_signal(barrier, 1, device_id=(mate, tp_index), device_id_type=MESH_IDS)
    pl.semaphore_wait(barrier, n)

    swap = _rcopy(x_ref, buf.at[seq_index], sa, rr.at[seq_index], (mate, tp_index))
    swap.start()

    def start_own(i, carry):
        m = lax.rem(me + i, n)
        _rcopy(x_ref, buf.at[seq_index], sx.at[m], rr.at[seq_index], peer(m)).start()
        return carry

    lax.fori_loop(1, n, start_own, 0)
    _rcopy(x_ref, buf.at[mate], sa, rr.at[mate], (mate, tp_index)).wait_recv()

    def start_mate(i, carry):
        m = lax.rem(me + i, n)
        _rcopy(buf.at[mate], buf.at[mate], sp.at[m], rr.at[mate], peer(m)).start()
        return carry

    lax.fori_loop(1, n, start_mate, 0)

    def finish(i, carry):
        m = lax.rem(me + i, n)
        j = m * 2 + core
        k = m * 2 + 1 - core
        _rcopy(x_ref, buf.at[j], sx.at[m], rr.at[j], peer(m)).wait_recv()
        _rcopy(x_ref, buf.at[k], sp.at[m], rr.at[k], peer(m)).wait_recv()
        _rcopy(x_ref, buf.at[seq_index], sx.at[m], rr.at[seq_index], peer(m)).wait_send()
        _rcopy(buf.at[mate], buf.at[mate], sp.at[m], rr.at[mate], peer(m)).wait_send()
        return carry

    lax.fori_loop(1, n, finish, 0)
    swap.wait_send()
    buf[seq_index] = x_ref[...]
    o_ref[...] = buf[...]


def gather_chip(x, count):
    shape = (count,) + x.shape
    n = count // 2
    return pl.pallas_call(
        _gather_chip_kernel,
        out_shape=jax.ShapeDtypeStruct(shape, x.dtype),
        in_specs=[pl.BlockSpec(memory_space=pltpu.VMEM)],
        out_specs=pl.BlockSpec(memory_space=pltpu.VMEM),
        scratch_shapes=[
            pltpu.VMEM(shape, x.dtype),
            pltpu.SemaphoreType.DMA((n,)),
            pltpu.SemaphoreType.DMA((n,)),
            pltpu.SemaphoreType.DMA((count,)),
            pltpu.SemaphoreType.DMA(()),
        ],
        compiler_params=pltpu.CompilerParams(
            has_side_effects=True,
            collective_id=_kernel_id(("gather_chip", shape, str(x.dtype))),
        ),
    )(x)


def _attention_kernel(scale, q_ref, k_ref, v_ref, mask_ref, o_ref, m_ref, l_ref):
    valid = mask_ref[...] > 0.5
    for half in range(q_ref.shape[0]):
        scores = lax.dot_general(
            q_ref[half], k_ref[...], (((1,), (1,)), ((), ())), preferred_element_type=jnp.float32
        )
        scores = jnp.where(valid, scores * scale, very_negative)
        top = jnp.max(scores, axis=1, keepdims=True)
        weights = jnp.where(valid, jnp.exp(scores - top), 0.0)
        total = jnp.sum(weights, axis=1, keepdims=True)
        weighted = jnp.dot(
            weights.astype(jnp.bfloat16), v_ref[...], preferred_element_type=jnp.float32
        )
        o_ref[half] = weighted[:, half * HEAD_DIM : (half + 1) * HEAD_DIM]
        m_ref[half] = jnp.broadcast_to(top, m_ref.shape[1:])
        l_ref[half] = jnp.broadcast_to(total, l_ref.shape[1:])


def cache_attention(q_pad, k_cache, v_cache, mask, layer_index, scale):
    heads, rows, lanes = q_pad.shape
    slots = k_cache.shape[1]
    per_block = lanes // HEAD_DIM
    out_spec = pl.BlockSpec((per_block, rows, lanes), lambda b: (b, 0, 0))
    return pl.pallas_call(
        functools.partial(_attention_kernel, scale),
        grid=(heads // per_block,),
        out_shape=[jax.ShapeDtypeStruct((heads, rows, HEAD_DIM), jnp.float32)]
        + [jax.ShapeDtypeStruct((heads, rows, lanes), jnp.float32)] * 2,
        in_specs=[
            pl.BlockSpec((per_block, rows, lanes), lambda b: (b, 0, 0)),
            pl.BlockSpec((None, slots, lanes), lambda b: (layer_index, 0, b)),
            pl.BlockSpec((None, slots, lanes), lambda b: (layer_index, 0, b)),
            pl.BlockSpec((rows, slots), lambda b: (0, 0)),
        ],
        out_specs=[pl.BlockSpec((per_block, rows, HEAD_DIM), lambda b: (b, 0, 0))] + [out_spec] * 2,
    )(q_pad, k_cache, v_cache, mask)


def per_device(
    token_ids,
    embedding,
    group_of,
    prefix_len,
    tail_len,
    block_map,
    k_cache,
    v_cache,
    ln_gain,
    ln_bias,
    w_qkv,
    w_fc1,
    b_fc1,
    w_out,
    w_fc2,
):
    tp_count = lax.axis_size("tp")
    seq_count = lax.axis_size("seq")
    all_count = tp_count * seq_count
    seq_index = lax.axis_index("seq")
    tp_index = lax.axis_index("tp")
    requests = token_ids.shape[0]
    new_tokens = token_ids.shape[1]
    rows = requests * new_tokens
    groups = prefix_len.shape[0]
    heads_local = HEADS // tp_count
    width = embedding.shape[1]
    score_scale = 1.0 / math.sqrt(HEAD_DIM)

    vocab_rows = embedding.shape[0]
    first_row = (seq_index * tp_count + tp_index) * vocab_rows
    local_ids = token_ids.reshape(-1) - first_row
    inside = (local_ids >= 0) & (local_ids < vocab_rows)
    picked = jnp.take(embedding, jnp.clip(local_ids, 0, vocab_rows - 1), axis=0)
    picked = jnp.where(inside[:, None], picked, jnp.zeros_like(picked))

    group_hit = group_of[:, None] == jnp.arange(groups, dtype=jnp.int32)[None, :]
    shared_len = jnp.sum(jnp.where(group_hit, prefix_len[None, :], 0), axis=1)
    base_positions = shared_len + tail_len
    positions = (base_positions[:, None] + jnp.arange(new_tokens, dtype=jnp.int32)[None, :]).reshape(-1)
    seg_len = jnp.concatenate([prefix_len, tail_len])
    seg_count = seg_len.shape[0]
    blocks_local = block_map.shape[0]
    seg_blk = block_map[:, 0]
    rank_blk = block_map[:, 1]
    seg_hit = seg_blk[:, None] == jnp.arange(seg_count, dtype=jnp.int32)[None, :]
    len_blk = jnp.sum(jnp.where(seg_hit, seg_len[None, :], 0), axis=1)
    slot_positions = rank_blk[:, None] * BLOCK + jnp.arange(BLOCK, dtype=jnp.int32)[None, :]
    live_slot = ((seg_blk[:, None] >= 0) & (slot_positions < len_blk[:, None])).reshape(-1)
    seg_slot = jnp.broadcast_to(seg_blk[:, None], (blocks_local, BLOCK)).reshape(-1)
    own_tail = seg_slot[None, :] == (groups + jnp.arange(requests, dtype=jnp.int32))[:, None]
    own_prompt = seg_slot[None, :] == group_of[:, None]
    allowed = (own_tail | own_prompt) & live_slot[None, :]
    allowed = jnp.repeat(allowed, new_tokens, axis=0)
    mask_f = allowed.astype(jnp.bfloat16)

    rows_local = w_qkv.shape[1]
    unit_count = w_fc2.shape[1]
    sub_width = w_out.shape[1]
    pieces = HEAD_DIM // sub_width
    my_head = seq_index // pieces
    my_piece = seq_index % pieces
    causal = (
        jnp.arange(new_tokens, dtype=jnp.int32)[None, :]
        <= jnp.arange(new_tokens, dtype=jnp.int32)[:, None]
    )

    half_rot = ROT // 2
    pair_width = 2 * sub_width
    qkv_t = w_qkv.transpose(2, 3, 0, 1).reshape(3, heads_local, HEAD_DIM, LAYERS * rows_local)
    q_t = qkv_t[0].reshape(heads_local, 1, HEAD_DIM // pair_width, 1, pair_width, LAYERS * rows_local)
    q_t = jnp.broadcast_to(
        q_t, (heads_local, 1, HEAD_DIM // pair_width, pieces // 2, pair_width, LAYERS * rows_local)
    )
    k_t = jnp.broadcast_to(
        qkv_t[1][:, None], (heads_local, pieces, HEAD_DIM, LAYERS * rows_local)
    )
    v_t = qkv_t[2].reshape(seq_count, sub_width, LAYERS * rows_local)
    f_t = w_fc1.transpose(2, 0, 1).reshape(seq_count, unit_count, LAYERS * rows_local)
    message = jnp.concatenate(
        [
            q_t.reshape(seq_count, pair_width, LAYERS * rows_local),
            k_t.reshape(seq_count, HEAD_DIM, LAYERS * rows_local),
            v_t,
            f_t,
        ],
        axis=1,
    )
    cols_mine = message.shape[1]
    start_states, got_w = opening(
        picked.reshape(2, all_count // 2, -1, 128),
        message,
        tp_count,
    )
    hidden_state = start_states.reshape(rows, width).astype(jnp.float32)
    w_mine = (
        got_w.reshape(seq_count, cols_mine, LAYERS, rows_local)
        .transpose(2, 1, 0, 3)
        .reshape(LAYERS, cols_mine, seq_count * rows_local)
    )
    q_end = pair_width
    k_end = q_end + HEAD_DIM
    v_end = k_end + sub_width
    angles = positions.astype(jnp.float32)[:, None] * jnp.exp(
        jnp.arange(half_rot, dtype=jnp.float32) * (-2.0 * math.log(10000.0) / ROT)
    )[None, :]
    cosine = jnp.cos(angles)
    sine_part = jnp.sin(angles)
    for layer_index in range(LAYERS):
        normed = layer_norm(hidden_state, ln_gain[layer_index], ln_bias[layer_index]).astype(
            jnp.bfloat16
        )
        local = jnp.einsum(
            "rc,kc->rk", normed, w_mine[layer_index], preferred_element_type=jnp.float32
        )
        q_pair = local[:, :q_end]
        low_half = q_pair[:, :half_rot]
        high_half = q_pair[:, half_rot:]
        q_rot = jnp.concatenate(
            [low_half * cosine - high_half * sine_part, high_half * cosine + low_half * sine_part],
            axis=1,
        )
        q_pair = jnp.where(my_piece < 2, q_rot, q_pair)
        q_piece = lax.dynamic_slice_in_dim(q_pair, (my_piece % 2) * sub_width, sub_width, 1)
        q_piece = q_piece.astype(jnp.bfloat16).T
        k_h = rotary(local[:, None, q_end:k_end], positions)[:, 0].astype(jnp.bfloat16)
        v_h = local[:, k_end:v_end].astype(jnp.bfloat16)
        pre_act = local[:, v_end:]
        pre_act = (
            pre_act
            + lax.dynamic_slice_in_dim(b_fc1[layer_index], seq_index * unit_count, unit_count, 0)[
                None, :
            ]
        )
        activated = jax.nn.gelu(pre_act, approximate=True).astype(jnp.bfloat16)
        q_all = gather_chip(q_piece, seq_count)
        queries = (
            q_all.reshape(heads_local, pieces, sub_width, rows)
            .transpose(3, 0, 1, 2)
            .reshape(rows, heads_local, HEAD_DIM)
        )
        per_block = 128 // HEAD_DIM
        same_half = (
            jnp.arange(per_block, dtype=jnp.int32)[:, None]
            == jnp.arange(per_block, dtype=jnp.int32)[None, :]
        )
        q_pairs = queries.reshape(rows, heads_local // per_block, per_block, HEAD_DIM).transpose(1, 2, 0, 3)
        q_pad = jnp.where(
            same_half[None, :, None, :, None], q_pairs[:, :, :, None, :], jnp.zeros((), jnp.bfloat16)
        ).reshape(heads_local, rows, 128)
        out_pad, max_pad, sum_pad = cache_attention(
            q_pad, k_cache, v_cache, mask_f, layer_index, score_scale
        )
        part_out = out_pad
        part_max = max_pad[:, :, 0]
        part_sum = sum_pad[:, :, 0]
        out_pieces = (
            part_out.reshape(heads_local, rows, pieces, sub_width)
            .transpose(0, 2, 3, 1)
            .reshape(heads_local * pieces, sub_width, rows)
        )
        max_rows = jnp.repeat(part_max, pieces, axis=0)[:, None, :]
        sum_rows = jnp.repeat(part_sum, pieces, axis=0)[:, None, :]
        pad_rows = jnp.zeros((heads_local * pieces, 6, rows), jnp.float32)
        stats = jnp.concatenate([max_rows, sum_rows, pad_rows], axis=1)
        got_out, got_stats = all_to_all_pair(out_pieces.astype(jnp.bfloat16), stats, False, tp_count)
        got_out = got_out.astype(jnp.float32)
        got_max = got_stats[:, 0, :]
        got_sum = got_stats[:, 1, :]

        q_h = lax.dynamic_index_in_dim(queries, my_head, 1, keepdims=False)
        q_h = q_h.reshape(requests, new_tokens, HEAD_DIM)
        k_h = k_h.reshape(requests, new_tokens, HEAD_DIM)
        v_h = v_h.reshape(requests, new_tokens, sub_width)
        fresh_scores = (
            jnp.einsum("rtd,rud->rtu", q_h, k_h, preferred_element_type=jnp.float32) * score_scale
        )
        fresh_scores = jnp.where(causal[None], fresh_scores, very_negative)
        fresh_max = jnp.max(fresh_scores, axis=2)
        fresh_weights = jnp.where(causal[None], jnp.exp(fresh_scores - fresh_max[..., None]), 0.0)
        fresh_sum = jnp.sum(fresh_weights, axis=2)
        fresh_out = jnp.einsum(
            "rtu,rud->rtd",
            fresh_weights.astype(jnp.bfloat16),
            v_h,
            preferred_element_type=jnp.float32,
        )
        fresh_max = fresh_max.reshape(rows)
        fresh_sum = fresh_sum.reshape(rows)
        fresh_out = fresh_out.reshape(rows, sub_width)

        top = jnp.maximum(jnp.max(got_max, axis=0), fresh_max)
        scale_cache = jnp.exp(got_max - top[None, :])
        scale_fresh = jnp.exp(fresh_max - top)
        denom = jnp.sum(got_sum * scale_cache, axis=0) + fresh_sum * scale_fresh
        numer = jnp.sum(got_out * scale_cache[:, None, :], axis=0).T + fresh_out * scale_fresh[:, None]
        my_cols = (numer / denom[:, None]).astype(jnp.bfloat16)

        update = jnp.dot(my_cols, w_out[layer_index], preferred_element_type=jnp.float32)
        update = update + jnp.dot(activated, w_fc2[layer_index], preferred_element_type=jnp.float32)
        update = allreduce_chip(
            update.astype(jnp.bfloat16).reshape(2, all_count // 2, -1, 128), tp_count
        )
        hidden_state = hidden_state + update.reshape(rows, width).astype(jnp.float32)
    return hidden_state.reshape(requests, new_tokens, width)


def solution(mesh):
    in_specs = (
        P(),
        P(("seq", "tp"), None),
        P(),
        P(),
        P(),
        P("seq", None),
        P(None, "seq", "tp"),
        P(None, "seq", "tp"),
        P(),
        P(),
        P(None, "seq", None, "tp"),
        P(None, "seq", "tp"),
        P(None, "tp"),
        P(None, ("tp", "seq"), None),
        P(None, ("tp", "seq"), None),
    )
    out_specs = P()
    return jax.shard_map(
        per_device, mesh=mesh, in_specs=in_specs, out_specs=out_specs, check_vma=False
    )
```
